32 devices in a mesh: replica: 4 (over y, x), fsdp: 8 (over z, core).
Axes of the slice: x: 2, y: 2, z: 4, core: 2. Of those that a mesh axis runs over, the one named last changes fastest.
Arguments:
- tokens: bfloat16 [16384, 2048], P(('replica', 'fsdp')), may hold values from -6 to 6
- segments: int32 [16384], P(('replica', 'fsdp')), may hold values from 0 to 8, as said below
- positions: int32 [16384], P(('replica', 'fsdp')), may hold values from 0 to 2431, as said below
- query_weight: bfloat16 [2048, 2048], P('fsdp'), may hold values from -0.125 to 0.125
- key_weight: bfloat16 [2048, 128], P('fsdp'), may hold values from -0.125 to 0.125
- value_weight: bfloat16 [2048, 128], P('fsdp'), may hold values from -0.125 to 0.125
- output_weight: bfloat16 [2048, 2048], P('fsdp'), may hold values from -2 to 2
- attn_gain: bfloat16 [2048], P('fsdp'), may hold values from 0.5 to 1.5
- gate_weight: bfloat16 [2048, 5632], P(None, 'fsdp'), may hold values from -0.125 to 0.125
- up_weight: bfloat16 [2048, 5632], P(None, 'fsdp'), may hold values from -0.125 to 0.125
- down_weight: bfloat16 [5632, 2048], P('fsdp'), may hold values from -0.078125 to 0.078125
- ffn_gain: bfloat16 [2048], P('fsdp'), may hold values from 0.5 to 1.5
- grad_out: bfloat16 [16384, 2048], P(('replica', 'fsdp')), may hold values from -6 to 6
Outputs:
- layer_out: bfloat16 [16384, 2048], P(('replica', 'fsdp'))
- input_grad: float32 [16384, 2048], P(('replica', 'fsdp'))
- query_grad: float32 [2048, 2048], P('fsdp')
- key_grad: float32 [2048, 128], P('fsdp')
- value_grad: float32 [2048, 128], P('fsdp')
- output_grad: float32 [2048, 2048], P('fsdp')
- attn_gain_grad: float32 [2048], P('fsdp')
- gate_grad: float32 [2048, 5632], P(None, 'fsdp')
- up_grad: float32 [2048, 5632], P(None, 'fsdp')
- down_grad: float32 [5632, 2048], P('fsdp')
- ffn_gain_grad: float32 [2048], P('fsdp')
The draws below stay inside these ranges and needn't reach their ends.
Inputs may be any that keep to these rules, and one draw needn't show every extreme that they name: `segments`: each aligned block of 4096 tokens is one group: 2048 prompt tokens with segment 0, then continuations 1 to 8 in order, each of 128 to 384 tokens; some continuation of every group has exactly 384 tokens. `positions`: prompt tokens hold 0 to 2047 in order; the tokens of a continuation hold 2048, 2049 and so on.
All inputs are finite; a program needn't handle non-finite values.
Results may differ from the reference program's by a relative error of at most 0.023.
Values may be sent and summed in bfloat16 or wider, within the bound.
A program may use at most 448 MiB of HBM per device.

```python
import jax
import jax.numpy as jnp
from jax import lax

D = 2048
HEADS = 16
HD = 128
FF = 5632
PROMPT = 2048
CONT = 256
BRANCHES = 8
GROUP_TOK = 4096
TOKENS = 16384


def group_layout(key):
    group_count = TOKENS // GROUP_TOK
    pair_count = BRANCHES // 2
    shift_key, flip_key = jax.random.split(jax.random.fold_in(key, 11))
    shifts = jax.random.randint(shift_key, (group_count, pair_count), 0, CONT // 2 + 1)
    shifts = shifts.at[:, 0].set(CONT // 2)
    flipped = jax.random.randint(flip_key, (group_count, pair_count), 0, 2)
    signed = shifts * (1 - 2 * flipped)
    lengths = jnp.stack([CONT + signed, CONT - signed], axis=2).reshape(group_count, BRANCHES)
    seg_ends = PROMPT + jnp.cumsum(lengths, axis=1)
    seg_starts = seg_ends - lengths
    local_index = jnp.arange(GROUP_TOK, dtype=jnp.int32)
    seg_ids = jnp.sum((local_index[None, :, None] >= seg_starts[:, None, :]).astype(jnp.int32), axis=2)
    labels = jnp.arange(1, BRANCHES + 1, dtype=jnp.int32)
    begins = jnp.sum(jnp.where(seg_ids[:, :, None] == labels[None, None, :], seg_starts[:, None, :], 0), axis=2)
    pos_ids = jnp.where(seg_ids == 0, local_index[None, :], PROMPT + local_index[None, :] - begins)
    return (seg_ids.reshape(-1).astype(jnp.int32), pos_ids.reshape(-1).astype(jnp.int32))


def draw_segments(key, part):
    return group_layout(key)[0]


def draw_positions(key, part):
    return group_layout(key)[1]


def block_levels(stream_key, extent, pieces, smallest, largest):
    def one(axis_at, shards_of):
        draws = jax.random.uniform(jax.random.fold_in(jax.random.fold_in(stream_key, 6), axis_at), (shards_of,), jnp.float32, smallest / len(pieces), largest / len(pieces))
        return jnp.repeat(jnp.exp(draws), extent[axis_at] // shards_of).reshape((-1,) + (1,) * (len(extent) - axis_at - 1))

    level = one(*pieces[0])
    for cut in pieces[1:]:
        level = level * one(*cut)
    return level


def noise(own_key, extent, spread, reach, cuts=(), kind=jnp.bfloat16):
    array = jax.random.normal(own_key, extent, jnp.float32) * spread
    if len(cuts) > 0:
        array = block_levels(own_key, extent, cuts, -0.22, 0.18) * array
    return jnp.clip(array, min=-reach, max=reach).astype(kind)


def setup_inputs(seed: int = 0) -> dict:
    arg_keys = jax.random.split(jax.random.key(seed), 14)
    tokens = noise(arg_keys[0], (TOKENS, D), 1.0, 6.0, ((0, 32),))
    segments = draw_segments(jax.random.fold_in(arg_keys[13], 71), 0)
    positions = draw_positions(jax.random.fold_in(arg_keys[13], 71), 0)
    query_weight = noise(arg_keys[3], (D, D), D ** -0.5, 0.125, ((0, 8),))
    key_weight = noise(arg_keys[4], (D, HD), D ** -0.5, 0.125, ((0, 8),))
    value_weight = noise(arg_keys[5], (D, HD), D ** -0.5, 0.125, ((0, 8),))
    output_weight = noise(arg_keys[6], (D, D), (max(D // 256, 1)) ** -0.5, 2.0, ((0, 8),))
    attn_gain = jnp.clip(1.0 + 0.1 * jax.random.normal(arg_keys[7], (D,), jnp.float32), 0.5, 1.5).astype(jnp.bfloat16)
    gate_weight = noise(arg_keys[8], (D, FF), D ** -0.5, 0.125, ((1, 8),))
    up_weight = noise(arg_keys[9], (D, FF), D ** -0.5, 0.125, ((1, 8),))
    down_weight = noise(arg_keys[10], (FF, D), FF ** -0.5, 0.078125, ((0, 8),))
    ffn_gain = jnp.clip(1.0 + 0.1 * jax.random.normal(arg_keys[11], (D,), jnp.float32), 0.5, 1.5).astype(jnp.bfloat16)
    grad_out = noise(arg_keys[12], (TOKENS, D), 1.0, 6.0, ((0, 32),))
    return dict(tokens=tokens, segments=segments, positions=positions, query_weight=query_weight, key_weight=key_weight, value_weight=value_weight, output_weight=output_weight, attn_gain=attn_gain, gate_weight=gate_weight, up_weight=up_weight, down_weight=down_weight, ffn_gain=ffn_gain, grad_out=grad_out)


@jax.custom_vjp
def low(v):
    return lax.optimization_barrier(v.astype(jnp.bfloat16)).astype(jnp.float32)

@jax.custom_vjp
def low_back(v):
    return v

def low_keep(v):
    return (low(v), None)

def low_pass(kept, grad):
    return (grad,)

def back_keep(v):
    return (v, None)

def back_low(kept, grad):
    return (low(grad),)
low.defvjp(low_keep, low_pass)
low_back.defvjp(back_keep, back_low)
EPSILON = 1e-05
ROPE_BASE = 10000.0
MASKED = -1e+30

def product(left, right):
    return jnp.dot(left, right, precision=lax.Precision.HIGHEST)

def rms_norm(values, gain):
    return values * lax.rsqrt(lax.optimization_barrier(jnp.mean(values * values, axis=-1, keepdims=True)) + EPSILON) * gain

def rope_tables(pos_ids, head_dim):
    half_width = head_dim // 2
    frequency = ROPE_BASE ** (-jnp.arange(half_width, dtype=jnp.float32) * 2.0 / head_dim)
    angles = pos_ids.astype(jnp.float32)[:, None] * frequency[None, :]
    return (jnp.cos(angles), jnp.sin(angles))

def rotate(values, cos_table, sin_table):
    half_width = values.shape[-1] // 2
    front_half = values[..., :half_width]
    back_half = values[..., half_width:]
    return jnp.concatenate([front_half * cos_table - back_half * sin_table, back_half * cos_table + front_half * sin_table], axis=-1)

def attend_group(operands):
    queries, key_rot, value_rows, seg_ids, pos_ids = operands
    visible = (pos_ids[None, :] <= pos_ids[:, None]) & ((seg_ids[None, :] == 0) | (seg_ids[None, :] == seg_ids[:, None]))
    scores = low_back(jnp.einsum('qhd,kd->hqk', queries, key_rot, precision=lax.Precision.HIGHEST) * HD ** (-0.5))
    scores = jnp.where(visible[None], scores, MASKED)
    weights = low(jax.nn.softmax(scores, axis=-1))
    return jnp.einsum('hqk,kd->qhd', weights, value_rows, precision=lax.Precision.HIGHEST)

def reference(tokens, segments, positions, query_weight, key_weight, value_weight, output_weight, attn_gain, gate_weight, up_weight, down_weight, ffn_gain, grad_out):
    cos_table, sin_table = rope_tables(positions, HD)
    groups = TOKENS // GROUP_TOK

    def forward(inputs, w_query, w_key, w_value, w_out, gain_attn, w_gate, w_up, w_down, gain_ffn):
        normed = low(rms_norm(inputs, gain_attn))
        query_raw = low_back(product(normed, w_query))
        key_raw = low_back(product(normed, w_key))
        value_rows = low(low_back(product(normed, w_value)))
        queries = low(rotate(query_raw.reshape(TOKENS, HEADS, HD), cos_table[:, None], sin_table[:, None]))
        key_rot = low(rotate(key_raw, cos_table, sin_table))
        mixed_rows = lax.map(jax.checkpoint(attend_group), (queries.reshape(groups, GROUP_TOK, HEADS, HD), key_rot.reshape(groups, GROUP_TOK, HD), value_rows.reshape(groups, GROUP_TOK, HD), segments.reshape(groups, GROUP_TOK), positions.reshape(groups, GROUP_TOK)))
        mixed_rows = low(low_back(mixed_rows.reshape(TOKENS, D)))
        branch = low_back(product(mixed_rows, w_out))
        hidden = inputs + branch
        normed_ffn = low(rms_norm(hidden, gain_ffn))
        gate_proj = low_back(product(normed_ffn, w_gate))
        up_proj = low_back(product(normed_ffn, w_up))
        activation = low(jax.nn.silu(gate_proj) * up_proj)
        return hidden + product(activation, w_down)
    result, pullback = jax.vjp(forward, tokens.astype(jnp.float32), query_weight.astype(jnp.float32), key_weight.astype(jnp.float32), value_weight.astype(jnp.float32), output_weight.astype(jnp.float32), attn_gain.astype(jnp.float32), gate_weight.astype(jnp.float32), up_weight.astype(jnp.float32), down_weight.astype(jnp.float32), ffn_gain.astype(jnp.float32))
    gradients = pullback(grad_out.astype(jnp.float32))
    return (result.astype(jnp.bfloat16), gradients[0], gradients[1], gradients[2], gradients[3], gradients[4], gradients[5], gradients[6], gradients[7], gradients[8], gradients[9])
```

```python
import functools

import jax
import jax.numpy as jnp
from jax import lax
from jax.experimental import pallas as pl
from jax.experimental.pallas import tpu as pltpu
from jax.sharding import PartitionSpec as P

GROUP_TOK = 4096
PROMPT = 2048
MAX_CONT = 384
EPSILON = 1e-05
ROPE_BASE = 10000.0
MASKED = -1e30
LOG2E = 1.4426950408889634

TILE = 128
CHUNK = 512
HEAD_GROUP = 4


def matmul(left, right):
    return jnp.dot(left, right, preferred_element_type=jnp.float32)


def contract(left, right, left_dim, right_dim):
    return lax.dot_general(
        left, right, (((left_dim,), (right_dim,)), ((), ())), preferred_element_type=jnp.float32
    )


def rope_tables(pos_ids, head_dim):
    half_width = head_dim // 2
    frequency = ROPE_BASE ** (-jnp.arange(half_width, dtype=jnp.float32) * 2.0 / head_dim)
    angles = pos_ids.astype(jnp.float32)[:, None] * frequency[None, :]
    cos_half, sin_half = jnp.cos(angles), jnp.sin(angles)
    return (
        jnp.concatenate([cos_half, cos_half], axis=1),
        jnp.concatenate([-sin_half, sin_half], axis=1),
    )


def swap_halves(values):
    half_width = values.shape[-1] // 2
    return jnp.concatenate([values[..., half_width:], values[..., :half_width]], axis=-1)


def norm_forward(values, gain):
    inverse = lax.rsqrt(jnp.mean(values * values, axis=-1, keepdims=True) + EPSILON)
    return (values * inverse * gain, inverse)


def norm_backward(values, inverse, gain, grad):
    scaled = grad * gain
    inner_mean = jnp.mean(scaled * values, axis=-1, keepdims=True)
    return (
        inverse * scaled - values * inverse**3 * inner_mean,
        jnp.sum(grad * values * inverse, axis=0),
    )


def swiglu_back(d_activation, gate_proj, up_proj):
    sigmoid_gate = jax.nn.sigmoid(gate_proj)
    d_gate = (
        d_activation * up_proj * sigmoid_gate * (1.0 + gate_proj * (1.0 - sigmoid_gate))
    ).astype(jnp.bfloat16)
    d_up = (d_activation * gate_proj * sigmoid_gate).astype(jnp.bfloat16)
    return (d_gate, d_up)


def stack_heads(block):
    heads = block.shape[1] // 128
    return jnp.concatenate([block[:, h * 128 : (h + 1) * 128] for h in range(heads)], axis=0)


def chunk_plan(base_ref):
    first = base_ref[0] + pl.program_id(0) * TILE
    in_prompt = first < PROMPT
    full = jnp.where(in_prompt, first // CHUNK, PROMPT // CHUNK)
    last = jnp.where(
        in_prompt, first // CHUNK * CHUNK, jnp.maximum(PROMPT, first + TILE - CHUNK)
    )
    return first, full, pl.multiple_of(last, TILE)


def attend_kernel(
    base_ref, q_ref, kv_ref, cos_ref, sin_ref, low_ref, mixed_ref, rot_ref, log_ref, values, top, acc
):
    factor = 128**-0.5 * LOG2E

    @pl.when((pl.program_id(0) == 0) & (pl.program_id(1) == 0))
    def _():
        values[:, :128] = kv_ref[:, 128:]
        values[:, 128:] = jnp.ones_like(values[:, 128:])

    first, full, last = chunk_plan(base_ref)
    cos_table, sin_table = cos_ref[...], sin_ref[...]
    pieces = []
    for h in range(HEAD_GROUP):
        raw = q_ref[:, h * 128 : (h + 1) * 128]
        turned = raw * cos_table + pltpu.roll(raw, 64, 1) * sin_table
        turned = turned.astype(jnp.bfloat16)
        rot_ref[:, h * 128 : (h + 1) * 128] = turned
        pieces.append(turned)
    queries = jnp.concatenate(pieces, axis=0)
    rows = queries.shape[0]
    top[...] = jnp.full_like(top, MASKED)
    acc[...] = jnp.zeros_like(acc)

    def step(start, masked):
        scores = contract(queries, kv_ref[pl.ds(start, CHUNK), :128], 1, 1) * factor
        if masked:
            key_at = start + lax.broadcasted_iota(jnp.int32, (rows, CHUNK), 1)
            row_at = lax.broadcasted_iota(jnp.int32, (rows, 1), 0) % TILE + first
            low = jnp.concatenate([low_ref[:, :1]] * HEAD_GROUP, axis=0)
            scores = jnp.where((key_at <= row_at) & (key_at >= low), scores, MASKED)
        before = top[:, :1]
        after = jnp.maximum(before, jnp.max(scores, axis=1, keepdims=True))
        weights = jnp.exp2(scores - after).astype(jnp.bfloat16)
        acc[...] = acc[...] * jnp.exp2(before - after) + matmul(
            weights, values[pl.ds(start, CHUNK), :]
        )
        top[...] = jnp.broadcast_to(after, top.shape)

    @pl.loop(0, full)
    def _(at):
        step(pl.multiple_of(at * CHUNK, CHUNK), False)

    step(last, True)
    total = acc[:, 128:]
    mixed = acc[:, :128] / total
    for h in range(HEAD_GROUP):
        mixed_ref[:, h * 128 : (h + 1) * 128] = mixed[h * TILE : (h + 1) * TILE].astype(jnp.bfloat16)
    log_ref[0, 0] = (top[...] + jnp.log2(total)).T[:8]


def attend(base, q_raw, kv, cos_table, sin_table, low):
    tok_rows, width = q_raw.shape
    tiles, groups = tok_rows // TILE, width // (128 * HEAD_GROUP)
    lanes, rows = 128 * HEAD_GROUP, TILE * HEAD_GROUP
    tile_spec = pl.BlockSpec((TILE, lanes), lambda i, g, b: (i, g))
    row_spec = pl.BlockSpec((TILE, 128), lambda i, g, b: (i, 0))
    pairs = tok_rows * (width // 128) * 2560
    return pl.pallas_call(
        attend_kernel,
        out_shape=(
            jax.ShapeDtypeStruct((tok_rows, width), jnp.bfloat16),
            jax.ShapeDtypeStruct((tok_rows, width), jnp.bfloat16),
            jax.ShapeDtypeStruct((tiles, groups, 8, rows), jnp.float32),
        ),
        grid_spec=pltpu.PrefetchScalarGridSpec(
            num_scalar_prefetch=1,
            grid=(tiles, groups),
            in_specs=[
                tile_spec,
                pl.BlockSpec(kv.shape, lambda i, g, b: (0, 0)),
                row_spec,
                row_spec,
                row_spec,
            ],
            out_specs=[
                tile_spec,
                tile_spec,
                pl.BlockSpec((1, 1, 8, rows), lambda i, g, b: (i, g, 0, 0)),
            ],
            scratch_shapes=[
                pltpu.VMEM(kv.shape, jnp.bfloat16),
                pltpu.VMEM((rows, 128), jnp.float32),
                pltpu.VMEM((rows, 256), jnp.float32),
            ],
        ),
        compiler_params=pltpu.CompilerParams(vmem_limit_bytes=40 << 20),
        cost_estimate=pl.CostEstimate(
            flops=pairs * 768, transcendentals=pairs, bytes_accessed=16 << 20
        ),
        name="attend",
    )(base, q_raw, kv, cos_table, sin_table, low)


def attend_back_kernel(
    base_ref,
    q_ref,
    kv_ref,
    cos_ref,
    sin_ref,
    low_ref,
    mixed_ref,
    d_mixed_ref,
    log_ref,
    d_q_ref,
    d_kv_ref,
    sums,
    d_q,
):
    scale = 128**-0.5
    factor = scale * LOG2E
    at_start = (pl.program_id(0) == 0) & (pl.program_id(1) == 0)
    at_end = (pl.program_id(0) == pl.num_programs(0) - 1) & (
        pl.program_id(1) == pl.num_programs(1) - 1
    )

    @pl.when(at_start)
    def _():
        sums[...] = jnp.zeros_like(sums)

    first, full, last = chunk_plan(base_ref)
    queries = stack_heads(q_ref[...])
    d_rows = stack_heads(d_mixed_ref[...])
    mixed = stack_heads(mixed_ref[...])
    rows = queries.shape[0]
    products = d_rows.astype(jnp.float32) * mixed.astype(jnp.float32)
    delta = jnp.sum(products.T, axis=0, keepdims=True)
    log_total = log_ref[0, 0, :1]
    d_q[...] = jnp.zeros_like(d_q)

    def step(start, masked):
        keys = kv_ref[pl.ds(start, CHUNK), :128]
        values = kv_ref[pl.ds(start, CHUNK), 128:]
        scores = contract(keys, queries, 1, 1) * factor
        probs = jnp.exp2(scores - log_total)
        if masked:
            key_at = start + lax.broadcasted_iota(jnp.int32, (CHUNK, rows), 0)
            row_at = lax.broadcasted_iota(jnp.int32, (1, rows), 1) % TILE + first
            low = jnp.concatenate([low_ref[:1]] * HEAD_GROUP, axis=1)
            probs = jnp.where((key_at <= row_at) & (key_at >= low), probs, 0.0)
        d_probs = contract(values, d_rows, 1, 1)
        d_scores = (probs * (d_probs - delta)).astype(jnp.bfloat16)
        sums[pl.ds(start, CHUNK), 128:] += matmul(probs.astype(jnp.bfloat16), d_rows)
        sums[pl.ds(start, CHUNK), :128] += matmul(d_scores, queries)
        d_q[...] += contract(d_scores, keys, 0, 0)

    @pl.loop(0, full)
    def _(at):
        step(pl.multiple_of(at * CHUNK, CHUNK), False)

    step(last, True)
    cos_table, sin_table = cos_ref[...] * scale, sin_ref[...] * scale
    for h in range(HEAD_GROUP):
        turned = d_q[h * TILE : (h + 1) * TILE]
        raw = turned * cos_table - pltpu.roll(turned, 64, 1) * sin_table
        d_q_ref[:, h * 128 : (h + 1) * 128] = raw.astype(jnp.bfloat16)

    @pl.when(at_end)
    def _():
        d_kv_ref[:, :128] = (sums[:, :128] * scale).astype(jnp.bfloat16)
        d_kv_ref[:, 128:] = sums[:, 128:].astype(jnp.bfloat16)


def attend_back(base, queries, kv, cos_table, sin_table, low, mixed, d_mixed, logs):
    tok_rows, width = queries.shape
    tiles, groups = tok_rows // TILE, width // (128 * HEAD_GROUP)
    lanes, rows = 128 * HEAD_GROUP, TILE * HEAD_GROUP
    tile_spec = pl.BlockSpec((TILE, lanes), lambda i, g, b: (i, g))
    row_spec = pl.BlockSpec((TILE, 128), lambda i, g, b: (i, 0))
    whole = pl.BlockSpec(kv.shape, lambda i, g, b: (0, 0))
    pairs = tok_rows * (width // 128) * 2560
    return pl.pallas_call(
        attend_back_kernel,
        out_shape=(
            jax.ShapeDtypeStruct((tok_rows, width), jnp.bfloat16),
            jax.ShapeDtypeStruct(kv.shape, jnp.bfloat16),
        ),
        grid_spec=pltpu.PrefetchScalarGridSpec(
            num_scalar_prefetch=1,
            grid=(tiles, groups),
            in_specs=[
                tile_spec,
                whole,
                row_spec,
                row_spec,
                pl.BlockSpec((8, TILE), lambda i, g, b: (0, i)),
                tile_spec,
                tile_spec,
                pl.BlockSpec((1, 1, 8, rows), lambda i, g, b: (i, g, 0, 0)),
            ],
            out_specs=[tile_spec, whole],
            scratch_shapes=[
                pltpu.VMEM(kv.shape, jnp.float32),
                pltpu.VMEM((rows, 128), jnp.float32),
            ],
        ),
        compiler_params=pltpu.CompilerParams(vmem_limit_bytes=48 << 20),
        cost_estimate=pl.CostEstimate(
            flops=pairs * 1280, transcendentals=pairs, bytes_accessed=16 << 20
        ),
        name="attend_back",
    )(base, queries, kv, cos_table, sin_table, low, mixed, d_mixed, logs)


def swap(value, step):
    copies = lax.axis_size("replica")
    return lax.ppermute(value, "replica", [(r, r ^ step) for r in range(copies)])


def gather_copies(block):
    half = block.shape[0] // 2
    beside, across = swap(block, 1), swap(block, 2)
    opposite = jnp.concatenate([swap(beside[:half], 2), swap(across[half:], 1)], axis=0)
    return [block, beside, across, opposite]


def scatter_copies(parts):
    own, beside, across, opposite = parts
    half = opposite.shape[0] // 2
    low = jnp.bfloat16
    first = swap(opposite[:half].astype(low), 1)
    second = swap(opposite[half:].astype(low), 2)
    across = jnp.concatenate(
        [across[:half].astype(jnp.float32) + first.astype(jnp.float32), across[half:]], axis=0
    )
    beside = jnp.concatenate(
        [beside[:half], beside[half:].astype(jnp.float32) + second.astype(jnp.float32)], axis=0
    )
    return (
        own.astype(jnp.float32)
        + swap(beside.astype(low), 1).astype(jnp.float32)
        + swap(across.astype(low), 2).astype(jnp.float32)
    )


def gather_shards(value):
    return lax.all_gather(value, "fsdp", axis=0, tiled=True)


def scatter_shards(value):
    return lax.psum_scatter(value, "fsdp", scatter_dimension=0, tiled=True)


def place(pieces, copy_index):
    out = jnp.zeros((len(pieces),) + pieces[0].shape, pieces[0].dtype)
    for step, piece in enumerate(pieces):
        out = lax.dynamic_update_index_in_dim(out, piece, copy_index ^ step, 0)
    return out


def quarter(shard, copy_index):
    rows = shard.shape[0] // lax.axis_size("replica")
    return lax.dynamic_slice_in_dim(shard, copy_index * rows, rows, 0)


def whole_weight(shard, copy_index):
    rows, width = shard.shape
    copies, fsdp_size = lax.axis_size("replica"), lax.axis_size("fsdp")
    pieces = gather_copies(gather_shards(quarter(shard, copy_index)))
    out = jnp.zeros((fsdp_size, copies, rows // copies, width), shard.dtype)
    for step, piece in enumerate(pieces):
        out = lax.dynamic_update_slice_in_dim(
            out, piece.reshape(fsdp_size, 1, rows // copies, width), copy_index ^ step, 1
        )
    return out.reshape(fsdp_size * rows, width)


def sum_weight_grad(partial, copy_index):
    rows, width = partial.shape
    copies, fsdp_size = lax.axis_size("replica"), lax.axis_size("fsdp")
    fine = rows // (copies * fsdp_size)
    view = partial.reshape(fsdp_size, copies, fine, width)
    parts = [
        lax.dynamic_slice_in_dim(view, copy_index ^ step, 1, 1).reshape(fsdp_size * fine, width)
        for step in range(copies)
    ]
    summed = scatter_shards(scatter_copies(parts).astype(jnp.bfloat16))
    return place(gather_copies(summed), copy_index).reshape(copies * fine, width).astype(jnp.float32)


def shards(
    tokens,
    segments,
    positions,
    query_weight,
    key_weight,
    value_weight,
    output_weight,
    attn_gain,
    gate_weight,
    up_weight,
    down_weight,
    ffn_gain,
    grad_out,
):
    tok_rows, model_width = tokens.shape
    head_dim = key_weight.shape[1]
    fsdp_size = lax.axis_size("fsdp")
    fsdp_index = lax.axis_index("fsdp")
    copy_index = lax.axis_index("replica")
    copies = lax.axis_size("replica")
    low = jnp.bfloat16

    gains = lax.all_gather(jnp.stack([attn_gain, ffn_gain]), "fsdp", axis=1, tiled=True)
    gain_attn = gains[0].astype(jnp.float32)
    gain_ffn = gains[1].astype(jnp.float32)
    w_qkv = whole_weight(
        jnp.concatenate([query_weight, key_weight, value_weight], axis=1), copy_index
    )
    inputs = tokens.astype(jnp.float32)
    normed_full, inverse_attn = norm_forward(inputs, gain_attn)
    normed = normed_full.astype(low)
    qkv = matmul(normed, w_qkv)
    query_raw = qkv[:, :model_width]
    key_raw = qkv[:, model_width : model_width + head_dim]
    value_rows = qkv[:, model_width + head_dim :].astype(low)
    cos_table, sin_table = rope_tables(positions, head_dim)
    key_rot = (key_raw * cos_table + swap_halves(key_raw) * sin_table).astype(low)
    kv_all = gather_shards(jnp.concatenate([key_rot, value_rows], axis=1))
    key_width = max(GROUP_TOK, tok_rows)
    window_start = fsdp_index * tok_rows // key_width * key_width
    one_group = fsdp_size * tok_rows == key_width
    kv = kv_all if one_group else lax.dynamic_slice_in_dim(kv_all, window_start, key_width, 0)

    base = (fsdp_index * tok_rows - window_start).astype(jnp.int32)
    row_at = base + jnp.arange(tok_rows, dtype=jnp.int32)
    lowest = jnp.where(positions < PROMPT, 0, row_at - (positions - PROMPT))
    base = base[None]
    mixed_rows, queries, logs = attend(
        base,
        query_raw,
        kv,
        cos_table,
        sin_table,
        jnp.broadcast_to(lowest[:, None], (tok_rows, 128)),
    )

    w_out = whole_weight(output_weight, copy_index)
    hidden = inputs + matmul(mixed_rows, w_out)
    normed_ffn_full, inverse_ffn = norm_forward(hidden, gain_ffn)
    normed_ffn = normed_ffn_full.astype(low)

    w_gate = gather_shards(quarter(gate_weight.T, copy_index))
    w_up = gather_shards(quarter(up_weight.T, copy_index))
    w_down = gather_shards(quarter(down_weight, copy_index))
    grad_blocks = gather_copies(grad_out)
    grads = jnp.concatenate(grad_blocks, axis=0)
    normed_blocks = gather_copies(normed_ffn)
    normed_all = jnp.concatenate(normed_blocks, axis=0)

    d_activation = contract(grads, w_down, 1, 1)
    gate_proj = contract(normed_all, w_gate, 1, 1)
    up_proj = contract(normed_all, w_up, 1, 1)
    activation = (jax.nn.silu(gate_proj) * up_proj).astype(low)
    d_gate, d_up = swiglu_back(d_activation, gate_proj, up_proj)
    d_normed_parts = matmul(d_gate, w_gate) + matmul(d_up, w_up)
    d_normed_ffn = scatter_copies(jnp.split(d_normed_parts, copies))
    out_parts = matmul(activation, w_down)
    layer_out = (hidden + scatter_copies(jnp.split(out_parts, copies))).astype(low)

    def ffn_grad(partial):
        summed = scatter_shards(partial.astype(low))
        pieces = place(gather_copies(summed), copy_index)
        return pieces.reshape(-1, model_width).astype(jnp.float32)

    gate_grad = ffn_grad(contract(d_gate, normed_all, 0, 0)).T
    up_grad = ffn_grad(contract(d_up, normed_all, 0, 0)).T
    down_grad = ffn_grad(contract(activation, grads, 0, 0))

    cotangent = grad_out.astype(jnp.float32)
    resid_ffn, ffn_gain_term = norm_backward(hidden, inverse_ffn, gain_ffn, d_normed_ffn)
    d_hidden = cotangent + resid_ffn
    d_branch = d_hidden.astype(low)
    d_mixed = contract(d_branch, w_out, 1, 1).astype(low)
    output_grad = sum_weight_grad(contract(mixed_rows, d_branch, 0, 0), copy_index)

    d_query_raw, d_kv = attend_back(
        base,
        queries,
        kv,
        cos_table,
        sin_table,
        jnp.broadcast_to(lowest[None, :], (8, tok_rows)),
        mixed_rows,
        d_mixed,
        logs,
    )
    query_grad = sum_weight_grad(contract(normed, d_query_raw, 0, 0), copy_index)
    if not one_group:
        d_kv = lax.dynamic_update_slice_in_dim(
            jnp.zeros((fsdp_size * tok_rows, 2 * head_dim), low), d_kv, window_start, 0
        )
    d_kv_sum = scatter_shards(d_kv).astype(jnp.float32)
    d_key = d_kv_sum[:, :head_dim]
    d_key_raw = (d_key * cos_table - swap_halves(d_key) * sin_table).astype(low)
    d_kv_raw = jnp.concatenate([d_key_raw, d_kv_sum[:, head_dim:].astype(low)], axis=1)
    kv_grad = sum_weight_grad(contract(normed, d_kv_raw, 0, 0), copy_index)
    d_normed = contract(d_query_raw, w_qkv[:, :model_width], 1, 1) + contract(
        d_kv_raw, w_qkv[:, model_width:], 1, 1
    )
    resid_attn, attn_gain_term = norm_backward(inputs, inverse_attn, gain_attn, d_normed)
    input_grad = d_hidden + resid_attn
    gain_terms = lax.psum(jnp.stack([attn_gain_term, ffn_gain_term]), ("replica", "fsdp"))
    gain_grads = lax.dynamic_slice_in_dim(
        gain_terms, fsdp_index * (model_width // fsdp_size), model_width // fsdp_size, 1
    )
    return (
        layer_out,
        input_grad,
        query_grad,
        kv_grad[:, :head_dim],
        kv_grad[:, head_dim:],
        output_grad,
        gain_grads[0],
        gate_grad,
        up_grad,
        down_grad,
        gain_grads[1],
    )


def solution(mesh):
    return jax.shard_map(
        shards,
        mesh=mesh,
        in_specs=(
            P(("replica", "fsdp"), None),
            P(("replica", "fsdp")),
            P(("replica", "fsdp")),
            P("fsdp", None),
            P("fsdp", None),
            P("fsdp", None),
            P("fsdp", None),
            P("fsdp"),
            P(None, "fsdp"),
            P(None, "fsdp"),
            P("fsdp", None),
            P("fsdp"),
            P(("replica", "fsdp"), None),
        ),
        out_specs=(
            P(("replica", "fsdp"), None),
            P(("replica", "fsdp"), None),
            P("fsdp", None),
            P("fsdp", None),
            P("fsdp", None),
            P("fsdp", None),
            P("fsdp"),
            P(None, "fsdp"),
            P(None, "fsdp"),
            P("fsdp", None),
            P("fsdp"),
        ),
        check_vma=False,
    )
```

```python
import functools

import jax
import jax.numpy as jnp
from jax import lax
from jax.experimental import pallas as pl
from jax.experimental.pallas import tpu as pltpu
from jax.sharding import PartitionSpec as P

GROUP_TOK = 4096
PROMPT = 2048
MAX_CONT = 384
EPSILON = 1e-05
ROPE_BASE = 10000.0
MASKED = -1e30
LOG2E = 1.4426950408889634

TILE = 128
CHUNK = 512
HEAD_GROUP = 4


def matmul(left, right):
    return jnp.dot(left, right, preferred_element_type=jnp.float32)


def contract(left, right, left_dim, right_dim):
    return lax.dot_general(
        left, right, (((left_dim,), (right_dim,)), ((), ())), preferred_element_type=jnp.float32
    )


def rope_tables(pos_ids, head_dim):
    half_width = head_dim // 2
    frequency = ROPE_BASE ** (-jnp.arange(half_width, dtype=jnp.float32) * 2.0 / head_dim)
    angles = pos_ids.astype(jnp.float32)[:, None] * frequency[None, :]
    cos_half, sin_half = jnp.cos(angles), jnp.sin(angles)
    return (
        jnp.concatenate([cos_half, cos_half], axis=1),
        jnp.concatenate([-sin_half, sin_half], axis=1),
    )


def swap_halves(values):
    half_width = values.shape[-1] // 2
    return jnp.concatenate([values[..., half_width:], values[..., :half_width]], axis=-1)


def norm_forward(values, gain):
    inverse = lax.rsqrt(jnp.mean(values * values, axis=-1, keepdims=True) + EPSILON)
    return (values * inverse * gain, inverse)


def norm_backward(values, inverse, gain, grad):
    scaled = grad * gain
    inner_mean = jnp.mean(scaled * values, axis=-1, keepdims=True)
    return (
        inverse * scaled - values * inverse**3 * inner_mean,
        jnp.sum(grad * values * inverse, axis=0),
    )


def swiglu_back(d_activation, gate_proj, up_proj):
    sigmoid_gate = jax.nn.sigmoid(gate_proj)
    d_gate = (
        d_activation * up_proj * sigmoid_gate * (1.0 + gate_proj * (1.0 - sigmoid_gate))
    ).astype(jnp.bfloat16)
    d_up = (d_activation * gate_proj * sigmoid_gate).astype(jnp.bfloat16)
    return (d_gate, d_up)


def stack_heads(block):
    heads = block.shape[1] // 128
    return jnp.concatenate([block[:, h * 128 : (h + 1) * 128] for h in range(heads)], axis=0)


def chunk_plan(base_ref):
    first = base_ref[0] + pl.program_id(0) * TILE
    in_prompt = first < PROMPT
    full = jnp.where(in_prompt, first // CHUNK, PROMPT // CHUNK)
    last = jnp.where(
        in_prompt, first // CHUNK * CHUNK, jnp.maximum(PROMPT, first + TILE - CHUNK)
    )
    return first, full, pl.multiple_of(last, TILE)


def attend_kernel(
    base_ref, q_ref, kv_ref, cos_ref, sin_ref, low_ref, mixed_ref, rot_ref, log_ref, values, top, acc
):
    factor = 128**-0.5 * LOG2E

    @pl.when((pl.program_id(0) == 0) & (pl.program_id(1) == 0))
    def _():
        values[:, :128] = kv_ref[:, 128:]
        values[:, 128:] = jnp.ones_like(values[:, 128:])

    first, full, last = chunk_plan(base_ref)
    cos_table, sin_table = cos_ref[...], sin_ref[...]
    pieces = []
    for h in range(HEAD_GROUP):
        raw = q_ref[:, h * 128 : (h + 1) * 128]
        turned = raw * cos_table + pltpu.roll(raw, 64, 1) * sin_table
        turned = turned.astype(jnp.bfloat16)
        rot_ref[:, h * 128 : (h + 1) * 128] = turned
        pieces.append(turned)
    queries = jnp.concatenate(pieces, axis=0)
    rows = queries.shape[0]
    top[...] = jnp.full_like(top, MASKED)
    acc[...] = jnp.zeros_like(acc)

    def step(start, masked):
        scores = contract(queries, kv_ref[pl.ds(start, CHUNK), :128], 1, 1) * factor
        if masked:
            key_at = start + lax.broadcasted_iota(jnp.int32, (rows, CHUNK), 1)
            row_at = lax.broadcasted_iota(jnp.int32, (rows, 1), 0) % TILE + first
            low = jnp.concatenate([low_ref[:, :1]] * HEAD_GROUP, axis=0)
            scores = jnp.where((key_at <= row_at) & (key_at >= low), scores, MASKED)
        before = top[:, :1]
        after = jnp.maximum(before, jnp.max(scores, axis=1, keepdims=True))
        weights = jnp.exp2(scores - after).astype(jnp.bfloat16)
        acc[...] = acc[...] * jnp.exp2(before - after) + matmul(
            weights, values[pl.ds(start, CHUNK), :]
        )
        top[...] = jnp.broadcast_to(after, top.shape)

    @pl.loop(0, full)
    def _(at):
        step(pl.multiple_of(at * CHUNK, CHUNK), False)

    step(last, True)
    total = acc[:, 128:]
    mixed = acc[:, :128] / total
    for h in range(HEAD_GROUP):
        mixed_ref[:, h * 128 : (h + 1) * 128] = mixed[h * TILE : (h + 1) * TILE].astype(jnp.bfloat16)
    log_ref[0, 0] = (top[...] + jnp.log2(total)).T[:8]


def attend(base, q_raw, kv, cos_table, sin_table, low):
    tok_rows, width = q_raw.shape
    tiles, groups = tok_rows // TILE, width // (128 * HEAD_GROUP)
    lanes, rows = 128 * HEAD_GROUP, TILE * HEAD_GROUP
    tile_spec = pl.BlockSpec((TILE, lanes), lambda i, g, b: (i, g))
    true_spec = pl.BlockSpec((TILE, lanes), lambda i, g, b: (i, g ^ b[1]))
    row_spec = pl.BlockSpec((TILE, 128), lambda i, g, b: (i, 0))
    pairs = tok_rows * (width // 128) * 2560
    return pl.pallas_call(
        attend_kernel,
        out_shape=(
            jax.ShapeDtypeStruct((tok_rows, width), jnp.bfloat16),
            jax.ShapeDtypeStruct((tok_rows, width), jnp.bfloat16),
            jax.ShapeDtypeStruct((tiles, groups, 8, rows), jnp.float32),
        ),
        grid_spec=pltpu.PrefetchScalarGridSpec(
            num_scalar_prefetch=1,
            grid=(tiles, groups),
            in_specs=[
                tile_spec,
                pl.BlockSpec(kv.shape, lambda i, g, b: (0, 0)),
                row_spec,
                row_spec,
                row_spec,
            ],
            out_specs=[
                true_spec,
                tile_spec,
                pl.BlockSpec((1, 1, 8, rows), lambda i, g, b: (i, g, 0, 0)),
            ],
            scratch_shapes=[
                pltpu.VMEM(kv.shape, jnp.bfloat16),
                pltpu.VMEM((rows, 128), jnp.float32),
                pltpu.VMEM((rows, 256), jnp.float32),
            ],
        ),
        compiler_params=pltpu.CompilerParams(vmem_limit_bytes=40 << 20),
        cost_estimate=pl.CostEstimate(
            flops=pairs * 768, transcendentals=pairs, bytes_accessed=16 << 20
        ),
        name="attend",
    )(base, q_raw, kv, cos_table, sin_table, low)


def attend_back_kernel(
    base_ref,
    q_ref,
    kv_ref,
    cos_ref,
    sin_ref,
    low_ref,
    mixed_ref,
    d_mixed_ref,
    log_ref,
    d_q_ref,
    d_kv_ref,
    sums,
    d_q,
):
    scale = 128**-0.5
    factor = scale * LOG2E
    at_start = (pl.program_id(0) == 0) & (pl.program_id(1) == 0)
    at_end = (pl.program_id(0) == pl.num_programs(0) - 1) & (
        pl.program_id(1) == pl.num_programs(1) - 1
    )

    @pl.when(at_start)
    def _():
        sums[...] = jnp.zeros_like(sums)

    first, full, last = chunk_plan(base_ref)
    queries = stack_heads(q_ref[...])
    d_rows = stack_heads(d_mixed_ref[...])
    mixed = stack_heads(mixed_ref[...])
    rows = queries.shape[0]
    products = d_rows.astype(jnp.float32) * mixed.astype(jnp.float32)
    delta = jnp.sum(products.T, axis=0, keepdims=True)
    log_total = log_ref[0, 0, :1]
    d_q[...] = jnp.zeros_like(d_q)

    def step(start, masked):
        keys = kv_ref[pl.ds(start, CHUNK), :128]
        values = kv_ref[pl.ds(start, CHUNK), 128:]
        scores = contract(keys, queries, 1, 1) * factor
        probs = jnp.exp2(scores - log_total)
        if masked:
            key_at = start + lax.broadcasted_iota(jnp.int32, (CHUNK, rows), 0)
            row_at = lax.broadcasted_iota(jnp.int32, (1, rows), 1) % TILE + first
            low = jnp.concatenate([low_ref[:1]] * HEAD_GROUP, axis=1)
            probs = jnp.where((key_at <= row_at) & (key_at >= low), probs, 0.0)
        d_probs = contract(values, d_rows, 1, 1)
        d_scores = (probs * (d_probs - delta)).astype(jnp.bfloat16)
        sums[pl.ds(start, CHUNK), 128:] += matmul(probs.astype(jnp.bfloat16), d_rows)
        sums[pl.ds(start, CHUNK), :128] += matmul(d_scores, queries)
        d_q[...] += contract(d_scores, keys, 0, 0)

    @pl.loop(0, full)
    def _(at):
        step(pl.multiple_of(at * CHUNK, CHUNK), False)

    step(last, True)
    cos_table, sin_table = cos_ref[...] * scale, sin_ref[...] * scale
    for h in range(HEAD_GROUP):
        turned = d_q[h * TILE : (h + 1) * TILE]
        raw = turned * cos_table - pltpu.roll(turned, 64, 1) * sin_table
        d_q_ref[:, h * 128 : (h + 1) * 128] = raw.astype(jnp.bfloat16)

    @pl.when(at_end)
    def _():
        d_kv_ref[:, :128] = (sums[:, :128] * scale).astype(jnp.bfloat16)
        d_kv_ref[:, 128:] = sums[:, 128:].astype(jnp.bfloat16)


def attend_back(base, queries, kv, cos_table, sin_table, low, mixed, d_mixed, logs):
    tok_rows, width = queries.shape
    tiles, groups = tok_rows // TILE, width // (128 * HEAD_GROUP)
    lanes, rows = 128 * HEAD_GROUP, TILE * HEAD_GROUP
    tile_spec = pl.BlockSpec((TILE, lanes), lambda i, g, b: (i, g))
    row_spec = pl.BlockSpec((TILE, 128), lambda i, g, b: (i, 0))
    true_spec = pl.BlockSpec((TILE, lanes), lambda i, g, b: (i, g ^ b[1]))
    whole = pl.BlockSpec(kv.shape, lambda i, g, b: (0, 0))
    pairs = tok_rows * (width // 128) * 2560
    return pl.pallas_call(
        attend_back_kernel,
        out_shape=(
            jax.ShapeDtypeStruct((tok_rows, width), jnp.bfloat16),
            jax.ShapeDtypeStruct(kv.shape, jnp.bfloat16),
        ),
        grid_spec=pltpu.PrefetchScalarGridSpec(
            num_scalar_prefetch=1,
            grid=(tiles, groups),
            in_specs=[
                tile_spec,
                whole,
                row_spec,
                row_spec,
                pl.BlockSpec((8, TILE), lambda i, g, b: (0, i)),
                true_spec,
                true_spec,
                pl.BlockSpec((1, 1, 8, rows), lambda i, g, b: (i, g, 0, 0)),
            ],
            out_specs=[tile_spec, whole],
            scratch_shapes=[
                pltpu.VMEM(kv.shape, jnp.float32),
                pltpu.VMEM((rows, 128), jnp.float32),
            ],
        ),
        compiler_params=pltpu.CompilerParams(vmem_limit_bytes=48 << 20),
        cost_estimate=pl.CostEstimate(
            flops=pairs * 1280, transcendentals=pairs, bytes_accessed=16 << 20
        ),
        name="attend_back",
    )(base, queries, kv, cos_table, sin_table, low, mixed, d_mixed, logs)


def swap(value, step):
    copies = lax.axis_size("replica")
    return lax.ppermute(value, "replica", [(r, r ^ step) for r in range(copies)])


def gather_copies(block):
    half = block.shape[0] // 2
    beside, across = swap(block, 1), swap(block, 2)
    opposite = jnp.concatenate([swap(beside[:half], 2), swap(across[half:], 1)], axis=0)
    return [block, beside, across, opposite]


def scatter_copies(parts):
    own, beside, across, opposite = parts
    half = opposite.shape[0] // 2
    low = jnp.bfloat16
    first = swap(opposite[:half].astype(low), 1)
    second = swap(opposite[half:].astype(low), 2)
    across = jnp.concatenate(
        [across[:half].astype(jnp.float32) + first.astype(jnp.float32), across[half:]], axis=0
    )
    beside = jnp.concatenate(
        [beside[:half], beside[half:].astype(jnp.float32) + second.astype(jnp.float32)], axis=0
    )
    return (
        own.astype(jnp.float32)
        + swap(beside.astype(low), 1).astype(jnp.float32)
        + swap(across.astype(low), 2).astype(jnp.float32)
    )


def gather_shards(value):
    return lax.all_gather(value, "fsdp", axis=0, tiled=True)


def scatter_shards(value):
    return lax.psum_scatter(value, "fsdp", scatter_dimension=0, tiled=True)


def reorder(pieces, copy_index):
    beside = (copy_index & 1) == 1
    across = (copy_index & 2) == 2
    a, b, c, d = pieces
    a, b, c, d = (
        jnp.where(beside, b, a),
        jnp.where(beside, a, b),
        jnp.where(beside, d, c),
        jnp.where(beside, c, d),
    )
    return [
        jnp.where(across, c, a),
        jnp.where(across, d, b),
        jnp.where(across, a, c),
        jnp.where(across, b, d),
    ]


def quarter(shard, copy_index, dim):
    size = shard.shape[dim] // lax.axis_size("replica")
    return lax.dynamic_slice_in_dim(shard, copy_index * size, size, dim)


def after(value, *others):
    return lax.optimization_barrier((value, others))[0]


def shards(
    tokens,
    segments,
    positions,
    query_weight,
    key_weight,
    value_weight,
    output_weight,
    attn_gain,
    gate_weight,
    up_weight,
    down_weight,
    ffn_gain,
    grad_out,
):
    tok_rows, model_width = tokens.shape
    head_dim = key_weight.shape[1]
    fsdp_size = lax.axis_size("fsdp")
    fsdp_index = lax.axis_index("fsdp")
    copy_index = lax.axis_index("replica")
    copies = lax.axis_size("replica")
    low = jnp.bfloat16
    lanes = model_width // copies

    w_kv = gather_shards(jnp.concatenate([key_weight, value_weight], axis=1))
    w_query = gather_copies(gather_shards(after(quarter(query_weight, copy_index, 1), w_kv)))
    gains = lax.all_gather(jnp.stack([attn_gain, ffn_gain]), "fsdp", axis=1, tiled=True)
    gain_attn = gains[0].astype(jnp.float32)
    gain_ffn = gains[1].astype(jnp.float32)
    inputs = tokens.astype(jnp.float32)
    normed_full, inverse_attn = norm_forward(inputs, gain_attn)
    normed = normed_full.astype(low)
    kv_raw = matmul(normed, w_kv)
    key_raw = kv_raw[:, :head_dim]
    value_rows = kv_raw[:, head_dim:].astype(low)
    cos_table, sin_table = rope_tables(positions, head_dim)
    key_rot = (key_raw * cos_table + swap_halves(key_raw) * sin_table).astype(low)
    kv_all = gather_shards(after(jnp.concatenate([key_rot, value_rows], axis=1), w_query[0]))
    key_width = max(GROUP_TOK, tok_rows)
    window_start = fsdp_index * tok_rows // key_width * key_width
    one_group = fsdp_size * tok_rows == key_width
    kv = kv_all if one_group else lax.dynamic_slice_in_dim(kv_all, window_start, key_width, 0)

    base = (fsdp_index * tok_rows - window_start).astype(jnp.int32)
    row_at = base + jnp.arange(tok_rows, dtype=jnp.int32)
    lowest = jnp.where(positions < PROMPT, 0, row_at - (positions - PROMPT))
    base = jnp.stack([base, copy_index.astype(jnp.int32)])
    w_out_quarter = gather_shards(after(quarter(output_weight, copy_index, 1), kv_all))
    w_down = gather_shards(after(quarter(down_weight, copy_index, 0), w_out_quarter))
    w_gate = gather_shards(after(quarter(gate_weight.T, copy_index, 0), w_down))
    w_up = gather_shards(after(quarter(up_weight.T, copy_index, 0), w_gate))
    query_raw = jnp.concatenate([matmul(normed, w) for w in w_query], axis=1)
    w_out = gather_copies(after(w_out_quarter, query_raw))
    grads = jnp.concatenate(gather_copies(after(grad_out, w_out[3])), axis=0)
    mixed_rows, queries, logs = attend(
        base,
        query_raw,
        kv,
        cos_table,
        sin_table,
        jnp.broadcast_to(lowest[:, None], (tok_rows, 128)),
    )

    branch = reorder([matmul(mixed_rows, w) for w in w_out], copy_index)
    hidden = inputs + jnp.concatenate(branch, axis=1)
    normed_ffn_full, inverse_ffn = norm_forward(hidden, gain_ffn)
    normed_ffn = normed_ffn_full.astype(low)

    normed_blocks = gather_copies(normed_ffn)
    d_activation = contract(after(grads, normed_ffn), w_down, 1, 1)
    normed_all = jnp.concatenate(after(normed_blocks, d_activation), axis=0)
    gate_proj = contract(normed_all, w_gate, 1, 1)
    up_proj = contract(normed_all, w_up, 1, 1)
    activation = (jax.nn.silu(gate_proj) * up_proj).astype(low)
    d_gate, d_up = swiglu_back(d_activation, gate_proj, up_proj)
    d_normed_parts = matmul(d_gate, w_gate) + matmul(d_up, w_up)
    own, beside, across, opposite = jnp.split(d_normed_parts, copies)
    half = tok_rows // 2
    first = swap(opposite[:half].astype(low), 1)
    second = swap(opposite[half:].astype(low), 2)
    beside_early = swap(beside[:half].astype(low), 1)
    across_early = swap(across[half:].astype(low), 2)
    gate_part = contract(d_gate, normed_all, 0, 0).astype(low)
    first = after(first, gate_part)
    second = after(second, gate_part)
    across_late = swap((across[:half] + first.astype(jnp.float32)).astype(low), 2)
    beside_late = swap((beside[half:] + second.astype(jnp.float32)).astype(low), 1)
    up_part = contract(after(d_up, gate_part), normed_all, 0, 0).astype(low)
    down_part = contract(after(activation, up_part), grads, 0, 0).astype(low)
    beside_late = after(beside_late, down_part)
    across_late = after(across_late, down_part)
    d_normed_ffn = (
        own
        + jnp.concatenate([beside_early, beside_late], axis=0).astype(jnp.float32)
        + jnp.concatenate([across_late, across_early], axis=0).astype(jnp.float32)
    )

    cotangent = grad_out.astype(jnp.float32)
    resid_ffn, ffn_gain_term = norm_backward(hidden, inverse_ffn, gain_ffn, d_normed_ffn)
    d_hidden = cotangent + resid_ffn
    d_branch = d_hidden.astype(low)
    d_branch_parts = reorder(jnp.split(d_branch, copies, axis=1), copy_index)
    d_mixed = sum(contract(d, w, 1, 1) for d, w in zip(d_branch_parts, w_out)).astype(low)

    gate_sum = scatter_shards(gate_part)
    up_sum = scatter_shards(after(up_part, gate_sum))
    d_query_raw, d_kv = attend_back(
        base,
        queries,
        kv,
        cos_table,
        sin_table,
        jnp.broadcast_to(lowest[None, :], (8, tok_rows)),
        mixed_rows,
        d_mixed,
        logs,
    )
    if not one_group:
        d_kv = lax.dynamic_update_slice_in_dim(
            jnp.zeros((fsdp_size * tok_rows, 2 * head_dim), low), d_kv, window_start, 0
        )
    d_kv_sum = scatter_shards(after(d_kv, up_sum))
    down_sum = scatter_shards(after(down_part, d_kv_sum))
    d_kv_sum = d_kv_sum.astype(jnp.float32)
    out_parts = matmul(after(activation, d_mixed), w_down)
    output_parts = [contract(mixed_rows, d, 0, 0) for d in d_branch_parts]
    layer_out = (hidden + scatter_copies(jnp.split(out_parts, copies))).astype(low)

    def to_copies(summed, dim):
        return jnp.concatenate(
            reorder(gather_copies(summed), copy_index), axis=dim
        ).astype(jnp.float32)

    query_parts = [
        contract(normed, d_query_raw[:, i * lanes : (i + 1) * lanes], 0, 0) for i in range(copies)
    ]
    output_sum = scatter_shards(after(scatter_copies(output_parts).astype(low), down_sum))
    query_sum = scatter_shards(after(scatter_copies(query_parts).astype(low), output_sum))
    gate_grad = to_copies(gate_sum, 0).T
    up_grad = to_copies(up_sum, 0).T
    down_grad = to_copies(down_sum, 0)

    d_key = d_kv_sum[:, :head_dim]
    d_key_raw = (d_key * cos_table - swap_halves(d_key) * sin_table).astype(low)
    d_kv_raw = jnp.concatenate([d_key_raw, d_kv_sum[:, head_dim:].astype(low)], axis=1)
    kv_sum = scatter_shards(contract(normed, d_kv_raw, 0, 0).astype(low))
    d_normed = contract(d_kv_raw, w_kv, 1, 1) + sum(
        contract(d_query_raw[:, i * lanes : (i + 1) * lanes], w_query[i], 1, 1) for i in range(copies)
    )
    resid_attn, attn_gain_term = norm_backward(inputs, inverse_attn, gain_attn, d_normed)
    input_grad = d_hidden + resid_attn
    kv_grad = lax.psum(kv_sum, "replica").astype(jnp.float32)
    output_grad = to_copies(output_sum, 1)
    query_grad = to_copies(query_sum, 1)
    gain_terms = lax.psum(jnp.stack([attn_gain_term, ffn_gain_term]), ("replica", "fsdp"))
    gain_grads = lax.dynamic_slice_in_dim(
        gain_terms, fsdp_index * (model_width // fsdp_size), model_width // fsdp_size, 1
    )
    return (
        layer_out,
        input_grad,
        query_grad,
        kv_grad[:, :head_dim],
        kv_grad[:, head_dim:],
        output_grad,
        gain_grads[0],
        gate_grad,
        up_grad,
        down_grad,
        gain_grads[1],
    )


def solution(mesh):
    return jax.shard_map(
        shards,
        mesh=mesh,
        in_specs=(
            P(("replica", "fsdp"), None),
            P(("replica", "fsdp")),
            P(("replica", "fsdp")),
            P("fsdp", None),
            P("fsdp", None),
            P("fsdp", None),
            P("fsdp", None),
            P("fsdp"),
            P(None, "fsdp"),
            P(None, "fsdp"),
            P("fsdp", None),
            P("fsdp"),
            P(("replica", "fsdp"), None),
        ),
        out_specs=(
            P(("replica", "fsdp"), None),
            P(("replica", "fsdp"), None),
            P("fsdp", None),
            P("fsdp", None),
            P("fsdp", None),
            P("fsdp", None),
            P("fsdp"),
            P(None, "fsdp"),
            P(None, "fsdp"),
            P("fsdp", None),
            P("fsdp"),
        ),
        check_vma=False,
    )
```

```python
import functools

import jax
import jax.numpy as jnp
from jax import lax
from jax.experimental import pallas as pl
from jax.experimental.pallas import tpu as pltpu
from jax.sharding import PartitionSpec as P

GROUP_TOK = 4096
PROMPT = 2048
MAX_CONT = 384
EPSILON = 1e-05
ROPE_BASE = 10000.0
MASKED = -1e30
LOG2E = 1.4426950408889634

TILE = 128
CHUNK = 512
HEAD_GROUP = 4


def matmul(left, right):
    return jnp.dot(left, right, preferred_element_type=jnp.float32)


def contract(left, right, left_dim, right_dim):
    return lax.dot_general(
        left, right, (((left_dim,), (right_dim,)), ((), ())), preferred_element_type=jnp.float32
    )


def rope_tables(pos_ids, head_dim):
    half_width = head_dim // 2
    frequency = ROPE_BASE ** (-jnp.arange(half_width, dtype=jnp.float32) * 2.0 / head_dim)
    angles = pos_ids.astype(jnp.float32)[:, None] * frequency[None, :]
    cos_half, sin_half = jnp.cos(angles), jnp.sin(angles)
    return (
        jnp.concatenate([cos_half, cos_half], axis=1),
        jnp.concatenate([-sin_half, sin_half], axis=1),
    )


def swap_halves(values):
    half_width = values.shape[-1] // 2
    return jnp.concatenate([values[..., half_width:], values[..., :half_width]], axis=-1)


def norm_forward(values, gain):
    inverse = lax.rsqrt(jnp.mean(values * values, axis=-1, keepdims=True) + EPSILON)
    return (values * inverse * gain, inverse)


def norm_backward(values, inverse, gain, grad):
    scaled = grad * gain
    inner_mean = jnp.mean(scaled * values, axis=-1, keepdims=True)
    return (
        inverse * scaled - values * inverse**3 * inner_mean,
        jnp.sum(grad * values * inverse, axis=0),
    )


def swiglu_back(d_activation, gate_proj, up_proj):
    sigmoid_gate = jax.nn.sigmoid(gate_proj)
    d_gate = (
        d_activation * up_proj * sigmoid_gate * (1.0 + gate_proj * (1.0 - sigmoid_gate))
    ).astype(jnp.bfloat16)
    d_up = (d_activation * gate_proj * sigmoid_gate).astype(jnp.bfloat16)
    return (d_gate, d_up)


def stack_heads(block):
    heads = block.shape[1] // 128
    return jnp.concatenate([block[:, h * 128 : (h + 1) * 128] for h in range(heads)], axis=0)


def chunk_plan(base_ref):
    first = base_ref[0] + pl.program_id(0) * TILE
    in_prompt = first < PROMPT
    full = jnp.where(in_prompt, first // CHUNK, PROMPT // CHUNK)
    last = jnp.where(
        in_prompt, first // CHUNK * CHUNK, jnp.maximum(PROMPT, first + TILE - CHUNK)
    )
    return first, full, pl.multiple_of(last, TILE)


def attend_kernel(
    base_ref, q_ref, kv_ref, low_ref, mixed_ref, log_ref, values, top, acc
):
    factor = 128**-0.5 * LOG2E

    @pl.when((pl.program_id(0) == 0) & (pl.program_id(1) == 0))
    def _():
        values[:, :128] = kv_ref[:, 128:]
        values[:, 128:] = jnp.ones_like(values[:, 128:])

    first, full, last = chunk_plan(base_ref)
    queries = stack_heads(q_ref[...])
    rows = queries.shape[0]
    top[...] = jnp.full_like(top, MASKED)
    acc[...] = jnp.zeros_like(acc)

    def step(start, masked):
        scores = contract(queries, kv_ref[pl.ds(start, CHUNK), :128], 1, 1) * factor
        if masked:
            key_at = start + lax.broadcasted_iota(jnp.int32, (rows, CHUNK), 1)
            row_at = lax.broadcasted_iota(jnp.int32, (rows, 1), 0) % TILE + first
            low = jnp.concatenate([low_ref[:, :1]] * HEAD_GROUP, axis=0)
            scores = jnp.where((key_at <= row_at) & (key_at >= low), scores, MASKED)
        before = top[:, :1]
        after = jnp.maximum(before, jnp.max(scores, axis=1, keepdims=True))
        weights = jnp.exp2(scores - after).astype(jnp.bfloat16)
        acc[...] = acc[...] * jnp.exp2(before - after) + matmul(
            weights, values[pl.ds(start, CHUNK), :]
        )
        top[...] = jnp.broadcast_to(after, top.shape)

    @pl.loop(0, full)
    def _(at):
        step(pl.multiple_of(at * CHUNK, CHUNK), False)

    step(last, True)
    total = acc[:, 128:]
    mixed = acc[:, :128] / total
    for h in range(HEAD_GROUP):
        mixed_ref[:, h * 128 : (h + 1) * 128] = mixed[h * TILE : (h + 1) * TILE].astype(jnp.bfloat16)
    log_ref[0, 0] = (top[...] + jnp.log2(total)).T[:8]


def attend(base, queries, kv, low):
    tok_rows, width = queries.shape
    tiles, groups = tok_rows // TILE, width // (128 * HEAD_GROUP)
    lanes, rows = 128 * HEAD_GROUP, TILE * HEAD_GROUP
    tile_spec = pl.BlockSpec((TILE, lanes), lambda i, g, b: (i, g))
    row_spec = pl.BlockSpec((TILE, 128), lambda i, g, b: (i, 0))
    pairs = tok_rows * (width // 128) * 2560
    return pl.pallas_call(
        attend_kernel,
        out_shape=(
            jax.ShapeDtypeStruct((tok_rows, width), jnp.bfloat16),
            jax.ShapeDtypeStruct((tiles, groups, 8, rows), jnp.float32),
        ),
        grid_spec=pltpu.PrefetchScalarGridSpec(
            num_scalar_prefetch=1,
            grid=(tiles, groups),
            in_specs=[
                tile_spec,
                pl.BlockSpec(kv.shape, lambda i, g, b: (0, 0)),
                row_spec,
            ],
            out_specs=[
                tile_spec,
                pl.BlockSpec((1, 1, 8, rows), lambda i, g, b: (i, g, 0, 0)),
            ],
            scratch_shapes=[
                pltpu.VMEM(kv.shape, jnp.bfloat16),
                pltpu.VMEM((rows, 128), jnp.float32),
                pltpu.VMEM((rows, 256), jnp.float32),
            ],
        ),
        compiler_params=pltpu.CompilerParams(vmem_limit_bytes=40 << 20),
        cost_estimate=pl.CostEstimate(
            flops=pairs * 768, transcendentals=pairs, bytes_accessed=16 << 20
        ),
        name="attend",
    )(base, queries, kv, low)


def attend_back_kernel(
    base_ref,
    q_ref,
    kv_ref,
    cos_ref,
    sin_ref,
    low_ref,
    mixed_ref,
    d_mixed_ref,
    log_ref,
    d_q_ref,
    d_kv_ref,
    sums,
    d_q,
):
    scale = 128**-0.5
    factor = scale * LOG2E
    at_start = (pl.program_id(0) == 0) & (pl.program_id(1) == 0)
    at_end = (pl.program_id(0) == pl.num_programs(0) - 1) & (
        pl.program_id(1) == pl.num_programs(1) - 1
    )

    @pl.when(at_start)
    def _():
        sums[...] = jnp.zeros_like(sums)

    first, full, last = chunk_plan(base_ref)
    queries = stack_heads(q_ref[...])
    d_rows = stack_heads(d_mixed_ref[...])
    mixed = stack_heads(mixed_ref[...])
    rows = queries.shape[0]
    products = d_rows.astype(jnp.float32) * mixed.astype(jnp.float32)
    delta = jnp.sum(products.T, axis=0, keepdims=True)
    log_total = log_ref[0, 0, :1]
    d_q[...] = jnp.zeros_like(d_q)

    def step(start, masked):
        keys = kv_ref[pl.ds(start, CHUNK), :128]
        values = kv_ref[pl.ds(start, CHUNK), 128:]
        scores = contract(keys, queries, 1, 1) * factor
        probs = jnp.exp2(scores - log_total)
        if masked:
            key_at = start + lax.broadcasted_iota(jnp.int32, (CHUNK, rows), 0)
            row_at = lax.broadcasted_iota(jnp.int32, (1, rows), 1) % TILE + first
            low = jnp.concatenate([low_ref[:1]] * HEAD_GROUP, axis=1)
            probs = jnp.where((key_at <= row_at) & (key_at >= low), probs, 0.0)
        d_probs = contract(values, d_rows, 1, 1)
        d_scores = (probs * (d_probs - delta)).astype(jnp.bfloat16)
        sums[pl.ds(start, CHUNK), 128:] += matmul(probs.astype(jnp.bfloat16), d_rows)
        sums[pl.ds(start, CHUNK), :128] += matmul(d_scores, queries)
        d_q[...] += contract(d_scores, keys, 0, 0)

    @pl.loop(0, full)
    def _(at):
        step(pl.multiple_of(at * CHUNK, CHUNK), False)

    step(last, True)
    cos_table, sin_table = cos_ref[...] * scale, sin_ref[...] * scale
    for h in range(HEAD_GROUP):
        turned = d_q[h * TILE : (h + 1) * TILE]
        raw = turned * cos_table - pltpu.roll(turned, 64, 1) * sin_table
        d_q_ref[:, h * 128 : (h + 1) * 128] = raw.astype(jnp.bfloat16)

    @pl.when(at_end)
    def _():
        d_kv_ref[:, :128] = (sums[:, :128] * scale).astype(jnp.bfloat16)
        d_kv_ref[:, 128:] = sums[:, 128:].astype(jnp.bfloat16)


def attend_back(base, queries, kv, cos_table, sin_table, low, mixed, d_mixed, logs):
    tok_rows, width = queries.shape
    tiles, groups = tok_rows // TILE, width // (128 * HEAD_GROUP)
    lanes, rows = 128 * HEAD_GROUP, TILE * HEAD_GROUP
    tile_spec = pl.BlockSpec((TILE, lanes), lambda i, g, b: (i, g))
    row_spec = pl.BlockSpec((TILE, 128), lambda i, g, b: (i, 0))
    whole = pl.BlockSpec(kv.shape, lambda i, g, b: (0, 0))
    pairs = tok_rows * (width // 128) * 2560
    return pl.pallas_call(
        attend_back_kernel,
        out_shape=(
            jax.ShapeDtypeStruct((tok_rows, width), jnp.bfloat16),
            jax.ShapeDtypeStruct(kv.shape, jnp.bfloat16),
        ),
        grid_spec=pltpu.PrefetchScalarGridSpec(
            num_scalar_prefetch=1,
            grid=(tiles, groups),
            in_specs=[
                tile_spec,
                whole,
                row_spec,
                row_spec,
                pl.BlockSpec((8, TILE), lambda i, g, b: (0, i)),
                tile_spec,
                tile_spec,
                pl.BlockSpec((1, 1, 8, rows), lambda i, g, b: (i, g, 0, 0)),
            ],
            out_specs=[tile_spec, whole],
            scratch_shapes=[
                pltpu.VMEM(kv.shape, jnp.float32),
                pltpu.VMEM((rows, 128), jnp.float32),
            ],
        ),
        compiler_params=pltpu.CompilerParams(vmem_limit_bytes=48 << 20),
        cost_estimate=pl.CostEstimate(
            flops=pairs * 1280, transcendentals=pairs, bytes_accessed=16 << 20
        ),
        name="attend_back",
    )(base, queries, kv, cos_table, sin_table, low, mixed, d_mixed, logs)


MESH = pl.DeviceIdType.MESH


def flip(index, bit):
    return index + bit - 2 * bit * (index // bit % 2)


class Chain:
    def __init__(self, place, count, at, replica, fsdp, sends, recvs):
        self.place, self.count, self.at = place, count, at
        self.replica, self.fsdp, self.sends, self.recvs = replica, fsdp, sends, recvs

    def copy(self, shard, way):
        target = self.fsdp + (2 if way == 0 else -2)
        return pltpu.make_async_remote_copy(
            src_ref=self.place(shard),
            dst_ref=self.place(shard),
            send_sem=self.sends.at[way, shard],
            recv_sem=self.recvs.at[way, shard],
            device_id=(self.replica, target),
            device_id_type=MESH,
        )

    def begin(self):
        @pl.when(self.at < self.count - 1)
        def _():
            self.copy(self.at, 0).start()

        @pl.when(self.at > 0)
        def _():
            self.copy(self.at, 1).start()

    def step(self, hop, arrived=None):
        left, right = self.at - hop, self.at + hop

        @pl.when(left >= 0)
        def _():
            self.copy(left, 0).wait_recv()

        @pl.when((left >= 0) & (self.at < self.count - 1))
        def _():
            self.copy(left, 0).start()

        if arrived is not None:

            @pl.when(left >= 0)
            def _():
                arrived(left)

        @pl.when(right < self.count)
        def _():
            self.copy(right, 1).wait_recv()

        @pl.when((right < self.count) & (self.at > 0))
        def _():
            self.copy(right, 1).start()

        if arrived is not None:

            @pl.when(right < self.count)
            def _():
                arrived(right)

    def finish(self):
        for hop in range(self.count):

            @pl.when((self.at - hop >= 0) & (self.at < self.count - 1))
            def _(hop=hop):
                self.copy(self.at - hop, 0).wait_send()

            @pl.when((self.at + hop < self.count) & (self.at > 0))
            def _(hop=hop):
                self.copy(self.at + hop, 1).wait_send()


class Spread:
    def __init__(self, buffer, count, at, core, replica, fsdp, sems):
        self.buffer, self.count, self.at, self.core = buffer, count, at, core
        self.replica, self.fsdp, self.sems = replica, fsdp, sems
        self.rows = buffer.shape[1] // 4

    def rows_of(self, shard, copy, half=None):
        start, size = copy * self.rows, self.rows
        if half is not None:
            size = size // 2
            start = start + half * size
        return self.buffer.at[2 * shard + self.core, pl.ds(start, size)]

    def copy(self, kind, shard):
        beside, across = flip(self.replica, 1), flip(self.replica, 2)
        if kind == 0:
            ref, target = self.rows_of(shard, self.replica), (beside, self.fsdp)
        elif kind == 1:
            ref, target = self.rows_of(shard, self.replica), (across, self.fsdp)
        elif kind == 2:
            ref, target = self.rows_of(shard, beside, 0), (across, self.fsdp)
        elif kind == 3:
            ref, target = self.rows_of(shard, across, 1), (beside, self.fsdp)
        else:
            ref, target = self.buffer.at[2 * shard + self.core], (self.replica, flip(self.fsdp, 1))
        return pltpu.make_async_remote_copy(
            src_ref=ref,
            dst_ref=ref,
            send_sem=self.sems.at[0, kind, shard],
            recv_sem=self.sems.at[1, kind, shard],
            device_id=target,
            device_id_type=MESH,
        )

    def recv(self, kind, shard):
        beside, across = flip(self.replica, 1), flip(self.replica, 2)
        if kind == 0:
            ref = self.rows_of(shard, beside)
        elif kind == 1:
            ref = self.rows_of(shard, across)
        elif kind < 4:
            ref = self.rows_of(shard, flip(beside, 2), kind - 2)
        else:
            ref = self.buffer.at[2 * shard + 1 - self.core]
        return pltpu.make_async_remote_copy(
            src_ref=ref,
            dst_ref=ref,
            send_sem=self.sems.at[0, kind, shard],
            recv_sem=self.sems.at[1, kind, shard],
            device_id=(self.replica, flip(self.fsdp, 1)),
            device_id_type=MESH,
        )

    def arrived(self, shard):
        self.copy(0, shard).start()
        self.copy(1, shard).start()

    def others(self):
        return [(self.at + hop) % self.count for hop in range(1, self.count)]

    def relay(self):
        for shard in self.others():
            self.recv(0, shard).wait_recv()
            self.copy(2, shard).start()
            self.recv(1, shard).wait_recv()
            self.copy(3, shard).start()

    def cores(self):
        self.copy(4, self.at).start()
        for shard in self.others():
            self.recv(2, shard).wait_recv()
            self.recv(3, shard).wait_recv()
            self.copy(4, shard).start()

    def finish(self):
        for shard in self.others() + [self.at]:
            self.recv(4, shard).wait_recv()
        for shard in self.others():
            for kind in range(5):
                self.copy(kind, shard).wait_send()
        self.copy(4, self.at).wait_send()


def project_kernel(
    fsdp_size,
    tokens_ref,
    wq_ref,
    wo_ref,
    kvg_ref,
    cos_ref,
    sin_ref,
    q_ref,
    normed_ref,
    gain_ref,
    wq_all,
    wo_all,
    kvg_all,
    kv_all,
    wq_vmem,
    kvg_vmem,
    kv_vmem,
    local_sems,
    kvg_sems,
    kvg_core,
    wq_line,
    wq_sems,
    wo_line,
    wo_sems,
    kv_sems,
    kv_core,
):
    replica, fsdp = lax.axis_index("replica"), lax.axis_index("fsdp")
    count, at, core = fsdp_size // 2, fsdp // 2, fsdp % 2
    width = tokens_ref.shape[1]
    partner = (replica, flip(fsdp, 1))

    barrier = pltpu.get_barrier_semaphore()
    for target in (partner, (flip(replica, 1), fsdp), (flip(replica, 2), fsdp)):
        pl.semaphore_signal(barrier, inc=1, device_id=target, device_id_type=MESH)

    @pl.when(at > 0)
    def _():
        pl.semaphore_signal(barrier, inc=1, device_id=(replica, fsdp - 2), device_id_type=MESH)

    @pl.when(at < count - 1)
    def _():
        pl.semaphore_signal(barrier, inc=1, device_id=(replica, fsdp + 2), device_id_type=MESH)

    own = [
        pltpu.make_async_copy(kvg_ref, kvg_all.at[fsdp], local_sems.at[0]),
        pltpu.make_async_copy(wq_ref, wq_all.at[fsdp], local_sems.at[1]),
        pltpu.make_async_copy(wo_ref, wo_all.at[fsdp], local_sems.at[2]),
    ]
    for copy in own:
        copy.start()
    inside = (at > 0) & (at < count - 1)

    @pl.when(inside)
    def _():
        pl.semaphore_wait(barrier, 5)

    @pl.when(jnp.logical_not(inside))
    def _():
        pl.semaphore_wait(barrier, 4)

    def core_copy(buffer, sems, shard, lands=False):
        ref = buffer.at[2 * shard + (1 - core if lands else core)]
        return pltpu.make_async_remote_copy(
            src_ref=ref,
            dst_ref=ref,
            send_sem=sems.at[0, shard],
            recv_sem=sems.at[1, shard],
            device_id=partner,
            device_id_type=MESH,
        )

    def line(place, sems):
        return Chain(place, count, at, replica, fsdp, sems.at[0], sems.at[1])

    kvg = line(lambda shard: kvg_all.at[2 * shard + core], kvg_sems)
    kv = line(lambda shard: kv_all.at[2 * shard + core], kv_sems)
    wq = Spread(wq_all, count, at, core, replica, fsdp, wq_sems)
    wo = Spread(wo_all, count, at, core, replica, fsdp, wo_sems)
    wq_chain = line(lambda shard: wq.rows_of(shard, replica), wq_line)
    wo_chain = line(lambda shard: wo.rows_of(shard, replica), wo_line)
    own[0].wait()
    kvg.begin()
    core_copy(kvg_all, kvg_core, at).start()
    own[1].wait()
    wq_chain.begin()
    own[2].wait()
    wo_chain.begin()

    inputs = tokens_ref[...].astype(jnp.float32)
    inverse = lax.rsqrt(jnp.mean(inputs * inputs, axis=1, keepdims=True) + EPSILON)

    for hop in range(1, count):
        kvg.step(hop, lambda shard: core_copy(kvg_all, kvg_core, shard).start())
        wq_chain.step(hop, wq.arrived)
        wo_chain.step(hop, wo.arrived)
    for shard in range(count):
        core_copy(kvg_all, kvg_core, shard, True).wait_recv()
    load = pltpu.make_async_copy(kvg_all, kvg_vmem, local_sems.at[0])
    load.start()
    load.wait()
    table = kvg_vmem[...].reshape(width, kvg_vmem.shape[2])
    gains = table[:, 256:].astype(jnp.float32).T[:8]
    gain_ref[...] = gains
    normed_ref[...] = (inputs * inverse * gains[:1]).astype(jnp.bfloat16)
    kv_raw = matmul(normed_ref[...], table[:, :256])
    cos_table, sin_table = cos_ref[...], sin_ref[...]
    key_raw = kv_raw[:, :128]
    key_rot = key_raw * cos_table + pltpu.roll(key_raw, 64, 1) * sin_table
    kv_vmem[:, :128] = key_rot.astype(jnp.bfloat16)
    kv_vmem[:, 128:] = kv_raw[:, 128:].astype(jnp.bfloat16)
    store = pltpu.make_async_copy(kv_vmem, kv_all.at[fsdp], local_sems.at[0])
    store.start()
    store.wait()
    kv.begin()
    core_copy(kv_all, kv_core, at).start()
    wq.relay()
    kv.step(1, lambda shard: core_copy(kv_all, kv_core, shard).start())
    wq.cores()
    wo.relay()
    for shard in wq.others() + [at]:
        wq.recv(4, shard).wait_recv()
    load = pltpu.make_async_copy(wq_all, wq_vmem, local_sems.at[1])
    load.start()
    for hop in range(2, count):
        kv.step(hop, lambda shard: core_copy(kv_all, kv_core, shard).start())
    load.wait()
    weight = wq_vmem.reshape(width, width)

    def columns(block):
        start = pl.multiple_of(block * 512, 512)
        raw = matmul(normed_ref[...], weight[:, pl.ds(start, 512)])
        for h in range(4):
            head = raw[:, h * 128 : (h + 1) * 128]
            turned = head * cos_table + pltpu.roll(head, 64, 1) * sin_table
            q_ref[:, pl.ds(start + h * 128, 128)] = turned.astype(jnp.bfloat16)

    pl.loop(0, width // 512)(columns)
    wo.cores()
    for shard in range(count):
        core_copy(kv_all, kv_core, shard, True).wait_recv()
    wo.finish()
    for shard in wq.others():
        for kind in range(5):
            wq.copy(kind, shard).wait_send()
    wq.copy(4, at).wait_send()
    for shard in range(count):
        core_copy(kvg_all, kvg_core, shard).wait_send()
        core_copy(kv_all, kv_core, shard).wait_send()
    for chain in (kvg, kv, wq_chain, wo_chain):
        chain.finish()


def project(tokens, wq, wo, kvg, cos_table, sin_table):
    rows, width = tokens.shape
    shard = wq.shape[0]
    fsdp_size = lax.axis_size("fsdp")
    count = fsdp_size // 2
    low = jnp.bfloat16
    vmem, hbm = pl.BlockSpec(memory_space=pltpu.VMEM), pl.BlockSpec(memory_space=pl.ANY)
    dma = pltpu.SemaphoreType.DMA
    return pl.pallas_call(
        functools.partial(project_kernel, fsdp_size),
        out_shape=(
            jax.ShapeDtypeStruct((rows, width), low),
            jax.ShapeDtypeStruct((rows, width), low),
            jax.ShapeDtypeStruct((8, width), jnp.float32),
            jax.ShapeDtypeStruct((fsdp_size, shard, width), low),
            jax.ShapeDtypeStruct((fsdp_size, shard, width), low),
            jax.ShapeDtypeStruct((fsdp_size, shard, kvg.shape[1]), low),
            jax.ShapeDtypeStruct((fsdp_size, rows, 256), low),
        ),
        in_specs=[vmem, hbm, hbm, hbm, vmem, vmem],
        out_specs=(vmem, vmem, vmem, hbm, hbm, hbm, hbm),
        scratch_shapes=[
            pltpu.VMEM((fsdp_size, shard, width), low),
            pltpu.VMEM((fsdp_size, shard, kvg.shape[1]), low),
            pltpu.VMEM((rows, 256), low),
            dma((3,)),
            dma((2, 2, count)),
            dma((2, count)),
            dma((2, 2, count)),
            dma((2, 5, count)),
            dma((2, 2, count)),
            dma((2, 5, count)),
            dma((2, 2, count)),
            dma((2, count)),
        ],
        compiler_params=pltpu.CompilerParams(
            collective_id=0, has_side_effects=True, vmem_limit_bytes=48 << 20
        ),
        cost_estimate=pl.CostEstimate(
            flops=2 * rows * width * (width + 256), transcendentals=0, bytes_accessed=40 << 20
        ),
        name="project",
    )(tokens, wq, wo, kvg, cos_table, sin_table)


def swap(value, step):
    copies = lax.axis_size("replica")
    return lax.ppermute(value, "replica", [(r, r ^ step) for r in range(copies)])


def gather_copies(block):
    half = block.shape[0] // 2
    beside, across = swap(block, 1), swap(block, 2)
    opposite = jnp.concatenate([swap(beside[:half], 2), swap(across[half:], 1)], axis=0)
    return [block, beside, across, opposite]


def scatter_copies(parts):
    own, beside, across, opposite = parts
    half = opposite.shape[0] // 2
    low = jnp.bfloat16
    first = swap(opposite[:half].astype(low), 1)
    second = swap(opposite[half:].astype(low), 2)
    across = jnp.concatenate(
        [across[:half].astype(jnp.float32) + first.astype(jnp.float32), across[half:]], axis=0
    )
    beside = jnp.concatenate(
        [beside[:half], beside[half:].astype(jnp.float32) + second.astype(jnp.float32)], axis=0
    )
    return (
        own.astype(jnp.float32)
        + swap(beside.astype(low), 1).astype(jnp.float32)
        + swap(across.astype(low), 2).astype(jnp.float32)
    )


def gather_shards(value):
    return lax.all_gather(value, "fsdp", axis=0, tiled=True)


def scatter_shards(value):
    return lax.psum_scatter(value, "fsdp", scatter_dimension=0, tiled=True)


def place(pieces, copy_index):
    out = jnp.zeros((len(pieces),) + pieces[0].shape, pieces[0].dtype)
    for step, piece in enumerate(pieces):
        out = lax.dynamic_update_index_in_dim(out, piece, copy_index ^ step, 0)
    return out


def quarter(shard, copy_index):
    rows = shard.shape[0] // lax.axis_size("replica")
    return lax.dynamic_slice_in_dim(shard, copy_index * rows, rows, 0)


def sum_weight_grad(partial, copy_index):
    rows, width = partial.shape
    copies, fsdp_size = lax.axis_size("replica"), lax.axis_size("fsdp")
    fine = rows // (copies * fsdp_size)
    view = partial.reshape(fsdp_size, copies, fine, width)
    parts = [
        lax.dynamic_slice_in_dim(view, copy_index ^ step, 1, 1).reshape(fsdp_size * fine, width)
        for step in range(copies)
    ]
    summed = scatter_shards(scatter_copies(parts).astype(jnp.bfloat16))
    return place(gather_copies(summed), copy_index).reshape(copies * fine, width).astype(jnp.float32)


def shards(
    tokens,
    segments,
    positions,
    query_weight,
    key_weight,
    value_weight,
    output_weight,
    attn_gain,
    gate_weight,
    up_weight,
    down_weight,
    ffn_gain,
    grad_out,
):
    tok_rows, model_width = tokens.shape
    head_dim = key_weight.shape[1]
    fsdp_size = lax.axis_size("fsdp")
    fsdp_index = lax.axis_index("fsdp")
    copy_index = lax.axis_index("replica")
    copies = lax.axis_size("replica")
    low = jnp.bfloat16

    cos_table, sin_table = rope_tables(positions, head_dim)
    gain_columns = jnp.stack([attn_gain, ffn_gain], axis=1)
    queries, normed, gains, w_query, w_out, w_kvg, kv_all = project(
        tokens,
        query_weight,
        output_weight,
        jnp.concatenate(
            [key_weight, value_weight, jnp.pad(gain_columns, ((0, 0), (0, 126)))], axis=1
        ),
        cos_table,
        sin_table,
    )
    w_query = w_query.reshape(model_width, model_width)
    w_out = w_out.reshape(model_width, model_width)
    w_kv = w_kvg.reshape(model_width, 3 * head_dim)[:, : 2 * head_dim]
    kv_all = kv_all.reshape(fsdp_size * tok_rows, 2 * head_dim)
    gain_attn, gain_ffn = gains[0], gains[1]
    inputs = tokens.astype(jnp.float32)
    inverse_attn = lax.rsqrt(jnp.mean(inputs * inputs, axis=-1, keepdims=True) + EPSILON)
    key_width = max(GROUP_TOK, tok_rows)
    window_start = fsdp_index * tok_rows // key_width * key_width
    one_group = fsdp_size * tok_rows == key_width
    kv = kv_all if one_group else lax.dynamic_slice_in_dim(kv_all, window_start, key_width, 0)

    base = (fsdp_index * tok_rows - window_start).astype(jnp.int32)
    row_at = base + jnp.arange(tok_rows, dtype=jnp.int32)
    lowest = jnp.where(positions < PROMPT, 0, row_at - (positions - PROMPT))
    base = base[None]
    mixed_rows, logs = attend(
        base, queries, kv, jnp.broadcast_to(lowest[:, None], (tok_rows, 128))
    )

    hidden = inputs + matmul(mixed_rows, w_out)
    normed_ffn_full, inverse_ffn = norm_forward(hidden, gain_ffn)
    normed_ffn = normed_ffn_full.astype(low)

    w_gate = gather_shards(quarter(gate_weight.T, copy_index))
    w_up = gather_shards(quarter(up_weight.T, copy_index))
    w_down = gather_shards(quarter(down_weight, copy_index))
    grad_blocks = gather_copies(grad_out)
    grads = jnp.concatenate(grad_blocks, axis=0)
    normed_blocks = gather_copies(normed_ffn)
    normed_all = jnp.concatenate(normed_blocks, axis=0)

    d_activation = contract(grads, w_down, 1, 1)
    gate_proj = contract(normed_all, w_gate, 1, 1)
    up_proj = contract(normed_all, w_up, 1, 1)
    activation = (jax.nn.silu(gate_proj) * up_proj).astype(low)
    d_gate, d_up = swiglu_back(d_activation, gate_proj, up_proj)
    d_normed_parts = matmul(d_gate, w_gate) + matmul(d_up, w_up)
    d_normed_ffn = scatter_copies(jnp.split(d_normed_parts, copies))
    out_parts = matmul(activation, w_down)
    layer_out = (hidden + scatter_copies(jnp.split(out_parts, copies))).astype(low)

    gate_part = contract(d_gate, normed_all, 0, 0).astype(low)
    up_part = contract(d_up, normed_all, 0, 0).astype(low)
    down_part = contract(activation, grads, 0, 0).astype(low)

    def ffn_grad(partial):
        summed = scatter_shards(partial)
        pieces = place(gather_copies(summed), copy_index)
        return pieces.reshape(-1, model_width).astype(jnp.float32)

    cotangent = grad_out.astype(jnp.float32)
    resid_ffn, ffn_gain_term = norm_backward(hidden, inverse_ffn, gain_ffn, d_normed_ffn)
    d_hidden = cotangent + resid_ffn
    d_branch = d_hidden.astype(low)
    d_mixed = contract(d_branch, w_out, 1, 1).astype(low)
    d_mixed, gate_part, up_part, down_part = lax.optimization_barrier(
        (d_mixed, gate_part, up_part, down_part)
    )
    gate_grad = ffn_grad(gate_part).T
    up_grad = ffn_grad(up_part).T
    down_grad = ffn_grad(down_part)
    output_grad = sum_weight_grad(contract(mixed_rows, d_branch, 0, 0), copy_index)

    d_query_raw, d_kv = attend_back(
        base,
        queries,
        kv,
        cos_table,
        sin_table,
        jnp.broadcast_to(lowest[None, :], (8, tok_rows)),
        mixed_rows,
        d_mixed,
        logs,
    )
    query_grad = sum_weight_grad(contract(normed, d_query_raw, 0, 0), copy_index)
    if not one_group:
        d_kv = lax.dynamic_update_slice_in_dim(
            jnp.zeros((fsdp_size * tok_rows, 2 * head_dim), low), d_kv, window_start, 0
        )
    d_kv_sum = scatter_shards(d_kv).astype(jnp.float32)
    d_key = d_kv_sum[:, :head_dim]
    d_key_raw = (d_key * cos_table - swap_halves(d_key) * sin_table).astype(low)
    d_kv_raw = jnp.concatenate([d_key_raw, d_kv_sum[:, head_dim:].astype(low)], axis=1)
    kv_grad = sum_weight_grad(contract(normed, d_kv_raw, 0, 0), copy_index)
    d_normed = contract(d_query_raw, w_query, 1, 1) + contract(
        d_kv_raw, w_kv, 1, 1
    )
    resid_attn, attn_gain_term = norm_backward(inputs, inverse_attn, gain_attn, d_normed)
    input_grad = d_hidden + resid_attn
    gain_terms = lax.psum(jnp.stack([attn_gain_term, ffn_gain_term]), ("replica", "fsdp"))
    gain_grads = lax.dynamic_slice_in_dim(
        gain_terms, fsdp_index * (model_width // fsdp_size), model_width // fsdp_size, 1
    )
    return (
        layer_out,
        input_grad,
        query_grad,
        kv_grad[:, :head_dim],
        kv_grad[:, head_dim:],
        output_grad,
        gain_grads[0],
        gate_grad,
        up_grad,
        down_grad,
        gain_grads[1],
    )


def solution(mesh):
    return jax.shard_map(
        shards,
        mesh=mesh,
        in_specs=(
            P(("replica", "fsdp"), None),
            P(("replica", "fsdp")),
            P(("replica", "fsdp")),
            P("fsdp", None),
            P("fsdp", None),
            P("fsdp", None),
            P("fsdp", None),
            P("fsdp"),
            P(None, "fsdp"),
            P(None, "fsdp"),
            P("fsdp", None),
            P("fsdp"),
            P(("replica", "fsdp"), None),
        ),
        out_specs=(
            P(("replica", "fsdp"), None),
            P(("replica", "fsdp"), None),
            P("fsdp", None),
            P("fsdp", None),
            P("fsdp", None),
            P("fsdp", None),
            P("fsdp"),
            P(None, "fsdp"),
            P(None, "fsdp"),
            P("fsdp", None),
            P("fsdp"),
        ),
        check_vma=False,
    )
```

```python
import functools

import jax
import jax.numpy as jnp
from jax import lax
from jax.experimental import pallas as pl
from jax.experimental.pallas import tpu as pltpu
from jax.sharding import PartitionSpec as P

GROUP_TOK = 4096
PROMPT = 2048
MAX_CONT = 384
EPSILON = 1e-05
ROPE_BASE = 10000.0
MASKED = -1e30
LOG2E = 1.4426950408889634

TILE = 128
CHUNK = 512
HEAD_GROUP = 4
HEAD_BLOCK = 4


def matmul(left, right):
    return jnp.dot(left, right, preferred_element_type=jnp.float32)


def contract(left, right, left_dim, right_dim):
    return lax.dot_general(
        left, right, (((left_dim,), (right_dim,)), ((), ())), preferred_element_type=jnp.float32
    )


def rope_tables(pos_ids, head_dim):
    half_width = head_dim // 2
    frequency = ROPE_BASE ** (-jnp.arange(half_width, dtype=jnp.float32) * 2.0 / head_dim)
    angles = pos_ids.astype(jnp.float32)[:, None] * frequency[None, :]
    cos_half, sin_half = jnp.cos(angles), jnp.sin(angles)
    return (
        jnp.concatenate([cos_half, cos_half], axis=1),
        jnp.concatenate([-sin_half, sin_half], axis=1),
    )


def swap_halves(values):
    half_width = values.shape[-1] // 2
    return jnp.concatenate([values[..., half_width:], values[..., :half_width]], axis=-1)


def norm_forward(values, gain):
    inverse = lax.rsqrt(jnp.mean(values * values, axis=-1, keepdims=True) + EPSILON)
    return (values * inverse * gain, inverse)


def norm_backward(values, inverse, gain, grad):
    scaled = grad * gain
    inner_mean = jnp.mean(scaled * values, axis=-1, keepdims=True)
    return (
        inverse * scaled - values * inverse**3 * inner_mean,
        jnp.sum(grad * values * inverse, axis=0),
    )


def swiglu_back(d_activation, gate_proj, up_proj):
    sigmoid_gate = jax.nn.sigmoid(gate_proj)
    d_gate = (
        d_activation * up_proj * sigmoid_gate * (1.0 + gate_proj * (1.0 - sigmoid_gate))
    ).astype(jnp.bfloat16)
    d_up = (d_activation * gate_proj * sigmoid_gate).astype(jnp.bfloat16)
    return (d_gate, d_up)


def stack_heads(block):
    heads = block.shape[1] // 128
    return jnp.concatenate([block[:, h * 128 : (h + 1) * 128] for h in range(heads)], axis=0)


def chunk_plan(base_ref):
    first = base_ref[0] + pl.program_id(0) * TILE
    in_prompt = first < PROMPT
    full = jnp.where(in_prompt, first // CHUNK, PROMPT // CHUNK)
    last = jnp.where(
        in_prompt, first // CHUNK * CHUNK, jnp.maximum(PROMPT, first + TILE - CHUNK)
    )
    return first, full, pl.multiple_of(last, TILE)


def attend_kernel(
    base_ref, q_ref, kv_ref, low_ref, mixed_ref, log_ref, values, top, acc
):
    factor = 128**-0.5 * LOG2E

    @pl.when((pl.program_id(0) == 0) & (pl.program_id(1) == 0))
    def _():
        values[:, :128] = kv_ref[:, 128:]
        values[:, 128:] = jnp.ones_like(values[:, 128:])

    first, full, last = chunk_plan(base_ref)
    queries = stack_heads(q_ref[...])
    rows = queries.shape[0]
    top[...] = jnp.full_like(top, MASKED)
    acc[...] = jnp.zeros_like(acc)

    def step(start, masked):
        scores = contract(queries, kv_ref[pl.ds(start, CHUNK), :128], 1, 1) * factor
        if masked:
            key_at = start + lax.broadcasted_iota(jnp.int32, (rows, CHUNK), 1)
            row_at = lax.broadcasted_iota(jnp.int32, (rows, 1), 0) % TILE + first
            low = jnp.concatenate([low_ref[:, :1]] * HEAD_GROUP, axis=0)
            scores = jnp.where((key_at <= row_at) & (key_at >= low), scores, MASKED)
        before = top[:, :1]
        after = jnp.maximum(before, jnp.max(scores, axis=1, keepdims=True))
        weights = jnp.exp2(scores - after).astype(jnp.bfloat16)
        acc[...] = acc[...] * jnp.exp2(before - after) + matmul(
            weights, values[pl.ds(start, CHUNK), :]
        )
        top[...] = jnp.broadcast_to(after, top.shape)

    @pl.loop(0, full)
    def _(at):
        step(pl.multiple_of(at * CHUNK, CHUNK), False)

    step(last, True)
    total = acc[:, 128:]
    mixed = acc[:, :128] / total
    for h in range(HEAD_GROUP):
        mixed_ref[:, h * 128 : (h + 1) * 128] = mixed[h * TILE : (h + 1) * TILE].astype(jnp.bfloat16)
    log_ref[0, 0] = (top[...] + jnp.log2(total)).T[:8]


def attend(base, queries, kv, low):
    tok_rows, width = queries.shape
    tiles, groups = tok_rows // TILE, width // (128 * HEAD_GROUP)
    lanes, rows = 128 * HEAD_GROUP, TILE * HEAD_GROUP
    tile_spec = pl.BlockSpec((TILE, lanes), lambda i, g, b: (i, g))
    row_spec = pl.BlockSpec((TILE, 128), lambda i, g, b: (i, 0))
    pairs = tok_rows * (width // 128) * 2560
    return pl.pallas_call(
        attend_kernel,
        out_shape=(
            jax.ShapeDtypeStruct((tok_rows, width), jnp.bfloat16),
            jax.ShapeDtypeStruct((tiles, groups, 8, rows), jnp.float32),
        ),
        grid_spec=pltpu.PrefetchScalarGridSpec(
            num_scalar_prefetch=1,
            grid=(tiles, groups),
            in_specs=[
                tile_spec,
                pl.BlockSpec(kv.shape, lambda i, g, b: (0, 0)),
                row_spec,
            ],
            out_specs=[
                tile_spec,
                pl.BlockSpec((1, 1, 8, rows), lambda i, g, b: (i, g, 0, 0)),
            ],
            scratch_shapes=[
                pltpu.VMEM(kv.shape, jnp.bfloat16),
                pltpu.VMEM((rows, 128), jnp.float32),
                pltpu.VMEM((rows, 256), jnp.float32),
            ],
        ),
        compiler_params=pltpu.CompilerParams(vmem_limit_bytes=40 << 20),
        cost_estimate=pl.CostEstimate(
            flops=pairs * 768, transcendentals=pairs, bytes_accessed=16 << 20
        ),
        name="attend",
    )(base, queries, kv, low)


def attend_back_kernel(
    base_ref,
    q_ref,
    kv_ref,
    cos_ref,
    sin_ref,
    low_ref,
    mixed_ref,
    d_mixed_ref,
    log_ref,
    d_q_ref,
    d_kv_ref,
    sums,
    d_q,
):
    scale = 128**-0.5
    factor = scale * LOG2E
    at_start = (pl.program_id(0) == 0) & (pl.program_id(1) == 0)
    at_end = (pl.program_id(0) == pl.num_programs(0) - 1) & (
        pl.program_id(1) == pl.num_programs(1) - 1
    )

    @pl.when(at_start)
    def _():
        sums[...] = jnp.zeros_like(sums)

    first, full, last = chunk_plan(base_ref)
    queries = stack_heads(q_ref[...])
    d_rows = stack_heads(d_mixed_ref[...])
    mixed = stack_heads(mixed_ref[...])
    rows = queries.shape[0]
    products = d_rows.astype(jnp.float32) * mixed.astype(jnp.float32)
    delta = jnp.sum(products.T, axis=0, keepdims=True)
    log_total = log_ref[0, 0, :1]
    d_q[...] = jnp.zeros_like(d_q)

    def step(start, masked):
        keys = kv_ref[pl.ds(start, CHUNK), :128]
        values = kv_ref[pl.ds(start, CHUNK), 128:]
        scores = contract(keys, queries, 1, 1) * factor
        probs = jnp.exp2(scores - log_total)
        if masked:
            key_at = start + lax.broadcasted_iota(jnp.int32, (CHUNK, rows), 0)
            row_at = lax.broadcasted_iota(jnp.int32, (1, rows), 1) % TILE + first
            low = jnp.concatenate([low_ref[:1]] * HEAD_GROUP, axis=1)
            probs = jnp.where((key_at <= row_at) & (key_at >= low), probs, 0.0)
        d_probs = contract(values, d_rows, 1, 1)
        d_scores = (probs * (d_probs - delta)).astype(jnp.bfloat16)
        sums[pl.ds(start, CHUNK), 128:] += matmul(probs.astype(jnp.bfloat16), d_rows)
        sums[pl.ds(start, CHUNK), :128] += matmul(d_scores, queries)
        d_q[...] += contract(d_scores, keys, 0, 0)

    @pl.loop(0, full)
    def _(at):
        step(pl.multiple_of(at * CHUNK, CHUNK), False)

    step(last, True)
    cos_table, sin_table = cos_ref[...] * scale, sin_ref[...] * scale
    for h in range(HEAD_GROUP):
        turned = d_q[h * TILE : (h + 1) * TILE]
        raw = turned * cos_table - pltpu.roll(turned, 64, 1) * sin_table
        d_q_ref[:, h * 128 : (h + 1) * 128] = raw.astype(jnp.bfloat16)

    @pl.when(at_end)
    def _():
        d_kv_ref[:, :128] = (sums[:, :128] * scale).astype(jnp.bfloat16)
        d_kv_ref[:, 128:] = sums[:, 128:].astype(jnp.bfloat16)


def attend_back(base, queries, kv, cos_table, sin_table, low, mixed, d_mixed, logs):
    tok_rows, width = queries.shape
    tiles, groups = tok_rows // TILE, width // (128 * HEAD_GROUP)
    lanes, rows = 128 * HEAD_GROUP, TILE * HEAD_GROUP
    tile_spec = pl.BlockSpec((TILE, lanes), lambda i, g, b: (i, g))
    row_spec = pl.BlockSpec((TILE, 128), lambda i, g, b: (i, 0))
    whole = pl.BlockSpec(kv.shape, lambda i, g, b: (0, 0))
    pairs = tok_rows * (width // 128) * 2560
    return pl.pallas_call(
        attend_back_kernel,
        out_shape=(
            jax.ShapeDtypeStruct((tok_rows, width), jnp.bfloat16),
            jax.ShapeDtypeStruct(kv.shape, jnp.bfloat16),
        ),
        grid_spec=pltpu.PrefetchScalarGridSpec(
            num_scalar_prefetch=1,
            grid=(tiles, groups),
            in_specs=[
                tile_spec,
                whole,
                row_spec,
                row_spec,
                pl.BlockSpec((8, TILE), lambda i, g, b: (0, i)),
                tile_spec,
                tile_spec,
                pl.BlockSpec((1, 1, 8, rows), lambda i, g, b: (i, g, 0, 0)),
            ],
            out_specs=[tile_spec, whole],
            scratch_shapes=[
                pltpu.VMEM(kv.shape, jnp.float32),
                pltpu.VMEM((rows, 128), jnp.float32),
            ],
        ),
        compiler_params=pltpu.CompilerParams(vmem_limit_bytes=48 << 20),
        cost_estimate=pl.CostEstimate(
            flops=pairs * 1280, transcendentals=pairs, bytes_accessed=16 << 20
        ),
        name="attend_back",
    )(base, queries, kv, cos_table, sin_table, low, mixed, d_mixed, logs)


MESH = pl.DeviceIdType.MESH


def flip(index, bit):
    return index + bit - 2 * bit * (index // bit % 2)


class Chain:
    def __init__(self, place, count, at, replica, fsdp, sends, recvs):
        self.place, self.count, self.at = place, count, at
        self.replica, self.fsdp, self.sends, self.recvs = replica, fsdp, sends, recvs

    def copy(self, shard, way):
        target = self.fsdp + (2 if way == 0 else -2)
        return pltpu.make_async_remote_copy(
            src_ref=self.place(shard),
            dst_ref=self.place(shard),
            send_sem=self.sends.at[way, shard],
            recv_sem=self.recvs.at[way, shard],
            device_id=(self.replica, target),
            device_id_type=MESH,
        )

    def begin(self):
        @pl.when(self.at < self.count - 1)
        def _():
            self.copy(self.at, 0).start()

        @pl.when(self.at > 0)
        def _():
            self.copy(self.at, 1).start()

    def step(self, hop, arrived=None):
        left, right = self.at - hop, self.at + hop

        @pl.when(left >= 0)
        def _():
            self.copy(left, 0).wait_recv()

        @pl.when((left >= 0) & (self.at < self.count - 1))
        def _():
            self.copy(left, 0).start()

        if arrived is not None:

            @pl.when(left >= 0)
            def _():
                arrived(left)

        @pl.when(right < self.count)
        def _():
            self.copy(right, 1).wait_recv()

        @pl.when((right < self.count) & (self.at > 0))
        def _():
            self.copy(right, 1).start()

        if arrived is not None:

            @pl.when(right < self.count)
            def _():
                arrived(right)

    def finish(self):
        for hop in range(self.count):

            @pl.when((self.at - hop >= 0) & (self.at < self.count - 1))
            def _(hop=hop):
                self.copy(self.at - hop, 0).wait_send()

            @pl.when((self.at + hop < self.count) & (self.at > 0))
            def _(hop=hop):
                self.copy(self.at + hop, 1).wait_send()


class Spread:
    def __init__(self, buffer, count, at, core, replica, fsdp, sems):
        self.buffer, self.count, self.at, self.core = buffer, count, at, core
        self.replica, self.fsdp, self.sems = replica, fsdp, sems
        self.rows = buffer.shape[1] // 4

    def rows_of(self, shard, copy, half=None):
        start, size = copy * self.rows, self.rows
        if half is not None:
            size = size // 2
            start = start + half * size
        return self.buffer.at[2 * shard + self.core, pl.ds(start, size)]

    def copy(self, kind, shard):
        beside, across = flip(self.replica, 1), flip(self.replica, 2)
        if kind == 0:
            ref, target = self.rows_of(shard, self.replica), (beside, self.fsdp)
        elif kind == 1:
            ref, target = self.rows_of(shard, self.replica), (across, self.fsdp)
        elif kind == 2:
            ref, target = self.rows_of(shard, beside, 0), (across, self.fsdp)
        elif kind == 3:
            ref, target = self.rows_of(shard, across, 1), (beside, self.fsdp)
        else:
            ref, target = self.buffer.at[2 * shard + self.core], (self.replica, flip(self.fsdp, 1))
        return pltpu.make_async_remote_copy(
            src_ref=ref,
            dst_ref=ref,
            send_sem=self.sems.at[0, kind, shard],
            recv_sem=self.sems.at[1, kind, shard],
            device_id=target,
            device_id_type=MESH,
        )

    def recv(self, kind, shard):
        beside, across = flip(self.replica, 1), flip(self.replica, 2)
        if kind == 0:
            ref = self.rows_of(shard, beside)
        elif kind == 1:
            ref = self.rows_of(shard, across)
        elif kind < 4:
            ref = self.rows_of(shard, flip(beside, 2), kind - 2)
        else:
            ref = self.buffer.at[2 * shard + 1 - self.core]
        return pltpu.make_async_remote_copy(
            src_ref=ref,
            dst_ref=ref,
            send_sem=self.sems.at[0, kind, shard],
            recv_sem=self.sems.at[1, kind, shard],
            device_id=(self.replica, flip(self.fsdp, 1)),
            device_id_type=MESH,
        )

    def arrived(self, shard):
        self.copy(0, shard).start()
        self.copy(1, shard).start()

    def others(self):
        return [(self.at + hop) % self.count for hop in range(1, self.count)]

    def relay(self):
        for shard in self.others():
            self.recv(0, shard).wait_recv()
            self.copy(2, shard).start()
            self.recv(1, shard).wait_recv()
            self.copy(3, shard).start()

    def cores(self):
        self.copy(4, self.at).start()
        for shard in self.others():
            self.recv(2, shard).wait_recv()
            self.recv(3, shard).wait_recv()
            self.copy(4, shard).start()

    def finish(self):
        for shard in self.others() + [self.at]:
            self.recv(4, shard).wait_recv()
        for shard in self.others():
            for kind in range(5):
                self.copy(kind, shard).wait_send()
        self.copy(4, self.at).wait_send()


def project_kernel(
    fsdp_size,
    tokens_ref,
    wq_ref,
    wo_ref,
    kvg_ref,
    cos_ref,
    sin_ref,
    q_ref,
    normed_ref,
    gain_ref,
    wq_all,
    wo_all,
    kvg_all,
    kv_all,
    wq_vmem,
    kvg_vmem,
    kv_vmem,
    local_sems,
    kvg_sems,
    kvg_core,
    wq_line,
    wq_sems,
    wo_line,
    wo_sems,
    kv_sems,
    kv_core,
):
    replica, fsdp = lax.axis_index("replica"), lax.axis_index("fsdp")
    count, at, core = fsdp_size // 2, fsdp // 2, fsdp % 2
    width = tokens_ref.shape[1]
    partner = (replica, flip(fsdp, 1))

    own = [
        pltpu.make_async_copy(kvg_ref, kvg_all.at[fsdp], local_sems.at[0]),
        pltpu.make_async_copy(wq_ref, wq_all.at[fsdp], local_sems.at[1]),
        pltpu.make_async_copy(wo_ref, wo_all.at[fsdp], local_sems.at[2]),
    ]
    for copy in own:
        copy.start()
    greet(replica, fsdp, at, count)

    def core_copy(buffer, sems, shard, lands=False):
        ref = buffer.at[2 * shard + (1 - core if lands else core)]
        return pltpu.make_async_remote_copy(
            src_ref=ref,
            dst_ref=ref,
            send_sem=sems.at[0, shard],
            recv_sem=sems.at[1, shard],
            device_id=partner,
            device_id_type=MESH,
        )

    def line(place, sems):
        return Chain(place, count, at, replica, fsdp, sems.at[0], sems.at[1])

    kvg = line(lambda shard: kvg_all.at[2 * shard + core], kvg_sems)
    kv = line(lambda shard: kv_all.at[2 * shard + core], kv_sems)
    wq = Spread(wq_all, count, at, core, replica, fsdp, wq_sems)
    wo = Spread(wo_all, count, at, core, replica, fsdp, wo_sems)
    wq_chain = line(lambda shard: wq.rows_of(shard, replica), wq_line)
    wo_chain = line(lambda shard: wo.rows_of(shard, replica), wo_line)
    own[0].wait()
    kvg.begin()
    core_copy(kvg_all, kvg_core, at).start()
    own[1].wait()
    wq_chain.begin()
    own[2].wait()
    wo_chain.begin()

    inputs = tokens_ref[...].astype(jnp.float32)
    inverse = lax.rsqrt(jnp.mean(inputs * inputs, axis=1, keepdims=True) + EPSILON)

    for hop in range(1, count):
        kvg.step(hop, lambda shard: core_copy(kvg_all, kvg_core, shard).start())
        wq_chain.step(hop, wq.arrived)
        wo_chain.step(hop, wo.arrived)
    for shard in range(count):
        core_copy(kvg_all, kvg_core, shard, True).wait_recv()
    load = pltpu.make_async_copy(kvg_all, kvg_vmem, local_sems.at[0])
    load.start()
    load.wait()
    table = kvg_vmem[...].reshape(width, kvg_vmem.shape[2])
    gains = table[:, 256:].astype(jnp.float32).T[:8]
    gain_ref[...] = gains
    normed_ref[...] = (inputs * inverse * gains[:1]).astype(jnp.bfloat16)
    kv_raw = matmul(normed_ref[...], table[:, :256])
    cos_table, sin_table = cos_ref[...], sin_ref[...]
    key_raw = kv_raw[:, :128]
    key_rot = key_raw * cos_table + pltpu.roll(key_raw, 64, 1) * sin_table
    kv_vmem[:, :128] = key_rot.astype(jnp.bfloat16)
    kv_vmem[:, 128:] = kv_raw[:, 128:].astype(jnp.bfloat16)
    store = pltpu.make_async_copy(kv_vmem, kv_all.at[fsdp], local_sems.at[0])
    store.start()
    store.wait()
    kv.begin()
    core_copy(kv_all, kv_core, at).start()
    wq.relay()
    kv.step(1, lambda shard: core_copy(kv_all, kv_core, shard).start())
    wq.cores()
    wo.relay()
    for shard in wq.others() + [at]:
        wq.recv(4, shard).wait_recv()
    load = pltpu.make_async_copy(wq_all, wq_vmem, local_sems.at[1])
    load.start()
    for hop in range(2, count):
        kv.step(hop, lambda shard: core_copy(kv_all, kv_core, shard).start())
    load.wait()
    weight = wq_vmem.reshape(width, width)

    def columns(block):
        start = pl.multiple_of(block * 512, 512)
        raw = matmul(normed_ref[...], weight[:, pl.ds(start, 512)])
        for h in range(4):
            head = raw[:, h * 128 : (h + 1) * 128]
            turned = head * cos_table + pltpu.roll(head, 64, 1) * sin_table
            q_ref[:, pl.ds(start + h * 128, 128)] = turned.astype(jnp.bfloat16)

    pl.loop(0, width // 512)(columns)
    wo.cores()
    for shard in range(count):
        core_copy(kv_all, kv_core, shard, True).wait_recv()
    wo.finish()
    for shard in wq.others():
        for kind in range(5):
            wq.copy(kind, shard).wait_send()
    wq.copy(4, at).wait_send()
    for shard in range(count):
        core_copy(kvg_all, kvg_core, shard).wait_send()
        core_copy(kv_all, kv_core, shard).wait_send()
    for chain in (kvg, kv, wq_chain, wo_chain):
        chain.finish()


def project(tokens, wq, wo, kvg, cos_table, sin_table):
    rows, width = tokens.shape
    shard = wq.shape[0]
    fsdp_size = lax.axis_size("fsdp")
    count = fsdp_size // 2
    low = jnp.bfloat16
    vmem, hbm = pl.BlockSpec(memory_space=pltpu.VMEM), pl.BlockSpec(memory_space=pl.ANY)
    dma = pltpu.SemaphoreType.DMA
    return pl.pallas_call(
        functools.partial(project_kernel, fsdp_size),
        out_shape=(
            jax.ShapeDtypeStruct((rows, width), low),
            jax.ShapeDtypeStruct((rows, width), low),
            jax.ShapeDtypeStruct((8, width), jnp.float32),
            jax.ShapeDtypeStruct((fsdp_size, shard, width), low),
            jax.ShapeDtypeStruct((fsdp_size, shard, width), low),
            jax.ShapeDtypeStruct((fsdp_size, shard, kvg.shape[1]), low),
            jax.ShapeDtypeStruct((fsdp_size, rows, 256), low),
        ),
        in_specs=[vmem, hbm, hbm, hbm, vmem, vmem],
        out_specs=(vmem, vmem, vmem, hbm, hbm, hbm, hbm),
        scratch_shapes=[
            pltpu.VMEM((fsdp_size, shard, width), low),
            pltpu.VMEM((fsdp_size, shard, kvg.shape[1]), low),
            pltpu.VMEM((rows, 256), low),
            dma((3,)),
            dma((2, 2, count)),
            dma((2, count)),
            dma((2, 2, count)),
            dma((2, 5, count)),
            dma((2, 2, count)),
            dma((2, 5, count)),
            dma((2, 2, count)),
            dma((2, count)),
        ],
        compiler_params=pltpu.CompilerParams(
            collective_id=0, has_side_effects=True, vmem_limit_bytes=48 << 20
        ),
        cost_estimate=pl.CostEstimate(
            flops=2 * rows * width * (width + 256), transcendentals=0, bytes_accessed=40 << 20
        ),
        name="project",
    )(tokens, wq, wo, kvg, cos_table, sin_table)


def greet(replica, fsdp, at, count):
    barrier = pltpu.get_barrier_semaphore()
    for target in (
        (replica, flip(fsdp, 1)),
        (flip(replica, 1), fsdp),
        (flip(replica, 2), fsdp),
    ):
        pl.semaphore_signal(barrier, inc=1, device_id=target, device_id_type=MESH)

    @pl.when(at > 0)
    def _():
        pl.semaphore_signal(barrier, inc=1, device_id=(replica, fsdp - 2), device_id_type=MESH)

    @pl.when(at < count - 1)
    def _():
        pl.semaphore_signal(barrier, inc=1, device_id=(replica, fsdp + 2), device_id_type=MESH)

    inside = (at > 0) & (at < count - 1)

    @pl.when(inside)
    def _():
        pl.semaphore_wait(barrier, 5)

    @pl.when(jnp.logical_not(inside))
    def _():
        pl.semaphore_wait(barrier, 4)


def add_into(ref, index, *others):
    total = ref[index].astype(jnp.float32)
    for other in others:
        total = total + other.astype(jnp.float32)
    ref[index] = total.astype(ref.dtype)


class Collect:
    def __init__(self, place, grad, core_in, line_in, core_sems, line_sems, copies=None):
        self.replica, self.fsdp, self.at, self.core, self.count = place
        self.grad, self.core_in, self.line_in = grad, core_in, line_in
        self.core_sems, self.line_sems = core_sems, line_sems
        self.beside, self.across = flip(self.replica, 1), flip(self.replica, 2)
        self.opposite = flip(self.beside, 2)
        if copies is None:
            self.rows = pl.ds(0, grad.shape[1])
        else:
            self.diag_in, self.quarter_in, self.full = copies[:3]
            self.diag_sems, self.quarter_sems, self.full_sems = copies[3:]
            self.size = grad.shape[1] // 4
            self.rows = self.quarter(self.replica)

    def quarter(self, copy, half=None):
        size = self.size if half is None else self.size // 2
        start = copy * self.size + (0 if half is None else half * size)
        return pl.ds(pl.multiple_of(start, size), size)

    def remote(self, src, dst, sems, index, target):
        return pltpu.make_async_remote_copy(
            src_ref=src,
            dst_ref=dst,
            send_sem=sems.at[(0,) + index],
            recv_sem=sems.at[(1,) + index],
            device_id=target,
            device_id_type=MESH,
        )

    def core_copy(self, shard):
        return self.remote(
            self.grad.at[2 * shard + 1 - self.core],
            self.core_in.at[shard],
            self.core_sems,
            (shard,),
            (self.replica, flip(self.fsdp, 1)),
        )

    def core_add(self, shard):
        self.core_copy(shard).wait_recv()
        add_into(self.grad, 2 * shard + self.core, self.core_in[shard])

    def diag_copy(self, shard, half):
        return self.remote(
            self.grad.at[2 * shard + self.core, self.quarter(self.opposite, half)],
            self.diag_in.at[half, shard],
            self.diag_sems,
            (half, shard),
            (self.beside if half == 0 else self.across, self.fsdp),
        )

    def diag_start(self, shard):
        self.diag_copy(shard, 0).start()
        self.diag_copy(shard, 1).start()

    def quarter_copy(self, shard, way):
        return self.remote(
            self.grad.at[2 * shard + self.core, self.quarter(self.across if way else self.beside)],
            self.quarter_in.at[way, shard],
            self.quarter_sems,
            (way, shard),
            (self.across if way else self.beside, self.fsdp),
        )

    def quarter_start(self, shard):
        at = 2 * shard + self.core
        for half, copy in ((0, self.across), (1, self.beside)):
            self.diag_copy(shard, half).wait_recv()
            add_into(self.grad, (at, self.quarter(copy, half)), self.diag_in[half, shard])
            self.quarter_copy(shard, 1 - half).start()

    def quarter_add(self, shard):
        self.quarter_copy(shard, 0).wait_recv()
        self.quarter_copy(shard, 1).wait_recv()
        add_into(
            self.grad,
            (2 * shard + self.core, self.rows),
            self.quarter_in[0, shard],
            self.quarter_in[1, shard],
        )

    def line_copy(self, shard, way):
        return self.remote(
            self.grad.at[2 * shard + self.core, self.rows],
            self.line_in.at[way, shard],
            self.line_sems,
            (way, shard),
            (self.replica, self.fsdp + (2 if way == 0 else -2)),
        )

    def line_receive(self, shard, way):
        self.line_copy(shard, way).wait_recv()
        add_into(self.grad, (2 * shard + self.core, self.rows), self.line_in[way, shard])

    def line_hop(self, hop):
        for way, shard, there, fed in (
            (0, self.at + hop, self.at + hop < self.count, self.at > 0),
            (1, self.at - hop, self.at - hop >= 0, self.at < self.count - 1),
        ):

            @pl.when(there & fed)
            def _(shard=shard, way=way):
                self.line_receive(shard, way)

            @pl.when(there)
            def _(shard=shard, way=way):
                self.line_copy(shard, way).start()

    def line_end(self):
        @pl.when(self.at > 0)
        def _():
            self.line_receive(self.at, 0)

        @pl.when(self.at < self.count - 1)
        def _():
            self.line_receive(self.at, 1)

    def full_copy(self, kind):
        own = self.replica
        rows, target = (
            (self.quarter(own), self.beside),
            (self.quarter(own), self.across),
            (self.quarter(self.beside, 0), self.across),
            (self.quarter(self.across, 1), self.beside),
        )[kind]
        return self.remote(
            self.full.at[rows],
            self.full.at[rows],
            self.full_sems,
            (kind,),
            (target, self.fsdp),
        )

    def full_recv(self, kind):
        rows = (
            self.quarter(self.beside),
            self.quarter(self.across),
            self.quarter(self.opposite, 0),
            self.quarter(self.opposite, 1),
        )[kind]
        ref = self.full.at[rows]
        self.remote(ref, ref, self.full_sems, (kind,), (self.beside, self.fsdp)).wait_recv()

    def gather_start(self):
        self.full[self.rows] = self.grad[2 * self.at + self.core, self.rows]
        self.full_copy(0).start()
        self.full_copy(1).start()

    def gather_relay(self):
        self.full_recv(0)
        self.full_copy(2).start()
        self.full_recv(1)
        self.full_copy(3).start()

    def gather_end(self):
        self.full_recv(2)
        self.full_recv(3)

    def drain(self):
        for shard in range(self.count):
            self.core_copy(shard).wait_send()
            if hasattr(self, "size"):
                for way in (0, 1):
                    self.diag_copy(shard, way).wait_send()
                    self.quarter_copy(shard, way).wait_send()
        for hop in range(1, self.count):

            @pl.when(self.at + hop < self.count)
            def _(hop=hop):
                self.line_copy(self.at + hop, 0).wait_send()

            @pl.when(self.at - hop >= 0)
            def _(hop=hop):
                self.line_copy(self.at - hop, 1).wait_send()

        if hasattr(self, "size"):
            for kind in range(4):
                self.full_copy(kind).wait_send()


def collect_scratch(fsdp_size, rows, width, copies=True):
    count = fsdp_size // 2
    low, dma = jnp.bfloat16, pltpu.SemaphoreType.DMA
    size = rows // 4 if copies else rows
    shapes = [
        pltpu.VMEM((fsdp_size, rows, width), low),
        pltpu.VMEM((count, rows, width), low),
        pltpu.VMEM((2, count, size, width), low),
        dma((2, count)),
        dma((2, 2, count)),
    ]
    if copies:
        shapes += [
            pltpu.VMEM((2, count, size // 2, width), low),
            pltpu.VMEM((2, count, size, width), low),
            pltpu.VMEM((rows, width), low),
            dma((2, 2, count)),
            dma((2, 2, count)),
            dma((2, 4)),
        ]
    return shapes


def make_collect(place, refs, copies=True):
    return Collect(place, *refs[:5], copies=refs[5:11] if copies else None)


def position(fsdp_size):
    replica, fsdp = lax.axis_index("replica"), lax.axis_index("fsdp")
    return replica, fsdp, fsdp // 2, fsdp % 2, fsdp_size // 2


def outer(collect, left_ref, right_ref, own_core):
    rows = collect.grad.shape[1]
    core = collect.core if own_core else 1 - collect.core

    @pl.loop(0, collect.count)
    def _(shard):
        start = pl.multiple_of((2 * shard + core) * rows, rows)
        part = contract(left_ref[:, pl.ds(start, rows)], right_ref[...], 0, 0)
        collect.grad[2 * shard + core] = part.astype(jnp.bfloat16)
        if not own_core:
            collect.core_copy(shard).start()


def each(count, step):
    for shard in range(count):
        step(shard)


def outer_kernel(fsdp_size, left_ref, right_ref, out_ref, *refs):
    place = position(fsdp_size)
    greet(*place[:3], place[4])
    sums = make_collect(place, refs)
    count = place[4]
    outer(sums, left_ref, right_ref, False)
    outer(sums, left_ref, right_ref, True)
    for shard in range(count):
        sums.core_add(shard)
        sums.diag_start(shard)
    each(count, sums.quarter_start)
    each(count, sums.quarter_add)
    for hop in range(count - 1, 0, -1):
        sums.line_hop(hop)
    sums.line_end()
    sums.gather_start()
    sums.gather_relay()
    sums.gather_end()
    out_ref[...] = sums.full[...].astype(jnp.float32)
    sums.drain()


def outer_sum(left, right, collective_id):
    fsdp_size = lax.axis_size("fsdp")
    rows, width = left.shape[1] // fsdp_size, right.shape[1]
    vmem = pl.BlockSpec(memory_space=pltpu.VMEM)
    return pl.pallas_call(
        functools.partial(outer_kernel, fsdp_size),
        out_shape=jax.ShapeDtypeStruct((rows, width), jnp.float32),
        in_specs=[vmem, vmem],
        out_specs=vmem,
        scratch_shapes=collect_scratch(fsdp_size, rows, width),
        compiler_params=pltpu.CompilerParams(
            collective_id=collective_id, has_side_effects=True, vmem_limit_bytes=56 << 20
        ),
        cost_estimate=pl.CostEstimate(
            flops=40 * left.shape[0] * left.shape[1] * width, transcendentals=0, bytes_accessed=8 << 20
        ),
        name="outer_sum",
    )(left, right)


def finish_kernel(
    fsdp_size,
    normed_ref,
    d_q_ref,
    tokens_ref,
    d_hidden_ref,
    gain_ref,
    term_ref,
    cos_ref,
    sin_ref,
    d_kv_ref,
    wq_ref,
    kvg_ref,
    ffn_ref,
    input_grad_ref,
    q_grad_ref,
    kv_grad_ref,
    ffn_all,
    wq_buf,
    kvg_vmem,
    d_kv_raw,
    term_sum,
    local_sems,
    ffn_sems,
    *refs,
):
    place = position(fsdp_size)
    replica, fsdp, at, core, count = place
    greet(replica, fsdp, at, count)
    q_sums = make_collect(place, refs[:11])
    kv_sums = make_collect(place, refs[11:22])
    d_kv = make_collect(place, refs[22:27], False)
    beside, across = flip(replica, 1), flip(replica, 2)
    width = tokens_ref.shape[1]
    half = width // 2

    def ffn_copy(kind, lands=False):
        piece = (replica, replica, beside, across)[kind]
        if lands:
            piece = (beside, across, flip(beside, 2), flip(beside, 2))[kind]
        columns = (slice(None), slice(None), pl.ds(0, half), pl.ds(half, half))[kind]
        src = ffn_all.at[piece, :, :, columns]
        return pltpu.make_async_remote_copy(
            src_ref=src,
            dst_ref=src,
            send_sem=ffn_sems.at[0, kind],
            recv_sem=ffn_sems.at[1, kind],
            device_id=((beside, across, across, beside)[kind], fsdp),
            device_id_type=MESH,
        )

    own_ffn = pltpu.make_async_copy(ffn_ref, ffn_all.at[replica], local_sems.at[0])
    own_ffn.start()
    load = pltpu.make_async_copy(d_kv_ref, d_kv.grad, local_sems.at[1])
    load.start()
    load_kvg = pltpu.make_async_copy(kvg_ref, kvg_vmem, local_sems.at[2])
    load_kvg.start()
    load.wait()
    each(count, lambda shard: d_kv.core_copy(shard).start())
    outer(q_sums, normed_ref, d_q_ref, False)
    each(count, d_kv.core_add)
    d_kv.line_hop(count - 1)
    outer(q_sums, normed_ref, d_q_ref, True)
    for hop in range(count - 2, 0, -1):
        d_kv.line_hop(hop)
    for shard in range(count):
        q_sums.core_add(shard)
        q_sums.diag_start(shard)
    d_kv.line_end()
    each(count, q_sums.quarter_start)
    own_ffn.wait()
    ffn_copy(0).start()
    ffn_copy(1).start()

    summed = d_kv.grad[fsdp].astype(jnp.float32)
    d_key = summed[:, :128]
    d_key = d_key * cos_ref[...] - pltpu.roll(d_key, 64, 1) * sin_ref[...]
    d_kv_raw[:, :128] = d_key.astype(jnp.bfloat16)
    d_kv_raw[:, 128:] = summed[:, 128:].astype(jnp.bfloat16)
    load_kvg.wait()
    rows = kvg_vmem.shape[1]

    def fetch(shard):
        return pltpu.make_async_copy(wq_ref.at[shard], wq_buf.at[shard % 2], local_sems.at[shard % 2])

    fetch(0).start()
    for shard in range(fsdp_size):
        fetch(shard).wait()
        if shard + 1 < fsdp_size:
            fetch(shard + 1).start()
        input_grad_ref[:, shard * rows : (shard + 1) * rows] = contract(
            d_q_ref[...], wq_buf[shard % 2], 1, 1
        ) + contract(d_kv_raw[...], kvg_vmem[shard, :, :256], 1, 1)
    each(count, q_sums.quarter_add)
    for hop in range(count - 1, 0, -1):
        q_sums.line_hop(hop)

    term_sum[...] = jnp.zeros_like(term_sum)

    @pl.loop(0, tokens_ref.shape[0] // 128)
    def _(block):
        part = pl.ds(pl.multiple_of(block * 128, 128), 128)
        d_normed = input_grad_ref[part]
        inputs = tokens_ref[part].astype(jnp.float32)
        inverse = lax.rsqrt(jnp.mean(inputs * inputs, axis=1, keepdims=True) + EPSILON)
        scaled = d_normed * gain_ref[:1]
        inner = jnp.mean(scaled * inputs, axis=1, keepdims=True)
        term_sum[:1] += jnp.sum(d_normed * inputs * inverse, axis=0, keepdims=True)
        input_grad_ref[part] = (
            d_hidden_ref[part] + inverse * scaled - inputs * (inverse**3 * inner)
        )

    term = term_sum[:1]
    line = lax.broadcasted_iota(jnp.int32, (128, width), 0)
    terms = jnp.where(line == 0, term, jnp.where(line == 1, term_ref[:1], 0.0)).T
    terms = terms.astype(jnp.bfloat16)
    for shard in range(fsdp_size):
        left = normed_ref[:, shard * rows : (shard + 1) * rows]
        kv_sums.grad[shard, :, :256] = contract(left, d_kv_raw[...], 0, 0).astype(jnp.bfloat16)
        kv_sums.grad[shard, :, 256:] = terms[shard * rows : (shard + 1) * rows]
    each(count, lambda shard: kv_sums.core_copy(shard).start())
    q_sums.line_end()
    q_sums.gather_start()
    for shard in range(count):
        kv_sums.core_add(shard)
        kv_sums.diag_start(shard)
    each(count, kv_sums.quarter_start)
    q_sums.gather_relay()
    each(count, kv_sums.quarter_add)
    for hop in range(count - 1, 0, -1):
        kv_sums.line_hop(hop)
    for kind in (0, 1):
        ffn_copy(kind, True).wait_recv()
        ffn_copy(2 + kind).start()
    kv_sums.line_end()
    kv_sums.gather_start()
    q_sums.gather_end()
    q_grad_ref[...] = q_sums.full[...].astype(jnp.float32)
    kv_sums.gather_relay()
    kv_sums.gather_end()
    kv_grad_ref[...] = kv_sums.full[...].astype(jnp.float32)
    for kind in (2, 3):
        ffn_copy(kind, True).wait_recv()
    for kind in range(4):
        ffn_copy(kind).wait_send()
    for sums in (q_sums, kv_sums, d_kv):
        sums.drain()


def finish(
    normed, d_q, tokens, d_hidden, gains, term, cos_table, sin_table, d_kv, wq_all, kvg_all, ffn
):
    fsdp_size, rows, width = wq_all.shape
    tok_rows = tokens.shape[0]
    low, dma = jnp.bfloat16, pltpu.SemaphoreType.DMA
    vmem, hbm = pl.BlockSpec(memory_space=pltpu.VMEM), pl.BlockSpec(memory_space=pl.ANY)
    return pl.pallas_call(
        functools.partial(finish_kernel, fsdp_size),
        out_shape=(
            jax.ShapeDtypeStruct((tok_rows, width), jnp.float32),
            jax.ShapeDtypeStruct((rows, width), jnp.float32),
            jax.ShapeDtypeStruct((rows, 384), jnp.float32),
            jax.ShapeDtypeStruct((4,) + ffn.shape, low),
        ),
        in_specs=[vmem] * 8 + [hbm] * 4,
        out_specs=(vmem, vmem, vmem, hbm),
        scratch_shapes=[
            pltpu.VMEM((2, rows, width), low),
            pltpu.VMEM((fsdp_size, rows, 384), low),
            pltpu.VMEM((tok_rows, 256), low),
            pltpu.VMEM((8, width), jnp.float32),
            dma((3,)),
            dma((2, 4)),
        ]
        + collect_scratch(fsdp_size, rows, width)
        + collect_scratch(fsdp_size, rows, 384)
        + collect_scratch(fsdp_size, tok_rows, 256, False),
        compiler_params=pltpu.CompilerParams(
            collective_id=2, has_side_effects=True, vmem_limit_bytes=60 << 20
        ),
        cost_estimate=pl.CostEstimate(
            flops=100 * tok_rows * width * width, transcendentals=0, bytes_accessed=40 << 20
        ),
        name="finish",
    )(normed, d_q, tokens, d_hidden, gains, term, cos_table, sin_table, d_kv, wq_all, kvg_all, ffn)


def swap(value, step):
    copies = lax.axis_size("replica")
    return lax.ppermute(value, "replica", [(r, r ^ step) for r in range(copies)])


def gather_copies(block):
    half = block.shape[0] // 2
    beside, across = swap(block, 1), swap(block, 2)
    opposite = jnp.concatenate([swap(beside[:half], 2), swap(across[half:], 1)], axis=0)
    return [block, beside, across, opposite]


def scatter_copies(parts):
    own, beside, across, opposite = parts
    half = opposite.shape[0] // 2
    low = jnp.bfloat16
    first = swap(opposite[:half].astype(low), 1)
    second = swap(opposite[half:].astype(low), 2)
    across = jnp.concatenate(
        [across[:half].astype(jnp.float32) + first.astype(jnp.float32), across[half:]], axis=0
    )
    beside = jnp.concatenate(
        [beside[:half], beside[half:].astype(jnp.float32) + second.astype(jnp.float32)], axis=0
    )
    return (
        own.astype(jnp.float32)
        + swap(beside.astype(low), 1).astype(jnp.float32)
        + swap(across.astype(low), 2).astype(jnp.float32)
    )


def gather_shards(value):
    return lax.all_gather(value, "fsdp", axis=0, tiled=True)


def scatter_shards(value):
    return lax.psum_scatter(value, "fsdp", scatter_dimension=0, tiled=True)


def after(value, *others):
    return lax.optimization_barrier((value, others))[0]


def quarter(shard, copy_index):
    rows = shard.shape[0] // lax.axis_size("replica")
    return lax.dynamic_slice_in_dim(shard, copy_index * rows, rows, 0)


def shards(
    tokens,
    segments,
    positions,
    query_weight,
    key_weight,
    value_weight,
    output_weight,
    attn_gain,
    gate_weight,
    up_weight,
    down_weight,
    ffn_gain,
    grad_out,
):
    tok_rows, model_width = tokens.shape
    head_dim = key_weight.shape[1]
    fsdp_size = lax.axis_size("fsdp")
    fsdp_index = lax.axis_index("fsdp")
    copy_index = lax.axis_index("replica")
    copies = lax.axis_size("replica")
    low = jnp.bfloat16

    cos_table, sin_table = rope_tables(positions, head_dim)
    gain_columns = jnp.stack([attn_gain, ffn_gain], axis=1)
    queries, normed, gains, wq_all, w_out, kvg_all, kv_all = project(
        tokens,
        query_weight,
        output_weight,
        jnp.concatenate(
            [key_weight, value_weight, jnp.pad(gain_columns, ((0, 0), (0, 126)))], axis=1
        ),
        cos_table,
        sin_table,
    )
    w_out = w_out.reshape(model_width, model_width)
    kv_all = kv_all.reshape(fsdp_size * tok_rows, 2 * head_dim)
    gain_ffn = gains[1]
    inputs = tokens.astype(jnp.float32)
    key_width = max(GROUP_TOK, tok_rows)
    window_start = fsdp_index * tok_rows // key_width * key_width
    one_group = fsdp_size * tok_rows == key_width
    kv = kv_all if one_group else lax.dynamic_slice_in_dim(kv_all, window_start, key_width, 0)

    base = (fsdp_index * tok_rows - window_start).astype(jnp.int32)
    row_at = base + jnp.arange(tok_rows, dtype=jnp.int32)
    lowest = jnp.where(positions < PROMPT, 0, row_at - (positions - PROMPT))
    base = base[None]
    mixed_rows, logs = attend(
        base, queries, kv, jnp.broadcast_to(lowest[:, None], (tok_rows, 128))
    )

    hidden = inputs + matmul(mixed_rows, w_out)
    normed_ffn_full, inverse_ffn = norm_forward(hidden, gain_ffn)
    normed_ffn = normed_ffn_full.astype(low)

    w_gate = gather_shards(quarter(gate_weight.T, copy_index))
    w_up = gather_shards(quarter(up_weight.T, copy_index))
    w_down = gather_shards(quarter(down_weight, copy_index))
    grad_blocks = gather_copies(grad_out)
    grads = jnp.concatenate(grad_blocks, axis=0)
    normed_blocks = gather_copies(normed_ffn)
    normed_all = jnp.concatenate(normed_blocks, axis=0)

    d_activation = contract(grads, w_down, 1, 1)
    gate_proj = contract(normed_all, w_gate, 1, 1)
    up_proj = contract(normed_all, w_up, 1, 1)
    activation = (jax.nn.silu(gate_proj) * up_proj).astype(low)
    d_gate, d_up = swiglu_back(d_activation, gate_proj, up_proj)
    d_normed_parts = matmul(d_gate, w_gate) + matmul(d_up, w_up)
    d_normed_ffn = scatter_copies(jnp.split(d_normed_parts, copies))
    out_parts = matmul(activation, w_down).astype(low)

    gate_part = contract(d_gate, normed_all, 0, 0).astype(low)
    up_part = contract(d_up, normed_all, 0, 0).astype(low)
    down_part = contract(activation, grads, 0, 0).astype(low)

    def ffn_grad(partial):
        summed = scatter_shards(partial)
        pieces = place(gather_copies(summed), copy_index)
        return pieces.reshape(-1, model_width).astype(jnp.float32)

    cotangent = grad_out.astype(jnp.float32)
    resid_ffn, ffn_gain_term = norm_backward(hidden, inverse_ffn, gain_ffn, d_normed_ffn)
    d_hidden = cotangent + resid_ffn
    d_branch = d_hidden.astype(low)
    d_mixed = contract(d_branch, w_out, 1, 1).astype(low)
    d_mixed = after(d_mixed, gate_part, up_part, down_part)
    gate_sum = scatter_shards(gate_part)
    up_sum = scatter_shards(up_part)
    down_sum = scatter_shards(down_part)
    output_grad = outer_sum(mixed_rows, d_branch, 1)
    own_out, *other_outs = jnp.split(after(out_parts, output_grad), copies)
    layer_out = hidden + own_out.astype(jnp.float32)
    for step, part in enumerate(other_outs):
        layer_out = layer_out + swap(part, step + 1).astype(jnp.float32)
    layer_out = layer_out.astype(low)
    d_query_raw, d_kv = attend_back(
        base,
        queries,
        kv,
        cos_table,
        sin_table,
        jnp.broadcast_to(lowest[None, :], (8, tok_rows)),
        mixed_rows,
        d_mixed,
        logs,
    )
    if not one_group:
        d_kv = lax.dynamic_update_slice_in_dim(
            jnp.zeros((fsdp_size * tok_rows, 2 * head_dim), low), d_kv, window_start, 0
        )
    input_grad, query_grad, kv_grad, ffn_all = finish(
        normed,
        d_query_raw,
        tokens,
        d_hidden,
        gains,
        jnp.broadcast_to(ffn_gain_term[None], (8, model_width)),
        cos_table,
        sin_table,
        d_kv.reshape(fsdp_size, tok_rows, 2 * head_dim),
        wq_all,
        kvg_all,
        jnp.stack([gate_sum, up_sum, down_sum]),
    )
    gate_grad, up_grad, down_grad = (
        ffn_all[:, i].reshape(-1, model_width).astype(jnp.float32) for i in range(3)
    )
    return (
        layer_out,
        input_grad,
        query_grad,
        kv_grad[:, :head_dim],
        kv_grad[:, head_dim : 2 * head_dim],
        output_grad,
        kv_grad[:, 2 * head_dim],
        gate_grad.T,
        up_grad.T,
        down_grad,
        kv_grad[:, 2 * head_dim + 1],
    )


def half_tables(pos_ids, head_dim):
    half_width = head_dim // 2
    frequency = ROPE_BASE ** (-jnp.arange(half_width, dtype=jnp.float32) * 2.0 / head_dim)
    angles = pos_ids.astype(jnp.float32)[:, None] * frequency[None, :]
    return (jnp.cos(angles), jnp.sin(angles))


def rotate(values, cos_table, sin_table):
    half_width = values.shape[-1] // 2
    front_half = values[..., :half_width]
    back_half = values[..., half_width:]
    return jnp.concatenate(
        [
            front_half * cos_table - back_half * sin_table,
            back_half * cos_table + front_half * sin_table,
        ],
        axis=-1,
    )


def any_shards(
    tokens,
    segments,
    positions,
    query_weight,
    key_weight,
    value_weight,
    output_weight,
    attn_gain,
    gate_weight,
    up_weight,
    down_weight,
    ffn_gain,
    grad_out,
):
    tok_rows, model_width = tokens.shape
    head_dim = key_weight.shape[1]
    head_count = model_width // head_dim
    block_count = head_count // HEAD_BLOCK
    block_width = HEAD_BLOCK * head_dim
    score_scale = head_dim ** (-0.5)
    fsdp_size = lax.axis_size("fsdp")
    fsdp_index = lax.axis_index("fsdp")
    gathered = (
        lax.all_gather(query_weight, "fsdp", axis=0, tiled=True),
        lax.all_gather(key_weight, "fsdp", axis=0, tiled=True),
        lax.all_gather(value_weight, "fsdp", axis=0, tiled=True),
        lax.all_gather(output_weight, "fsdp", axis=0, tiled=True),
        lax.all_gather(attn_gain, "fsdp", axis=0, tiled=True),
        lax.all_gather(ffn_gain, "fsdp", axis=0, tiled=True),
    )
    w_query, w_key, w_value, w_out, gain_attn, gain_ffn = gathered
    gain_attn = gain_attn.astype(jnp.float32)
    gain_ffn = gain_ffn.astype(jnp.float32)
    inputs = tokens.astype(jnp.float32)
    normed_full, inverse_attn = norm_forward(inputs, gain_attn)
    normed = normed_full.astype(jnp.bfloat16)
    query_raw = matmul(normed, w_query)
    key_raw = matmul(normed, w_key)
    value_rows = matmul(normed, w_value).astype(jnp.bfloat16)
    cos_table, sin_table = half_tables(positions, head_dim)
    queries = rotate(
        query_raw.reshape(tok_rows, head_count, head_dim), cos_table[:, None], sin_table[:, None]
    ).astype(jnp.bfloat16)
    key_rot = rotate(key_raw, cos_table, sin_table).astype(jnp.bfloat16)
    key_rows, value_all = (
        lax.all_gather(key_rot, "fsdp", axis=0, tiled=True),
        lax.all_gather(value_rows, "fsdp", axis=0, tiled=True),
    )
    seg_all, pos_all = (
        lax.all_gather(segments, "fsdp", axis=0, tiled=True),
        lax.all_gather(positions, "fsdp", axis=0, tiled=True),
    )
    key_width = max(GROUP_TOK, tok_rows)
    window_start = fsdp_index * tok_rows // GROUP_TOK * GROUP_TOK
    key_window = lax.dynamic_slice_in_dim(key_rows, window_start, key_width, 0)
    value_window = lax.dynamic_slice_in_dim(value_all, window_start, key_width, 0)
    seg_window = lax.dynamic_slice_in_dim(seg_all, window_start, key_width, 0)
    pos_window = lax.dynamic_slice_in_dim(pos_all, window_start, key_width, 0)
    key_index = window_start + jnp.arange(key_width, dtype=jnp.int32)
    query_index = fsdp_index * tok_rows + jnp.arange(tok_rows, dtype=jnp.int32)
    visible = (
        (key_index[None, :] // GROUP_TOK == query_index[:, None] // GROUP_TOK)
        & (pos_window[None, :] <= positions[:, None])
        & ((seg_window[None, :] == 0) | (seg_window[None, :] == segments[:, None]))
    )
    query_blocks = queries.reshape(tok_rows, block_count, block_width).transpose(1, 0, 2)

    def block_scores(query_block):
        flat_queries = query_block.reshape(tok_rows * HEAD_BLOCK, head_dim)
        scores = (
            contract(flat_queries, key_window, 1, 1).reshape(tok_rows, HEAD_BLOCK, key_width)
            * score_scale
        )
        return (flat_queries, scores)

    def attend_block(query_block):
        flat_queries, scores = block_scores(query_block)
        scores = jnp.where(visible[:, None, :], scores, MASKED)
        row_max = jnp.max(scores, axis=-1, keepdims=True)
        exp_scores = jnp.exp(scores - row_max)
        totals = jnp.sum(exp_scores, axis=-1, keepdims=True)
        weights = (
            (exp_scores / totals).astype(jnp.bfloat16).reshape(tok_rows * HEAD_BLOCK, key_width)
        )
        mixed_block = matmul(weights, value_window).reshape(tok_rows, block_width)
        return (mixed_block, (row_max + jnp.log(totals))[..., 0])

    mixed_blocks, log_totals = lax.map(attend_block, query_blocks)
    mixed_rows = mixed_blocks.transpose(1, 0, 2).reshape(tok_rows, model_width).astype(jnp.bfloat16)
    hidden = inputs + matmul(mixed_rows, w_out)
    normed_ffn_full, inverse_ffn = norm_forward(hidden, gain_ffn)
    normed_ffn = normed_ffn_full.astype(jnp.bfloat16)
    cotangent = grad_out.astype(jnp.float32)
    w_gate, w_up, w_down = (
        lax.all_gather(gate_weight, "fsdp", axis=1, tiled=True),
        lax.all_gather(up_weight, "fsdp", axis=1, tiled=True),
        lax.all_gather(down_weight, "fsdp", axis=0, tiled=True),
    )
    gate_proj = matmul(normed_ffn, w_gate)
    up_proj = matmul(normed_ffn, w_up)
    activation = (jax.nn.silu(gate_proj) * up_proj).astype(jnp.bfloat16)
    layer_out = (hidden + matmul(activation, w_down)).astype(jnp.bfloat16)
    d_activation = contract(grad_out, w_down, 1, 1)
    d_gate, d_up = swiglu_back(d_activation, gate_proj, up_proj)
    d_normed_ffn = contract(d_gate, w_gate, 1, 1) + contract(d_up, w_up, 1, 1)
    gate_up_part = lax.psum_scatter(
        jnp.concatenate(
            [contract(d_gate, normed_ffn, 0, 0), contract(d_up, normed_ffn, 0, 0)], axis=1
        ).astype(jnp.bfloat16),
        "fsdp",
        scatter_dimension=0,
        tiled=True,
    ).astype(jnp.float32)
    gate_part = gate_up_part[:, :model_width].T
    up_part = gate_up_part[:, model_width:].T
    down_part = lax.psum_scatter(
        contract(activation, grad_out, 0, 0).astype(jnp.bfloat16),
        "fsdp",
        scatter_dimension=0,
        tiled=True,
    )
    resid_ffn, ffn_gain_term = norm_backward(hidden, inverse_ffn, gain_ffn, d_normed_ffn)
    d_hidden = cotangent + resid_ffn
    d_branch = d_hidden.astype(jnp.bfloat16)
    d_mixed = contract(d_branch, w_out, 1, 1).astype(jnp.bfloat16)
    d_mixed_blocks = d_mixed.reshape(tok_rows, block_count, block_width).transpose(1, 0, 2)

    def back_block(totals, block_items):
        query_block, d_block, log_block = block_items
        flat_queries, scores = block_scores(query_block)
        probs = jnp.where(visible[:, None, :], jnp.exp(scores - log_block[..., None]), 0.0)
        d_flat = d_block.reshape(tok_rows * HEAD_BLOCK, head_dim)
        d_probs = contract(d_flat, value_window, 1, 1).reshape(tok_rows, HEAD_BLOCK, key_width)
        row_delta = jnp.sum(probs * d_probs, axis=-1, keepdims=True)
        d_scores = (
            (probs * (d_probs - row_delta))
            .astype(jnp.bfloat16)
            .reshape(tok_rows * HEAD_BLOCK, key_width)
        )
        weights = probs.astype(jnp.bfloat16).reshape(tok_rows * HEAD_BLOCK, key_width)
        d_query_block = matmul(d_scores, key_window) * score_scale
        key_total = totals[0] + contract(d_scores, flat_queries, 0, 0) * score_scale
        value_total = totals[1] + contract(weights, d_flat, 0, 0)
        return ((key_total, value_total), d_query_block.reshape(tok_rows, block_width))

    zero_window = jnp.zeros((key_width, head_dim), jnp.float32)
    window_grads, d_query_blocks = lax.scan(
        back_block, (zero_window, zero_window), (query_blocks, d_mixed_blocks, log_totals)
    )
    d_queries = d_query_blocks.transpose(1, 0, 2).reshape(tok_rows, head_count, head_dim)
    d_query_raw = (
        rotate(d_queries, cos_table[:, None], -sin_table[:, None])
        .astype(jnp.bfloat16)
        .reshape(tok_rows, model_width)
    )
    row_zeros = jnp.zeros((fsdp_size * tok_rows, head_dim), jnp.float32)
    key_term = lax.dynamic_update_slice_in_dim(row_zeros, window_grads[0], window_start, 0)
    value_term = lax.dynamic_update_slice_in_dim(row_zeros, window_grads[1], window_start, 0)
    key_sum, value_sum = (
        lax.psum_scatter(
            key_term.astype(jnp.bfloat16), "fsdp", scatter_dimension=0, tiled=True
        ).astype(jnp.float32),
        lax.psum_scatter(
            value_term.astype(jnp.bfloat16), "fsdp", scatter_dimension=0, tiled=True
        ).astype(jnp.float32),
    )
    d_key_raw = rotate(key_sum, cos_table, -sin_table).astype(jnp.bfloat16)
    d_value = value_sum.astype(jnp.bfloat16)
    d_normed = (
        contract(d_query_raw, w_query, 1, 1)
        + contract(d_key_raw, w_key, 1, 1)
        + contract(d_value, w_value, 1, 1)
    )
    resid_attn, attn_gain_term = norm_backward(inputs, inverse_attn, gain_attn, d_normed)
    input_grad = d_hidden + resid_attn
    attn_part = lax.psum_scatter(
        jnp.concatenate(
            [
                contract(normed, d_query_raw, 0, 0),
                contract(normed, d_key_raw, 0, 0),
                contract(normed, d_value, 0, 0),
                contract(mixed_rows, d_branch, 0, 0),
            ],
            axis=1,
        ).astype(jnp.bfloat16),
        "fsdp",
        scatter_dimension=0,
        tiled=True,
    )
    attn_gain_part, ffn_gain_part = (
        lax.psum_scatter(attn_gain_term, "fsdp", scatter_dimension=0, tiled=True),
        lax.psum_scatter(ffn_gain_term, "fsdp", scatter_dimension=0, tiled=True),
    )
    summed = (
        lax.psum(attn_part, "replica").astype(jnp.float32),
        lax.psum(attn_gain_part.astype(jnp.bfloat16), "replica").astype(jnp.float32),
        lax.psum(ffn_gain_part.astype(jnp.bfloat16), "replica").astype(jnp.float32),
        lax.psum(gate_part.astype(jnp.bfloat16), "replica").astype(jnp.float32),
        lax.psum(up_part.astype(jnp.bfloat16), "replica").astype(jnp.float32),
        lax.psum(down_part, "replica").astype(jnp.float32),
    )
    attn_total, attn_gain_grad, ffn_gain_grad, gate_grad, up_grad, down_grad = summed
    query_grad = attn_total[:, :model_width]
    key_grad = attn_total[:, model_width : model_width + head_dim]
    value_grad = attn_total[:, model_width + head_dim : model_width + 2 * head_dim]
    output_grad = attn_total[:, model_width + 2 * head_dim :]
    return (
        layer_out,
        input_grad,
        query_grad,
        key_grad,
        value_grad,
        output_grad,
        attn_gain_grad,
        gate_grad,
        up_grad,
        down_grad,
        ffn_gain_grad,
    )


def suits(mesh):
    fsdp_size = mesh.shape["fsdp"]
    return mesh.shape["replica"] == 4 and fsdp_size % 2 == 0 and 2048 % (128 * fsdp_size) == 0


def solution(mesh):
    return jax.shard_map(
        shards if suits(mesh) else any_shards,
        mesh=mesh,
        in_specs=(
            P(("replica", "fsdp"), None),
            P(("replica", "fsdp")),
            P(("replica", "fsdp")),
            P("fsdp", None),
            P("fsdp", None),
            P("fsdp", None),
            P("fsdp", None),
            P("fsdp"),
            P(None, "fsdp"),
            P(None, "fsdp"),
            P("fsdp", None),
            P("fsdp"),
            P(("replica", "fsdp"), None),
        ),
        out_specs=(
            P(("replica", "fsdp"), None),
            P(("replica", "fsdp"), None),
            P("fsdp", None),
            P("fsdp", None),
            P("fsdp", None),
            P("fsdp", None),
            P("fsdp"),
            P(None, "fsdp"),
            P(None, "fsdp"),
            P("fsdp", None),
            P("fsdp"),
        ),
        check_vma=False,
    )
```

```python
import functools

import jax
import jax.numpy as jnp
from jax import lax
from jax.experimental import pallas as pl
from jax.experimental.pallas import tpu as pltpu
from jax.sharding import PartitionSpec as P

GROUP_TOK = 4096
PROMPT = 2048
MAX_CONT = 384
EPSILON = 1e-05
ROPE_BASE = 10000.0
MASKED = -1e30
LOG2E = 1.4426950408889634

TILE = 128
CHUNK = 512
HEAD_GROUP = 4
FFN_ROWS = 256
HEAD_BLOCK = 4


def matmul(left, right):
    return jnp.dot(left, right, preferred_element_type=jnp.float32)


def contract(left, right, left_dim, right_dim):
    return lax.dot_general(
        left, right, (((left_dim,), (right_dim,)), ((), ())), preferred_element_type=jnp.float32
    )


def rope_tables(pos_ids, head_dim):
    half_width = head_dim // 2
    frequency = ROPE_BASE ** (-jnp.arange(half_width, dtype=jnp.float32) * 2.0 / head_dim)
    angles = pos_ids.astype(jnp.float32)[:, None] * frequency[None, :]
    cos_half, sin_half = jnp.cos(angles), jnp.sin(angles)
    return (
        jnp.concatenate([cos_half, cos_half], axis=1),
        jnp.concatenate([-sin_half, sin_half], axis=1),
    )


def swap_halves(values):
    half_width = values.shape[-1] // 2
    return jnp.concatenate([values[..., half_width:], values[..., :half_width]], axis=-1)


def norm_forward(values, gain):
    inverse = lax.rsqrt(jnp.mean(values * values, axis=-1, keepdims=True) + EPSILON)
    return (values * inverse * gain, inverse)


def norm_backward(values, inverse, gain, grad):
    scaled = grad * gain
    inner_mean = jnp.mean(scaled * values, axis=-1, keepdims=True)
    return (
        inverse * scaled - values * inverse**3 * inner_mean,
        jnp.sum(grad * values * inverse, axis=0),
    )


def swiglu_back(d_activation, gate_proj, up_proj):
    sigmoid_gate = jax.nn.sigmoid(gate_proj)
    d_gate = (
        d_activation * up_proj * sigmoid_gate * (1.0 + gate_proj * (1.0 - sigmoid_gate))
    ).astype(jnp.bfloat16)
    d_up = (d_activation * gate_proj * sigmoid_gate).astype(jnp.bfloat16)
    return (d_gate, d_up)


MESH = pl.DeviceIdType.MESH


def flip(index, bit):
    return index + bit - 2 * bit * (index // bit % 2)


class Exchange:
    def __init__(self, buffer, sems):
        self.replica, self.fsdp = lax.axis_index("replica"), lax.axis_index("fsdp")
        self.buffer, self.sems = buffer, sems
        self.beside, self.across = flip(self.replica, 1), flip(self.replica, 2)
        self.half = buffer.shape[1] // 2

    def greet(self):
        barrier = pltpu.get_barrier_semaphore()
        for target in (self.beside, self.across):
            pl.semaphore_signal(
                barrier, inc=1, device_id=(target, self.fsdp), device_id_type=MESH
            )
        pl.semaphore_wait(barrier, 2)

    def copy(self, kind):
        first, second = pl.ds(0, self.half), pl.ds(self.half, self.half)
        source, dest, target = (
            (self.buffer.at[0], self.buffer.at[1], self.beside),
            (self.buffer.at[0], self.buffer.at[2], self.across),
            (self.buffer.at[1, first], self.buffer.at[3, first], self.across),
            (self.buffer.at[2, second], self.buffer.at[3, second], self.beside),
        )[kind]
        return pltpu.make_async_remote_copy(
            src_ref=source,
            dst_ref=dest,
            send_sem=self.sems.at[0, kind],
            recv_sem=self.sems.at[1, kind],
            device_id=(target, self.fsdp),
            device_id_type=MESH,
        )

    def begin(self):
        self.copy(0).start()
        self.copy(1).start()

    def relay(self):
        self.copy(0).wait_recv()
        self.copy(2).start()
        self.copy(1).wait_recv()
        self.copy(3).start()

    def end(self):
        self.copy(2).wait_recv()
        self.copy(3).wait_recv()

    def drain(self):
        for kind in range(4):
            self.copy(kind).wait_send()


def ffn_kernel(
    x_ref,
    grads_ref,
    gate_ref,
    up_ref,
    down_ref,
    x_all,
    act_all,
    d_gate_all,
    d_up_all,
    d_x_all,
    gate_w,
    up_w,
    down_w,
    block,
    d_act,
    act,
    d_gate,
    d_up,
    d_x,
    load_sems,
    store_sems,
    x_sems,
):
    exchange = Exchange(x_all, x_sems)
    exchange.greet()
    own = pltpu.make_async_copy(x_ref, x_all.at[0], load_sems.at[0])
    own.start()
    loads = [
        pltpu.make_async_copy(src, dst, load_sems.at[1 + i])
        for i, (src, dst) in enumerate(
            ((down_ref, down_w), (gate_ref, gate_w), (up_ref, up_w))
        )
    ]
    for load in loads:
        load.start()

    def fetch(source, at, slot):
        return pltpu.make_async_copy(source.at[at], block.at[slot], load_sems.at[4 + slot])

    fetch(grads_ref, 0, 0).start()
    own.wait()
    exchange.begin()
    loads[0].wait()
    rows = d_act.shape[1]
    parts = rows // FFN_ROWS
    for at in range(4):
        fetch(grads_ref, at, at % 2).wait()
        if at < 3:
            fetch(grads_ref, at + 1, (at + 1) % 2).start()

        @pl.loop(0, parts)
        def _(part, at=at):
            some = pl.ds(pl.multiple_of(part * FFN_ROWS, FFN_ROWS), FFN_ROWS)
            d_act[at, some] = contract(block[at % 2, some], down_w[...], 1, 1).astype(jnp.bfloat16)

    loads[1].wait()
    loads[2].wait()

    def stores(at):
        return [
            pltpu.make_async_copy(src, dst.at[at], store_sems.at[i])
            for i, (src, dst) in enumerate(
                ((act, act_all), (d_gate, d_gate_all), (d_up, d_up_all), (d_x, d_x_all))
            )
        ]

    for at in range(4):
        if at == 1:
            exchange.relay()
        if at == 3:
            exchange.end()
        load = fetch(x_all, at, 0)
        load.start()
        load.wait()
        if at > 0:
            for store in stores(at - 1):
                store.wait()

        @pl.loop(0, parts)
        def _(part, at=at):
            some = pl.ds(pl.multiple_of(part * FFN_ROWS, FFN_ROWS), FFN_ROWS)
            x = block[0, some]
            gate = contract(x, gate_w[...], 1, 1)
            up = contract(x, up_w[...], 1, 1)
            slope = jax.nn.sigmoid(gate)
            d = d_act[at, some].astype(jnp.float32)
            swish = gate * slope
            act[some] = (swish * up).astype(jnp.bfloat16)
            by_gate = (d * up * (slope + swish * (1.0 - slope))).astype(jnp.bfloat16)
            by_up = (d * swish).astype(jnp.bfloat16)
            d_gate[some] = by_gate
            d_up[some] = by_up
            d_x[some] = (matmul(by_gate, gate_w[...]) + matmul(by_up, up_w[...])).astype(
                jnp.bfloat16
            )

        for store in stores(at):
            store.start()
    for store in stores(3):
        store.wait()
    exchange.drain()


def feed_forward(x, grads, w_gate, w_up, w_down):
    rows, width = x.shape
    hidden = w_gate.shape[0]
    low, dma = jnp.bfloat16, pltpu.SemaphoreType.DMA
    hbm = pl.BlockSpec(memory_space=pl.ANY)
    wide = jax.ShapeDtypeStruct((4, rows, width), low)
    thin = jax.ShapeDtypeStruct((4, rows, hidden), low)
    return pl.pallas_call(
        ffn_kernel,
        out_shape=(wide, thin, thin, thin, wide),
        in_specs=[hbm] * 5,
        out_specs=(hbm,) * 5,
        scratch_shapes=[pltpu.VMEM((hidden, width), low)] * 3
        + [
            pltpu.VMEM((2, rows, width), low),
            pltpu.VMEM((4, rows, hidden), low),
            pltpu.VMEM((rows, hidden), low),
            pltpu.VMEM((rows, hidden), low),
            pltpu.VMEM((rows, hidden), low),
            pltpu.VMEM((rows, width), low),
            dma((6,)),
            dma((4,)),
            dma((2, 4)),
        ],
        compiler_params=pltpu.CompilerParams(
            collective_id=3, has_side_effects=True, vmem_limit_bytes=50 << 20
        ),
        cost_estimate=pl.CostEstimate(
            flops=40 * rows * width * hidden, transcendentals=0, bytes_accessed=40 << 20
        ),
        name="feed_forward",
    )(x, grads, w_gate, w_up, w_down)


def stack_heads(block):
    heads = block.shape[1] // 128
    return jnp.concatenate([block[:, h * 128 : (h + 1) * 128] for h in range(heads)], axis=0)


def chunk_plan(tok_rows):
    first = lax.axis_index("fsdp") * tok_rows % GROUP_TOK + pl.program_id(0) * TILE
    in_prompt = first < PROMPT
    full = jnp.where(in_prompt, first // CHUNK, PROMPT // CHUNK)
    last = jnp.where(
        in_prompt, first // CHUNK * CHUNK, jnp.maximum(PROMPT, first + TILE - CHUNK)
    )
    return first, full, pl.multiple_of(last, TILE)


def attend_kernel(
    tok_rows,
    q_ref,
    kv_ref,
    low_ref,
    grads_ref,
    mixed_ref,
    log_ref,
    grads_all,
    values,
    top,
    acc,
    sems,
    own_sem,
):
    factor = 128**-0.5 * LOG2E

    exchange = Exchange(grads_all, sems)
    own = pltpu.make_async_copy(grads_ref, grads_all.at[0], own_sem)

    @pl.when((pl.program_id(0) == 0) & (pl.program_id(1) == 0))
    def _():
        own.start()
        exchange.greet()
        own.wait()
        exchange.begin()
        values[:, :128] = kv_ref[:, 128:]
        values[:, 128:] = jnp.ones_like(values[:, 128:])

    @pl.when((pl.program_id(0) == pl.num_programs(0) // 2) & (pl.program_id(1) == 0))
    def _():
        exchange.relay()

    first, full, last = chunk_plan(tok_rows)
    queries = stack_heads(q_ref[...])
    rows = queries.shape[0]
    top[...] = jnp.full_like(top, MASKED)
    acc[...] = jnp.zeros_like(acc)

    def step(start, masked):
        scores = contract(queries, kv_ref[pl.ds(start, CHUNK), :128], 1, 1) * factor
        if masked:
            key_at = start + lax.broadcasted_iota(jnp.int32, (rows, CHUNK), 1)
            row_at = lax.broadcasted_iota(jnp.int32, (rows, 1), 0) % TILE + first
            low = jnp.concatenate([low_ref[:, :1]] * HEAD_GROUP, axis=0)
            scores = jnp.where((key_at <= row_at) & (key_at >= low), scores, MASKED)
        before = top[:, :1]
        after = jnp.maximum(before, jnp.max(scores, axis=1, keepdims=True))
        weights = jnp.exp2(scores - after).astype(jnp.bfloat16)
        acc[...] = acc[...] * jnp.exp2(before - after) + matmul(
            weights, values[pl.ds(start, CHUNK), :]
        )
        top[...] = jnp.broadcast_to(after, top.shape)

    @pl.loop(0, full)
    def _(at):
        step(pl.multiple_of(at * CHUNK, CHUNK), False)

    step(last, True)
    total = acc[:, 128:]
    mixed = acc[:, :128] / total
    for h in range(HEAD_GROUP):
        mixed_ref[:, h * 128 : (h + 1) * 128] = mixed[h * TILE : (h + 1) * TILE].astype(jnp.bfloat16)
    log_ref[0, 0] = (top[...] + jnp.log2(total)).T[:8]

    @pl.when(
        (pl.program_id(0) == pl.num_programs(0) - 1) & (pl.program_id(1) == pl.num_programs(1) - 1)
    )
    def _():
        exchange.end()
        exchange.drain()


def attend(queries, kv, low, grads):
    tok_rows, width = queries.shape
    tiles, groups = tok_rows // TILE, width // (128 * HEAD_GROUP)
    lanes, rows = 128 * HEAD_GROUP, TILE * HEAD_GROUP
    tile_spec = pl.BlockSpec((TILE, lanes), lambda i, g: (i, g))
    hbm = pl.BlockSpec(memory_space=pl.ANY)
    pairs = tok_rows * (width // 128) * 2560
    return pl.pallas_call(
        functools.partial(attend_kernel, tok_rows),
        out_shape=(
            jax.ShapeDtypeStruct((tok_rows, width), jnp.bfloat16),
            jax.ShapeDtypeStruct((tiles, groups, 8, rows), jnp.float32),
            jax.ShapeDtypeStruct((4,) + grads.shape, jnp.bfloat16),
        ),
        grid=(tiles, groups),
        in_specs=[
            tile_spec,
            pl.BlockSpec(kv.shape, lambda i, g: (0, 0)),
            pl.BlockSpec((TILE, 128), lambda i, g: (i, 0)),
            hbm,
        ],
        out_specs=[
            tile_spec,
            pl.BlockSpec((1, 1, 8, rows), lambda i, g: (i, g, 0, 0)),
            hbm,
        ],
        scratch_shapes=[
            pltpu.VMEM(kv.shape, jnp.bfloat16),
            pltpu.VMEM((rows, 128), jnp.float32),
            pltpu.VMEM((rows, 256), jnp.float32),
            pltpu.SemaphoreType.DMA((2, 4)),
            pltpu.SemaphoreType.DMA,
        ],
        compiler_params=pltpu.CompilerParams(
            collective_id=4, has_side_effects=True, vmem_limit_bytes=40 << 20
        ),
        cost_estimate=pl.CostEstimate(
            flops=pairs * 3000, transcendentals=pairs, bytes_accessed=16 << 20
        ),
        name="attend",
    )(queries, kv, low, grads)


def attend_back_kernel(
    tok_rows,
    q_ref,
    kv_ref,
    cos_ref,
    sin_ref,
    low_ref,
    mixed_ref,
    d_mixed_ref,
    log_ref,
    d_q_ref,
    d_kv_ref,
    sums,
    d_q,
):
    scale = 128**-0.5
    factor = scale * LOG2E
    at_start = (pl.program_id(0) == 0) & (pl.program_id(1) == 0)
    at_end = (pl.program_id(0) == pl.num_programs(0) - 1) & (
        pl.program_id(1) == pl.num_programs(1) - 1
    )

    @pl.when(at_start)
    def _():
        sums[...] = jnp.zeros_like(sums)

    first, full, last = chunk_plan(tok_rows)
    queries = stack_heads(q_ref[...])
    d_rows = stack_heads(d_mixed_ref[...])
    mixed = stack_heads(mixed_ref[...])
    rows = queries.shape[0]
    products = d_rows.astype(jnp.float32) * mixed.astype(jnp.float32)
    delta = jnp.sum(products.T, axis=0, keepdims=True)
    log_total = log_ref[0, 0, :1]
    d_q[...] = jnp.zeros_like(d_q)

    def step(start, masked):
        keys = kv_ref[pl.ds(start, CHUNK), :128]
        values = kv_ref[pl.ds(start, CHUNK), 128:]
        scores = contract(keys, queries, 1, 1) * factor
        probs = jnp.exp2(scores - log_total)
        if masked:
            key_at = start + lax.broadcasted_iota(jnp.int32, (CHUNK, rows), 0)
            row_at = lax.broadcasted_iota(jnp.int32, (1, rows), 1) % TILE + first
            low = jnp.concatenate([low_ref[:1]] * HEAD_GROUP, axis=1)
            probs = jnp.where((key_at <= row_at) & (key_at >= low), probs, 0.0)
        d_probs = contract(values, d_rows, 1, 1)
        d_scores = (probs * (d_probs - delta)).astype(jnp.bfloat16)
        sums[pl.ds(start, CHUNK), 128:] += matmul(probs.astype(jnp.bfloat16), d_rows)
        sums[pl.ds(start, CHUNK), :128] += matmul(d_scores, queries)
        d_q[...] += contract(d_scores, keys, 0, 0)

    @pl.loop(0, full)
    def _(at):
        step(pl.multiple_of(at * CHUNK, CHUNK), False)

    step(last, True)
    cos_table, sin_table = cos_ref[...] * scale, sin_ref[...] * scale
    for h in range(HEAD_GROUP):
        turned = d_q[h * TILE : (h + 1) * TILE]
        raw = turned * cos_table - pltpu.roll(turned, 64, 1) * sin_table
        d_q_ref[:, h * 128 : (h + 1) * 128] = raw.astype(jnp.bfloat16)

    @pl.when(at_end)
    def _():
        d_kv_ref[:, :128] = (sums[:, :128] * scale).astype(jnp.bfloat16)
        d_kv_ref[:, 128:] = sums[:, 128:].astype(jnp.bfloat16)


def attend_back(queries, kv, cos_table, sin_table, low, mixed, d_mixed, logs):
    tok_rows, width = queries.shape
    tiles, groups = tok_rows // TILE, width // (128 * HEAD_GROUP)
    lanes, rows = 128 * HEAD_GROUP, TILE * HEAD_GROUP
    tile_spec = pl.BlockSpec((TILE, lanes), lambda i, g: (i, g))
    row_spec = pl.BlockSpec((TILE, 128), lambda i, g: (i, 0))
    whole = pl.BlockSpec(kv.shape, lambda i, g: (0, 0))
    pairs = tok_rows * (width // 128) * 2560
    return pl.pallas_call(
        functools.partial(attend_back_kernel, tok_rows),
        out_shape=(
            jax.ShapeDtypeStruct((tok_rows, width), jnp.bfloat16),
            jax.ShapeDtypeStruct(kv.shape, jnp.bfloat16),
        ),
        grid=(tiles, groups),
        in_specs=[
            tile_spec,
            whole,
            row_spec,
            row_spec,
            pl.BlockSpec((8, TILE), lambda i, g: (0, i)),
            tile_spec,
            tile_spec,
            pl.BlockSpec((1, 1, 8, rows), lambda i, g: (i, g, 0, 0)),
        ],
        out_specs=[tile_spec, whole],
        scratch_shapes=[
            pltpu.VMEM(kv.shape, jnp.float32),
            pltpu.VMEM((rows, 128), jnp.float32),
        ],
        compiler_params=pltpu.CompilerParams(vmem_limit_bytes=48 << 20),
        cost_estimate=pl.CostEstimate(
            flops=pairs * 3000, transcendentals=pairs, bytes_accessed=16 << 20
        ),
        name="attend_back",
    )(queries, kv, cos_table, sin_table, low, mixed, d_mixed, logs)


class Chain:
    def __init__(self, place, count, at, replica, fsdp, sends, recvs):
        self.place, self.count, self.at = place, count, at
        self.replica, self.fsdp, self.sends, self.recvs = replica, fsdp, sends, recvs

    def copy(self, shard, way):
        target = self.fsdp + (2 if way == 0 else -2)
        return pltpu.make_async_remote_copy(
            src_ref=self.place(shard),
            dst_ref=self.place(shard),
            send_sem=self.sends.at[way, shard],
            recv_sem=self.recvs.at[way, shard],
            device_id=(self.replica, target),
            device_id_type=MESH,
        )

    def begin(self):
        @pl.when(self.at < self.count - 1)
        def _():
            self.copy(self.at, 0).start()

        @pl.when(self.at > 0)
        def _():
            self.copy(self.at, 1).start()

    def step(self, hop, arrived=None):
        left, right = self.at - hop, self.at + hop

        @pl.when(left >= 0)
        def _():
            self.copy(left, 0).wait_recv()

        @pl.when((left >= 0) & (self.at < self.count - 1))
        def _():
            self.copy(left, 0).start()

        if arrived is not None:

            @pl.when(left >= 0)
            def _():
                arrived(left)

        @pl.when(right < self.count)
        def _():
            self.copy(right, 1).wait_recv()

        @pl.when((right < self.count) & (self.at > 0))
        def _():
            self.copy(right, 1).start()

        if arrived is not None:

            @pl.when(right < self.count)
            def _():
                arrived(right)

    def finish(self):
        for hop in range(self.count):

            @pl.when((self.at - hop >= 0) & (self.at < self.count - 1))
            def _(hop=hop):
                self.copy(self.at - hop, 0).wait_send()

            @pl.when((self.at + hop < self.count) & (self.at > 0))
            def _(hop=hop):
                self.copy(self.at + hop, 1).wait_send()


class Spread:
    def __init__(self, buffer, count, at, core, replica, fsdp, sems):
        self.buffer, self.count, self.at, self.core = buffer, count, at, core
        self.replica, self.fsdp, self.sems = replica, fsdp, sems
        self.rows = buffer.shape[1] // 4

    def rows_of(self, shard, copy, half=None):
        start, size = copy * self.rows, self.rows
        if half is not None:
            size = size // 2
            start = start + half * size
        return self.buffer.at[2 * shard + self.core, pl.ds(start, size)]

    def copy(self, kind, shard):
        beside, across = flip(self.replica, 1), flip(self.replica, 2)
        if kind == 0:
            ref, target = self.rows_of(shard, self.replica), (beside, self.fsdp)
        elif kind == 1:
            ref, target = self.rows_of(shard, self.replica), (across, self.fsdp)
        elif kind == 2:
            ref, target = self.rows_of(shard, beside, 0), (across, self.fsdp)
        elif kind == 3:
            ref, target = self.rows_of(shard, across, 1), (beside, self.fsdp)
        else:
            ref, target = self.buffer.at[2 * shard + self.core], (self.replica, flip(self.fsdp, 1))
        return pltpu.make_async_remote_copy(
            src_ref=ref,
            dst_ref=ref,
            send_sem=self.sems.at[0, kind, shard],
            recv_sem=self.sems.at[1, kind, shard],
            device_id=target,
            device_id_type=MESH,
        )

    def recv(self, kind, shard):
        beside, across = flip(self.replica, 1), flip(self.replica, 2)
        if kind == 0:
            ref = self.rows_of(shard, beside)
        elif kind == 1:
            ref = self.rows_of(shard, across)
        elif kind < 4:
            ref = self.rows_of(shard, flip(beside, 2), kind - 2)
        else:
            ref = self.buffer.at[2 * shard + 1 - self.core]
        return pltpu.make_async_remote_copy(
            src_ref=ref,
            dst_ref=ref,
            send_sem=self.sems.at[0, kind, shard],
            recv_sem=self.sems.at[1, kind, shard],
            device_id=(self.replica, flip(self.fsdp, 1)),
            device_id_type=MESH,
        )

    def arrived(self, shard):
        self.copy(0, shard).start()
        self.copy(1, shard).start()

    def others(self):
        return [(self.at + hop) % self.count for hop in range(1, self.count)]

    def relay(self):
        for shard in self.others():
            self.recv(0, shard).wait_recv()
            self.copy(2, shard).start()
            self.recv(1, shard).wait_recv()
            self.copy(3, shard).start()

    def cores(self):
        self.copy(4, self.at).start()
        for shard in self.others():
            self.recv(2, shard).wait_recv()
            self.recv(3, shard).wait_recv()
            self.copy(4, shard).start()

    def finish(self):
        for shard in self.others() + [self.at]:
            self.recv(4, shard).wait_recv()
        for shard in self.others():
            for kind in range(5):
                self.copy(kind, shard).wait_send()
        self.copy(4, self.at).wait_send()


def project_kernel(
    fsdp_size,
    tokens_ref,
    wq_ref,
    wo_ref,
    kvg_ref,
    cos_ref,
    sin_ref,
    q_ref,
    normed_ref,
    gain_ref,
    wq_all,
    wo_all,
    kvg_all,
    kv_all,
    wq_vmem,
    kvg_vmem,
    kv_vmem,
    local_sems,
    kvg_sems,
    kvg_core,
    wq_line,
    wq_sems,
    wo_line,
    wo_sems,
    kv_sems,
    kv_core,
):
    replica, fsdp = lax.axis_index("replica"), lax.axis_index("fsdp")
    count, at, core = fsdp_size // 2, fsdp // 2, fsdp % 2
    width = tokens_ref.shape[1]
    partner = (replica, flip(fsdp, 1))

    own = [
        pltpu.make_async_copy(kvg_ref, kvg_all.at[fsdp], local_sems.at[0]),
        pltpu.make_async_copy(wq_ref, wq_all.at[fsdp], local_sems.at[1]),
        pltpu.make_async_copy(wo_ref, wo_all.at[fsdp], local_sems.at[2]),
    ]
    for copy in own:
        copy.start()
    greet(replica, fsdp, at, count)

    def core_copy(buffer, sems, shard, lands=False):
        ref = buffer.at[2 * shard + (1 - core if lands else core)]
        return pltpu.make_async_remote_copy(
            src_ref=ref,
            dst_ref=ref,
            send_sem=sems.at[0, shard],
            recv_sem=sems.at[1, shard],
            device_id=partner,
            device_id_type=MESH,
        )

    def line(place, sems):
        return Chain(place, count, at, replica, fsdp, sems.at[0], sems.at[1])

    kvg = line(lambda shard: kvg_all.at[2 * shard + core], kvg_sems)
    kv = line(lambda shard: kv_all.at[2 * shard + core], kv_sems)
    wq = Spread(wq_all, count, at, core, replica, fsdp, wq_sems)
    wo = Spread(wo_all, count, at, core, replica, fsdp, wo_sems)
    wq_chain = line(lambda shard: wq.rows_of(shard, replica), wq_line)
    wo_chain = line(lambda shard: wo.rows_of(shard, replica), wo_line)
    own[0].wait()
    kvg.begin()
    core_copy(kvg_all, kvg_core, at).start()
    own[1].wait()
    wq_chain.begin()
    own[2].wait()
    wo_chain.begin()

    inputs = tokens_ref[...].astype(jnp.float32)
    inverse = lax.rsqrt(jnp.mean(inputs * inputs, axis=1, keepdims=True) + EPSILON)

    for hop in range(1, count):
        kvg.step(hop, lambda shard: core_copy(kvg_all, kvg_core, shard).start())
        wq_chain.step(hop, wq.arrived)
        wo_chain.step(hop, wo.arrived)
    for shard in range(count):
        core_copy(kvg_all, kvg_core, shard, True).wait_recv()
    load = pltpu.make_async_copy(kvg_all, kvg_vmem, local_sems.at[0])
    load.start()
    load.wait()
    table = kvg_vmem[...].reshape(width, kvg_vmem.shape[2])
    gains = table[:, 256:].astype(jnp.float32).T[:8]
    gain_ref[...] = gains
    normed_ref[...] = (inputs * inverse * gains[:1]).astype(jnp.bfloat16)
    kv_raw = matmul(normed_ref[...], table[:, :256])
    cos_table, sin_table = cos_ref[...], sin_ref[...]
    key_raw = kv_raw[:, :128]
    key_rot = key_raw * cos_table + pltpu.roll(key_raw, 64, 1) * sin_table
    kv_vmem[:, :128] = key_rot.astype(jnp.bfloat16)
    kv_vmem[:, 128:] = kv_raw[:, 128:].astype(jnp.bfloat16)
    store = pltpu.make_async_copy(kv_vmem, kv_all.at[fsdp], local_sems.at[0])
    store.start()
    store.wait()
    kv.begin()
    core_copy(kv_all, kv_core, at).start()
    wq.relay()
    kv.step(1, lambda shard: core_copy(kv_all, kv_core, shard).start())
    wq.cores()
    wo.relay()
    for shard in wq.others() + [at]:
        wq.recv(4, shard).wait_recv()
    load = pltpu.make_async_copy(wq_all, wq_vmem, local_sems.at[1])
    load.start()
    for hop in range(2, count):
        kv.step(hop, lambda shard: core_copy(kv_all, kv_core, shard).start())
    load.wait()
    weight = wq_vmem.reshape(width, width)

    def columns(block):
        start = pl.multiple_of(block * 512, 512)
        raw = matmul(normed_ref[...], weight[:, pl.ds(start, 512)])
        for h in range(4):
            head = raw[:, h * 128 : (h + 1) * 128]
            turned = head * cos_table + pltpu.roll(head, 64, 1) * sin_table
            q_ref[:, pl.ds(start + h * 128, 128)] = turned.astype(jnp.bfloat16)

    pl.loop(0, width // 512)(columns)
    wo.cores()
    for shard in range(count):
        core_copy(kv_all, kv_core, shard, True).wait_recv()
    wo.finish()
    for shard in wq.others():
        for kind in range(5):
            wq.copy(kind, shard).wait_send()
    wq.copy(4, at).wait_send()
    for shard in range(count):
        core_copy(kvg_all, kvg_core, shard).wait_send()
        core_copy(kv_all, kv_core, shard).wait_send()
    for chain in (kvg, kv, wq_chain, wo_chain):
        chain.finish()


def project(tokens, wq, wo, kvg, cos_table, sin_table):
    rows, width = tokens.shape
    shard = wq.shape[0]
    fsdp_size = lax.axis_size("fsdp")
    count = fsdp_size // 2
    low = jnp.bfloat16
    vmem, hbm = pl.BlockSpec(memory_space=pltpu.VMEM), pl.BlockSpec(memory_space=pl.ANY)
    dma = pltpu.SemaphoreType.DMA
    return pl.pallas_call(
        functools.partial(project_kernel, fsdp_size),
        out_shape=(
            jax.ShapeDtypeStruct((rows, width), low),
            jax.ShapeDtypeStruct((rows, width), low),
            jax.ShapeDtypeStruct((8, width), jnp.float32),
            jax.ShapeDtypeStruct((fsdp_size, shard, width), low),
            jax.ShapeDtypeStruct((fsdp_size, shard, width), low),
            jax.ShapeDtypeStruct((fsdp_size, shard, kvg.shape[1]), low),
            jax.ShapeDtypeStruct((fsdp_size, rows, 256), low),
        ),
        in_specs=[vmem, hbm, hbm, hbm, vmem, vmem],
        out_specs=(vmem, vmem, vmem, hbm, hbm, hbm, hbm),
        scratch_shapes=[
            pltpu.VMEM((fsdp_size, shard, width), low),
            pltpu.VMEM((fsdp_size, shard, kvg.shape[1]), low),
            pltpu.VMEM((rows, 256), low),
            dma((3,)),
            dma((2, 2, count)),
            dma((2, count)),
            dma((2, 2, count)),
            dma((2, 5, count)),
            dma((2, 2, count)),
            dma((2, 5, count)),
            dma((2, 2, count)),
            dma((2, count)),
        ],
        compiler_params=pltpu.CompilerParams(
            collective_id=0, has_side_effects=True, vmem_limit_bytes=48 << 20
        ),
        cost_estimate=pl.CostEstimate(
            flops=2 * rows * width * (width + 256), transcendentals=0, bytes_accessed=40 << 20
        ),
        name="project",
    )(tokens, wq, wo, kvg, cos_table, sin_table)


def greet(replica, fsdp, at, count):
    barrier = pltpu.get_barrier_semaphore()
    for target in (
        (replica, flip(fsdp, 1)),
        (flip(replica, 1), fsdp),
        (flip(replica, 2), fsdp),
    ):
        pl.semaphore_signal(barrier, inc=1, device_id=target, device_id_type=MESH)

    @pl.when(at > 0)
    def _():
        pl.semaphore_signal(barrier, inc=1, device_id=(replica, fsdp - 2), device_id_type=MESH)

    @pl.when(at < count - 1)
    def _():
        pl.semaphore_signal(barrier, inc=1, device_id=(replica, fsdp + 2), device_id_type=MESH)

    inside = (at > 0) & (at < count - 1)

    @pl.when(inside)
    def _():
        pl.semaphore_wait(barrier, 5)

    @pl.when(jnp.logical_not(inside))
    def _():
        pl.semaphore_wait(barrier, 4)


def add_into(ref, index, *others):
    total = ref[index].astype(jnp.float32)
    for other in others:
        total = total + other.astype(jnp.float32)
    ref[index] = total.astype(ref.dtype)


class Collect:
    def __init__(self, place, grad, core_in, line_in, core_sems, line_sems, copies=None):
        self.replica, self.fsdp, self.at, self.core, self.count = place
        self.grad, self.core_in, self.line_in = grad, core_in, line_in
        self.core_sems, self.line_sems = core_sems, line_sems
        self.beside, self.across = flip(self.replica, 1), flip(self.replica, 2)
        self.opposite = flip(self.beside, 2)
        if copies is None:
            self.rows = pl.ds(0, grad.shape[1])
        else:
            self.diag_in, self.quarter_in, self.full = copies[:3]
            self.diag_sems, self.quarter_sems, self.full_sems = copies[3:]
            self.size = grad.shape[1] // 4
            self.rows = self.quarter(self.replica)

    def quarter(self, copy, half=None):
        size = self.size if half is None else self.size // 2
        start = copy * self.size + (0 if half is None else half * size)
        return pl.ds(pl.multiple_of(start, size), size)

    def remote(self, src, dst, sems, index, target):
        return pltpu.make_async_remote_copy(
            src_ref=src,
            dst_ref=dst,
            send_sem=sems.at[(0,) + index],
            recv_sem=sems.at[(1,) + index],
            device_id=target,
            device_id_type=MESH,
        )

    def core_copy(self, shard):
        return self.remote(
            self.grad.at[2 * shard + 1 - self.core],
            self.core_in.at[shard],
            self.core_sems,
            (shard,),
            (self.replica, flip(self.fsdp, 1)),
        )

    def core_add(self, shard):
        self.core_copy(shard).wait_recv()
        add_into(self.grad, 2 * shard + self.core, self.core_in[shard])

    def diag_copy(self, shard, half):
        return self.remote(
            self.grad.at[2 * shard + self.core, self.quarter(self.opposite, half)],
            self.diag_in.at[half, shard],
            self.diag_sems,
            (half, shard),
            (self.beside if half == 0 else self.across, self.fsdp),
        )

    def diag_start(self, shard):
        self.diag_copy(shard, 0).start()
        self.diag_copy(shard, 1).start()

    def quarter_copy(self, shard, way):
        return self.remote(
            self.grad.at[2 * shard + self.core, self.quarter(self.across if way else self.beside)],
            self.quarter_in.at[way, shard],
            self.quarter_sems,
            (way, shard),
            (self.across if way else self.beside, self.fsdp),
        )

    def quarter_start(self, shard):
        at = 2 * shard + self.core
        for half, copy in ((0, self.across), (1, self.beside)):
            self.diag_copy(shard, half).wait_recv()
            add_into(self.grad, (at, self.quarter(copy, half)), self.diag_in[half, shard])
            self.quarter_copy(shard, 1 - half).start()

    def quarter_add(self, shard):
        self.quarter_copy(shard, 0).wait_recv()
        self.quarter_copy(shard, 1).wait_recv()
        add_into(
            self.grad,
            (2 * shard + self.core, self.rows),
            self.quarter_in[0, shard],
            self.quarter_in[1, shard],
        )

    def line_copy(self, shard, way):
        return self.remote(
            self.grad.at[2 * shard + self.core, self.rows],
            self.line_in.at[way, shard],
            self.line_sems,
            (way, shard),
            (self.replica, self.fsdp + (2 if way == 0 else -2)),
        )

    def line_receive(self, shard, way):
        self.line_copy(shard, way).wait_recv()
        add_into(self.grad, (2 * shard + self.core, self.rows), self.line_in[way, shard])

    def line_hop(self, hop):
        for way, shard, there, fed in (
            (0, self.at + hop, self.at + hop < self.count, self.at > 0),
            (1, self.at - hop, self.at - hop >= 0, self.at < self.count - 1),
        ):

            @pl.when(there & fed)
            def _(shard=shard, way=way):
                self.line_receive(shard, way)

            @pl.when(there)
            def _(shard=shard, way=way):
                self.line_copy(shard, way).start()

    def line_end(self):
        @pl.when(self.at > 0)
        def _():
            self.line_receive(self.at, 0)

        @pl.when(self.at < self.count - 1)
        def _():
            self.line_receive(self.at, 1)

    def full_copy(self, kind):
        own = self.replica
        rows, target = (
            (self.quarter(own), self.beside),
            (self.quarter(own), self.across),
            (self.quarter(self.beside, 0), self.across),
            (self.quarter(self.across, 1), self.beside),
        )[kind]
        return self.remote(
            self.full.at[rows],
            self.full.at[rows],
            self.full_sems,
            (kind,),
            (target, self.fsdp),
        )

    def full_recv(self, kind):
        rows = (
            self.quarter(self.beside),
            self.quarter(self.across),
            self.quarter(self.opposite, 0),
            self.quarter(self.opposite, 1),
        )[kind]
        ref = self.full.at[rows]
        self.remote(ref, ref, self.full_sems, (kind,), (self.beside, self.fsdp)).wait_recv()

    def gather_start(self):
        self.full[self.rows] = self.grad[2 * self.at + self.core, self.rows]
        self.full_copy(0).start()
        self.full_copy(1).start()

    def gather_relay(self):
        self.full_recv(0)
        self.full_copy(2).start()
        self.full_recv(1)
        self.full_copy(3).start()

    def gather_end(self):
        self.full_recv(2)
        self.full_recv(3)

    def drain(self):
        for shard in range(self.count):
            self.core_copy(shard).wait_send()
            if hasattr(self, "size"):
                for way in (0, 1):
                    self.diag_copy(shard, way).wait_send()
                    self.quarter_copy(shard, way).wait_send()
        for hop in range(1, self.count):

            @pl.when(self.at + hop < self.count)
            def _(hop=hop):
                self.line_copy(self.at + hop, 0).wait_send()

            @pl.when(self.at - hop >= 0)
            def _(hop=hop):
                self.line_copy(self.at - hop, 1).wait_send()

        if hasattr(self, "size"):
            for kind in range(4):
                self.full_copy(kind).wait_send()


def collect_scratch(fsdp_size, rows, width, copies=True):
    count = fsdp_size // 2
    low, dma = jnp.bfloat16, pltpu.SemaphoreType.DMA
    size = rows // 4 if copies else rows
    shapes = [
        pltpu.VMEM((fsdp_size, rows, width), low),
        pltpu.VMEM((count, rows, width), low),
        pltpu.VMEM((2, count, size, width), low),
        dma((2, count)),
        dma((2, 2, count)),
    ]
    if copies:
        shapes += [
            pltpu.VMEM((2, count, size // 2, width), low),
            pltpu.VMEM((2, count, size, width), low),
            pltpu.VMEM((rows, width), low),
            dma((2, 2, count)),
            dma((2, 2, count)),
            dma((2, 4)),
        ]
    return shapes


def make_collect(place, refs, copies=True):
    return Collect(place, *refs[:5], copies=refs[5:11] if copies else None)


def position(fsdp_size):
    replica, fsdp = lax.axis_index("replica"), lax.axis_index("fsdp")
    return replica, fsdp, fsdp // 2, fsdp % 2, fsdp_size // 2


def outer(collect, left_ref, right_ref, own_core):
    rows = collect.grad.shape[1]
    core = collect.core if own_core else 1 - collect.core

    @pl.loop(0, collect.count)
    def _(shard):
        start = pl.multiple_of((2 * shard + core) * rows, rows)
        part = contract(left_ref[:, pl.ds(start, rows)], right_ref[...], 0, 0)
        collect.grad[2 * shard + core] = part.astype(jnp.bfloat16)
        if not own_core:
            collect.core_copy(shard).start()


def each(count, step):
    for shard in range(count):
        step(shard)


def outer_kernel(fsdp_size, left_ref, right_ref, out_ref, *refs):
    place = position(fsdp_size)
    greet(*place[:3], place[4])
    sums = make_collect(place, refs)
    count = place[4]
    outer(sums, left_ref, right_ref, False)
    outer(sums, left_ref, right_ref, True)
    for shard in range(count):
        sums.core_add(shard)
        sums.diag_start(shard)
    each(count, sums.quarter_start)
    each(count, sums.quarter_add)
    for hop in range(count - 1, 0, -1):
        sums.line_hop(hop)
    sums.line_end()
    sums.gather_start()
    sums.gather_relay()
    sums.gather_end()
    out_ref[...] = sums.full[...].astype(jnp.float32)
    sums.drain()


def outer_sum(left, right, collective_id):
    fsdp_size = lax.axis_size("fsdp")
    rows, width = left.shape[1] // fsdp_size, right.shape[1]
    vmem = pl.BlockSpec(memory_space=pltpu.VMEM)
    return pl.pallas_call(
        functools.partial(outer_kernel, fsdp_size),
        out_shape=jax.ShapeDtypeStruct((rows, width), jnp.float32),
        in_specs=[vmem, vmem],
        out_specs=vmem,
        scratch_shapes=collect_scratch(fsdp_size, rows, width),
        compiler_params=pltpu.CompilerParams(
            collective_id=collective_id, has_side_effects=True, vmem_limit_bytes=50 << 20
        ),
        cost_estimate=pl.CostEstimate(
            flops=40 * left.shape[0] * left.shape[1] * width, transcendentals=0, bytes_accessed=8 << 20
        ),
        name="outer_sum",
    )(left, right)


def finish_kernel(
    fsdp_size,
    normed_ref,
    d_q_ref,
    tokens_ref,
    d_hidden_ref,
    gain_ref,
    term_ref,
    cos_ref,
    sin_ref,
    d_kv_ref,
    wq_ref,
    kvg_ref,
    ffn_ref,
    input_grad_ref,
    q_grad_ref,
    kv_grad_ref,
    ffn_all,
    wq_buf,
    kvg_vmem,
    d_kv_raw,
    term_sum,
    hidden_buf,
    local_sems,
    ffn_sems,
    *refs,
):
    place = position(fsdp_size)
    replica, fsdp, at, core, count = place
    greet(replica, fsdp, at, count)
    q_sums = make_collect(place, refs[:11])
    kv_sums = make_collect(place, refs[11:22])
    d_kv = make_collect(place, refs[22:27], False)
    beside, across = flip(replica, 1), flip(replica, 2)
    width = tokens_ref.shape[1]
    half = width // 2

    def ffn_copy(kind, lands=False):
        piece = (replica, replica, beside, across)[kind]
        if lands:
            piece = (beside, across, flip(beside, 2), flip(beside, 2))[kind]
        columns = (slice(None), slice(None), pl.ds(0, half), pl.ds(half, half))[kind]
        src = ffn_all.at[piece, :, :, columns]
        return pltpu.make_async_remote_copy(
            src_ref=src,
            dst_ref=src,
            send_sem=ffn_sems.at[0, kind],
            recv_sem=ffn_sems.at[1, kind],
            device_id=((beside, across, across, beside)[kind], fsdp),
            device_id_type=MESH,
        )

    own_ffn = pltpu.make_async_copy(ffn_ref, ffn_all.at[replica], local_sems.at[0])
    own_ffn.start()
    load = pltpu.make_async_copy(d_kv_ref, d_kv.grad, local_sems.at[1])
    load.start()
    load_kvg = pltpu.make_async_copy(kvg_ref, kvg_vmem, local_sems.at[2])
    load_kvg.start()
    load.wait()
    each(count, lambda shard: d_kv.core_copy(shard).start())
    outer(q_sums, normed_ref, d_q_ref, False)
    each(count, d_kv.core_add)
    d_kv.line_hop(count - 1)
    outer(q_sums, normed_ref, d_q_ref, True)
    for hop in range(count - 2, 0, -1):
        d_kv.line_hop(hop)
    for shard in range(count):
        q_sums.core_add(shard)
        q_sums.diag_start(shard)
    d_kv.line_end()
    each(count, q_sums.quarter_start)
    own_ffn.wait()
    ffn_copy(0).start()
    ffn_copy(1).start()

    summed = d_kv.grad[fsdp].astype(jnp.float32)
    d_key = summed[:, :128]
    d_key = d_key * cos_ref[...] - pltpu.roll(d_key, 64, 1) * sin_ref[...]
    d_kv_raw[:, :128] = d_key.astype(jnp.bfloat16)
    d_kv_raw[:, 128:] = summed[:, 128:].astype(jnp.bfloat16)
    load_kvg.wait()
    rows = kvg_vmem.shape[1]

    def fetch(shard):
        return pltpu.make_async_copy(wq_ref.at[shard], wq_buf.at[shard % 2], local_sems.at[shard % 2])

    fetch(0).start()
    for shard in range(fsdp_size):
        fetch(shard).wait()
        if shard + 1 < fsdp_size:
            fetch(shard + 1).start()
        input_grad_ref[:, shard * rows : (shard + 1) * rows] = contract(
            d_q_ref[...], wq_buf[shard % 2], 1, 1
        ) + contract(d_kv_raw[...], kvg_vmem[shard, :, :256], 1, 1)
    each(count, q_sums.quarter_add)
    for hop in range(count - 1, 0, -1):
        q_sums.line_hop(hop)

    term_sum[...] = jnp.zeros_like(term_sum)

    @pl.loop(0, tokens_ref.shape[0] // 128)
    def _(block):
        part = pl.ds(pl.multiple_of(block * 128, 128), 128)
        fetch_hidden = pltpu.make_async_copy(d_hidden_ref.at[part], hidden_buf, local_sems.at[0])
        fetch_hidden.start()
        d_normed = input_grad_ref[part]
        inputs = tokens_ref[part].astype(jnp.float32)
        inverse = lax.rsqrt(jnp.mean(inputs * inputs, axis=1, keepdims=True) + EPSILON)
        scaled = d_normed * gain_ref[:1]
        inner = jnp.mean(scaled * inputs, axis=1, keepdims=True)
        term_sum[:1] += jnp.sum(d_normed * inputs * inverse, axis=0, keepdims=True)
        step = inverse * scaled - inputs * (inverse**3 * inner)
        fetch_hidden.wait()
        input_grad_ref[part] = hidden_buf[...] + step

    term = term_sum[:1]
    line = lax.broadcasted_iota(jnp.int32, (128, width), 0)
    terms = jnp.where(line == 0, term, jnp.where(line == 1, term_ref[:1], 0.0)).T
    terms = terms.astype(jnp.bfloat16)
    for shard in range(fsdp_size):
        left = normed_ref[:, shard * rows : (shard + 1) * rows]
        kv_sums.grad[shard, :, :256] = contract(left, d_kv_raw[...], 0, 0).astype(jnp.bfloat16)
        kv_sums.grad[shard, :, 256:] = terms[shard * rows : (shard + 1) * rows]
    each(count, lambda shard: kv_sums.core_copy(shard).start())
    q_sums.line_end()
    q_sums.gather_start()
    for shard in range(count):
        kv_sums.core_add(shard)
        kv_sums.diag_start(shard)
    each(count, kv_sums.quarter_start)
    q_sums.gather_relay()
    each(count, kv_sums.quarter_add)
    for hop in range(count - 1, 0, -1):
        kv_sums.line_hop(hop)
    for kind in (0, 1):
        ffn_copy(kind, True).wait_recv()
        ffn_copy(2 + kind).start()
    kv_sums.line_end()
    kv_sums.gather_start()
    q_sums.gather_end()
    q_grad_ref[...] = q_sums.full[...].astype(jnp.float32)
    kv_sums.gather_relay()
    kv_sums.gather_end()
    kv_grad_ref[...] = kv_sums.full[...].astype(jnp.float32)
    for kind in (2, 3):
        ffn_copy(kind, True).wait_recv()
    for kind in range(4):
        ffn_copy(kind).wait_send()
    for sums in (q_sums, kv_sums, d_kv):
        sums.drain()


def finish(
    normed, d_q, tokens, d_hidden, gains, term, cos_table, sin_table, d_kv, wq_all, kvg_all, ffn
):
    fsdp_size, rows, width = wq_all.shape
    tok_rows = tokens.shape[0]
    low, dma = jnp.bfloat16, pltpu.SemaphoreType.DMA
    vmem, hbm = pl.BlockSpec(memory_space=pltpu.VMEM), pl.BlockSpec(memory_space=pl.ANY)
    return pl.pallas_call(
        functools.partial(finish_kernel, fsdp_size),
        out_shape=(
            jax.ShapeDtypeStruct((tok_rows, width), jnp.float32),
            jax.ShapeDtypeStruct((rows, width), jnp.float32),
            jax.ShapeDtypeStruct((rows, 384), jnp.float32),
            jax.ShapeDtypeStruct((4,) + ffn.shape, low),
        ),
        in_specs=[vmem] * 3 + [hbm] + [vmem] * 4 + [hbm] * 4,
        out_specs=(vmem, vmem, vmem, hbm),
        scratch_shapes=[
            pltpu.VMEM((2, rows, width), low),
            pltpu.VMEM((fsdp_size, rows, 384), low),
            pltpu.VMEM((tok_rows, 256), low),
            pltpu.VMEM((8, width), jnp.float32),
            pltpu.VMEM((128, width), jnp.float32),
            dma((3,)),
            dma((2, 4)),
        ]
        + collect_scratch(fsdp_size, rows, width)
        + collect_scratch(fsdp_size, rows, 384)
        + collect_scratch(fsdp_size, tok_rows, 256, False),
        compiler_params=pltpu.CompilerParams(
            collective_id=2, has_side_effects=True, vmem_limit_bytes=54 << 20
        ),
        cost_estimate=pl.CostEstimate(
            flops=100 * tok_rows * width * width, transcendentals=0, bytes_accessed=40 << 20
        ),
        name="finish",
    )(normed, d_q, tokens, d_hidden, gains, term, cos_table, sin_table, d_kv, wq_all, kvg_all, ffn)


def swap(value, step):
    copies = lax.axis_size("replica")
    return lax.ppermute(value, "replica", [(r, r ^ step) for r in range(copies)])


def gather_copies(block):
    half = block.shape[0] // 2
    beside, across = swap(block, 1), swap(block, 2)
    opposite = jnp.concatenate([swap(beside[:half], 2), swap(across[half:], 1)], axis=0)
    return [block, beside, across, opposite]


def scatter_copies(parts):
    own, beside, across, opposite = parts
    half = opposite.shape[0] // 2
    low = jnp.bfloat16
    first = swap(opposite[:half].astype(low), 1)
    second = swap(opposite[half:].astype(low), 2)
    across = jnp.concatenate(
        [across[:half].astype(jnp.float32) + first.astype(jnp.float32), across[half:]], axis=0
    )
    beside = jnp.concatenate(
        [beside[:half], beside[half:].astype(jnp.float32) + second.astype(jnp.float32)], axis=0
    )
    return (
        own.astype(jnp.float32)
        + swap(beside.astype(low), 1).astype(jnp.float32)
        + swap(across.astype(low), 2).astype(jnp.float32)
    )


def gather_shards(value):
    return lax.all_gather(value, "fsdp", axis=0, tiled=True)


def scatter_shards(value):
    return lax.psum_scatter(value, "fsdp", scatter_dimension=0, tiled=True)


def after(value, *others):
    return lax.optimization_barrier((value, others))[0]


def quarter(shard, copy_index):
    rows = shard.shape[0] // lax.axis_size("replica")
    return lax.dynamic_slice_in_dim(shard, copy_index * rows, rows, 0)


def shards(
    tokens,
    segments,
    positions,
    query_weight,
    key_weight,
    value_weight,
    output_weight,
    attn_gain,
    gate_weight,
    up_weight,
    down_weight,
    ffn_gain,
    grad_out,
):
    tok_rows, model_width = tokens.shape
    head_dim = key_weight.shape[1]
    fsdp_size = lax.axis_size("fsdp")
    fsdp_index = lax.axis_index("fsdp")
    copy_index = lax.axis_index("replica")
    copies = lax.axis_size("replica")
    low = jnp.bfloat16

    cos_table, sin_table = rope_tables(positions, head_dim)
    gain_columns = jnp.stack([attn_gain, ffn_gain], axis=1)
    queries, normed, gains, wq_all, w_out, kvg_all, kv_all = project(
        tokens,
        query_weight,
        output_weight,
        jnp.concatenate(
            [key_weight, value_weight, jnp.pad(gain_columns, ((0, 0), (0, 126)))], axis=1
        ),
        cos_table,
        sin_table,
    )
    w_out = w_out.reshape(model_width, model_width)
    kv_all = kv_all.reshape(fsdp_size * tok_rows, 2 * head_dim)
    gain_ffn = gains[1]
    inputs = tokens.astype(jnp.float32)
    key_width = max(GROUP_TOK, tok_rows)
    window_start = fsdp_index * tok_rows // key_width * key_width
    one_group = fsdp_size * tok_rows == key_width
    kv = kv_all if one_group else lax.dynamic_slice_in_dim(kv_all, window_start, key_width, 0)

    row_at = fsdp_index * tok_rows - window_start + jnp.arange(tok_rows, dtype=jnp.int32)
    lowest = jnp.where(positions < PROMPT, 0, row_at - (positions - PROMPT))
    w_gate = gather_shards(after(quarter(gate_weight.T, copy_index), normed))
    w_up = gather_shards(after(quarter(up_weight.T, copy_index), normed))
    w_down = gather_shards(after(quarter(down_weight, copy_index), normed))
    mixed_rows, logs, grads = attend(
        queries, kv, jnp.broadcast_to(lowest[:, None], (tok_rows, 128)), grad_out
    )

    hidden = inputs + matmul(mixed_rows, w_out)
    normed_ffn_full, inverse_ffn = norm_forward(hidden, gain_ffn)
    normed_ffn = normed_ffn_full.astype(low)

    x_all, activation, d_gate, d_up, d_normed_parts = feed_forward(
        normed_ffn, grads, w_gate, w_up, w_down
    )
    d_normed_ffn = scatter_copies(list(d_normed_parts))
    all_rows = copies * tok_rows
    x_all, grads = x_all.reshape(all_rows, -1), grads.reshape(all_rows, -1)
    activation = activation.reshape(all_rows, -1)
    gate_part = contract(d_gate.reshape(all_rows, -1), x_all, 0, 0).astype(low)
    up_part = contract(d_up.reshape(all_rows, -1), x_all, 0, 0).astype(low)
    down_part = contract(activation, grads, 0, 0).astype(low)
    out_parts = matmul(activation, w_down).astype(low)

    cotangent = grad_out.astype(jnp.float32)
    resid_ffn, ffn_gain_term = norm_backward(hidden, inverse_ffn, gain_ffn, d_normed_ffn)
    d_hidden = cotangent + resid_ffn
    d_branch = d_hidden.astype(low)
    d_mixed = contract(d_branch, w_out, 1, 1).astype(low)
    d_mixed = after(d_mixed, gate_part, up_part, down_part)
    gate_sum = scatter_shards(gate_part)
    up_sum = scatter_shards(up_part)
    down_sum = scatter_shards(down_part)
    output_grad = outer_sum(mixed_rows, d_branch, 1)
    own_out, *other_outs = jnp.split(after(out_parts, output_grad), copies)
    layer_out = hidden + own_out.astype(jnp.float32)
    for step, part in enumerate(other_outs):
        layer_out = layer_out + swap(part, step + 1).astype(jnp.float32)
    layer_out = layer_out.astype(low)
    d_query_raw, d_kv = attend_back(
        queries,
        kv,
        cos_table,
        sin_table,
        jnp.broadcast_to(lowest[None, :], (8, tok_rows)),
        mixed_rows,
        d_mixed,
        logs,
    )
    if not one_group:
        d_kv = lax.dynamic_update_slice_in_dim(
            jnp.zeros((fsdp_size * tok_rows, 2 * head_dim), low), d_kv, window_start, 0
        )
    input_grad, query_grad, kv_grad, ffn_all = finish(
        normed,
        d_query_raw,
        tokens,
        d_hidden,
        gains,
        jnp.broadcast_to(ffn_gain_term[None], (8, model_width)),
        cos_table,
        sin_table,
        d_kv.reshape(fsdp_size, tok_rows, 2 * head_dim),
        wq_all,
        kvg_all,
        jnp.stack([gate_sum, up_sum, down_sum]),
    )
    gate_grad, up_grad, down_grad = (
        ffn_all[:, i].reshape(-1, model_width).astype(jnp.float32) for i in range(3)
    )
    return (
        layer_out,
        input_grad,
        query_grad,
        kv_grad[:, :head_dim],
        kv_grad[:, head_dim : 2 * head_dim],
        output_grad,
        kv_grad[:, 2 * head_dim],
        gate_grad.T,
        up_grad.T,
        down_grad,
        kv_grad[:, 2 * head_dim + 1],
    )


def half_tables(pos_ids, head_dim):
    half_width = head_dim // 2
    frequency = ROPE_BASE ** (-jnp.arange(half_width, dtype=jnp.float32) * 2.0 / head_dim)
    angles = pos_ids.astype(jnp.float32)[:, None] * frequency[None, :]
    return (jnp.cos(angles), jnp.sin(angles))


def rotate(values, cos_table, sin_table):
    half_width = values.shape[-1] // 2
    front_half = values[..., :half_width]
    back_half = values[..., half_width:]
    return jnp.concatenate(
        [
            front_half * cos_table - back_half * sin_table,
            back_half * cos_table + front_half * sin_table,
        ],
        axis=-1,
    )


def any_shards(
    tokens,
    segments,
    positions,
    query_weight,
    key_weight,
    value_weight,
    output_weight,
    attn_gain,
    gate_weight,
    up_weight,
    down_weight,
    ffn_gain,
    grad_out,
):
    tok_rows, model_width = tokens.shape
    head_dim = key_weight.shape[1]
    head_count = model_width // head_dim
    block_count = head_count // HEAD_BLOCK
    block_width = HEAD_BLOCK * head_dim
    score_scale = head_dim ** (-0.5)
    fsdp_size = lax.axis_size("fsdp")
    fsdp_index = lax.axis_index("fsdp")
    gathered = (
        lax.all_gather(query_weight, "fsdp", axis=0, tiled=True),
        lax.all_gather(key_weight, "fsdp", axis=0, tiled=True),
        lax.all_gather(value_weight, "fsdp", axis=0, tiled=True),
        lax.all_gather(output_weight, "fsdp", axis=0, tiled=True),
        lax.all_gather(attn_gain, "fsdp", axis=0, tiled=True),
        lax.all_gather(ffn_gain, "fsdp", axis=0, tiled=True),
    )
    w_query, w_key, w_value, w_out, gain_attn, gain_ffn = gathered
    gain_attn = gain_attn.astype(jnp.float32)
    gain_ffn = gain_ffn.astype(jnp.float32)
    inputs = tokens.astype(jnp.float32)
    normed_full, inverse_attn = norm_forward(inputs, gain_attn)
    normed = normed_full.astype(jnp.bfloat16)
    query_raw = matmul(normed, w_query)
    key_raw = matmul(normed, w_key)
    value_rows = matmul(normed, w_value).astype(jnp.bfloat16)
    cos_table, sin_table = half_tables(positions, head_dim)
    queries = rotate(
        query_raw.reshape(tok_rows, head_count, head_dim), cos_table[:, None], sin_table[:, None]
    ).astype(jnp.bfloat16)
    key_rot = rotate(key_raw, cos_table, sin_table).astype(jnp.bfloat16)
    key_rows, value_all = (
        lax.all_gather(key_rot, "fsdp", axis=0, tiled=True),
        lax.all_gather(value_rows, "fsdp", axis=0, tiled=True),
    )
    seg_all, pos_all = (
        lax.all_gather(segments, "fsdp", axis=0, tiled=True),
        lax.all_gather(positions, "fsdp", axis=0, tiled=True),
    )
    key_width = max(GROUP_TOK, tok_rows)
    window_start = fsdp_index * tok_rows // GROUP_TOK * GROUP_TOK
    key_window = lax.dynamic_slice_in_dim(key_rows, window_start, key_width, 0)
    value_window = lax.dynamic_slice_in_dim(value_all, window_start, key_width, 0)
    seg_window = lax.dynamic_slice_in_dim(seg_all, window_start, key_width, 0)
    pos_window = lax.dynamic_slice_in_dim(pos_all, window_start, key_width, 0)
    key_index = window_start + jnp.arange(key_width, dtype=jnp.int32)
    query_index = fsdp_index * tok_rows + jnp.arange(tok_rows, dtype=jnp.int32)
    visible = (
        (key_index[None, :] // GROUP_TOK == query_index[:, None] // GROUP_TOK)
        & (pos_window[None, :] <= positions[:, None])
        & ((seg_window[None, :] == 0) | (seg_window[None, :] == segments[:, None]))
    )
    query_blocks = queries.reshape(tok_rows, block_count, block_width).transpose(1, 0, 2)

    def block_scores(query_block):
        flat_queries = query_block.reshape(tok_rows * HEAD_BLOCK, head_dim)
        scores = (
            contract(flat_queries, key_window, 1, 1).reshape(tok_rows, HEAD_BLOCK, key_width)
            * score_scale
        )
        return (flat_queries, scores)

    def attend_block(query_block):
        flat_queries, scores = block_scores(query_block)
        scores = jnp.where(visible[:, None, :], scores, MASKED)
        row_max = jnp.max(scores, axis=-1, keepdims=True)
        exp_scores = jnp.exp(scores - row_max)
        totals = jnp.sum(exp_scores, axis=-1, keepdims=True)
        weights = (
            (exp_scores / totals).astype(jnp.bfloat16).reshape(tok_rows * HEAD_BLOCK, key_width)
        )
        mixed_block = matmul(weights, value_window).reshape(tok_rows, block_width)
        return (mixed_block, (row_max + jnp.log(totals))[..., 0])

    mixed_blocks, log_totals = lax.map(attend_block, query_blocks)
    mixed_rows = mixed_blocks.transpose(1, 0, 2).reshape(tok_rows, model_width).astype(jnp.bfloat16)
    hidden = inputs + matmul(mixed_rows, w_out)
    normed_ffn_full, inverse_ffn = norm_forward(hidden, gain_ffn)
    normed_ffn = normed_ffn_full.astype(jnp.bfloat16)
    cotangent = grad_out.astype(jnp.float32)
    w_gate, w_up, w_down = (
        lax.all_gather(gate_weight, "fsdp", axis=1, tiled=True),
        lax.all_gather(up_weight, "fsdp", axis=1, tiled=True),
        lax.all_gather(down_weight, "fsdp", axis=0, tiled=True),
    )
    gate_proj = matmul(normed_ffn, w_gate)
    up_proj = matmul(normed_ffn, w_up)
    activation = (jax.nn.silu(gate_proj) * up_proj).astype(jnp.bfloat16)
    layer_out = (hidden + matmul(activation, w_down)).astype(jnp.bfloat16)
    d_activation = contract(grad_out, w_down, 1, 1)
    d_gate, d_up = swiglu_back(d_activation, gate_proj, up_proj)
    d_normed_ffn = contract(d_gate, w_gate, 1, 1) + contract(d_up, w_up, 1, 1)
    gate_up_part = lax.psum_scatter(
        jnp.concatenate(
            [contract(d_gate, normed_ffn, 0, 0), contract(d_up, normed_ffn, 0, 0)], axis=1
        ).astype(jnp.bfloat16),
        "fsdp",
        scatter_dimension=0,
        tiled=True,
    ).astype(jnp.float32)
    gate_part = gate_up_part[:, :model_width].T
    up_part = gate_up_part[:, model_width:].T
    down_part = lax.psum_scatter(
        contract(activation, grad_out, 0, 0).astype(jnp.bfloat16),
        "fsdp",
        scatter_dimension=0,
        tiled=True,
    )
    resid_ffn, ffn_gain_term = norm_backward(hidden, inverse_ffn, gain_ffn, d_normed_ffn)
    d_hidden = cotangent + resid_ffn
    d_branch = d_hidden.astype(jnp.bfloat16)
    d_mixed = contract(d_branch, w_out, 1, 1).astype(jnp.bfloat16)
    d_mixed_blocks = d_mixed.reshape(tok_rows, block_count, block_width).transpose(1, 0, 2)

    def back_block(totals, block_items):
        query_block, d_block, log_block = block_items
        flat_queries, scores = block_scores(query_block)
        probs = jnp.where(visible[:, None, :], jnp.exp(scores - log_block[..., None]), 0.0)
        d_flat = d_block.reshape(tok_rows * HEAD_BLOCK, head_dim)
        d_probs = contract(d_flat, value_window, 1, 1).reshape(tok_rows, HEAD_BLOCK, key_width)
        row_delta = jnp.sum(probs * d_probs, axis=-1, keepdims=True)
        d_scores = (
            (probs * (d_probs - row_delta))
            .astype(jnp.bfloat16)
            .reshape(tok_rows * HEAD_BLOCK, key_width)
        )
        weights = probs.astype(jnp.bfloat16).reshape(tok_rows * HEAD_BLOCK, key_width)
        d_query_block = matmul(d_scores, key_window) * score_scale
        key_total = totals[0] + contract(d_scores, flat_queries, 0, 0) * score_scale
        value_total = totals[1] + contract(weights, d_flat, 0, 0)
        return ((key_total, value_total), d_query_block.reshape(tok_rows, block_width))

    zero_window = jnp.zeros((key_width, head_dim), jnp.float32)
    window_grads, d_query_blocks = lax.scan(
        back_block, (zero_window, zero_window), (query_blocks, d_mixed_blocks, log_totals)
    )
    d_queries = d_query_blocks.transpose(1, 0, 2).reshape(tok_rows, head_count, head_dim)
    d_query_raw = (
        rotate(d_queries, cos_table[:, None], -sin_table[:, None])
        .astype(jnp.bfloat16)
        .reshape(tok_rows, model_width)
    )
    row_zeros = jnp.zeros((fsdp_size * tok_rows, head_dim), jnp.float32)
    key_term = lax.dynamic_update_slice_in_dim(row_zeros, window_grads[0], window_start, 0)
    value_term = lax.dynamic_update_slice_in_dim(row_zeros, window_grads[1], window_start, 0)
    key_sum, value_sum = (
        lax.psum_scatter(
            key_term.astype(jnp.bfloat16), "fsdp", scatter_dimension=0, tiled=True
        ).astype(jnp.float32),
        lax.psum_scatter(
            value_term.astype(jnp.bfloat16), "fsdp", scatter_dimension=0, tiled=True
        ).astype(jnp.float32),
    )
    d_key_raw = rotate(key_sum, cos_table, -sin_table).astype(jnp.bfloat16)
    d_value = value_sum.astype(jnp.bfloat16)
    d_normed = (
        contract(d_query_raw, w_query, 1, 1)
        + contract(d_key_raw, w_key, 1, 1)
        + contract(d_value, w_value, 1, 1)
    )
    resid_attn, attn_gain_term = norm_backward(inputs, inverse_attn, gain_attn, d_normed)
    input_grad = d_hidden + resid_attn
    attn_part = lax.psum_scatter(
        jnp.concatenate(
            [
                contract(normed, d_query_raw, 0, 0),
                contract(normed, d_key_raw, 0, 0),
                contract(normed, d_value, 0, 0),
                contract(mixed_rows, d_branch, 0, 0),
            ],
            axis=1,
        ).astype(jnp.bfloat16),
        "fsdp",
        scatter_dimension=0,
        tiled=True,
    )
    attn_gain_part, ffn_gain_part = (
        lax.psum_scatter(attn_gain_term, "fsdp", scatter_dimension=0, tiled=True),
        lax.psum_scatter(ffn_gain_term, "fsdp", scatter_dimension=0, tiled=True),
    )
    summed = (
        lax.psum(attn_part, "replica").astype(jnp.float32),
        lax.psum(attn_gain_part.astype(jnp.bfloat16), "replica").astype(jnp.float32),
        lax.psum(ffn_gain_part.astype(jnp.bfloat16), "replica").astype(jnp.float32),
        lax.psum(gate_part.astype(jnp.bfloat16), "replica").astype(jnp.float32),
        lax.psum(up_part.astype(jnp.bfloat16), "replica").astype(jnp.float32),
        lax.psum(down_part, "replica").astype(jnp.float32),
    )
    attn_total, attn_gain_grad, ffn_gain_grad, gate_grad, up_grad, down_grad = summed
    query_grad = attn_total[:, :model_width]
    key_grad = attn_total[:, model_width : model_width + head_dim]
    value_grad = attn_total[:, model_width + head_dim : model_width + 2 * head_dim]
    output_grad = attn_total[:, model_width + 2 * head_dim :]
    return (
        layer_out,
        input_grad,
        query_grad,
        key_grad,
        value_grad,
        output_grad,
        attn_gain_grad,
        gate_grad,
        up_grad,
        down_grad,
        ffn_gain_grad,
    )


def suits(mesh):
    fsdp_size = mesh.shape["fsdp"]
    return mesh.shape["replica"] == 4 and fsdp_size % 2 == 0 and 2048 % (128 * fsdp_size) == 0


def solution(mesh):
    return jax.shard_map(
        shards if suits(mesh) else any_shards,
        mesh=mesh,
        in_specs=(
            P(("replica", "fsdp"), None),
            P(("replica", "fsdp")),
            P(("replica", "fsdp")),
            P("fsdp", None),
            P("fsdp", None),
            P("fsdp", None),
            P("fsdp", None),
            P("fsdp"),
            P(None, "fsdp"),
            P(None, "fsdp"),
            P("fsdp", None),
            P("fsdp"),
            P(("replica", "fsdp"), None),
        ),
        out_specs=(
            P(("replica", "fsdp"), None),
            P(("replica", "fsdp"), None),
            P("fsdp", None),
            P("fsdp", None),
            P("fsdp", None),
            P("fsdp", None),
            P("fsdp"),
            P(None, "fsdp"),
            P(None, "fsdp"),
            P("fsdp", None),
            P("fsdp"),
        ),
        check_vma=False,
    )
```

```python
import functools

import jax
import jax.numpy as jnp
from jax import lax
from jax.experimental import pallas as pl
from jax.experimental.pallas import tpu as pltpu
from jax.sharding import PartitionSpec as P

GROUP_TOK = 4096
PROMPT = 2048
MAX_CONT = 384
EPSILON = 1e-05
ROPE_BASE = 10000.0
MASKED = -1e30
LOG2E = 1.4426950408889634

TILE = 128
CHUNK = 512
HEAD_GROUP = 4
FFN_ROWS = 256
HEAD_BLOCK = 4


def matmul(left, right):
    return jnp.dot(left, right, preferred_element_type=jnp.float32)


def contract(left, right, left_dim, right_dim):
    return lax.dot_general(
        left, right, (((left_dim,), (right_dim,)), ((), ())), preferred_element_type=jnp.float32
    )


def rope_tables(pos_ids, head_dim):
    half_width = head_dim // 2
    frequency = ROPE_BASE ** (-jnp.arange(half_width, dtype=jnp.float32) * 2.0 / head_dim)
    angles = pos_ids.astype(jnp.float32)[:, None] * frequency[None, :]
    cos_half, sin_half = jnp.cos(angles), jnp.sin(angles)
    return (
        jnp.concatenate([cos_half, cos_half], axis=1),
        jnp.concatenate([-sin_half, sin_half], axis=1),
    )


def swap_halves(values):
    half_width = values.shape[-1] // 2
    return jnp.concatenate([values[..., half_width:], values[..., :half_width]], axis=-1)


def norm_forward(values, gain):
    inverse = lax.rsqrt(jnp.mean(values * values, axis=-1, keepdims=True) + EPSILON)
    return (values * inverse * gain, inverse)


def norm_backward(values, inverse, gain, grad):
    scaled = grad * gain
    inner_mean = jnp.mean(scaled * values, axis=-1, keepdims=True)
    return (
        inverse * scaled - values * inverse**3 * inner_mean,
        jnp.sum(grad * values * inverse, axis=0),
    )


def swiglu_back(d_activation, gate_proj, up_proj):
    sigmoid_gate = jax.nn.sigmoid(gate_proj)
    d_gate = (
        d_activation * up_proj * sigmoid_gate * (1.0 + gate_proj * (1.0 - sigmoid_gate))
    ).astype(jnp.bfloat16)
    d_up = (d_activation * gate_proj * sigmoid_gate).astype(jnp.bfloat16)
    return (d_gate, d_up)


MESH = pl.DeviceIdType.MESH


def flip(index, bit):
    return index + bit - 2 * bit * (index // bit % 2)


class Exchange:
    def __init__(self, buffer, sems):
        self.replica, self.fsdp = lax.axis_index("replica"), lax.axis_index("fsdp")
        self.buffer, self.sems = buffer, sems
        self.beside, self.across = flip(self.replica, 1), flip(self.replica, 2)
        self.half = buffer.shape[1] // 2

    def greet(self):
        barrier = pltpu.get_barrier_semaphore()
        for target in (self.beside, self.across):
            pl.semaphore_signal(
                barrier, inc=1, device_id=(target, self.fsdp), device_id_type=MESH
            )
        pl.semaphore_wait(barrier, 2)

    def copy(self, kind):
        first, second = pl.ds(0, self.half), pl.ds(self.half, self.half)
        source, dest, target = (
            (self.buffer.at[0], self.buffer.at[1], self.beside),
            (self.buffer.at[0], self.buffer.at[2], self.across),
            (self.buffer.at[1, first], self.buffer.at[3, first], self.across),
            (self.buffer.at[2, second], self.buffer.at[3, second], self.beside),
        )[kind]
        return pltpu.make_async_remote_copy(
            src_ref=source,
            dst_ref=dest,
            send_sem=self.sems.at[0, kind],
            recv_sem=self.sems.at[1, kind],
            device_id=(target, self.fsdp),
            device_id_type=MESH,
        )

    def begin(self):
        self.copy(0).start()
        self.copy(1).start()

    def relay(self):
        self.copy(0).wait_recv()
        self.copy(2).start()
        self.copy(1).wait_recv()
        self.copy(3).start()

    def end(self):
        self.copy(2).wait_recv()
        self.copy(3).wait_recv()

    def drain(self):
        for kind in range(4):
            self.copy(kind).wait_send()


def ffn_kernel(
    x_ref,
    grads_ref,
    gate_ref,
    up_ref,
    down_ref,
    x_all,
    act_all,
    d_gate_all,
    d_up_all,
    d_x_own,
    d_x_beside,
    d_x_across,
    d_x_got,
    gate_w,
    up_w,
    down_w,
    block,
    d_act,
    act,
    d_gate,
    d_up,
    d_x,
    load_sems,
    store_sems,
    x_sems,
    far_sems,
):
    exchange = Exchange(x_all, x_sems)
    exchange.greet()
    own = pltpu.make_async_copy(x_ref, x_all.at[0], load_sems.at[0])
    own.start()
    loads = [
        pltpu.make_async_copy(src, dst, load_sems.at[1 + i])
        for i, (src, dst) in enumerate(
            ((down_ref, down_w), (gate_ref, gate_w), (up_ref, up_w))
        )
    ]
    for load in loads:
        load.start()

    def fetch(source, at, slot):
        return pltpu.make_async_copy(source.at[at], block.at[slot], load_sems.at[4 + slot])

    fetch(grads_ref, 0, 0).start()
    own.wait()
    exchange.begin()
    loads[0].wait()
    rows = d_act.shape[1]
    parts = rows // FFN_ROWS
    for at in range(4):
        fetch(grads_ref, at, at % 2).wait()
        if at < 3:
            fetch(grads_ref, at + 1, (at + 1) % 2).start()

        @pl.loop(0, parts)
        def _(part, at=at):
            some = pl.ds(pl.multiple_of(part * FFN_ROWS, FFN_ROWS), FFN_ROWS)
            d_act[at, some] = contract(block[at % 2, some], down_w[...], 1, 1).astype(jnp.bfloat16)

    loads[1].wait()
    loads[2].wait()

    def stores(at):
        pairs = [(act, act_all.at[at]), (d_gate, d_gate_all.at[at]), (d_up, d_up_all.at[at])]
        if at < 3:
            pairs.append((d_x, (d_x_own, d_x_beside, d_x_across)[at]))
        return [
            pltpu.make_async_copy(src, dst, store_sems.at[i])
            for i, (src, dst) in enumerate(pairs)
        ]

    def far(half):
        size = rows // 2
        return pltpu.make_async_remote_copy(
            src_ref=block.at[1, pl.ds(half * size, size)],
            dst_ref=d_x_got.at[half],
            send_sem=far_sems.at[0, half],
            recv_sem=far_sems.at[1, half],
            device_id=((exchange.beside, exchange.across)[half], exchange.fsdp),
            device_id_type=MESH,
        )

    order = (0, 1, 3, 2)
    for turn, at in enumerate(order):
        if at == 1:
            exchange.relay()
        if at == 3:
            exchange.end()
        load = fetch(x_all, at, 0)
        load.start()
        load.wait()
        if turn > 0:
            for store in stores(order[turn - 1]):
                store.wait()

        @pl.loop(0, parts)
        def _(part, at=at):
            some = pl.ds(pl.multiple_of(part * FFN_ROWS, FFN_ROWS), FFN_ROWS)
            x = block[0, some]
            gate = contract(x, gate_w[...], 1, 1)
            up = contract(x, up_w[...], 1, 1)
            slope = jax.nn.sigmoid(gate)
            d = d_act[at, some].astype(jnp.float32)
            swish = gate * slope
            act[some] = (swish * up).astype(jnp.bfloat16)
            by_gate = (d * up * (slope + swish * (1.0 - slope))).astype(jnp.bfloat16)
            by_up = (d * swish).astype(jnp.bfloat16)
            d_gate[some] = by_gate
            d_up[some] = by_up
            (block.at[1] if at == 3 else d_x)[some] = (
                matmul(by_gate, gate_w[...]) + matmul(by_up, up_w[...])
            ).astype(jnp.bfloat16)

        for store in stores(at):
            store.start()
        if at == 3:
            far(0).start()
            far(1).start()
    for store in stores(order[3]):
        store.wait()
    far(0).wait()
    far(1).wait()
    exchange.drain()


def feed_forward(x, grads, w_gate, w_up, w_down):
    rows, width = x.shape
    hidden = w_gate.shape[0]
    low, dma = jnp.bfloat16, pltpu.SemaphoreType.DMA
    hbm = pl.BlockSpec(memory_space=pl.ANY)
    block = jax.ShapeDtypeStruct((rows, width), low)
    halves = jax.ShapeDtypeStruct((2, rows // 2, width), low)
    wide = jax.ShapeDtypeStruct((4, rows, width), low)
    thin = jax.ShapeDtypeStruct((4, rows, hidden), low)
    return pl.pallas_call(
        ffn_kernel,
        out_shape=(wide, thin, thin, thin, block, block, block, halves),
        in_specs=[hbm] * 5,
        out_specs=(hbm,) * 8,
        scratch_shapes=[pltpu.VMEM((hidden, width), low)] * 3
        + [
            pltpu.VMEM((2, rows, width), low),
            pltpu.VMEM((4, rows, hidden), low),
            pltpu.VMEM((rows, hidden), low),
            pltpu.VMEM((rows, hidden), low),
            pltpu.VMEM((rows, hidden), low),
            pltpu.VMEM((rows, width), low),
            dma((6,)),
            dma((4,)),
            dma((2, 4)),
            dma((2, 2)),
        ],
        compiler_params=pltpu.CompilerParams(
            collective_id=3, has_side_effects=True, vmem_limit_bytes=50 << 20
        ),
        cost_estimate=pl.CostEstimate(
            flops=40 * rows * width * hidden, transcendentals=0, bytes_accessed=40 << 20
        ),
        name="feed_forward",
    )(x, grads, w_gate, w_up, w_down)


def stack_heads(block):
    heads = block.shape[1] // 128
    return jnp.concatenate([block[:, h * 128 : (h + 1) * 128] for h in range(heads)], axis=0)


def chunk_plan(tok_rows):
    first = lax.axis_index("fsdp") * tok_rows % GROUP_TOK + pl.program_id(0) * TILE
    in_prompt = first < PROMPT
    full = jnp.where(in_prompt, first // CHUNK, PROMPT // CHUNK)
    last = jnp.where(
        in_prompt, first // CHUNK * CHUNK, jnp.maximum(PROMPT, first + TILE - CHUNK)
    )
    return first, full, pl.multiple_of(last, TILE)


def attend_kernel(
    tok_rows,
    q_ref,
    kv_ref,
    low_ref,
    grads_ref,
    mixed_ref,
    log_ref,
    grads_all,
    values,
    top,
    acc,
    sems,
    own_sem,
):
    factor = 128**-0.5 * LOG2E

    exchange = Exchange(grads_all, sems)
    own = pltpu.make_async_copy(grads_ref, grads_all.at[0], own_sem)

    @pl.when((pl.program_id(0) == 0) & (pl.program_id(1) == 0))
    def _():
        own.start()
        exchange.greet()
        own.wait()
        exchange.begin()
        values[:, :128] = kv_ref[:, 128:]
        values[:, 128:] = jnp.ones_like(values[:, 128:])

    @pl.when((pl.program_id(0) == pl.num_programs(0) // 2) & (pl.program_id(1) == 0))
    def _():
        exchange.relay()

    first, full, last = chunk_plan(tok_rows)
    queries = stack_heads(q_ref[...])
    rows = queries.shape[0]
    top[...] = jnp.full_like(top, MASKED)
    acc[...] = jnp.zeros_like(acc)

    def step(start, masked):
        scores = contract(queries, kv_ref[pl.ds(start, CHUNK), :128], 1, 1) * factor
        if masked:
            key_at = start + lax.broadcasted_iota(jnp.int32, (rows, CHUNK), 1)
            row_at = lax.broadcasted_iota(jnp.int32, (rows, 1), 0) % TILE + first
            low = jnp.concatenate([low_ref[:, :1]] * HEAD_GROUP, axis=0)
            scores = jnp.where((key_at <= row_at) & (key_at >= low), scores, MASKED)
        before = top[:, :1]
        after = jnp.maximum(before, jnp.max(scores, axis=1, keepdims=True))
        weights = jnp.exp2(scores - after).astype(jnp.bfloat16)
        acc[...] = acc[...] * jnp.exp2(before - after) + matmul(
            weights, values[pl.ds(start, CHUNK), :]
        )
        top[...] = jnp.broadcast_to(after, top.shape)

    @pl.loop(0, full)
    def _(at):
        step(pl.multiple_of(at * CHUNK, CHUNK), False)

    step(last, True)
    total = acc[:, 128:]
    mixed = acc[:, :128] / total
    for h in range(HEAD_GROUP):
        mixed_ref[:, h * 128 : (h + 1) * 128] = mixed[h * TILE : (h + 1) * TILE].astype(jnp.bfloat16)
    log_ref[0, 0] = (top[...] + jnp.log2(total)).T[:8]

    @pl.when(
        (pl.program_id(0) == pl.num_programs(0) - 1) & (pl.program_id(1) == pl.num_programs(1) - 1)
    )
    def _():
        exchange.end()
        exchange.drain()


def attend(queries, kv, low, grads):
    tok_rows, width = queries.shape
    tiles, groups = tok_rows // TILE, width // (128 * HEAD_GROUP)
    lanes, rows = 128 * HEAD_GROUP, TILE * HEAD_GROUP
    tile_spec = pl.BlockSpec((TILE, lanes), lambda i, g: (i, g))
    hbm = pl.BlockSpec(memory_space=pl.ANY)
    pairs = tok_rows * (width // 128) * 2560
    return pl.pallas_call(
        functools.partial(attend_kernel, tok_rows),
        out_shape=(
            jax.ShapeDtypeStruct((tok_rows, width), jnp.bfloat16),
            jax.ShapeDtypeStruct((tiles, groups, 8, rows), jnp.float32),
            jax.ShapeDtypeStruct((4,) + grads.shape, jnp.bfloat16),
        ),
        grid=(tiles, groups),
        in_specs=[
            tile_spec,
            pl.BlockSpec(kv.shape, lambda i, g: (0, 0)),
            pl.BlockSpec((TILE, 128), lambda i, g: (i, 0)),
            hbm,
        ],
        out_specs=[
            tile_spec,
            pl.BlockSpec((1, 1, 8, rows), lambda i, g: (i, g, 0, 0)),
            hbm,
        ],
        scratch_shapes=[
            pltpu.VMEM(kv.shape, jnp.bfloat16),
            pltpu.VMEM((rows, 128), jnp.float32),
            pltpu.VMEM((rows, 256), jnp.float32),
            pltpu.SemaphoreType.DMA((2, 4)),
            pltpu.SemaphoreType.DMA,
        ],
        compiler_params=pltpu.CompilerParams(
            collective_id=4, has_side_effects=True, vmem_limit_bytes=40 << 20
        ),
        cost_estimate=pl.CostEstimate(
            flops=pairs * 3000, transcendentals=pairs, bytes_accessed=16 << 20
        ),
        name="attend",
    )(queries, kv, low, grads)


def attend_back_kernel(
    fsdp_size,
    tok_rows,
    q_ref,
    kv_ref,
    cos_ref,
    sin_ref,
    low_ref,
    mixed_ref,
    d_mixed_ref,
    log_ref,
    rows_ref,
    branch_ref,
    d_q_ref,
    d_kv_ref,
    output_ref,
    sums,
    d_q,
    *refs,
):
    scale = 128**-0.5
    factor = scale * LOG2E
    at_end = (pl.program_id(0) == pl.num_programs(0) - 1) & (
        pl.program_id(1) == pl.num_programs(1) - 1
    )

    place = position(fsdp_size)
    grad = make_collect(place, refs)
    count = place[4]

    def begin():
        sums[...] = jnp.zeros_like(sums)
        greet(*place[:3], count)
        outer(grad, rows_ref, branch_ref, False)
        outer(grad, rows_ref, branch_ref, True)

    def cores():
        for shard in range(count):
            grad.core_add(shard)
            grad.diag_start(shard)

    def sum_quarters():
        each(count, grad.quarter_add)
        grad.line_hop(count - 1)

    def hops():
        for hop in range(count - 2, 0, -1):
            grad.line_hop(hop)

    def gather():
        grad.line_end()
        grad.gather_start()

    stages = {
        0: begin,
        1: cores,
        5: lambda: each(count, grad.quarter_start),
        10: sum_quarters,
        11: hops,
        12: gather,
        14: grad.gather_relay,
    }
    now = pl.program_id(0) * pl.num_programs(1) + pl.program_id(1)
    for step_at, stage in stages.items():
        pl.when(now == step_at)(stage)

    first, full, last = chunk_plan(tok_rows)
    queries = stack_heads(q_ref[...])
    d_rows = stack_heads(d_mixed_ref[...])
    mixed = stack_heads(mixed_ref[...])
    rows = queries.shape[0]
    products = d_rows.astype(jnp.float32) * mixed.astype(jnp.float32)
    delta = jnp.sum(products.T, axis=0, keepdims=True)
    log_total = log_ref[0, 0, :1]
    d_q[...] = jnp.zeros_like(d_q)

    def step(start, masked):
        keys = kv_ref[pl.ds(start, CHUNK), :128]
        values = kv_ref[pl.ds(start, CHUNK), 128:]
        scores = contract(keys, queries, 1, 1) * factor
        probs = jnp.exp2(scores - log_total)
        if masked:
            key_at = start + lax.broadcasted_iota(jnp.int32, (CHUNK, rows), 0)
            row_at = lax.broadcasted_iota(jnp.int32, (1, rows), 1) % TILE + first
            low = jnp.concatenate([low_ref[:1]] * HEAD_GROUP, axis=1)
            probs = jnp.where((key_at <= row_at) & (key_at >= low), probs, 0.0)
        d_probs = contract(values, d_rows, 1, 1)
        d_scores = (probs * (d_probs - delta)).astype(jnp.bfloat16)
        sums[pl.ds(start, CHUNK), 128:] += matmul(probs.astype(jnp.bfloat16), d_rows)
        sums[pl.ds(start, CHUNK), :128] += matmul(d_scores, queries)
        d_q[...] += contract(d_scores, keys, 0, 0)

    @pl.loop(0, full)
    def _(at):
        step(pl.multiple_of(at * CHUNK, CHUNK), False)

    step(last, True)
    cos_table, sin_table = cos_ref[...] * scale, sin_ref[...] * scale
    for h in range(HEAD_GROUP):
        turned = d_q[h * TILE : (h + 1) * TILE]
        raw = turned * cos_table - pltpu.roll(turned, 64, 1) * sin_table
        d_q_ref[:, h * 128 : (h + 1) * 128] = raw.astype(jnp.bfloat16)

    @pl.when(at_end)
    def _():
        d_kv_ref[:, :128] = (sums[:, :128] * scale).astype(jnp.bfloat16)
        d_kv_ref[:, 128:] = sums[:, 128:].astype(jnp.bfloat16)
        grad.gather_end()
        output_ref[...] = grad.full[...].astype(jnp.float32)
        grad.drain()


def attend_back(queries, kv, cos_table, sin_table, low, mixed, d_mixed, logs, d_branch):
    tok_rows, width = queries.shape
    fsdp_size = lax.axis_size("fsdp")
    shard = width // fsdp_size
    tiles, groups = tok_rows // TILE, width // (128 * HEAD_GROUP)
    lanes, rows = 128 * HEAD_GROUP, TILE * HEAD_GROUP
    tile_spec = pl.BlockSpec((TILE, lanes), lambda i, g: (i, g))
    row_spec = pl.BlockSpec((TILE, 128), lambda i, g: (i, 0))
    whole = pl.BlockSpec(kv.shape, lambda i, g: (0, 0))
    pairs = tok_rows * (width // 128) * 2560
    return pl.pallas_call(
        functools.partial(attend_back_kernel, fsdp_size, tok_rows),
        out_shape=(
            jax.ShapeDtypeStruct((tok_rows, width), jnp.bfloat16),
            jax.ShapeDtypeStruct(kv.shape, jnp.bfloat16),
            jax.ShapeDtypeStruct((shard, width), jnp.float32),
        ),
        grid=(tiles, groups),
        in_specs=[
            tile_spec,
            whole,
            row_spec,
            row_spec,
            pl.BlockSpec((8, TILE), lambda i, g: (0, i)),
            tile_spec,
            tile_spec,
            pl.BlockSpec((1, 1, 8, rows), lambda i, g: (i, g, 0, 0)),
            pl.BlockSpec(mixed.shape, lambda i, g: (0, 0)),
            pl.BlockSpec(mixed.shape, lambda i, g: (0, 0)),
        ],
        out_specs=[tile_spec, whole, pl.BlockSpec((shard, width), lambda i, g: (0, 0))],
        scratch_shapes=[
            pltpu.VMEM(kv.shape, jnp.float32),
            pltpu.VMEM((rows, 128), jnp.float32),
        ]
        + collect_scratch(fsdp_size, shard, width),
        compiler_params=pltpu.CompilerParams(
            collective_id=1, has_side_effects=True, vmem_limit_bytes=50 << 20
        ),
        cost_estimate=pl.CostEstimate(
            flops=pairs * 3000, transcendentals=pairs, bytes_accessed=16 << 20
        ),
        name="attend_back",
    )(queries, kv, cos_table, sin_table, low, mixed, d_mixed, logs, mixed, d_branch)


class Chain:
    def __init__(self, place, count, at, replica, fsdp, sends, recvs):
        self.place, self.count, self.at = place, count, at
        self.replica, self.fsdp, self.sends, self.recvs = replica, fsdp, sends, recvs

    def copy(self, shard, way):
        target = self.fsdp + (2 if way == 0 else -2)
        return pltpu.make_async_remote_copy(
            src_ref=self.place(shard),
            dst_ref=self.place(shard),
            send_sem=self.sends.at[way, shard],
            recv_sem=self.recvs.at[way, shard],
            device_id=(self.replica, target),
            device_id_type=MESH,
        )

    def begin(self):
        @pl.when(self.at < self.count - 1)
        def _():
            self.copy(self.at, 0).start()

        @pl.when(self.at > 0)
        def _():
            self.copy(self.at, 1).start()

    def step(self, hop, arrived=None):
        left, right = self.at - hop, self.at + hop

        @pl.when(left >= 0)
        def _():
            self.copy(left, 0).wait_recv()

        @pl.when((left >= 0) & (self.at < self.count - 1))
        def _():
            self.copy(left, 0).start()

        if arrived is not None:

            @pl.when(left >= 0)
            def _():
                arrived(left)

        @pl.when(right < self.count)
        def _():
            self.copy(right, 1).wait_recv()

        @pl.when((right < self.count) & (self.at > 0))
        def _():
            self.copy(right, 1).start()

        if arrived is not None:

            @pl.when(right < self.count)
            def _():
                arrived(right)

    def finish(self):
        for hop in range(self.count):

            @pl.when((self.at - hop >= 0) & (self.at < self.count - 1))
            def _(hop=hop):
                self.copy(self.at - hop, 0).wait_send()

            @pl.when((self.at + hop < self.count) & (self.at > 0))
            def _(hop=hop):
                self.copy(self.at + hop, 1).wait_send()


class Spread:
    def __init__(self, buffer, count, at, core, replica, fsdp, sems):
        self.buffer, self.count, self.at, self.core = buffer, count, at, core
        self.replica, self.fsdp, self.sems = replica, fsdp, sems
        self.rows = buffer.shape[1] // 4

    def rows_of(self, shard, copy, half=None):
        start, size = copy * self.rows, self.rows
        if half is not None:
            size = size // 2
            start = start + half * size
        return self.buffer.at[2 * shard + self.core, pl.ds(start, size)]

    def copy(self, kind, shard):
        beside, across = flip(self.replica, 1), flip(self.replica, 2)
        if kind == 0:
            ref, target = self.rows_of(shard, self.replica), (beside, self.fsdp)
        elif kind == 1:
            ref, target = self.rows_of(shard, self.replica), (across, self.fsdp)
        elif kind == 2:
            ref, target = self.rows_of(shard, beside, 0), (across, self.fsdp)
        elif kind == 3:
            ref, target = self.rows_of(shard, across, 1), (beside, self.fsdp)
        else:
            ref, target = self.buffer.at[2 * shard + self.core], (self.replica, flip(self.fsdp, 1))
        return pltpu.make_async_remote_copy(
            src_ref=ref,
            dst_ref=ref,
            send_sem=self.sems.at[0, kind, shard],
            recv_sem=self.sems.at[1, kind, shard],
            device_id=target,
            device_id_type=MESH,
        )

    def recv(self, kind, shard):
        beside, across = flip(self.replica, 1), flip(self.replica, 2)
        if kind == 0:
            ref = self.rows_of(shard, beside)
        elif kind == 1:
            ref = self.rows_of(shard, across)
        elif kind < 4:
            ref = self.rows_of(shard, flip(beside, 2), kind - 2)
        else:
            ref = self.buffer.at[2 * shard + 1 - self.core]
        return pltpu.make_async_remote_copy(
            src_ref=ref,
            dst_ref=ref,
            send_sem=self.sems.at[0, kind, shard],
            recv_sem=self.sems.at[1, kind, shard],
            device_id=(self.replica, flip(self.fsdp, 1)),
            device_id_type=MESH,
        )

    def arrived(self, shard):
        self.copy(0, shard).start()
        self.copy(1, shard).start()

    def others(self):
        return [(self.at + hop) % self.count for hop in range(1, self.count)]

    def relay(self):
        for shard in self.others():
            self.recv(0, shard).wait_recv()
            self.copy(2, shard).start()
            self.recv(1, shard).wait_recv()
            self.copy(3, shard).start()

    def cores(self):
        self.copy(4, self.at).start()
        for shard in self.others():
            self.recv(2, shard).wait_recv()
            self.recv(3, shard).wait_recv()
            self.copy(4, shard).start()

    def finish(self):
        for shard in self.others() + [self.at]:
            self.recv(4, shard).wait_recv()
        for shard in self.others():
            for kind in range(5):
                self.copy(kind, shard).wait_send()
        self.copy(4, self.at).wait_send()


def project_kernel(
    fsdp_size,
    tokens_ref,
    wq_ref,
    wo_ref,
    kvg_ref,
    cos_ref,
    sin_ref,
    q_ref,
    normed_ref,
    gain_ref,
    wq_all,
    wo_all,
    kvg_all,
    kv_all,
    wq_vmem,
    kvg_vmem,
    kv_vmem,
    local_sems,
    kvg_sems,
    kvg_core,
    wq_line,
    wq_sems,
    wo_line,
    wo_sems,
    kv_sems,
    kv_core,
):
    replica, fsdp = lax.axis_index("replica"), lax.axis_index("fsdp")
    count, at, core = fsdp_size // 2, fsdp // 2, fsdp % 2
    width = tokens_ref.shape[1]
    partner = (replica, flip(fsdp, 1))

    own = [
        pltpu.make_async_copy(kvg_ref, kvg_all.at[fsdp], local_sems.at[0]),
        pltpu.make_async_copy(wq_ref, wq_all.at[fsdp], local_sems.at[1]),
        pltpu.make_async_copy(wo_ref, wo_all.at[fsdp], local_sems.at[2]),
    ]
    for copy in own:
        copy.start()
    greet(replica, fsdp, at, count)

    def core_copy(buffer, sems, shard, lands=False):
        ref = buffer.at[2 * shard + (1 - core if lands else core)]
        return pltpu.make_async_remote_copy(
            src_ref=ref,
            dst_ref=ref,
            send_sem=sems.at[0, shard],
            recv_sem=sems.at[1, shard],
            device_id=partner,
            device_id_type=MESH,
        )

    def line(place, sems):
        return Chain(place, count, at, replica, fsdp, sems.at[0], sems.at[1])

    kvg = line(lambda shard: kvg_all.at[2 * shard + core], kvg_sems)
    kv = line(lambda shard: kv_all.at[2 * shard + core], kv_sems)
    wq = Spread(wq_all, count, at, core, replica, fsdp, wq_sems)
    wo = Spread(wo_all, count, at, core, replica, fsdp, wo_sems)
    wq_chain = line(lambda shard: wq.rows_of(shard, replica), wq_line)
    wo_chain = line(lambda shard: wo.rows_of(shard, replica), wo_line)
    own[0].wait()
    kvg.begin()
    core_copy(kvg_all, kvg_core, at).start()
    own[1].wait()
    wq_chain.begin()
    own[2].wait()
    wo_chain.begin()

    inputs = tokens_ref[...].astype(jnp.float32)
    inverse = lax.rsqrt(jnp.mean(inputs * inputs, axis=1, keepdims=True) + EPSILON)

    for hop in range(1, count):
        kvg.step(hop, lambda shard: core_copy(kvg_all, kvg_core, shard).start())
        wq_chain.step(hop, wq.arrived)
        wo_chain.step(hop, wo.arrived)
    for shard in range(count):
        core_copy(kvg_all, kvg_core, shard, True).wait_recv()
    load = pltpu.make_async_copy(kvg_all, kvg_vmem, local_sems.at[0])
    load.start()
    load.wait()
    table = kvg_vmem[...].reshape(width, kvg_vmem.shape[2])
    gains = table[:, 256:].astype(jnp.float32).T[:8]
    gain_ref[...] = gains
    normed_ref[...] = (inputs * inverse * gains[:1]).astype(jnp.bfloat16)
    kv_raw = matmul(normed_ref[...], table[:, :256])
    cos_table, sin_table = cos_ref[...], sin_ref[...]
    key_raw = kv_raw[:, :128]
    key_rot = key_raw * cos_table + pltpu.roll(key_raw, 64, 1) * sin_table
    kv_vmem[:, :128] = key_rot.astype(jnp.bfloat16)
    kv_vmem[:, 128:] = kv_raw[:, 128:].astype(jnp.bfloat16)
    store = pltpu.make_async_copy(kv_vmem, kv_all.at[fsdp], local_sems.at[0])
    store.start()
    store.wait()
    kv.begin()
    core_copy(kv_all, kv_core, at).start()
    wq.relay()
    kv.step(1, lambda shard: core_copy(kv_all, kv_core, shard).start())
    wq.cores()
    wo.relay()
    for shard in wq.others() + [at]:
        wq.recv(4, shard).wait_recv()
    load = pltpu.make_async_copy(wq_all, wq_vmem, local_sems.at[1])
    load.start()
    for hop in range(2, count):
        kv.step(hop, lambda shard: core_copy(kv_all, kv_core, shard).start())
    load.wait()
    weight = wq_vmem.reshape(width, width)

    def columns(block):
        start = pl.multiple_of(block * 512, 512)
        raw = matmul(normed_ref[...], weight[:, pl.ds(start, 512)])
        for h in range(4):
            head = raw[:, h * 128 : (h + 1) * 128]
            turned = head * cos_table + pltpu.roll(head, 64, 1) * sin_table
            q_ref[:, pl.ds(start + h * 128, 128)] = turned.astype(jnp.bfloat16)

    pl.loop(0, width // 512)(columns)
    wo.cores()
    for shard in range(count):
        core_copy(kv_all, kv_core, shard, True).wait_recv()
    wo.finish()
    for shard in wq.others():
        for kind in range(5):
            wq.copy(kind, shard).wait_send()
    wq.copy(4, at).wait_send()
    for shard in range(count):
        core_copy(kvg_all, kvg_core, shard).wait_send()
        core_copy(kv_all, kv_core, shard).wait_send()
    for chain in (kvg, kv, wq_chain, wo_chain):
        chain.finish()


def project(tokens, wq, wo, kvg, cos_table, sin_table):
    rows, width = tokens.shape
    shard = wq.shape[0]
    fsdp_size = lax.axis_size("fsdp")
    count = fsdp_size // 2
    low = jnp.bfloat16
    vmem, hbm = pl.BlockSpec(memory_space=pltpu.VMEM), pl.BlockSpec(memory_space=pl.ANY)
    dma = pltpu.SemaphoreType.DMA
    return pl.pallas_call(
        functools.partial(project_kernel, fsdp_size),
        out_shape=(
            jax.ShapeDtypeStruct((rows, width), low),
            jax.ShapeDtypeStruct((rows, width), low),
            jax.ShapeDtypeStruct((8, width), jnp.float32),
            jax.ShapeDtypeStruct((fsdp_size, shard, width), low),
            jax.ShapeDtypeStruct((fsdp_size, shard, width), low),
            jax.ShapeDtypeStruct((fsdp_size, shard, kvg.shape[1]), low),
            jax.ShapeDtypeStruct((fsdp_size, rows, 256), low),
        ),
        in_specs=[vmem, hbm, hbm, hbm, vmem, vmem],
        out_specs=(vmem, vmem, vmem, hbm, hbm, hbm, hbm),
        scratch_shapes=[
            pltpu.VMEM((fsdp_size, shard, width), low),
            pltpu.VMEM((fsdp_size, shard, kvg.shape[1]), low),
            pltpu.VMEM((rows, 256), low),
            dma((3,)),
            dma((2, 2, count)),
            dma((2, count)),
            dma((2, 2, count)),
            dma((2, 5, count)),
            dma((2, 2, count)),
            dma((2, 5, count)),
            dma((2, 2, count)),
            dma((2, count)),
        ],
        compiler_params=pltpu.CompilerParams(
            collective_id=0, has_side_effects=True, vmem_limit_bytes=48 << 20
        ),
        cost_estimate=pl.CostEstimate(
            flops=2 * rows * width * (width + 256), transcendentals=0, bytes_accessed=40 << 20
        ),
        name="project",
    )(tokens, wq, wo, kvg, cos_table, sin_table)


def greet(replica, fsdp, at, count):
    barrier = pltpu.get_barrier_semaphore()
    for target in (
        (replica, flip(fsdp, 1)),
        (flip(replica, 1), fsdp),
        (flip(replica, 2), fsdp),
    ):
        pl.semaphore_signal(barrier, inc=1, device_id=target, device_id_type=MESH)

    @pl.when(at > 0)
    def _():
        pl.semaphore_signal(barrier, inc=1, device_id=(replica, fsdp - 2), device_id_type=MESH)

    @pl.when(at < count - 1)
    def _():
        pl.semaphore_signal(barrier, inc=1, device_id=(replica, fsdp + 2), device_id_type=MESH)

    inside = (at > 0) & (at < count - 1)

    @pl.when(inside)
    def _():
        pl.semaphore_wait(barrier, 5)

    @pl.when(jnp.logical_not(inside))
    def _():
        pl.semaphore_wait(barrier, 4)


def add_into(ref, index, *others):
    total = ref[index].astype(jnp.float32)
    for other in others:
        total = total + other.astype(jnp.float32)
    ref[index] = total.astype(ref.dtype)


class Collect:
    def __init__(self, place, grad, core_in, line_in, core_sems, line_sems, copies=None):
        self.replica, self.fsdp, self.at, self.core, self.count = place
        self.grad, self.core_in, self.line_in = grad, core_in, line_in
        self.core_sems, self.line_sems = core_sems, line_sems
        self.beside, self.across = flip(self.replica, 1), flip(self.replica, 2)
        self.opposite = flip(self.beside, 2)
        if copies is None:
            self.rows = pl.ds(0, grad.shape[1])
        else:
            self.diag_in, self.quarter_in, self.full = copies[:3]
            self.diag_sems, self.quarter_sems, self.full_sems = copies[3:]
            self.size = grad.shape[1] // 4
            self.rows = self.quarter(self.replica)

    def quarter(self, copy, half=None):
        size = self.size if half is None else self.size // 2
        start = copy * self.size + (0 if half is None else half * size)
        return pl.ds(pl.multiple_of(start, size), size)

    def remote(self, src, dst, sems, index, target):
        return pltpu.make_async_remote_copy(
            src_ref=src,
            dst_ref=dst,
            send_sem=sems.at[(0,) + index],
            recv_sem=sems.at[(1,) + index],
            device_id=target,
            device_id_type=MESH,
        )

    def core_copy(self, shard):
        return self.remote(
            self.grad.at[2 * shard + 1 - self.core],
            self.core_in.at[shard],
            self.core_sems,
            (shard,),
            (self.replica, flip(self.fsdp, 1)),
        )

    def core_add(self, shard):
        self.core_copy(shard).wait_recv()
        add_into(self.grad, 2 * shard + self.core, self.core_in[shard])

    def diag_copy(self, shard, half):
        return self.remote(
            self.grad.at[2 * shard + self.core, self.quarter(self.opposite, half)],
            self.diag_in.at[half, shard],
            self.diag_sems,
            (half, shard),
            (self.beside if half == 0 else self.across, self.fsdp),
        )

    def diag_start(self, shard):
        self.diag_copy(shard, 0).start()
        self.diag_copy(shard, 1).start()

    def quarter_copy(self, shard, way):
        return self.remote(
            self.grad.at[2 * shard + self.core, self.quarter(self.across if way else self.beside)],
            self.quarter_in.at[way, shard],
            self.quarter_sems,
            (way, shard),
            (self.across if way else self.beside, self.fsdp),
        )

    def quarter_start(self, shard):
        at = 2 * shard + self.core
        for half, copy in ((0, self.across), (1, self.beside)):
            self.diag_copy(shard, half).wait_recv()
            add_into(self.grad, (at, self.quarter(copy, half)), self.diag_in[half, shard])
            self.quarter_copy(shard, 1 - half).start()

    def quarter_add(self, shard):
        self.quarter_copy(shard, 0).wait_recv()
        self.quarter_copy(shard, 1).wait_recv()
        add_into(
            self.grad,
            (2 * shard + self.core, self.rows),
            self.quarter_in[0, shard],
            self.quarter_in[1, shard],
        )

    def line_copy(self, shard, way):
        return self.remote(
            self.grad.at[2 * shard + self.core, self.rows],
            self.line_in.at[way, shard],
            self.line_sems,
            (way, shard),
            (self.replica, self.fsdp + (2 if way == 0 else -2)),
        )

    def line_receive(self, shard, way):
        self.line_copy(shard, way).wait_recv()
        add_into(self.grad, (2 * shard + self.core, self.rows), self.line_in[way, shard])

    def line_hop(self, hop):
        for way, shard, there, fed in (
            (0, self.at + hop, self.at + hop < self.count, self.at > 0),
            (1, self.at - hop, self.at - hop >= 0, self.at < self.count - 1),
        ):

            @pl.when(there & fed)
            def _(shard=shard, way=way):
                self.line_receive(shard, way)

            @pl.when(there)
            def _(shard=shard, way=way):
                self.line_copy(shard, way).start()

    def line_end(self):
        @pl.when(self.at > 0)
        def _():
            self.line_receive(self.at, 0)

        @pl.when(self.at < self.count - 1)
        def _():
            self.line_receive(self.at, 1)

    def full_copy(self, kind):
        own = self.replica
        rows, target = (
            (self.quarter(own), self.beside),
            (self.quarter(own), self.across),
            (self.quarter(self.beside, 0), self.across),
            (self.quarter(self.across, 1), self.beside),
        )[kind]
        return self.remote(
            self.full.at[rows],
            self.full.at[rows],
            self.full_sems,
            (kind,),
            (target, self.fsdp),
        )

    def full_recv(self, kind):
        rows = (
            self.quarter(self.beside),
            self.quarter(self.across),
            self.quarter(self.opposite, 0),
            self.quarter(self.opposite, 1),
        )[kind]
        ref = self.full.at[rows]
        self.remote(ref, ref, self.full_sems, (kind,), (self.beside, self.fsdp)).wait_recv()

    def gather_start(self):
        self.full[self.rows] = self.grad[2 * self.at + self.core, self.rows]
        self.full_copy(0).start()
        self.full_copy(1).start()

    def gather_relay(self):
        self.full_recv(0)
        self.full_copy(2).start()
        self.full_recv(1)
        self.full_copy(3).start()

    def gather_end(self):
        self.full_recv(2)
        self.full_recv(3)

    def drain(self):
        for shard in range(self.count):
            self.core_copy(shard).wait_send()
            if hasattr(self, "size"):
                for way in (0, 1):
                    self.diag_copy(shard, way).wait_send()
                    self.quarter_copy(shard, way).wait_send()
        for hop in range(1, self.count):

            @pl.when(self.at + hop < self.count)
            def _(hop=hop):
                self.line_copy(self.at + hop, 0).wait_send()

            @pl.when(self.at - hop >= 0)
            def _(hop=hop):
                self.line_copy(self.at - hop, 1).wait_send()

        if hasattr(self, "size"):
            for kind in range(4):
                self.full_copy(kind).wait_send()


def collect_scratch(fsdp_size, rows, width, copies=True):
    count = fsdp_size // 2
    low, dma = jnp.bfloat16, pltpu.SemaphoreType.DMA
    size = rows // 4 if copies else rows
    shapes = [
        pltpu.VMEM((fsdp_size, rows, width), low),
        pltpu.VMEM((count, rows, width), low),
        pltpu.VMEM((2, count, size, width), low),
        dma((2, count)),
        dma((2, 2, count)),
    ]
    if copies:
        shapes += [
            pltpu.VMEM((2, count, size // 2, width), low),
            pltpu.VMEM((2, count, size, width), low),
            pltpu.VMEM((rows, width), low),
            dma((2, 2, count)),
            dma((2, 2, count)),
            dma((2, 4)),
        ]
    return shapes


def make_collect(place, refs, copies=True):
    return Collect(place, *refs[:5], copies=refs[5:11] if copies else None)


def position(fsdp_size):
    replica, fsdp = lax.axis_index("replica"), lax.axis_index("fsdp")
    return replica, fsdp, fsdp // 2, fsdp % 2, fsdp_size // 2


def outer(collect, left_ref, right_ref, own_core):
    rows = collect.grad.shape[1]
    core = collect.core if own_core else 1 - collect.core

    @pl.loop(0, collect.count)
    def _(shard):
        start = pl.multiple_of((2 * shard + core) * rows, rows)
        part = contract(left_ref[:, pl.ds(start, rows)], right_ref[...], 0, 0)
        collect.grad[2 * shard + core] = part.astype(jnp.bfloat16)
        if not own_core:
            collect.core_copy(shard).start()


def each(count, step):
    for shard in range(count):
        step(shard)


def finish_kernel(
    fsdp_size,
    normed_ref,
    d_q_ref,
    tokens_ref,
    d_hidden_ref,
    gain_ref,
    term_ref,
    cos_ref,
    sin_ref,
    d_kv_ref,
    wq_ref,
    kvg_ref,
    ffn_ref,
    input_grad_ref,
    q_grad_ref,
    kv_grad_ref,
    ffn_all,
    wq_buf,
    kvg_vmem,
    d_kv_raw,
    term_sum,
    hidden_buf,
    local_sems,
    ffn_sems,
    *refs,
):
    place = position(fsdp_size)
    replica, fsdp, at, core, count = place
    greet(replica, fsdp, at, count)
    q_sums = make_collect(place, refs[:11])
    kv_sums = make_collect(place, refs[11:22])
    d_kv = make_collect(place, refs[22:27], False)
    beside, across = flip(replica, 1), flip(replica, 2)
    width = tokens_ref.shape[1]
    half = width // 2

    def ffn_copy(kind, lands=False):
        piece = (replica, replica, beside, across)[kind]
        if lands:
            piece = (beside, across, flip(beside, 2), flip(beside, 2))[kind]
        columns = (slice(None), slice(None), pl.ds(0, half), pl.ds(half, half))[kind]
        src = ffn_all.at[piece, :, :, columns]
        return pltpu.make_async_remote_copy(
            src_ref=src,
            dst_ref=src,
            send_sem=ffn_sems.at[0, kind],
            recv_sem=ffn_sems.at[1, kind],
            device_id=((beside, across, across, beside)[kind], fsdp),
            device_id_type=MESH,
        )

    own_ffn = pltpu.make_async_copy(ffn_ref, ffn_all.at[replica], local_sems.at[0])
    own_ffn.start()
    load = pltpu.make_async_copy(d_kv_ref, d_kv.grad, local_sems.at[1])
    load.start()
    load_kvg = pltpu.make_async_copy(kvg_ref, kvg_vmem, local_sems.at[2])
    load_kvg.start()
    load.wait()
    each(count, lambda shard: d_kv.core_copy(shard).start())
    own_ffn.wait()
    ffn_copy(0).start()
    ffn_copy(1).start()
    outer(q_sums, normed_ref, d_q_ref, False)
    each(count, d_kv.core_add)
    d_kv.line_hop(count - 1)
    outer(q_sums, normed_ref, d_q_ref, True)
    for hop in range(count - 2, 0, -1):
        d_kv.line_hop(hop)
    for shard in range(count):
        q_sums.core_add(shard)
        q_sums.diag_start(shard)
    d_kv.line_end()
    each(count, q_sums.quarter_start)

    summed = d_kv.grad[fsdp].astype(jnp.float32)
    d_key = summed[:, :128]
    d_key = d_key * cos_ref[...] - pltpu.roll(d_key, 64, 1) * sin_ref[...]
    d_kv_raw[:, :128] = d_key.astype(jnp.bfloat16)
    d_kv_raw[:, 128:] = summed[:, 128:].astype(jnp.bfloat16)
    load_kvg.wait()
    rows = kvg_vmem.shape[1]

    def fetch(shard):
        return pltpu.make_async_copy(wq_ref.at[shard], wq_buf.at[shard % 2], local_sems.at[shard % 2])

    fetch(0).start()
    for shard in range(fsdp_size):
        fetch(shard).wait()
        if shard + 1 < fsdp_size:
            fetch(shard + 1).start()
        input_grad_ref[:, shard * rows : (shard + 1) * rows] = contract(
            d_q_ref[...], wq_buf[shard % 2], 1, 1
        ) + contract(d_kv_raw[...], kvg_vmem[shard, :, :256], 1, 1)
    for kind in (0, 1):
        ffn_copy(kind, True).wait_recv()
        ffn_copy(2 + kind).start()
    each(count, q_sums.quarter_add)
    for hop in range(count - 1, 0, -1):
        q_sums.line_hop(hop)

    term_sum[...] = jnp.zeros_like(term_sum)

    @pl.loop(0, tokens_ref.shape[0] // 128)
    def _(block):
        part = pl.ds(pl.multiple_of(block * 128, 128), 128)
        fetch_hidden = pltpu.make_async_copy(d_hidden_ref.at[part], hidden_buf, local_sems.at[0])
        fetch_hidden.start()
        d_normed = input_grad_ref[part]
        inputs = tokens_ref[part].astype(jnp.float32)
        inverse = lax.rsqrt(jnp.mean(inputs * inputs, axis=1, keepdims=True) + EPSILON)
        scaled = d_normed * gain_ref[:1]
        inner = jnp.mean(scaled * inputs, axis=1, keepdims=True)
        term_sum[:1] += jnp.sum(d_normed * inputs * inverse, axis=0, keepdims=True)
        step = inverse * scaled - inputs * (inverse**3 * inner)
        fetch_hidden.wait()
        input_grad_ref[part] = hidden_buf[...] + step

    term = term_sum[:1]
    line = lax.broadcasted_iota(jnp.int32, (128, width), 0)
    terms = jnp.where(line == 0, term, jnp.where(line == 1, term_ref[:1], 0.0)).T
    terms = terms.astype(jnp.bfloat16)
    for shard in range(fsdp_size):
        left = normed_ref[:, shard * rows : (shard + 1) * rows]
        kv_sums.grad[shard, :, :256] = contract(left, d_kv_raw[...], 0, 0).astype(jnp.bfloat16)
        kv_sums.grad[shard, :, 256:] = terms[shard * rows : (shard + 1) * rows]
    each(count, lambda shard: kv_sums.core_copy(shard).start())
    q_sums.line_end()
    q_sums.gather_start()
    for shard in range(count):
        kv_sums.core_add(shard)
        kv_sums.diag_start(shard)
    each(count, kv_sums.quarter_start)
    q_sums.gather_relay()
    each(count, kv_sums.quarter_add)
    for hop in range(count - 1, 0, -1):
        kv_sums.line_hop(hop)
    kv_sums.line_end()
    kv_sums.gather_start()
    q_sums.gather_end()
    q_grad_ref[...] = q_sums.full[...].astype(jnp.float32)
    kv_sums.gather_relay()
    kv_sums.gather_end()
    kv_grad_ref[...] = kv_sums.full[...].astype(jnp.float32)
    for kind in (2, 3):
        ffn_copy(kind, True).wait_recv()
    for kind in range(4):
        ffn_copy(kind).wait_send()
    for sums in (q_sums, kv_sums, d_kv):
        sums.drain()


def finish(
    normed, d_q, tokens, d_hidden, gains, term, cos_table, sin_table, d_kv, wq_all, kvg_all, ffn
):
    fsdp_size, rows, width = wq_all.shape
    tok_rows = tokens.shape[0]
    low, dma = jnp.bfloat16, pltpu.SemaphoreType.DMA
    vmem, hbm = pl.BlockSpec(memory_space=pltpu.VMEM), pl.BlockSpec(memory_space=pl.ANY)
    return pl.pallas_call(
        functools.partial(finish_kernel, fsdp_size),
        out_shape=(
            jax.ShapeDtypeStruct((tok_rows, width), jnp.float32),
            jax.ShapeDtypeStruct((rows, width), jnp.float32),
            jax.ShapeDtypeStruct((rows, 384), jnp.float32),
            jax.ShapeDtypeStruct((4,) + ffn.shape, low),
        ),
        in_specs=[vmem] * 3 + [hbm] + [vmem] * 4 + [hbm] * 4,
        out_specs=(vmem, vmem, vmem, hbm),
        scratch_shapes=[
            pltpu.VMEM((2, rows, width), low),
            pltpu.VMEM((fsdp_size, rows, 384), low),
            pltpu.VMEM((tok_rows, 256), low),
            pltpu.VMEM((8, width), jnp.float32),
            pltpu.VMEM((128, width), jnp.float32),
            dma((3,)),
            dma((2, 4)),
        ]
        + collect_scratch(fsdp_size, rows, width)
        + collect_scratch(fsdp_size, rows, 384)
        + collect_scratch(fsdp_size, tok_rows, 256, False),
        compiler_params=pltpu.CompilerParams(
            collective_id=2, has_side_effects=True, vmem_limit_bytes=54 << 20
        ),
        cost_estimate=pl.CostEstimate(
            flops=100 * tok_rows * width * width, transcendentals=0, bytes_accessed=40 << 20
        ),
        name="finish",
    )(normed, d_q, tokens, d_hidden, gains, term, cos_table, sin_table, d_kv, wq_all, kvg_all, ffn)


def swap(value, step):
    copies = lax.axis_size("replica")
    return lax.ppermute(value, "replica", [(r, r ^ step) for r in range(copies)])


def pass_on(beside, across, got):
    half = got.shape[1]
    low, wide = jnp.bfloat16, jnp.float32
    got = got.astype(wide)
    across = jnp.concatenate([across[:half].astype(wide) + got[0], across[half:].astype(wide)])
    beside = jnp.concatenate([beside[:half].astype(wide), beside[half:].astype(wide) + got[1]])
    return beside.astype(low), across.astype(low)


def gather_shards(value):
    return lax.all_gather(value, "fsdp", axis=0, tiled=True)


def scatter_shards(value):
    return lax.psum_scatter(value, "fsdp", scatter_dimension=0, tiled=True)


def after(value, *others):
    return lax.optimization_barrier((value, others))[0]


def quarter(shard, copy_index):
    rows = shard.shape[0] // lax.axis_size("replica")
    return lax.dynamic_slice_in_dim(shard, copy_index * rows, rows, 0)


def shards(
    tokens,
    segments,
    positions,
    query_weight,
    key_weight,
    value_weight,
    output_weight,
    attn_gain,
    gate_weight,
    up_weight,
    down_weight,
    ffn_gain,
    grad_out,
):
    tok_rows, model_width = tokens.shape
    head_dim = key_weight.shape[1]
    fsdp_size = lax.axis_size("fsdp")
    fsdp_index = lax.axis_index("fsdp")
    copy_index = lax.axis_index("replica")
    copies = lax.axis_size("replica")
    low = jnp.bfloat16

    w_down = gather_shards(quarter(down_weight, copy_index))
    cos_table, sin_table = rope_tables(positions, head_dim)
    gain_columns = jnp.stack([attn_gain, ffn_gain], axis=1)
    queries, normed, gains, wq_all, w_out, kvg_all, kv_all = project(
        tokens,
        query_weight,
        output_weight,
        jnp.concatenate(
            [key_weight, value_weight, jnp.pad(gain_columns, ((0, 0), (0, 126)))], axis=1
        ),
        cos_table,
        sin_table,
    )
    w_out = w_out.reshape(model_width, model_width)
    kv_all = kv_all.reshape(fsdp_size * tok_rows, 2 * head_dim)
    gain_ffn = gains[1]
    inputs = tokens.astype(jnp.float32)
    key_width = max(GROUP_TOK, tok_rows)
    window_start = fsdp_index * tok_rows // key_width * key_width
    one_group = fsdp_size * tok_rows == key_width
    kv = kv_all if one_group else lax.dynamic_slice_in_dim(kv_all, window_start, key_width, 0)

    row_at = fsdp_index * tok_rows - window_start + jnp.arange(tok_rows, dtype=jnp.int32)
    lowest = jnp.where(positions < PROMPT, 0, row_at - (positions - PROMPT))
    w_gate = gather_shards(after(quarter(gate_weight.T, copy_index), normed))
    w_up = gather_shards(after(quarter(up_weight.T, copy_index), normed))
    mixed_rows, logs, grads = attend(
        queries, kv, jnp.broadcast_to(lowest[:, None], (tok_rows, 128)), after(grad_out, w_down)
    )

    hidden = inputs + matmul(mixed_rows, w_out)
    normed_ffn_full, inverse_ffn = norm_forward(hidden, gain_ffn)
    normed_ffn = normed_ffn_full.astype(low)

    x_all, activation, d_gate, d_up, *d_normed_parts = feed_forward(
        normed_ffn, grads, w_gate, w_up, w_down
    )
    own_part, *other_parts = d_normed_parts
    beside, across = pass_on(*other_parts)
    all_rows = copies * tok_rows
    x_all, grads = x_all.reshape(all_rows, -1), grads.reshape(all_rows, -1)
    activation = activation.reshape(all_rows, -1)
    d_gate = after(d_gate, beside, across)
    gate_part = contract(d_gate.reshape(all_rows, -1), x_all, 0, 0).astype(low)
    d_up, activation = after((d_up, activation), gate_part)
    d_normed_ffn = (
        own_part.astype(jnp.float32)
        + swap(beside, 1).astype(jnp.float32)
        + swap(across, 2).astype(jnp.float32)
    )
    up_part = contract(d_up.reshape(all_rows, -1), x_all, 0, 0).astype(low)
    down_part = contract(activation, grads, 0, 0).astype(low)
    out_parts = matmul(activation, w_down).astype(low)

    cotangent = grad_out.astype(jnp.float32)
    resid_ffn, ffn_gain_term = norm_backward(hidden, inverse_ffn, gain_ffn, d_normed_ffn)
    d_hidden = cotangent + resid_ffn
    d_branch = d_hidden.astype(low)
    d_mixed = contract(d_branch, w_out, 1, 1).astype(low)
    d_mixed = after(d_mixed, gate_part, up_part, down_part)
    gate_sum = scatter_shards(gate_part)
    up_sum = scatter_shards(up_part)
    down_sum = scatter_shards(down_part)
    own_out, *other_outs = jnp.split(after(out_parts, d_mixed), copies)
    other_outs = [swap(part, step + 1) for step, part in enumerate(other_outs)]
    d_query_raw, d_kv, output_grad = attend_back(
        queries,
        kv,
        cos_table,
        sin_table,
        jnp.broadcast_to(lowest[None, :], (8, tok_rows)),
        mixed_rows,
        d_mixed,
        logs,
        d_branch,
    )
    layer_out = hidden + own_out.astype(jnp.float32)
    for part in after(other_outs, d_kv):
        layer_out = layer_out + part.astype(jnp.float32)
    layer_out = layer_out.astype(low)
    if not one_group:
        d_kv = lax.dynamic_update_slice_in_dim(
            jnp.zeros((fsdp_size * tok_rows, 2 * head_dim), low), d_kv, window_start, 0
        )
    input_grad, query_grad, kv_grad, ffn_all = finish(
        normed,
        d_query_raw,
        tokens,
        d_hidden,
        gains,
        jnp.broadcast_to(ffn_gain_term[None], (8, model_width)),
        cos_table,
        sin_table,
        d_kv.reshape(fsdp_size, tok_rows, 2 * head_dim),
        wq_all,
        kvg_all,
        jnp.stack([gate_sum, up_sum, down_sum]),
    )
    gate_grad, up_grad, down_grad = (
        ffn_all[:, i].reshape(-1, model_width).astype(jnp.float32) for i in range(3)
    )
    return (
        layer_out,
        input_grad,
        query_grad,
        kv_grad[:, :head_dim],
        kv_grad[:, head_dim : 2 * head_dim],
        output_grad,
        kv_grad[:, 2 * head_dim],
        gate_grad.T,
        up_grad.T,
        down_grad,
        kv_grad[:, 2 * head_dim + 1],
    )


def half_tables(pos_ids, head_dim):
    half_width = head_dim // 2
    frequency = ROPE_BASE ** (-jnp.arange(half_width, dtype=jnp.float32) * 2.0 / head_dim)
    angles = pos_ids.astype(jnp.float32)[:, None] * frequency[None, :]
    return (jnp.cos(angles), jnp.sin(angles))


def rotate(values, cos_table, sin_table):
    half_width = values.shape[-1] // 2
    front_half = values[..., :half_width]
    back_half = values[..., half_width:]
    return jnp.concatenate(
        [
            front_half * cos_table - back_half * sin_table,
            back_half * cos_table + front_half * sin_table,
        ],
        axis=-1,
    )


def any_shards(
    tokens,
    segments,
    positions,
    query_weight,
    key_weight,
    value_weight,
    output_weight,
    attn_gain,
    gate_weight,
    up_weight,
    down_weight,
    ffn_gain,
    grad_out,
):
    tok_rows, model_width = tokens.shape
    head_dim = key_weight.shape[1]
    head_count = model_width // head_dim
    block_count = head_count // HEAD_BLOCK
    block_width = HEAD_BLOCK * head_dim
    score_scale = head_dim ** (-0.5)
    fsdp_size = lax.axis_size("fsdp")
    fsdp_index = lax.axis_index("fsdp")
    gathered = (
        lax.all_gather(query_weight, "fsdp", axis=0, tiled=True),
        lax.all_gather(key_weight, "fsdp", axis=0, tiled=True),
        lax.all_gather(value_weight, "fsdp", axis=0, tiled=True),
        lax.all_gather(output_weight, "fsdp", axis=0, tiled=True),
        lax.all_gather(attn_gain, "fsdp", axis=0, tiled=True),
        lax.all_gather(ffn_gain, "fsdp", axis=0, tiled=True),
    )
    w_query, w_key, w_value, w_out, gain_attn, gain_ffn = gathered
    gain_attn = gain_attn.astype(jnp.float32)
    gain_ffn = gain_ffn.astype(jnp.float32)
    inputs = tokens.astype(jnp.float32)
    normed_full, inverse_attn = norm_forward(inputs, gain_attn)
    normed = normed_full.astype(jnp.bfloat16)
    query_raw = matmul(normed, w_query)
    key_raw = matmul(normed, w_key)
    value_rows = matmul(normed, w_value).astype(jnp.bfloat16)
    cos_table, sin_table = half_tables(positions, head_dim)
    queries = rotate(
        query_raw.reshape(tok_rows, head_count, head_dim), cos_table[:, None], sin_table[:, None]
    ).astype(jnp.bfloat16)
    key_rot = rotate(key_raw, cos_table, sin_table).astype(jnp.bfloat16)
    key_rows, value_all = (
        lax.all_gather(key_rot, "fsdp", axis=0, tiled=True),
        lax.all_gather(value_rows, "fsdp", axis=0, tiled=True),
    )
    seg_all, pos_all = (
        lax.all_gather(segments, "fsdp", axis=0, tiled=True),
        lax.all_gather(positions, "fsdp", axis=0, tiled=True),
    )
    key_width = max(GROUP_TOK, tok_rows)
    window_start = fsdp_index * tok_rows // GROUP_TOK * GROUP_TOK
    key_window = lax.dynamic_slice_in_dim(key_rows, window_start, key_width, 0)
    value_window = lax.dynamic_slice_in_dim(value_all, window_start, key_width, 0)
    seg_window = lax.dynamic_slice_in_dim(seg_all, window_start, key_width, 0)
    pos_window = lax.dynamic_slice_in_dim(pos_all, window_start, key_width, 0)
    key_index = window_start + jnp.arange(key_width, dtype=jnp.int32)
    query_index = fsdp_index * tok_rows + jnp.arange(tok_rows, dtype=jnp.int32)
    visible = (
        (key_index[None, :] // GROUP_TOK == query_index[:, None] // GROUP_TOK)
        & (pos_window[None, :] <= positions[:, None])
        & ((seg_window[None, :] == 0) | (seg_window[None, :] == segments[:, None]))
    )
    query_blocks = queries.reshape(tok_rows, block_count, block_width).transpose(1, 0, 2)

    def block_scores(query_block):
        flat_queries = query_block.reshape(tok_rows * HEAD_BLOCK, head_dim)
        scores = (
            contract(flat_queries, key_window, 1, 1).reshape(tok_rows, HEAD_BLOCK, key_width)
            * score_scale
        )
        return (flat_queries, scores)

    def attend_block(query_block):
        flat_queries, scores = block_scores(query_block)
        scores = jnp.where(visible[:, None, :], scores, MASKED)
        row_max = jnp.max(scores, axis=-1, keepdims=True)
        exp_scores = jnp.exp(scores - row_max)
        totals = jnp.sum(exp_scores, axis=-1, keepdims=True)
        weights = (
            (exp_scores / totals).astype(jnp.bfloat16).reshape(tok_rows * HEAD_BLOCK, key_width)
        )
        mixed_block = matmul(weights, value_window).reshape(tok_rows, block_width)
        return (mixed_block, (row_max + jnp.log(totals))[..., 0])

    mixed_blocks, log_totals = lax.map(attend_block, query_blocks)
    mixed_rows = mixed_blocks.transpose(1, 0, 2).reshape(tok_rows, model_width).astype(jnp.bfloat16)
    hidden = inputs + matmul(mixed_rows, w_out)
    normed_ffn_full, inverse_ffn = norm_forward(hidden, gain_ffn)
    normed_ffn = normed_ffn_full.astype(jnp.bfloat16)
    cotangent = grad_out.astype(jnp.float32)
    w_gate, w_up, w_down = (
        lax.all_gather(gate_weight, "fsdp", axis=1, tiled=True),
        lax.all_gather(up_weight, "fsdp", axis=1, tiled=True),
        lax.all_gather(down_weight, "fsdp", axis=0, tiled=True),
    )
    gate_proj = matmul(normed_ffn, w_gate)
    up_proj = matmul(normed_ffn, w_up)
    activation = (jax.nn.silu(gate_proj) * up_proj).astype(jnp.bfloat16)
    layer_out = (hidden + matmul(activation, w_down)).astype(jnp.bfloat16)
    d_activation = contract(grad_out, w_down, 1, 1)
    d_gate, d_up = swiglu_back(d_activation, gate_proj, up_proj)
    d_normed_ffn = contract(d_gate, w_gate, 1, 1) + contract(d_up, w_up, 1, 1)
    gate_up_part = lax.psum_scatter(
        jnp.concatenate(
            [contract(d_gate, normed_ffn, 0, 0), contract(d_up, normed_ffn, 0, 0)], axis=1
        ).astype(jnp.bfloat16),
        "fsdp",
        scatter_dimension=0,
        tiled=True,
    ).astype(jnp.float32)
    gate_part = gate_up_part[:, :model_width].T
    up_part = gate_up_part[:, model_width:].T
    down_part = lax.psum_scatter(
        contract(activation, grad_out, 0, 0).astype(jnp.bfloat16),
        "fsdp",
        scatter_dimension=0,
        tiled=True,
    )
    resid_ffn, ffn_gain_term = norm_backward(hidden, inverse_ffn, gain_ffn, d_normed_ffn)
    d_hidden = cotangent + resid_ffn
    d_branch = d_hidden.astype(jnp.bfloat16)
    d_mixed = contract(d_branch, w_out, 1, 1).astype(jnp.bfloat16)
    d_mixed_blocks = d_mixed.reshape(tok_rows, block_count, block_width).transpose(1, 0, 2)

    def back_block(totals, block_items):
        query_block, d_block, log_block = block_items
        flat_queries, scores = block_scores(query_block)
        probs = jnp.where(visible[:, None, :], jnp.exp(scores - log_block[..., None]), 0.0)
        d_flat = d_block.reshape(tok_rows * HEAD_BLOCK, head_dim)
        d_probs = contract(d_flat, value_window, 1, 1).reshape(tok_rows, HEAD_BLOCK, key_width)
        row_delta = jnp.sum(probs * d_probs, axis=-1, keepdims=True)
        d_scores = (
            (probs * (d_probs - row_delta))
            .astype(jnp.bfloat16)
            .reshape(tok_rows * HEAD_BLOCK, key_width)
        )
        weights = probs.astype(jnp.bfloat16).reshape(tok_rows * HEAD_BLOCK, key_width)
        d_query_block = matmul(d_scores, key_window) * score_scale
        key_total = totals[0] + contract(d_scores, flat_queries, 0, 0) * score_scale
        value_total = totals[1] + contract(weights, d_flat, 0, 0)
        return ((key_total, value_total), d_query_block.reshape(tok_rows, block_width))

    zero_window = jnp.zeros((key_width, head_dim), jnp.float32)
    window_grads, d_query_blocks = lax.scan(
        back_block, (zero_window, zero_window), (query_blocks, d_mixed_blocks, log_totals)
    )
    d_queries = d_query_blocks.transpose(1, 0, 2).reshape(tok_rows, head_count, head_dim)
    d_query_raw = (
        rotate(d_queries, cos_table[:, None], -sin_table[:, None])
        .astype(jnp.bfloat16)
        .reshape(tok_rows, model_width)
    )
    row_zeros = jnp.zeros((fsdp_size * tok_rows, head_dim), jnp.float32)
    key_term = lax.dynamic_update_slice_in_dim(row_zeros, window_grads[0], window_start, 0)
    value_term = lax.dynamic_update_slice_in_dim(row_zeros, window_grads[1], window_start, 0)
    key_sum, value_sum = (
        lax.psum_scatter(
            key_term.astype(jnp.bfloat16), "fsdp", scatter_dimension=0, tiled=True
        ).astype(jnp.float32),
        lax.psum_scatter(
            value_term.astype(jnp.bfloat16), "fsdp", scatter_dimension=0, tiled=True
        ).astype(jnp.float32),
    )
    d_key_raw = rotate(key_sum, cos_table, -sin_table).astype(jnp.bfloat16)
    d_value = value_sum.astype(jnp.bfloat16)
    d_normed = (
        contract(d_query_raw, w_query, 1, 1)
        + contract(d_key_raw, w_key, 1, 1)
        + contract(d_value, w_value, 1, 1)
    )
    resid_attn, attn_gain_term = norm_backward(inputs, inverse_attn, gain_attn, d_normed)
    input_grad = d_hidden + resid_attn
    attn_part = lax.psum_scatter(
        jnp.concatenate(
            [
                contract(normed, d_query_raw, 0, 0),
                contract(normed, d_key_raw, 0, 0),
                contract(normed, d_value, 0, 0),
                contract(mixed_rows, d_branch, 0, 0),
            ],
            axis=1,
        ).astype(jnp.bfloat16),
        "fsdp",
        scatter_dimension=0,
        tiled=True,
    )
    attn_gain_part, ffn_gain_part = (
        lax.psum_scatter(attn_gain_term, "fsdp", scatter_dimension=0, tiled=True),
        lax.psum_scatter(ffn_gain_term, "fsdp", scatter_dimension=0, tiled=True),
    )
    summed = (
        lax.psum(attn_part, "replica").astype(jnp.float32),
        lax.psum(attn_gain_part.astype(jnp.bfloat16), "replica").astype(jnp.float32),
        lax.psum(ffn_gain_part.astype(jnp.bfloat16), "replica").astype(jnp.float32),
        lax.psum(gate_part.astype(jnp.bfloat16), "replica").astype(jnp.float32),
        lax.psum(up_part.astype(jnp.bfloat16), "replica").astype(jnp.float32),
        lax.psum(down_part, "replica").astype(jnp.float32),
    )
    attn_total, attn_gain_grad, ffn_gain_grad, gate_grad, up_grad, down_grad = summed
    query_grad = attn_total[:, :model_width]
    key_grad = attn_total[:, model_width : model_width + head_dim]
    value_grad = attn_total[:, model_width + head_dim : model_width + 2 * head_dim]
    output_grad = attn_total[:, model_width + 2 * head_dim :]
    return (
        layer_out,
        input_grad,
        query_grad,
        key_grad,
        value_grad,
        output_grad,
        attn_gain_grad,
        gate_grad,
        up_grad,
        down_grad,
        ffn_gain_grad,
    )


def suits(mesh):
    fsdp_size = mesh.shape["fsdp"]
    return mesh.shape["replica"] == 4 and fsdp_size % 2 == 0 and 2048 % (128 * fsdp_size) == 0


def solution(mesh):
    return jax.shard_map(
        shards if suits(mesh) else any_shards,
        mesh=mesh,
        in_specs=(
            P(("replica", "fsdp"), None),
            P(("replica", "fsdp")),
            P(("replica", "fsdp")),
            P("fsdp", None),
            P("fsdp", None),
            P("fsdp", None),
            P("fsdp", None),
            P("fsdp"),
            P(None, "fsdp"),
            P(None, "fsdp"),
            P("fsdp", None),
            P("fsdp"),
            P(("replica", "fsdp"), None),
        ),
        out_specs=(
            P(("replica", "fsdp"), None),
            P(("replica", "fsdp"), None),
            P("fsdp", None),
            P("fsdp", None),
            P("fsdp", None),
            P("fsdp", None),
            P("fsdp"),
            P(None, "fsdp"),
            P(None, "fsdp"),
            P("fsdp", None),
            P("fsdp"),
        ),
        check_vma=False,
    )
```

```python
import functools

import jax
import jax.numpy as jnp
from jax import lax
from jax.experimental import pallas as pl
from jax.experimental.pallas import tpu as pltpu
from jax.sharding import PartitionSpec as P

GROUP_TOK = 4096
PROMPT = 2048
MAX_CONT = 384
EPSILON = 1e-05
ROPE_BASE = 10000.0
MASKED = -1e30
LOG2E = 1.4426950408889634

TILE = 128
CHUNK = 512
HEAD_GROUP = 4
FFN_ROWS = 256
HEAD_BLOCK = 4


def matmul(left, right):
    return jnp.dot(left, right, preferred_element_type=jnp.float32)


def contract(left, right, left_dim, right_dim):
    return lax.dot_general(
        left, right, (((left_dim,), (right_dim,)), ((), ())), preferred_element_type=jnp.float32
    )


def rope_tables(pos_ids, head_dim):
    half_width = head_dim // 2
    frequency = ROPE_BASE ** (-jnp.arange(half_width, dtype=jnp.float32) * 2.0 / head_dim)
    angles = pos_ids.astype(jnp.float32)[:, None] * frequency[None, :]
    cos_half, sin_half = jnp.cos(angles), jnp.sin(angles)
    return (
        jnp.concatenate([cos_half, cos_half], axis=1),
        jnp.concatenate([-sin_half, sin_half], axis=1),
    )


def swap_halves(values):
    half_width = values.shape[-1] // 2
    return jnp.concatenate([values[..., half_width:], values[..., :half_width]], axis=-1)


def norm_forward(values, gain):
    inverse = lax.rsqrt(jnp.mean(values * values, axis=-1, keepdims=True) + EPSILON)
    return (values * inverse * gain, inverse)


def norm_backward(values, inverse, gain, grad):
    scaled = grad * gain
    inner_mean = jnp.mean(scaled * values, axis=-1, keepdims=True)
    return (
        inverse * scaled - values * inverse**3 * inner_mean,
        jnp.sum(grad * values * inverse, axis=0),
    )


def swiglu_back(d_activation, gate_proj, up_proj):
    sigmoid_gate = jax.nn.sigmoid(gate_proj)
    d_gate = (
        d_activation * up_proj * sigmoid_gate * (1.0 + gate_proj * (1.0 - sigmoid_gate))
    ).astype(jnp.bfloat16)
    d_up = (d_activation * gate_proj * sigmoid_gate).astype(jnp.bfloat16)
    return (d_gate, d_up)


MESH = pl.DeviceIdType.MESH


def flip(index, bit):
    return index + bit - 2 * bit * (index // bit % 2)


class Exchange:
    def __init__(self, source, buffer, sems):
        self.replica, self.fsdp = lax.axis_index("replica"), lax.axis_index("fsdp")
        self.source, self.buffer, self.sems = source, buffer, sems
        self.beside, self.across = flip(self.replica, 1), flip(self.replica, 2)
        self.half = buffer.shape[1] // 2

    def greet(self):
        barrier = pltpu.get_barrier_semaphore()
        for target in (self.beside, self.across):
            pl.semaphore_signal(
                barrier, inc=1, device_id=(target, self.fsdp), device_id_type=MESH
            )
        pl.semaphore_wait(barrier, 2)

    def copy(self, kind):
        first, second = pl.ds(0, self.half), pl.ds(self.half, self.half)
        source, dest, target = (
            (self.source, self.buffer.at[1], self.beside),
            (self.source, self.buffer.at[2], self.across),
            (self.buffer.at[1, first], self.buffer.at[3, first], self.across),
            (self.buffer.at[2, second], self.buffer.at[3, second], self.beside),
        )[kind]
        return pltpu.make_async_remote_copy(
            src_ref=source,
            dst_ref=dest,
            send_sem=self.sems.at[0, kind],
            recv_sem=self.sems.at[1, kind],
            device_id=(target, self.fsdp),
            device_id_type=MESH,
        )

    def begin(self):
        self.copy(0).start()
        self.copy(1).start()

    def relay(self):
        self.copy(0).wait_recv()
        self.copy(2).start()
        self.copy(1).wait_recv()
        self.copy(3).start()

    def end(self):
        self.copy(2).wait_recv()
        self.copy(3).wait_recv()

    def drain(self):
        for kind in range(4):
            self.copy(kind).wait_send()


def ffn_kernel(
    x_ref,
    grads_ref,
    gate_ref,
    up_ref,
    down_ref,
    x_all,
    act_all,
    d_gate_all,
    d_up_all,
    d_x_own,
    d_x_beside,
    d_x_across,
    d_x_got,
    gate_w,
    up_w,
    down_w,
    block,
    d_act,
    act,
    d_gate,
    d_up,
    d_x,
    load_sems,
    store_sems,
    x_sems,
    far_sems,
):
    exchange = Exchange(x_ref, x_all, x_sems)
    exchange.greet()
    exchange.begin()
    loads = [
        pltpu.make_async_copy(src, dst, load_sems.at[1 + i])
        for i, (src, dst) in enumerate(
            ((down_ref, down_w), (gate_ref, gate_w), (up_ref, up_w))
        )
    ]
    for load in loads:
        load.start()

    def fetch(source, at, slot):
        return pltpu.make_async_copy(source.at[at], block.at[slot], load_sems.at[4 + slot])

    fetch(grads_ref, 0, 0).start()
    loads[0].wait()
    rows = d_act.shape[1]
    parts = rows // FFN_ROWS
    for at in range(4):
        fetch(grads_ref, at, at % 2).wait()
        if at < 3:
            fetch(grads_ref, at + 1, (at + 1) % 2).start()

        @pl.loop(0, parts)
        def _(part, at=at):
            some = pl.ds(pl.multiple_of(part * FFN_ROWS, FFN_ROWS), FFN_ROWS)
            d_act[at, some] = contract(block[at % 2, some], down_w[...], 1, 1).astype(jnp.bfloat16)

    loads[1].wait()
    loads[2].wait()

    def stores(at):
        pairs = [(act, act_all.at[at]), (d_gate, d_gate_all.at[at]), (d_up, d_up_all.at[at])]
        if at < 3:
            pairs.append((d_x, (d_x_own, d_x_beside, d_x_across)[at]))
        return [
            pltpu.make_async_copy(src, dst, store_sems.at[i])
            for i, (src, dst) in enumerate(pairs)
        ]

    def far(half):
        size = rows // 2
        return pltpu.make_async_remote_copy(
            src_ref=block.at[1, pl.ds(half * size, size)],
            dst_ref=d_x_got.at[half],
            send_sem=far_sems.at[0, half],
            recv_sem=far_sems.at[1, half],
            device_id=((exchange.beside, exchange.across)[half], exchange.fsdp),
            device_id_type=MESH,
        )

    order = (0, 1, 3, 2)
    for turn, at in enumerate(order):
        if at == 1:
            exchange.relay()
        if at == 3:
            exchange.end()
        load = (
            fetch(x_all, at, 0)
            if at
            else pltpu.make_async_copy(x_ref, block.at[0], load_sems.at[0])
        )
        load.start()
        load.wait()
        if at == 0:
            keep = pltpu.make_async_copy(block.at[0], x_all.at[0], load_sems.at[0])
            keep.start()
        if turn > 0:
            for store in stores(order[turn - 1]):
                store.wait()

        @pl.loop(0, parts)
        def _(part, at=at):
            some = pl.ds(pl.multiple_of(part * FFN_ROWS, FFN_ROWS), FFN_ROWS)
            x = block[0, some]
            gate = contract(x, gate_w[...], 1, 1)
            up = contract(x, up_w[...], 1, 1)
            slope = jax.nn.sigmoid(gate)
            d = d_act[at, some].astype(jnp.float32)
            swish = gate * slope
            act[some] = (swish * up).astype(jnp.bfloat16)
            by_gate = (d * up * (slope + swish * (1.0 - slope))).astype(jnp.bfloat16)
            by_up = (d * swish).astype(jnp.bfloat16)
            d_gate[some] = by_gate
            d_up[some] = by_up
            (block.at[1] if at == 3 else d_x)[some] = (
                matmul(by_gate, gate_w[...]) + matmul(by_up, up_w[...])
            ).astype(jnp.bfloat16)

        for store in stores(at):
            store.start()
        if at == 0:
            keep.wait()
        if at == 3:
            far(0).start()
            far(1).start()
    for store in stores(order[3]):
        store.wait()
    far(0).wait()
    far(1).wait()
    exchange.drain()


def feed_forward(x, grads, w_gate, w_up, w_down):
    rows, width = x.shape
    hidden = w_gate.shape[0]
    low, dma = jnp.bfloat16, pltpu.SemaphoreType.DMA
    hbm = pl.BlockSpec(memory_space=pl.ANY)
    block = jax.ShapeDtypeStruct((rows, width), low)
    halves = jax.ShapeDtypeStruct((2, rows // 2, width), low)
    wide = jax.ShapeDtypeStruct((4, rows, width), low)
    thin = jax.ShapeDtypeStruct((4, rows, hidden), low)
    return pl.pallas_call(
        ffn_kernel,
        out_shape=(wide, thin, thin, thin, block, block, block, halves),
        in_specs=[hbm] * 5,
        out_specs=(hbm,) * 8,
        scratch_shapes=[pltpu.VMEM((hidden, width), low)] * 3
        + [
            pltpu.VMEM((2, rows, width), low),
            pltpu.VMEM((4, rows, hidden), low),
            pltpu.VMEM((rows, hidden), low),
            pltpu.VMEM((rows, hidden), low),
            pltpu.VMEM((rows, hidden), low),
            pltpu.VMEM((rows, width), low),
            dma((6,)),
            dma((4,)),
            dma((2, 4)),
            dma((2, 2)),
        ],
        compiler_params=pltpu.CompilerParams(
            collective_id=3, has_side_effects=True, vmem_limit_bytes=50 << 20
        ),
        cost_estimate=pl.CostEstimate(
            flops=40 * rows * width * hidden, transcendentals=0, bytes_accessed=40 << 20
        ),
        name="feed_forward",
    )(x, grads, w_gate, w_up, w_down)


def stack_heads(block):
    heads = block.shape[1] // 128
    return jnp.concatenate([block[:, h * 128 : (h + 1) * 128] for h in range(heads)], axis=0)


def chunk_plan(tok_rows):
    first = lax.axis_index("fsdp") * tok_rows % GROUP_TOK + pl.program_id(0) * TILE
    in_prompt = first < PROMPT
    full = jnp.where(in_prompt, first // CHUNK, PROMPT // CHUNK)
    last = jnp.where(
        in_prompt, first // CHUNK * CHUNK, jnp.maximum(PROMPT, first + TILE - CHUNK)
    )
    return first, full, pl.multiple_of(last, TILE)


def attend_kernel(
    tok_rows,
    q_ref,
    kv_ref,
    low_ref,
    grads_ref,
    mixed_ref,
    log_ref,
    grads_all,
    values,
    top,
    acc,
    own_rows,
    sems,
    own_sem,
):
    factor = 128**-0.5 * LOG2E

    exchange = Exchange(grads_ref, grads_all, sems)
    load_own = pltpu.make_async_copy(grads_ref, own_rows, own_sem)
    keep_own = pltpu.make_async_copy(own_rows, grads_all.at[0], own_sem)

    @pl.when((pl.program_id(0) == 0) & (pl.program_id(1) == 0))
    def _():
        load_own.start()
        exchange.greet()
        exchange.begin()
        load_own.wait()
        keep_own.start()
        values[:, :128] = kv_ref[:, 128:]
        values[:, 128:] = jnp.ones_like(values[:, 128:])

    @pl.when((pl.program_id(0) == pl.num_programs(0) // 2) & (pl.program_id(1) == 0))
    def _():
        exchange.relay()

    first, full, last = chunk_plan(tok_rows)
    queries = stack_heads(q_ref[...])
    rows = queries.shape[0]
    top[...] = jnp.full_like(top, MASKED)
    acc[...] = jnp.zeros_like(acc)

    def step(start, masked):
        scores = contract(queries, kv_ref[pl.ds(start, CHUNK), :128], 1, 1) * factor
        if masked:
            key_at = start + lax.broadcasted_iota(jnp.int32, (rows, CHUNK), 1)
            row_at = lax.broadcasted_iota(jnp.int32, (rows, 1), 0) % TILE + first
            low = jnp.concatenate([low_ref[:, :1]] * HEAD_GROUP, axis=0)
            scores = jnp.where((key_at <= row_at) & (key_at >= low), scores, MASKED)
        before = top[:, :1]
        after = jnp.maximum(before, jnp.max(scores, axis=1, keepdims=True))
        weights = jnp.exp2(scores - after).astype(jnp.bfloat16)
        acc[...] = acc[...] * jnp.exp2(before - after) + matmul(
            weights, values[pl.ds(start, CHUNK), :]
        )
        top[...] = jnp.broadcast_to(after, top.shape)

    @pl.loop(0, full)
    def _(at):
        step(pl.multiple_of(at * CHUNK, CHUNK), False)

    step(last, True)
    total = acc[:, 128:]
    mixed = acc[:, :128] / total
    for h in range(HEAD_GROUP):
        mixed_ref[:, h * 128 : (h + 1) * 128] = mixed[h * TILE : (h + 1) * TILE].astype(jnp.bfloat16)
    log_ref[0, 0] = (top[...] + jnp.log2(total)).T[:8]

    @pl.when(
        (pl.program_id(0) == pl.num_programs(0) - 1) & (pl.program_id(1) == pl.num_programs(1) - 1)
    )
    def _():
        keep_own.wait()
        exchange.end()
        exchange.drain()


def attend(queries, kv, low, grads):
    tok_rows, width = queries.shape
    tiles, groups = tok_rows // TILE, width // (128 * HEAD_GROUP)
    lanes, rows = 128 * HEAD_GROUP, TILE * HEAD_GROUP
    tile_spec = pl.BlockSpec((TILE, lanes), lambda i, g: (i, g))
    hbm = pl.BlockSpec(memory_space=pl.ANY)
    pairs = tok_rows * (width // 128) * 2560
    return pl.pallas_call(
        functools.partial(attend_kernel, tok_rows),
        out_shape=(
            jax.ShapeDtypeStruct((tok_rows, width), jnp.bfloat16),
            jax.ShapeDtypeStruct((tiles, groups, 8, rows), jnp.float32),
            jax.ShapeDtypeStruct((4,) + grads.shape, jnp.bfloat16),
        ),
        grid=(tiles, groups),
        in_specs=[
            tile_spec,
            pl.BlockSpec(kv.shape, lambda i, g: (0, 0)),
            pl.BlockSpec((TILE, 128), lambda i, g: (i, 0)),
            hbm,
        ],
        out_specs=[
            tile_spec,
            pl.BlockSpec((1, 1, 8, rows), lambda i, g: (i, g, 0, 0)),
            hbm,
        ],
        scratch_shapes=[
            pltpu.VMEM(kv.shape, jnp.bfloat16),
            pltpu.VMEM((rows, 128), jnp.float32),
            pltpu.VMEM((rows, 256), jnp.float32),
            pltpu.VMEM(grads.shape, jnp.bfloat16),
            pltpu.SemaphoreType.DMA((2, 4)),
            pltpu.SemaphoreType.DMA,
        ],
        compiler_params=pltpu.CompilerParams(
            collective_id=4, has_side_effects=True, vmem_limit_bytes=40 << 20
        ),
        cost_estimate=pl.CostEstimate(
            flops=pairs * 3000, transcendentals=pairs, bytes_accessed=16 << 20
        ),
        name="attend",
    )(queries, kv, low, grads)


def attend_back_kernel(
    fsdp_size,
    tok_rows,
    q_ref,
    kv_ref,
    cos_ref,
    sin_ref,
    low_ref,
    mixed_ref,
    d_mixed_ref,
    log_ref,
    rows_ref,
    branch_ref,
    d_q_ref,
    d_kv_ref,
    output_ref,
    sums,
    d_q,
    *refs,
):
    scale = 128**-0.5
    factor = scale * LOG2E
    at_end = (pl.program_id(0) == pl.num_programs(0) - 1) & (
        pl.program_id(1) == pl.num_programs(1) - 1
    )

    place = position(fsdp_size)
    grad = make_collect(place, refs)
    count = place[4]

    def begin():
        sums[...] = jnp.zeros_like(sums)
        greet(*place[:3], count)
        outer(grad, rows_ref, branch_ref, False)
        outer(grad, rows_ref, branch_ref, True)

    def cores():
        for shard in range(count):
            grad.core_add(shard)
            grad.diag_start(shard)

    def sum_quarters():
        each(count, grad.quarter_add)
        grad.line_hop(count - 1)

    def hops():
        for hop in range(count - 2, 0, -1):
            grad.line_hop(hop)

    def gather():
        grad.line_end()
        grad.gather_start()

    stages = {
        0: begin,
        1: cores,
        5: lambda: each(count, grad.quarter_start),
        10: sum_quarters,
        11: hops,
        12: gather,
        14: grad.gather_relay,
    }
    now = pl.program_id(0) * pl.num_programs(1) + pl.program_id(1)
    for step_at, stage in stages.items():
        pl.when(now == step_at)(stage)

    first, full, last = chunk_plan(tok_rows)
    queries = stack_heads(q_ref[...])
    d_rows = stack_heads(d_mixed_ref[...])
    mixed = stack_heads(mixed_ref[...])
    rows = queries.shape[0]
    products = d_rows.astype(jnp.float32) * mixed.astype(jnp.float32)
    delta = jnp.sum(products.T, axis=0, keepdims=True)
    log_total = log_ref[0, 0, :1]
    d_q[...] = jnp.zeros_like(d_q)

    def step(start, masked):
        keys = kv_ref[pl.ds(start, CHUNK), :128]
        values = kv_ref[pl.ds(start, CHUNK), 128:]
        scores = contract(keys, queries, 1, 1) * factor
        probs = jnp.exp2(scores - log_total)
        if masked:
            key_at = start + lax.broadcasted_iota(jnp.int32, (CHUNK, rows), 0)
            row_at = lax.broadcasted_iota(jnp.int32, (1, rows), 1) % TILE + first
            low = jnp.concatenate([low_ref[:1]] * HEAD_GROUP, axis=1)
            probs = jnp.where((key_at <= row_at) & (key_at >= low), probs, 0.0)
        d_probs = contract(values, d_rows, 1, 1)
        d_scores = (probs * (d_probs - delta)).astype(jnp.bfloat16)
        sums[pl.ds(start, CHUNK), 128:] += matmul(probs.astype(jnp.bfloat16), d_rows)
        sums[pl.ds(start, CHUNK), :128] += matmul(d_scores, queries)
        d_q[...] += contract(d_scores, keys, 0, 0)

    @pl.loop(0, full)
    def _(at):
        step(pl.multiple_of(at * CHUNK, CHUNK), False)

    step(last, True)
    cos_table, sin_table = cos_ref[...] * scale, sin_ref[...] * scale
    for h in range(HEAD_GROUP):
        turned = d_q[h * TILE : (h + 1) * TILE]
        raw = turned * cos_table - pltpu.roll(turned, 64, 1) * sin_table
        d_q_ref[:, h * 128 : (h + 1) * 128] = raw.astype(jnp.bfloat16)

    @pl.when(at_end)
    def _():
        d_kv_ref[:, :128] = (sums[:, :128] * scale).astype(jnp.bfloat16)
        d_kv_ref[:, 128:] = sums[:, 128:].astype(jnp.bfloat16)
        grad.gather_end()
        output_ref[...] = grad.full[...].astype(jnp.float32)
        grad.drain()


def attend_back(queries, kv, cos_table, sin_table, low, mixed, d_mixed, logs, d_branch):
    tok_rows, width = queries.shape
    fsdp_size = lax.axis_size("fsdp")
    shard = width // fsdp_size
    tiles, groups = tok_rows // TILE, width // (128 * HEAD_GROUP)
    lanes, rows = 128 * HEAD_GROUP, TILE * HEAD_GROUP
    tile_spec = pl.BlockSpec((TILE, lanes), lambda i, g: (i, g))
    row_spec = pl.BlockSpec((TILE, 128), lambda i, g: (i, 0))
    whole = pl.BlockSpec(kv.shape, lambda i, g: (0, 0))
    pairs = tok_rows * (width // 128) * 2560
    return pl.pallas_call(
        functools.partial(attend_back_kernel, fsdp_size, tok_rows),
        out_shape=(
            jax.ShapeDtypeStruct((tok_rows, width), jnp.bfloat16),
            jax.ShapeDtypeStruct(kv.shape, jnp.bfloat16),
            jax.ShapeDtypeStruct((shard, width), jnp.float32),
        ),
        grid=(tiles, groups),
        in_specs=[
            tile_spec,
            whole,
            row_spec,
            row_spec,
            pl.BlockSpec((8, TILE), lambda i, g: (0, i)),
            tile_spec,
            tile_spec,
            pl.BlockSpec((1, 1, 8, rows), lambda i, g: (i, g, 0, 0)),
            pl.BlockSpec(mixed.shape, lambda i, g: (0, 0)),
            pl.BlockSpec(mixed.shape, lambda i, g: (0, 0)),
        ],
        out_specs=[tile_spec, whole, pl.BlockSpec((shard, width), lambda i, g: (0, 0))],
        scratch_shapes=[
            pltpu.VMEM(kv.shape, jnp.float32),
            pltpu.VMEM((rows, 128), jnp.float32),
        ]
        + collect_scratch(fsdp_size, shard, width),
        compiler_params=pltpu.CompilerParams(
            collective_id=1, has_side_effects=True, vmem_limit_bytes=50 << 20
        ),
        cost_estimate=pl.CostEstimate(
            flops=pairs * 3000, transcendentals=pairs, bytes_accessed=16 << 20
        ),
        name="attend_back",
    )(queries, kv, cos_table, sin_table, low, mixed, d_mixed, logs, mixed, d_branch)


class Chain:
    def __init__(self, place, count, at, replica, fsdp, sends, recvs):
        self.place, self.count, self.at = place, count, at
        self.replica, self.fsdp, self.sends, self.recvs = replica, fsdp, sends, recvs

    def copy(self, shard, way):
        target = self.fsdp + (2 if way == 0 else -2)
        return pltpu.make_async_remote_copy(
            src_ref=self.place(shard),
            dst_ref=self.place(shard),
            send_sem=self.sends.at[way, shard],
            recv_sem=self.recvs.at[way, shard],
            device_id=(self.replica, target),
            device_id_type=MESH,
        )

    def begin(self):
        @pl.when(self.at < self.count - 1)
        def _():
            self.copy(self.at, 0).start()

        @pl.when(self.at > 0)
        def _():
            self.copy(self.at, 1).start()

    def step(self, hop, arrived=None):
        left, right = self.at - hop, self.at + hop

        @pl.when(left >= 0)
        def _():
            self.copy(left, 0).wait_recv()

        @pl.when((left >= 0) & (self.at < self.count - 1))
        def _():
            self.copy(left, 0).start()

        if arrived is not None:

            @pl.when(left >= 0)
            def _():
                arrived(left)

        @pl.when(right < self.count)
        def _():
            self.copy(right, 1).wait_recv()

        @pl.when((right < self.count) & (self.at > 0))
        def _():
            self.copy(right, 1).start()

        if arrived is not None:

            @pl.when(right < self.count)
            def _():
                arrived(right)

    def finish(self):
        for hop in range(self.count):

            @pl.when((self.at - hop >= 0) & (self.at < self.count - 1))
            def _(hop=hop):
                self.copy(self.at - hop, 0).wait_send()

            @pl.when((self.at + hop < self.count) & (self.at > 0))
            def _(hop=hop):
                self.copy(self.at + hop, 1).wait_send()


class Spread:
    def __init__(self, buffer, count, at, core, replica, fsdp, sems):
        self.buffer, self.count, self.at, self.core = buffer, count, at, core
        self.replica, self.fsdp, self.sems = replica, fsdp, sems
        self.rows = buffer.shape[1] // 4

    def rows_of(self, shard, copy, half=None):
        start, size = copy * self.rows, self.rows
        if half is not None:
            size = size // 2
            start = start + half * size
        return self.buffer.at[2 * shard + self.core, pl.ds(start, size)]

    def copy(self, kind, shard):
        beside, across = flip(self.replica, 1), flip(self.replica, 2)
        if kind == 0:
            ref, target = self.rows_of(shard, self.replica), (beside, self.fsdp)
        elif kind == 1:
            ref, target = self.rows_of(shard, self.replica), (across, self.fsdp)
        elif kind == 2:
            ref, target = self.rows_of(shard, beside, 0), (across, self.fsdp)
        elif kind == 3:
            ref, target = self.rows_of(shard, across, 1), (beside, self.fsdp)
        else:
            ref, target = self.buffer.at[2 * shard + self.core], (self.replica, flip(self.fsdp, 1))
        return pltpu.make_async_remote_copy(
            src_ref=ref,
            dst_ref=ref,
            send_sem=self.sems.at[0, kind, shard],
            recv_sem=self.sems.at[1, kind, shard],
            device_id=target,
            device_id_type=MESH,
        )

    def recv(self, kind, shard):
        beside, across = flip(self.replica, 1), flip(self.replica, 2)
        if kind == 0:
            ref = self.rows_of(shard, beside)
        elif kind == 1:
            ref = self.rows_of(shard, across)
        elif kind < 4:
            ref = self.rows_of(shard, flip(beside, 2), kind - 2)
        else:
            ref = self.buffer.at[2 * shard + 1 - self.core]
        return pltpu.make_async_remote_copy(
            src_ref=ref,
            dst_ref=ref,
            send_sem=self.sems.at[0, kind, shard],
            recv_sem=self.sems.at[1, kind, shard],
            device_id=(self.replica, flip(self.fsdp, 1)),
            device_id_type=MESH,
        )

    def arrived(self, shard):
        self.copy(0, shard).start()
        self.copy(1, shard).start()

    def others(self):
        return [(self.at + hop) % self.count for hop in range(1, self.count)]

    def relay(self):
        for shard in self.others():
            self.recv(0, shard).wait_recv()
            self.copy(2, shard).start()
            self.recv(1, shard).wait_recv()
            self.copy(3, shard).start()

    def cores(self):
        self.copy(4, self.at).start()
        for shard in self.others():
            self.recv(2, shard).wait_recv()
            self.recv(3, shard).wait_recv()
            self.copy(4, shard).start()

    def finish(self):
        for shard in self.others() + [self.at]:
            self.recv(4, shard).wait_recv()
        for shard in self.others():
            for kind in range(5):
                self.copy(kind, shard).wait_send()
        self.copy(4, self.at).wait_send()


def project_kernel(
    fsdp_size,
    tokens_ref,
    wq_ref,
    wo_ref,
    kvg_ref,
    cos_ref,
    sin_ref,
    q_ref,
    normed_ref,
    gain_ref,
    wq_all,
    wo_all,
    kvg_all,
    kv_all,
    wq_vmem,
    kvg_vmem,
    kv_vmem,
    local_sems,
    kvg_sems,
    kvg_core,
    wq_line,
    wq_sems,
    wo_line,
    wo_sems,
    kv_sems,
    kv_core,
):
    replica, fsdp = lax.axis_index("replica"), lax.axis_index("fsdp")
    count, at, core = fsdp_size // 2, fsdp // 2, fsdp % 2
    width = tokens_ref.shape[1]
    partner = (replica, flip(fsdp, 1))

    spare = flip(fsdp, 1)
    load_own = [
        pltpu.make_async_copy(kvg_ref, kvg_vmem.at[fsdp], local_sems.at[0]),
        pltpu.make_async_copy(wq_ref, wq_vmem.at[fsdp], local_sems.at[1]),
        pltpu.make_async_copy(wo_ref, wq_vmem.at[spare], local_sems.at[2]),
    ]
    own = [
        pltpu.make_async_copy(kvg_vmem.at[fsdp], kvg_all.at[fsdp], local_sems.at[0]),
        pltpu.make_async_copy(wq_vmem.at[fsdp], wq_all.at[fsdp], local_sems.at[1]),
        pltpu.make_async_copy(wq_vmem.at[spare], wo_all.at[fsdp], local_sems.at[2]),
    ]
    for copy in load_own:
        copy.start()
    for load, copy in zip(load_own, own):
        load.wait()
        copy.start()
    greet(replica, fsdp, at, count)

    def core_copy(buffer, sems, shard, lands=False):
        ref = buffer.at[2 * shard + (1 - core if lands else core)]
        return pltpu.make_async_remote_copy(
            src_ref=ref,
            dst_ref=ref,
            send_sem=sems.at[0, shard],
            recv_sem=sems.at[1, shard],
            device_id=partner,
            device_id_type=MESH,
        )

    def line(place, sems):
        return Chain(place, count, at, replica, fsdp, sems.at[0], sems.at[1])

    kvg = line(lambda shard: kvg_all.at[2 * shard + core], kvg_sems)
    kv = line(lambda shard: kv_all.at[2 * shard + core], kv_sems)
    wq = Spread(wq_all, count, at, core, replica, fsdp, wq_sems)
    wo = Spread(wo_all, count, at, core, replica, fsdp, wo_sems)
    wq_chain = line(lambda shard: wq.rows_of(shard, replica), wq_line)
    wo_chain = line(lambda shard: wo.rows_of(shard, replica), wo_line)
    own[0].wait()
    kvg.begin()
    core_copy(kvg_all, kvg_core, at).start()
    own[1].wait()
    wq_chain.begin()
    own[2].wait()
    wo_chain.begin()

    inputs = tokens_ref[...].astype(jnp.float32)
    inverse = lax.rsqrt(jnp.mean(inputs * inputs, axis=1, keepdims=True) + EPSILON)

    for hop in range(1, count):
        kvg.step(hop, lambda shard: core_copy(kvg_all, kvg_core, shard).start())
        wq_chain.step(hop, wq.arrived)
        wo_chain.step(hop, wo.arrived)
    for shard in range(count):
        core_copy(kvg_all, kvg_core, shard, True).wait_recv()
    load = pltpu.make_async_copy(kvg_all, kvg_vmem, local_sems.at[0])
    load.start()
    load.wait()
    table = kvg_vmem[...].reshape(width, kvg_vmem.shape[2])
    gains = table[:, 256:].astype(jnp.float32).T[:8]
    gain_ref[...] = gains
    normed_ref[...] = (inputs * inverse * gains[:1]).astype(jnp.bfloat16)
    kv_raw = matmul(normed_ref[...], table[:, :256])
    cos_table, sin_table = cos_ref[...], sin_ref[...]
    key_raw = kv_raw[:, :128]
    key_rot = key_raw * cos_table + pltpu.roll(key_raw, 64, 1) * sin_table
    kv_vmem[:, :128] = key_rot.astype(jnp.bfloat16)
    kv_vmem[:, 128:] = kv_raw[:, 128:].astype(jnp.bfloat16)
    store = pltpu.make_async_copy(kv_vmem, kv_all.at[fsdp], local_sems.at[0])
    store.start()
    store.wait()
    kv.begin()
    core_copy(kv_all, kv_core, at).start()
    wq.relay()
    kv.step(1, lambda shard: core_copy(kv_all, kv_core, shard).start())
    wq.cores()
    wo.relay()
    for shard in wq.others() + [at]:
        wq.recv(4, shard).wait_recv()
    load = pltpu.make_async_copy(wq_all, wq_vmem, local_sems.at[1])
    load.start()
    for hop in range(2, count):
        kv.step(hop, lambda shard: core_copy(kv_all, kv_core, shard).start())
    load.wait()
    weight = wq_vmem.reshape(width, width)

    def columns(block):
        start = pl.multiple_of(block * 512, 512)
        raw = matmul(normed_ref[...], weight[:, pl.ds(start, 512)])
        for h in range(4):
            head = raw[:, h * 128 : (h + 1) * 128]
            turned = head * cos_table + pltpu.roll(head, 64, 1) * sin_table
            q_ref[:, pl.ds(start + h * 128, 128)] = turned.astype(jnp.bfloat16)

    pl.loop(0, width // 512)(columns)
    wo.cores()
    for shard in range(count):
        core_copy(kv_all, kv_core, shard, True).wait_recv()
    wo.finish()
    for shard in wq.others():
        for kind in range(5):
            wq.copy(kind, shard).wait_send()
    wq.copy(4, at).wait_send()
    for shard in range(count):
        core_copy(kvg_all, kvg_core, shard).wait_send()
        core_copy(kv_all, kv_core, shard).wait_send()
    for chain in (kvg, kv, wq_chain, wo_chain):
        chain.finish()


def project(tokens, wq, wo, kvg, cos_table, sin_table):
    rows, width = tokens.shape
    shard = wq.shape[0]
    fsdp_size = lax.axis_size("fsdp")
    count = fsdp_size // 2
    low = jnp.bfloat16
    vmem, hbm = pl.BlockSpec(memory_space=pltpu.VMEM), pl.BlockSpec(memory_space=pl.ANY)
    dma = pltpu.SemaphoreType.DMA
    return pl.pallas_call(
        functools.partial(project_kernel, fsdp_size),
        out_shape=(
            jax.ShapeDtypeStruct((rows, width), low),
            jax.ShapeDtypeStruct((rows, width), low),
            jax.ShapeDtypeStruct((8, width), jnp.float32),
            jax.ShapeDtypeStruct((fsdp_size, shard, width), low),
            jax.ShapeDtypeStruct((fsdp_size, shard, width), low),
            jax.ShapeDtypeStruct((fsdp_size, shard, kvg.shape[1]), low),
            jax.ShapeDtypeStruct((fsdp_size, rows, 256), low),
        ),
        in_specs=[vmem, hbm, hbm, hbm, vmem, vmem],
        out_specs=(vmem, vmem, vmem, hbm, hbm, hbm, hbm),
        scratch_shapes=[
            pltpu.VMEM((fsdp_size, shard, width), low),
            pltpu.VMEM((fsdp_size, shard, kvg.shape[1]), low),
            pltpu.VMEM((rows, 256), low),
            dma((3,)),
            dma((2, 2, count)),
            dma((2, count)),
            dma((2, 2, count)),
            dma((2, 5, count)),
            dma((2, 2, count)),
            dma((2, 5, count)),
            dma((2, 2, count)),
            dma((2, count)),
        ],
        compiler_params=pltpu.CompilerParams(
            collective_id=0, has_side_effects=True, vmem_limit_bytes=48 << 20
        ),
        cost_estimate=pl.CostEstimate(
            flops=2 * rows * width * (width + 256), transcendentals=0, bytes_accessed=40 << 20
        ),
        name="project",
    )(tokens, wq, wo, kvg, cos_table, sin_table)


def greet(replica, fsdp, at, count):
    barrier = pltpu.get_barrier_semaphore()
    for target in (
        (replica, flip(fsdp, 1)),
        (flip(replica, 1), fsdp),
        (flip(replica, 2), fsdp),
    ):
        pl.semaphore_signal(barrier, inc=1, device_id=target, device_id_type=MESH)

    @pl.when(at > 0)
    def _():
        pl.semaphore_signal(barrier, inc=1, device_id=(replica, fsdp - 2), device_id_type=MESH)

    @pl.when(at < count - 1)
    def _():
        pl.semaphore_signal(barrier, inc=1, device_id=(replica, fsdp + 2), device_id_type=MESH)

    inside = (at > 0) & (at < count - 1)

    @pl.when(inside)
    def _():
        pl.semaphore_wait(barrier, 5)

    @pl.when(jnp.logical_not(inside))
    def _():
        pl.semaphore_wait(barrier, 4)


def add_into(ref, index, *others):
    total = ref[index].astype(jnp.float32)
    for other in others:
        total = total + other.astype(jnp.float32)
    ref[index] = total.astype(ref.dtype)


class Collect:
    def __init__(self, place, grad, core_in, line_in, core_sems, line_sems, copies=None):
        self.replica, self.fsdp, self.at, self.core, self.count = place
        self.grad, self.core_in, self.line_in = grad, core_in, line_in
        self.core_sems, self.line_sems = core_sems, line_sems
        self.beside, self.across = flip(self.replica, 1), flip(self.replica, 2)
        self.opposite = flip(self.beside, 2)
        if copies is None:
            self.rows = pl.ds(0, grad.shape[1])
        else:
            self.diag_in, self.quarter_in, self.full = copies[:3]
            self.diag_sems, self.quarter_sems, self.full_sems = copies[3:]
            self.size = grad.shape[1] // 4
            self.rows = self.quarter(self.replica)

    def quarter(self, copy, half=None):
        size = self.size if half is None else self.size // 2
        start = copy * self.size + (0 if half is None else half * size)
        return pl.ds(pl.multiple_of(start, size), size)

    def remote(self, src, dst, sems, index, target):
        return pltpu.make_async_remote_copy(
            src_ref=src,
            dst_ref=dst,
            send_sem=sems.at[(0,) + index],
            recv_sem=sems.at[(1,) + index],
            device_id=target,
            device_id_type=MESH,
        )

    def core_copy(self, shard):
        return self.remote(
            self.grad.at[2 * shard + 1 - self.core],
            self.core_in.at[shard],
            self.core_sems,
            (shard,),
            (self.replica, flip(self.fsdp, 1)),
        )

    def core_add(self, shard):
        self.core_copy(shard).wait_recv()
        add_into(self.grad, 2 * shard + self.core, self.core_in[shard])

    def diag_copy(self, shard, half):
        return self.remote(
            self.grad.at[2 * shard + self.core, self.quarter(self.opposite, half)],
            self.diag_in.at[half, shard],
            self.diag_sems,
            (half, shard),
            (self.beside if half == 0 else self.across, self.fsdp),
        )

    def diag_start(self, shard):
        self.diag_copy(shard, 0).start()
        self.diag_copy(shard, 1).start()

    def quarter_copy(self, shard, way):
        return self.remote(
            self.grad.at[2 * shard + self.core, self.quarter(self.across if way else self.beside)],
            self.quarter_in.at[way, shard],
            self.quarter_sems,
            (way, shard),
            (self.across if way else self.beside, self.fsdp),
        )

    def quarter_start(self, shard):
        at = 2 * shard + self.core
        for half, copy in ((0, self.across), (1, self.beside)):
            self.diag_copy(shard, half).wait_recv()
            add_into(self.grad, (at, self.quarter(copy, half)), self.diag_in[half, shard])
            self.quarter_copy(shard, 1 - half).start()

    def quarter_add(self, shard):
        self.quarter_copy(shard, 0).wait_recv()
        self.quarter_copy(shard, 1).wait_recv()
        add_into(
            self.grad,
            (2 * shard + self.core, self.rows),
            self.quarter_in[0, shard],
            self.quarter_in[1, shard],
        )

    def line_copy(self, shard, way):
        return self.remote(
            self.grad.at[2 * shard + self.core, self.rows],
            self.line_in.at[way, shard],
            self.line_sems,
            (way, shard),
            (self.replica, self.fsdp + (2 if way == 0 else -2)),
        )

    def line_receive(self, shard, way):
        self.line_copy(shard, way).wait_recv()
        add_into(self.grad, (2 * shard + self.core, self.rows), self.line_in[way, shard])

    def line_hop(self, hop):
        for way, shard, there, fed in (
            (0, self.at + hop, self.at + hop < self.count, self.at > 0),
            (1, self.at - hop, self.at - hop >= 0, self.at < self.count - 1),
        ):

            @pl.when(there & fed)
            def _(shard=shard, way=way):
                self.line_receive(shard, way)

            @pl.when(there)
            def _(shard=shard, way=way):
                self.line_copy(shard, way).start()

    def line_end(self):
        @pl.when(self.at > 0)
        def _():
            self.line_receive(self.at, 0)

        @pl.when(self.at < self.count - 1)
        def _():
            self.line_receive(self.at, 1)

    def full_copy(self, kind):
        own = self.replica
        rows, target = (
            (self.quarter(own), self.beside),
            (self.quarter(own), self.across),
            (self.quarter(self.beside, 0), self.across),
            (self.quarter(self.across, 1), self.beside),
        )[kind]
        return self.remote(
            self.full.at[rows],
            self.full.at[rows],
            self.full_sems,
            (kind,),
            (target, self.fsdp),
        )

    def full_recv(self, kind):
        rows = (
            self.quarter(self.beside),
            self.quarter(self.across),
            self.quarter(self.opposite, 0),
            self.quarter(self.opposite, 1),
        )[kind]
        ref = self.full.at[rows]
        self.remote(ref, ref, self.full_sems, (kind,), (self.beside, self.fsdp)).wait_recv()

    def gather_start(self):
        self.full[self.rows] = self.grad[2 * self.at + self.core, self.rows]
        self.full_copy(0).start()
        self.full_copy(1).start()

    def gather_relay(self):
        self.full_recv(0)
        self.full_copy(2).start()
        self.full_recv(1)
        self.full_copy(3).start()

    def gather_end(self):
        self.full_recv(2)
        self.full_recv(3)

    def drain(self):
        for shard in range(self.count):
            self.core_copy(shard).wait_send()
            if hasattr(self, "size"):
                for way in (0, 1):
                    self.diag_copy(shard, way).wait_send()
                    self.quarter_copy(shard, way).wait_send()
        for hop in range(1, self.count):

            @pl.when(self.at + hop < self.count)
            def _(hop=hop):
                self.line_copy(self.at + hop, 0).wait_send()

            @pl.when(self.at - hop >= 0)
            def _(hop=hop):
                self.line_copy(self.at - hop, 1).wait_send()

        if hasattr(self, "size"):
            for kind in range(4):
                self.full_copy(kind).wait_send()


def collect_scratch(fsdp_size, rows, width, copies=True):
    count = fsdp_size // 2
    low, dma = jnp.bfloat16, pltpu.SemaphoreType.DMA
    size = rows // 4 if copies else rows
    shapes = [
        pltpu.VMEM((fsdp_size, rows, width), low),
        pltpu.VMEM((count, rows, width), low),
        pltpu.VMEM((2, count, size, width), low),
        dma((2, count)),
        dma((2, 2, count)),
    ]
    if copies:
        shapes += [
            pltpu.VMEM((2, count, size // 2, width), low),
            pltpu.VMEM((2, count, size, width), low),
            pltpu.VMEM((rows, width), low),
            dma((2, 2, count)),
            dma((2, 2, count)),
            dma((2, 4)),
        ]
    return shapes


def make_collect(place, refs, copies=True):
    return Collect(place, *refs[:5], copies=refs[5:11] if copies else None)


def position(fsdp_size):
    replica, fsdp = lax.axis_index("replica"), lax.axis_index("fsdp")
    return replica, fsdp, fsdp // 2, fsdp % 2, fsdp_size // 2


def outer(collect, left_ref, right_ref, own_core):
    rows = collect.grad.shape[1]
    core = collect.core if own_core else 1 - collect.core

    @pl.loop(0, collect.count)
    def _(shard):
        start = pl.multiple_of((2 * shard + core) * rows, rows)
        part = contract(left_ref[:, pl.ds(start, rows)], right_ref[...], 0, 0)
        collect.grad[2 * shard + core] = part.astype(jnp.bfloat16)
        if not own_core:
            collect.core_copy(shard).start()


def each(count, step):
    for shard in range(count):
        step(shard)


def finish_kernel(
    fsdp_size,
    normed_ref,
    d_q_ref,
    tokens_ref,
    d_hidden_ref,
    gain_ref,
    term_ref,
    cos_ref,
    sin_ref,
    d_kv_ref,
    wq_ref,
    kvg_ref,
    ffn_ref,
    input_grad_ref,
    q_grad_ref,
    kv_grad_ref,
    ffn_all,
    wq_buf,
    kvg_vmem,
    d_kv_raw,
    term_sum,
    hidden_buf,
    local_sems,
    ffn_sems,
    *refs,
):
    place = position(fsdp_size)
    replica, fsdp, at, core, count = place
    greet(replica, fsdp, at, count)
    q_sums = make_collect(place, refs[:11])
    kv_sums = make_collect(place, refs[11:22])
    d_kv = make_collect(place, refs[22:27], False)
    beside, across = flip(replica, 1), flip(replica, 2)
    width = tokens_ref.shape[1]
    half = width // 2

    def ffn_copy(kind, lands=False):
        piece = (replica, replica, beside, across)[kind]
        if lands:
            piece = (beside, across, flip(beside, 2), flip(beside, 2))[kind]
        columns = (slice(None), slice(None), pl.ds(0, half), pl.ds(half, half))[kind]
        dst = ffn_all.at[piece, :, :, columns]
        return pltpu.make_async_remote_copy(
            src_ref=ffn_ref if kind < 2 and not lands else dst,
            dst_ref=dst,
            send_sem=ffn_sems.at[0, kind],
            recv_sem=ffn_sems.at[1, kind],
            device_id=((beside, across, across, beside)[kind], fsdp),
            device_id_type=MESH,
        )

    ffn_copy(0).start()
    ffn_copy(1).start()
    ffn_rows = ffn_ref.shape[1]

    def keep_ffn(part, slot, out):
        held = wq_buf.at[slot, pl.ds(0, ffn_rows)]
        place_at = ffn_all.at[replica, part]
        return pltpu.make_async_copy(
            held if out else ffn_ref.at[part], place_at if out else held, local_sems.at[0]
        )

    load = pltpu.make_async_copy(d_kv_ref, d_kv.grad, local_sems.at[1])
    load.start()
    load_kvg = pltpu.make_async_copy(kvg_ref, kvg_vmem, local_sems.at[2])
    load_kvg.start()
    load.wait()
    each(count, lambda shard: d_kv.core_copy(shard).start())
    outer(q_sums, normed_ref, d_q_ref, False)
    for part in range(3):
        for out in (False, True):
            keep_ffn(part, 0, out).start()
            keep_ffn(part, 0, out).wait()
    each(count, d_kv.core_add)
    d_kv.line_hop(count - 1)
    outer(q_sums, normed_ref, d_q_ref, True)
    for hop in range(count - 2, 0, -1):
        d_kv.line_hop(hop)
    for shard in range(count):
        q_sums.core_add(shard)
        q_sums.diag_start(shard)
    d_kv.line_end()
    each(count, q_sums.quarter_start)

    summed = d_kv.grad[fsdp].astype(jnp.float32)
    d_key = summed[:, :128]
    d_key = d_key * cos_ref[...] - pltpu.roll(d_key, 64, 1) * sin_ref[...]
    d_kv_raw[:, :128] = d_key.astype(jnp.bfloat16)
    d_kv_raw[:, 128:] = summed[:, 128:].astype(jnp.bfloat16)
    load_kvg.wait()
    rows = kvg_vmem.shape[1]

    def fetch(shard):
        return pltpu.make_async_copy(wq_ref.at[shard], wq_buf.at[shard % 2], local_sems.at[shard % 2])

    fetch(0).start()
    for shard in range(fsdp_size):
        fetch(shard).wait()
        if shard + 1 < fsdp_size:
            fetch(shard + 1).start()
        input_grad_ref[:, shard * rows : (shard + 1) * rows] = contract(
            d_q_ref[...], wq_buf[shard % 2], 1, 1
        ) + contract(d_kv_raw[...], kvg_vmem[shard, :, :256], 1, 1)
    for kind in (0, 1):
        ffn_copy(kind, True).wait_recv()
        ffn_copy(2 + kind).start()
    each(count, q_sums.quarter_add)
    for hop in range(count - 1, 0, -1):
        q_sums.line_hop(hop)

    term_sum[...] = jnp.zeros_like(term_sum)

    @pl.loop(0, tokens_ref.shape[0] // 128)
    def _(block):
        part = pl.ds(pl.multiple_of(block * 128, 128), 128)
        fetch_hidden = pltpu.make_async_copy(d_hidden_ref.at[part], hidden_buf, local_sems.at[0])
        fetch_hidden.start()
        d_normed = input_grad_ref[part]
        inputs = tokens_ref[part].astype(jnp.float32)
        inverse = lax.rsqrt(jnp.mean(inputs * inputs, axis=1, keepdims=True) + EPSILON)
        scaled = d_normed * gain_ref[:1]
        inner = jnp.mean(scaled * inputs, axis=1, keepdims=True)
        term_sum[:1] += jnp.sum(d_normed * inputs * inverse, axis=0, keepdims=True)
        step = inverse * scaled - inputs * (inverse**3 * inner)
        fetch_hidden.wait()
        input_grad_ref[part] = hidden_buf[...] + step

    term = term_sum[:1]
    line = lax.broadcasted_iota(jnp.int32, (128, width), 0)
    terms = jnp.where(line == 0, term, jnp.where(line == 1, term_ref[:1], 0.0)).T
    terms = terms.astype(jnp.bfloat16)
    for shard in range(fsdp_size):
        left = normed_ref[:, shard * rows : (shard + 1) * rows]
        kv_sums.grad[shard, :, :256] = contract(left, d_kv_raw[...], 0, 0).astype(jnp.bfloat16)
        kv_sums.grad[shard, :, 256:] = terms[shard * rows : (shard + 1) * rows]
    each(count, lambda shard: kv_sums.core_copy(shard).start())
    q_sums.line_end()
    q_sums.gather_start()
    for shard in range(count):
        kv_sums.core_add(shard)
        kv_sums.diag_start(shard)
    each(count, kv_sums.quarter_start)
    q_sums.gather_relay()
    each(count, kv_sums.quarter_add)
    for hop in range(count - 1, 0, -1):
        kv_sums.line_hop(hop)
    kv_sums.line_end()
    kv_sums.gather_start()
    q_sums.gather_end()
    q_grad_ref[...] = q_sums.full[...].astype(jnp.float32)
    kv_sums.gather_relay()
    kv_sums.gather_end()
    kv_grad_ref[...] = kv_sums.full[...].astype(jnp.float32)
    for kind in (2, 3):
        ffn_copy(kind, True).wait_recv()
    for kind in range(4):
        ffn_copy(kind).wait_send()
    for sums in (q_sums, kv_sums, d_kv):
        sums.drain()


def finish(
    normed, d_q, tokens, d_hidden, gains, term, cos_table, sin_table, d_kv, wq_all, kvg_all, ffn
):
    fsdp_size, rows, width = wq_all.shape
    tok_rows = tokens.shape[0]
    low, dma = jnp.bfloat16, pltpu.SemaphoreType.DMA
    vmem, hbm = pl.BlockSpec(memory_space=pltpu.VMEM), pl.BlockSpec(memory_space=pl.ANY)
    return pl.pallas_call(
        functools.partial(finish_kernel, fsdp_size),
        out_shape=(
            jax.ShapeDtypeStruct((tok_rows, width), jnp.float32),
            jax.ShapeDtypeStruct((rows, width), jnp.float32),
            jax.ShapeDtypeStruct((rows, 384), jnp.float32),
            jax.ShapeDtypeStruct((4,) + ffn.shape, low),
        ),
        in_specs=[vmem] * 3 + [hbm] + [vmem] * 4 + [hbm] * 4,
        out_specs=(vmem, vmem, vmem, hbm),
        scratch_shapes=[
            pltpu.VMEM((2, rows, width), low),
            pltpu.VMEM((fsdp_size, rows, 384), low),
            pltpu.VMEM((tok_rows, 256), low),
            pltpu.VMEM((8, width), jnp.float32),
            pltpu.VMEM((128, width), jnp.float32),
            dma((3,)),
            dma((2, 4)),
        ]
        + collect_scratch(fsdp_size, rows, width)
        + collect_scratch(fsdp_size, rows, 384)
        + collect_scratch(fsdp_size, tok_rows, 256, False),
        compiler_params=pltpu.CompilerParams(
            collective_id=2, has_side_effects=True, vmem_limit_bytes=54 << 20
        ),
        cost_estimate=pl.CostEstimate(
            flops=100 * tok_rows * width * width, transcendentals=0, bytes_accessed=40 << 20
        ),
        name="finish",
    )(normed, d_q, tokens, d_hidden, gains, term, cos_table, sin_table, d_kv, wq_all, kvg_all, ffn)


def swap(value, step):
    copies = lax.axis_size("replica")
    return lax.ppermute(value, "replica", [(r, r ^ step) for r in range(copies)])


def pass_on(beside, across, got):
    half = got.shape[1]
    low, wide = jnp.bfloat16, jnp.float32
    got = got.astype(wide)
    across = jnp.concatenate([across[:half].astype(wide) + got[0], across[half:].astype(wide)])
    beside = jnp.concatenate([beside[:half].astype(wide), beside[half:].astype(wide) + got[1]])
    return beside.astype(low), across.astype(low)


def gather_shards(value):
    return lax.all_gather(value, "fsdp", axis=0, tiled=True)


def scatter_shards(value):
    return lax.psum_scatter(value, "fsdp", scatter_dimension=0, tiled=True)


def after(value, *others):
    return lax.optimization_barrier((value, others))[0]


def quarter(shard, copy_index):
    rows = shard.shape[0] // lax.axis_size("replica")
    return lax.dynamic_slice_in_dim(shard, copy_index * rows, rows, 0)


def shards(
    tokens,
    segments,
    positions,
    query_weight,
    key_weight,
    value_weight,
    output_weight,
    attn_gain,
    gate_weight,
    up_weight,
    down_weight,
    ffn_gain,
    grad_out,
):
    tok_rows, model_width = tokens.shape
    head_dim = key_weight.shape[1]
    fsdp_size = lax.axis_size("fsdp")
    fsdp_index = lax.axis_index("fsdp")
    copy_index = lax.axis_index("replica")
    copies = lax.axis_size("replica")
    low = jnp.bfloat16

    w_down = gather_shards(quarter(down_weight, copy_index))
    cos_table, sin_table = rope_tables(positions, head_dim)
    gain_columns = jnp.stack([attn_gain, ffn_gain], axis=1)
    queries, normed, gains, wq_all, w_out, kvg_all, kv_all = project(
        tokens,
        query_weight,
        output_weight,
        jnp.concatenate(
            [key_weight, value_weight, jnp.pad(gain_columns, ((0, 0), (0, 126)))], axis=1
        ),
        cos_table,
        sin_table,
    )
    w_out = w_out.reshape(model_width, model_width)
    kv_all = kv_all.reshape(fsdp_size * tok_rows, 2 * head_dim)
    gain_ffn = gains[1]
    inputs = tokens.astype(jnp.float32)
    key_width = max(GROUP_TOK, tok_rows)
    window_start = fsdp_index * tok_rows // key_width * key_width
    one_group = fsdp_size * tok_rows == key_width
    kv = kv_all if one_group else lax.dynamic_slice_in_dim(kv_all, window_start, key_width, 0)

    row_at = fsdp_index * tok_rows - window_start + jnp.arange(tok_rows, dtype=jnp.int32)
    lowest = jnp.where(positions < PROMPT, 0, row_at - (positions - PROMPT))
    w_gate = gather_shards(after(quarter(gate_weight.T, copy_index), normed))
    w_up = gather_shards(after(quarter(up_weight.T, copy_index), normed))
    mixed_rows, logs, grads = attend(
        queries, kv, jnp.broadcast_to(lowest[:, None], (tok_rows, 128)), after(grad_out, w_down)
    )

    hidden = inputs + matmul(mixed_rows, w_out)
    normed_ffn_full, inverse_ffn = norm_forward(hidden, gain_ffn)
    normed_ffn = normed_ffn_full.astype(low)

    x_all, activation, d_gate, d_up, *d_normed_parts = feed_forward(
        normed_ffn, grads, w_gate, w_up, w_down
    )
    own_part, *other_parts = d_normed_parts
    beside, across = pass_on(*other_parts)
    all_rows = copies * tok_rows
    x_all, grads = x_all.reshape(all_rows, -1), grads.reshape(all_rows, -1)
    activation = activation.reshape(all_rows, -1)
    d_gate = after(d_gate, beside, across)
    gate_part = contract(d_gate.reshape(all_rows, -1), x_all, 0, 0).astype(low)
    d_up, activation = after((d_up, activation), gate_part)
    d_normed_ffn = (
        own_part.astype(jnp.float32)
        + swap(beside, 1).astype(jnp.float32)
        + swap(across, 2).astype(jnp.float32)
    )
    up_part = contract(d_up.reshape(all_rows, -1), x_all, 0, 0).astype(low)
    down_part = contract(activation, grads, 0, 0).astype(low)
    out_parts = matmul(activation, w_down).astype(low)

    cotangent = grad_out.astype(jnp.float32)
    resid_ffn, ffn_gain_term = norm_backward(hidden, inverse_ffn, gain_ffn, d_normed_ffn)
    d_hidden = cotangent + resid_ffn
    d_branch = d_hidden.astype(low)
    d_mixed = contract(d_branch, w_out, 1, 1).astype(low)
    d_mixed = after(d_mixed, gate_part, up_part, down_part)
    gate_sum = scatter_shards(gate_part)
    up_sum = scatter_shards(up_part)
    down_sum = scatter_shards(down_part)
    own_out, *other_outs = jnp.split(after(out_parts, d_mixed), copies)
    other_outs = [swap(part, step + 1) for step, part in enumerate(other_outs)]
    d_query_raw, d_kv, output_grad = attend_back(
        queries,
        kv,
        cos_table,
        sin_table,
        jnp.broadcast_to(lowest[None, :], (8, tok_rows)),
        mixed_rows,
        d_mixed,
        logs,
        d_branch,
    )
    layer_out = hidden + own_out.astype(jnp.float32)
    for part in after(other_outs, d_kv):
        layer_out = layer_out + part.astype(jnp.float32)
    layer_out = layer_out.astype(low)
    if not one_group:
        d_kv = lax.dynamic_update_slice_in_dim(
            jnp.zeros((fsdp_size * tok_rows, 2 * head_dim), low), d_kv, window_start, 0
        )
    input_grad, query_grad, kv_grad, ffn_all = finish(
        normed,
        d_query_raw,
        tokens,
        d_hidden,
        gains,
        jnp.broadcast_to(ffn_gain_term[None], (8, model_width)),
        cos_table,
        sin_table,
        d_kv.reshape(fsdp_size, tok_rows, 2 * head_dim),
        wq_all,
        kvg_all,
        jnp.stack([gate_sum, up_sum, down_sum]),
    )
    gate_grad, up_grad, down_grad = (
        ffn_all[:, i].reshape(-1, model_width).astype(jnp.float32) for i in range(3)
    )
    return (
        layer_out,
        input_grad,
        query_grad,
        kv_grad[:, :head_dim],
        kv_grad[:, head_dim : 2 * head_dim],
        output_grad,
        kv_grad[:, 2 * head_dim],
        gate_grad.T,
        up_grad.T,
        down_grad,
        kv_grad[:, 2 * head_dim + 1],
    )


def half_tables(pos_ids, head_dim):
    half_width = head_dim // 2
    frequency = ROPE_BASE ** (-jnp.arange(half_width, dtype=jnp.float32) * 2.0 / head_dim)
    angles = pos_ids.astype(jnp.float32)[:, None] * frequency[None, :]
    return (jnp.cos(angles), jnp.sin(angles))


def rotate(values, cos_table, sin_table):
    half_width = values.shape[-1] // 2
    front_half = values[..., :half_width]
    back_half = values[..., half_width:]
    return jnp.concatenate(
        [
            front_half * cos_table - back_half * sin_table,
            back_half * cos_table + front_half * sin_table,
        ],
        axis=-1,
    )


def any_shards(
    tokens,
    segments,
    positions,
    query_weight,
    key_weight,
    value_weight,
    output_weight,
    attn_gain,
    gate_weight,
    up_weight,
    down_weight,
    ffn_gain,
    grad_out,
):
    tok_rows, model_width = tokens.shape
    head_dim = key_weight.shape[1]
    head_count = model_width // head_dim
    block_count = head_count // HEAD_BLOCK
    block_width = HEAD_BLOCK * head_dim
    score_scale = head_dim ** (-0.5)
    fsdp_size = lax.axis_size("fsdp")
    fsdp_index = lax.axis_index("fsdp")
    gathered = (
        lax.all_gather(query_weight, "fsdp", axis=0, tiled=True),
        lax.all_gather(key_weight, "fsdp", axis=0, tiled=True),
        lax.all_gather(value_weight, "fsdp", axis=0, tiled=True),
        lax.all_gather(output_weight, "fsdp", axis=0, tiled=True),
        lax.all_gather(attn_gain, "fsdp", axis=0, tiled=True),
        lax.all_gather(ffn_gain, "fsdp", axis=0, tiled=True),
    )
    w_query, w_key, w_value, w_out, gain_attn, gain_ffn = gathered
    gain_attn = gain_attn.astype(jnp.float32)
    gain_ffn = gain_ffn.astype(jnp.float32)
    inputs = tokens.astype(jnp.float32)
    normed_full, inverse_attn = norm_forward(inputs, gain_attn)
    normed = normed_full.astype(jnp.bfloat16)
    query_raw = matmul(normed, w_query)
    key_raw = matmul(normed, w_key)
    value_rows = matmul(normed, w_value).astype(jnp.bfloat16)
    cos_table, sin_table = half_tables(positions, head_dim)
    queries = rotate(
        query_raw.reshape(tok_rows, head_count, head_dim), cos_table[:, None], sin_table[:, None]
    ).astype(jnp.bfloat16)
    key_rot = rotate(key_raw, cos_table, sin_table).astype(jnp.bfloat16)
    key_rows, value_all = (
        lax.all_gather(key_rot, "fsdp", axis=0, tiled=True),
        lax.all_gather(value_rows, "fsdp", axis=0, tiled=True),
    )
    seg_all, pos_all = (
        lax.all_gather(segments, "fsdp", axis=0, tiled=True),
        lax.all_gather(positions, "fsdp", axis=0, tiled=True),
    )
    key_width = max(GROUP_TOK, tok_rows)
    window_start = fsdp_index * tok_rows // GROUP_TOK * GROUP_TOK
    key_window = lax.dynamic_slice_in_dim(key_rows, window_start, key_width, 0)
    value_window = lax.dynamic_slice_in_dim(value_all, window_start, key_width, 0)
    seg_window = lax.dynamic_slice_in_dim(seg_all, window_start, key_width, 0)
    pos_window = lax.dynamic_slice_in_dim(pos_all, window_start, key_width, 0)
    key_index = window_start + jnp.arange(key_width, dtype=jnp.int32)
    query_index = fsdp_index * tok_rows + jnp.arange(tok_rows, dtype=jnp.int32)
    visible = (
        (key_index[None, :] // GROUP_TOK == query_index[:, None] // GROUP_TOK)
        & (pos_window[None, :] <= positions[:, None])
        & ((seg_window[None, :] == 0) | (seg_window[None, :] == segments[:, None]))
    )
    query_blocks = queries.reshape(tok_rows, block_count, block_width).transpose(1, 0, 2)

    def block_scores(query_block):
        flat_queries = query_block.reshape(tok_rows * HEAD_BLOCK, head_dim)
        scores = (
            contract(flat_queries, key_window, 1, 1).reshape(tok_rows, HEAD_BLOCK, key_width)
            * score_scale
        )
        return (flat_queries, scores)

    def attend_block(query_block):
        flat_queries, scores = block_scores(query_block)
        scores = jnp.where(visible[:, None, :], scores, MASKED)
        row_max = jnp.max(scores, axis=-1, keepdims=True)
        exp_scores = jnp.exp(scores - row_max)
        totals = jnp.sum(exp_scores, axis=-1, keepdims=True)
        weights = (
            (exp_scores / totals).astype(jnp.bfloat16).reshape(tok_rows * HEAD_BLOCK, key_width)
        )
        mixed_block = matmul(weights, value_window).reshape(tok_rows, block_width)
        return (mixed_block, (row_max + jnp.log(totals))[..., 0])

    mixed_blocks, log_totals = lax.map(attend_block, query_blocks)
    mixed_rows = mixed_blocks.transpose(1, 0, 2).reshape(tok_rows, model_width).astype(jnp.bfloat16)
    hidden = inputs + matmul(mixed_rows, w_out)
    normed_ffn_full, inverse_ffn = norm_forward(hidden, gain_ffn)
    normed_ffn = normed_ffn_full.astype(jnp.bfloat16)
    cotangent = grad_out.astype(jnp.float32)
    w_gate, w_up, w_down = (
        lax.all_gather(gate_weight, "fsdp", axis=1, tiled=True),
        lax.all_gather(up_weight, "fsdp", axis=1, tiled=True),
        lax.all_gather(down_weight, "fsdp", axis=0, tiled=True),
    )
    gate_proj = matmul(normed_ffn, w_gate)
    up_proj = matmul(normed_ffn, w_up)
    activation = (jax.nn.silu(gate_proj) * up_proj).astype(jnp.bfloat16)
    layer_out = (hidden + matmul(activation, w_down)).astype(jnp.bfloat16)
    d_activation = contract(grad_out, w_down, 1, 1)
    d_gate, d_up = swiglu_back(d_activation, gate_proj, up_proj)
    d_normed_ffn = contract(d_gate, w_gate, 1, 1) + contract(d_up, w_up, 1, 1)
    gate_up_part = lax.psum_scatter(
        jnp.concatenate(
            [contract(d_gate, normed_ffn, 0, 0), contract(d_up, normed_ffn, 0, 0)], axis=1
        ).astype(jnp.bfloat16),
        "fsdp",
        scatter_dimension=0,
        tiled=True,
    ).astype(jnp.float32)
    gate_part = gate_up_part[:, :model_width].T
    up_part = gate_up_part[:, model_width:].T
    down_part = lax.psum_scatter(
        contract(activation, grad_out, 0, 0).astype(jnp.bfloat16),
        "fsdp",
        scatter_dimension=0,
        tiled=True,
    )
    resid_ffn, ffn_gain_term = norm_backward(hidden, inverse_ffn, gain_ffn, d_normed_ffn)
    d_hidden = cotangent + resid_ffn
    d_branch = d_hidden.astype(jnp.bfloat16)
    d_mixed = contract(d_branch, w_out, 1, 1).astype(jnp.bfloat16)
    d_mixed_blocks = d_mixed.reshape(tok_rows, block_count, block_width).transpose(1, 0, 2)

    def back_block(totals, block_items):
        query_block, d_block, log_block = block_items
        flat_queries, scores = block_scores(query_block)
        probs = jnp.where(visible[:, None, :], jnp.exp(scores - log_block[..., None]), 0.0)
        d_flat = d_block.reshape(tok_rows * HEAD_BLOCK, head_dim)
        d_probs = contract(d_flat, value_window, 1, 1).reshape(tok_rows, HEAD_BLOCK, key_width)
        row_delta = jnp.sum(probs * d_probs, axis=-1, keepdims=True)
        d_scores = (
            (probs * (d_probs - row_delta))
            .astype(jnp.bfloat16)
            .reshape(tok_rows * HEAD_BLOCK, key_width)
        )
        weights = probs.astype(jnp.bfloat16).reshape(tok_rows * HEAD_BLOCK, key_width)
        d_query_block = matmul(d_scores, key_window) * score_scale
        key_total = totals[0] + contract(d_scores, flat_queries, 0, 0) * score_scale
        value_total = totals[1] + contract(weights, d_flat, 0, 0)
        return ((key_total, value_total), d_query_block.reshape(tok_rows, block_width))

    zero_window = jnp.zeros((key_width, head_dim), jnp.float32)
    window_grads, d_query_blocks = lax.scan(
        back_block, (zero_window, zero_window), (query_blocks, d_mixed_blocks, log_totals)
    )
    d_queries = d_query_blocks.transpose(1, 0, 2).reshape(tok_rows, head_count, head_dim)
    d_query_raw = (
        rotate(d_queries, cos_table[:, None], -sin_table[:, None])
        .astype(jnp.bfloat16)
        .reshape(tok_rows, model_width)
    )
    row_zeros = jnp.zeros((fsdp_size * tok_rows, head_dim), jnp.float32)
    key_term = lax.dynamic_update_slice_in_dim(row_zeros, window_grads[0], window_start, 0)
    value_term = lax.dynamic_update_slice_in_dim(row_zeros, window_grads[1], window_start, 0)
    key_sum, value_sum = (
        lax.psum_scatter(
            key_term.astype(jnp.bfloat16), "fsdp", scatter_dimension=0, tiled=True
        ).astype(jnp.float32),
        lax.psum_scatter(
            value_term.astype(jnp.bfloat16), "fsdp", scatter_dimension=0, tiled=True
        ).astype(jnp.float32),
    )
    d_key_raw = rotate(key_sum, cos_table, -sin_table).astype(jnp.bfloat16)
    d_value = value_sum.astype(jnp.bfloat16)
    d_normed = (
        contract(d_query_raw, w_query, 1, 1)
        + contract(d_key_raw, w_key, 1, 1)
        + contract(d_value, w_value, 1, 1)
    )
    resid_attn, attn_gain_term = norm_backward(inputs, inverse_attn, gain_attn, d_normed)
    input_grad = d_hidden + resid_attn
    attn_part = lax.psum_scatter(
        jnp.concatenate(
            [
                contract(normed, d_query_raw, 0, 0),
                contract(normed, d_key_raw, 0, 0),
                contract(normed, d_value, 0, 0),
                contract(mixed_rows, d_branch, 0, 0),
            ],
            axis=1,
        ).astype(jnp.bfloat16),
        "fsdp",
        scatter_dimension=0,
        tiled=True,
    )
    attn_gain_part, ffn_gain_part = (
        lax.psum_scatter(attn_gain_term, "fsdp", scatter_dimension=0, tiled=True),
        lax.psum_scatter(ffn_gain_term, "fsdp", scatter_dimension=0, tiled=True),
    )
    summed = (
        lax.psum(attn_part, "replica").astype(jnp.float32),
        lax.psum(attn_gain_part.astype(jnp.bfloat16), "replica").astype(jnp.float32),
        lax.psum(ffn_gain_part.astype(jnp.bfloat16), "replica").astype(jnp.float32),
        lax.psum(gate_part.astype(jnp.bfloat16), "replica").astype(jnp.float32),
        lax.psum(up_part.astype(jnp.bfloat16), "replica").astype(jnp.float32),
        lax.psum(down_part, "replica").astype(jnp.float32),
    )
    attn_total, attn_gain_grad, ffn_gain_grad, gate_grad, up_grad, down_grad = summed
    query_grad = attn_total[:, :model_width]
    key_grad = attn_total[:, model_width : model_width + head_dim]
    value_grad = attn_total[:, model_width + head_dim : model_width + 2 * head_dim]
    output_grad = attn_total[:, model_width + 2 * head_dim :]
    return (
        layer_out,
        input_grad,
        query_grad,
        key_grad,
        value_grad,
        output_grad,
        attn_gain_grad,
        gate_grad,
        up_grad,
        down_grad,
        ffn_gain_grad,
    )


def suits(mesh):
    fsdp_size = mesh.shape["fsdp"]
    return mesh.shape["replica"] == 4 and fsdp_size % 2 == 0 and 2048 % (128 * fsdp_size) == 0


def solution(mesh):
    return jax.shard_map(
        shards if suits(mesh) else any_shards,
        mesh=mesh,
        in_specs=(
            P(("replica", "fsdp"), None),
            P(("replica", "fsdp")),
            P(("replica", "fsdp")),
            P("fsdp", None),
            P("fsdp", None),
            P("fsdp", None),
            P("fsdp", None),
            P("fsdp"),
            P(None, "fsdp"),
            P(None, "fsdp"),
            P("fsdp", None),
            P("fsdp"),
            P(("replica", "fsdp"), None),
        ),
        out_specs=(
            P(("replica", "fsdp"), None),
            P(("replica", "fsdp"), None),
            P("fsdp", None),
            P("fsdp", None),
            P("fsdp", None),
            P("fsdp", None),
            P("fsdp"),
            P(None, "fsdp"),
            P(None, "fsdp"),
            P("fsdp", None),
            P("fsdp"),
        ),
        check_vma=False,
    )
```

```python
import functools

import jax
import jax.numpy as jnp
from jax import lax
from jax.experimental import pallas as pl
from jax.experimental.pallas import tpu as pltpu
from jax.sharding import PartitionSpec as P

GROUP_TOK = 4096
PROMPT = 2048
MAX_CONT = 384
EPSILON = 1e-05
ROPE_BASE = 10000.0
MASKED = -1e30
LOG2E = 1.4426950408889634

TILE = 128
CHUNK = 512
HEAD_GROUP = 4
FFN_ROWS = 256
HEAD_BLOCK = 4


def matmul(left, right):
    return jnp.dot(left, right, preferred_element_type=jnp.float32)


def contract(left, right, left_dim, right_dim):
    return lax.dot_general(
        left, right, (((left_dim,), (right_dim,)), ((), ())), preferred_element_type=jnp.float32
    )


def rope_tables(pos_ids, head_dim):
    half_width = head_dim // 2
    frequency = ROPE_BASE ** (-jnp.arange(half_width, dtype=jnp.float32) * 2.0 / head_dim)
    angles = pos_ids.astype(jnp.float32)[:, None] * frequency[None, :]
    cos_half, sin_half = jnp.cos(angles), jnp.sin(angles)
    return (
        jnp.concatenate([cos_half, cos_half], axis=1),
        jnp.concatenate([-sin_half, sin_half], axis=1),
    )


def swap_halves(values):
    half_width = values.shape[-1] // 2
    return jnp.concatenate([values[..., half_width:], values[..., :half_width]], axis=-1)


def norm_forward(values, gain):
    inverse = lax.rsqrt(jnp.mean(values * values, axis=-1, keepdims=True) + EPSILON)
    return (values * inverse * gain, inverse)


def norm_backward(values, inverse, gain, grad):
    scaled = grad * gain
    inner_mean = jnp.mean(scaled * values, axis=-1, keepdims=True)
    return (
        inverse * scaled - values * inverse**3 * inner_mean,
        jnp.sum(grad * values * inverse, axis=0),
    )


def swiglu_back(d_activation, gate_proj, up_proj):
    sigmoid_gate = jax.nn.sigmoid(gate_proj)
    d_gate = (
        d_activation * up_proj * sigmoid_gate * (1.0 + gate_proj * (1.0 - sigmoid_gate))
    ).astype(jnp.bfloat16)
    d_up = (d_activation * gate_proj * sigmoid_gate).astype(jnp.bfloat16)
    return (d_gate, d_up)


MESH = pl.DeviceIdType.MESH


def flip(index, bit):
    return index + bit - 2 * bit * (index // bit % 2)


class Exchange:
    def __init__(self, source, buffer, sems):
        self.replica, self.fsdp = lax.axis_index("replica"), lax.axis_index("fsdp")
        self.source, self.buffer, self.sems = source, buffer, sems
        self.beside, self.across = flip(self.replica, 1), flip(self.replica, 2)
        self.half = buffer.shape[1] // 2

    def greet(self):
        barrier = pltpu.get_barrier_semaphore()
        for target in (self.beside, self.across):
            pl.semaphore_signal(
                barrier, inc=1, device_id=(target, self.fsdp), device_id_type=MESH
            )
        pl.semaphore_wait(barrier, 2)

    def copy(self, kind):
        first, second = pl.ds(0, self.half), pl.ds(self.half, self.half)
        source, dest, target = (
            (self.source, self.buffer.at[1], self.beside),
            (self.source, self.buffer.at[2], self.across),
            (self.buffer.at[1, first], self.buffer.at[3, first], self.across),
            (self.buffer.at[2, second], self.buffer.at[3, second], self.beside),
        )[kind]
        return pltpu.make_async_remote_copy(
            src_ref=source,
            dst_ref=dest,
            send_sem=self.sems.at[0, kind],
            recv_sem=self.sems.at[1, kind],
            device_id=(target, self.fsdp),
            device_id_type=MESH,
        )

    def begin(self):
        self.copy(0).start()
        self.copy(1).start()

    def relay(self):
        self.copy(0).wait_recv()
        self.copy(2).start()
        self.copy(1).wait_recv()
        self.copy(3).start()

    def end(self):
        self.copy(2).wait_recv()
        self.copy(3).wait_recv()

    def drain(self):
        for kind in range(4):
            self.copy(kind).wait_send()


def ffn_kernel(
    x_ref,
    grads_ref,
    gate_ref,
    up_ref,
    down_ref,
    x_all,
    act_all,
    d_gate_all,
    d_up_all,
    d_x_own,
    d_x_beside,
    d_x_across,
    d_x_got,
    out_own,
    out_beside,
    out_across,
    out_got,
    gate_w,
    up_w,
    down_w,
    block,
    d_act,
    act,
    d_gate,
    d_up,
    d_x,
    out,
    out_far,
    load_sems,
    store_sems,
    x_sems,
    far_sems,
):
    exchange = Exchange(x_ref, x_all, x_sems)
    exchange.greet()
    exchange.begin()
    loads = [
        pltpu.make_async_copy(src, dst, load_sems.at[1 + i])
        for i, (src, dst) in enumerate(
            ((down_ref, down_w), (gate_ref, gate_w), (up_ref, up_w))
        )
    ]
    for load in loads:
        load.start()

    def fetch(source, at, slot):
        return pltpu.make_async_copy(source.at[at], block.at[slot], load_sems.at[4 + slot])

    fetch(grads_ref, 0, 0).start()
    loads[0].wait()
    rows = d_act.shape[1]
    parts = rows // FFN_ROWS
    for at in range(4):
        fetch(grads_ref, at, at % 2).wait()
        if at < 3:
            fetch(grads_ref, at + 1, (at + 1) % 2).start()

        @pl.loop(0, parts)
        def _(part, at=at):
            some = pl.ds(pl.multiple_of(part * FFN_ROWS, FFN_ROWS), FFN_ROWS)
            d_act[at, some] = contract(block[at % 2, some], down_w[...], 1, 1).astype(jnp.bfloat16)

    loads[1].wait()
    loads[2].wait()

    def stores(at):
        pairs = [(act, act_all.at[at]), (d_gate, d_gate_all.at[at]), (d_up, d_up_all.at[at])]
        if at < 3:
            pairs.append((d_x, (d_x_own, d_x_beside, d_x_across)[at]))
            pairs.append((out, (out_own, out_beside, out_across)[at]))
        return [
            pltpu.make_async_copy(src, dst, store_sems.at[i])
            for i, (src, dst) in enumerate(pairs)
        ]

    def far(kind):
        size, half = rows // 2, kind % 2
        source = block.at[1] if kind < 2 else out_far
        return pltpu.make_async_remote_copy(
            src_ref=source.at[pl.ds(half * size, size)],
            dst_ref=(d_x_got if kind < 2 else out_got).at[half],
            send_sem=far_sems.at[0, kind],
            recv_sem=far_sems.at[1, kind],
            device_id=((exchange.beside, exchange.across)[half], exchange.fsdp),
            device_id_type=MESH,
        )

    order = (0, 1, 3, 2)
    for turn, at in enumerate(order):
        if at == 1:
            exchange.relay()
        if at == 3:
            exchange.end()
        load = (
            fetch(x_all, at, 0)
            if at
            else pltpu.make_async_copy(x_ref, block.at[0], load_sems.at[0])
        )
        load.start()
        load.wait()
        if at == 0:
            keep = pltpu.make_async_copy(block.at[0], x_all.at[0], load_sems.at[0])
            keep.start()
        if turn > 0:
            for store in stores(order[turn - 1]):
                store.wait()

        @pl.loop(0, parts)
        def _(part, at=at):
            some = pl.ds(pl.multiple_of(part * FFN_ROWS, FFN_ROWS), FFN_ROWS)
            x = block[0, some]
            gate = contract(x, gate_w[...], 1, 1)
            up = contract(x, up_w[...], 1, 1)
            slope = jax.nn.sigmoid(gate)
            d = d_act[at, some].astype(jnp.float32)
            swish = gate * slope
            act[some] = (swish * up).astype(jnp.bfloat16)
            by_gate = (d * up * (slope + swish * (1.0 - slope))).astype(jnp.bfloat16)
            by_up = (d * swish).astype(jnp.bfloat16)
            d_gate[some] = by_gate
            d_up[some] = by_up
            (out_far if at == 3 else out)[some] = matmul(act[some], down_w[...]).astype(
                jnp.bfloat16
            )
            (block.at[1] if at == 3 else d_x)[some] = (
                matmul(by_gate, gate_w[...]) + matmul(by_up, up_w[...])
            ).astype(jnp.bfloat16)

        for store in stores(at):
            store.start()
        if at == 0:
            keep.wait()
        if at == 3:
            for kind in range(4):
                far(kind).start()
    for store in stores(order[3]):
        store.wait()
    for kind in range(4):
        far(kind).wait()
    exchange.drain()


def feed_forward(x, grads, w_gate, w_up, w_down):
    rows, width = x.shape
    hidden = w_gate.shape[0]
    low, dma = jnp.bfloat16, pltpu.SemaphoreType.DMA
    hbm = pl.BlockSpec(memory_space=pl.ANY)
    block = jax.ShapeDtypeStruct((rows, width), low)
    halves = jax.ShapeDtypeStruct((2, rows // 2, width), low)
    wide = jax.ShapeDtypeStruct((4, rows, width), low)
    thin = jax.ShapeDtypeStruct((4, rows, hidden), low)
    return pl.pallas_call(
        ffn_kernel,
        out_shape=(wide, thin, thin, thin, block, block, block, halves, block, block, block, halves),
        in_specs=[hbm] * 5,
        out_specs=(hbm,) * 12,
        scratch_shapes=[pltpu.VMEM((hidden, width), low)] * 3
        + [
            pltpu.VMEM((2, rows, width), low),
            pltpu.VMEM((4, rows, hidden), low),
            pltpu.VMEM((rows, hidden), low),
            pltpu.VMEM((rows, hidden), low),
            pltpu.VMEM((rows, hidden), low),
            pltpu.VMEM((rows, width), low),
            pltpu.VMEM((rows, width), low),
            pltpu.VMEM((rows, width), low),
            dma((6,)),
            dma((5,)),
            dma((2, 4)),
            dma((2, 4)),
        ],
        compiler_params=pltpu.CompilerParams(
            collective_id=3, has_side_effects=True, vmem_limit_bytes=50 << 20
        ),
        cost_estimate=pl.CostEstimate(
            flops=40 * rows * width * hidden, transcendentals=0, bytes_accessed=40 << 20
        ),
        name="feed_forward",
    )(x, grads, w_gate, w_up, w_down)


def stack_heads(block):
    heads = block.shape[1] // 128
    return jnp.concatenate([block[:, h * 128 : (h + 1) * 128] for h in range(heads)], axis=0)


def chunk_plan(tok_rows):
    first = lax.axis_index("fsdp") * tok_rows % GROUP_TOK + pl.program_id(0) * TILE
    in_prompt = first < PROMPT
    full = jnp.where(in_prompt, first // CHUNK, PROMPT // CHUNK)
    last = jnp.where(
        in_prompt, first // CHUNK * CHUNK, jnp.maximum(PROMPT, first + TILE - CHUNK)
    )
    return first, full, pl.multiple_of(last, TILE)


def attend_kernel(
    tok_rows,
    q_ref,
    kv_ref,
    low_ref,
    grads_ref,
    mixed_ref,
    log_ref,
    grads_all,
    values,
    top,
    acc,
    own_rows,
    sems,
    own_sem,
):
    factor = 128**-0.5 * LOG2E

    exchange = Exchange(grads_ref, grads_all, sems)
    load_own = pltpu.make_async_copy(grads_ref, own_rows, own_sem)
    keep_own = pltpu.make_async_copy(own_rows, grads_all.at[0], own_sem)

    @pl.when((pl.program_id(0) == 0) & (pl.program_id(1) == 0))
    def _():
        load_own.start()
        exchange.greet()
        exchange.begin()
        load_own.wait()
        keep_own.start()
        values[:, :128] = kv_ref[:, 128:]
        values[:, 128:] = jnp.ones_like(values[:, 128:])

    @pl.when((pl.program_id(0) == pl.num_programs(0) // 2) & (pl.program_id(1) == 0))
    def _():
        exchange.relay()

    first, full, last = chunk_plan(tok_rows)
    queries = stack_heads(q_ref[...])
    rows = queries.shape[0]
    top[...] = jnp.full_like(top, MASKED)
    acc[...] = jnp.zeros_like(acc)

    def step(start, masked):
        scores = contract(queries, kv_ref[pl.ds(start, CHUNK), :128], 1, 1) * factor
        if masked:
            key_at = start + lax.broadcasted_iota(jnp.int32, (rows, CHUNK), 1)
            row_at = lax.broadcasted_iota(jnp.int32, (rows, 1), 0) % TILE + first
            low = jnp.concatenate([low_ref[:, :1]] * HEAD_GROUP, axis=0)
            scores = jnp.where((key_at <= row_at) & (key_at >= low), scores, MASKED)
        before = top[:, :1]
        after = jnp.maximum(before, jnp.max(scores, axis=1, keepdims=True))
        weights = jnp.exp2(scores - after).astype(jnp.bfloat16)
        acc[...] = acc[...] * jnp.exp2(before - after) + matmul(
            weights, values[pl.ds(start, CHUNK), :]
        )
        top[...] = jnp.broadcast_to(after, top.shape)

    @pl.loop(0, full)
    def _(at):
        step(pl.multiple_of(at * CHUNK, CHUNK), False)

    step(last, True)
    total = acc[:, 128:]
    mixed = acc[:, :128] / total
    for h in range(HEAD_GROUP):
        mixed_ref[:, h * 128 : (h + 1) * 128] = mixed[h * TILE : (h + 1) * TILE].astype(jnp.bfloat16)
    log_ref[0, 0] = (top[...] + jnp.log2(total)).T[:8]

    @pl.when(
        (pl.program_id(0) == pl.num_programs(0) - 1) & (pl.program_id(1) == pl.num_programs(1) - 1)
    )
    def _():
        keep_own.wait()
        exchange.end()
        exchange.drain()


def attend(queries, kv, low, grads):
    tok_rows, width = queries.shape
    tiles, groups = tok_rows // TILE, width // (128 * HEAD_GROUP)
    lanes, rows = 128 * HEAD_GROUP, TILE * HEAD_GROUP
    tile_spec = pl.BlockSpec((TILE, lanes), lambda i, g: (i, g))
    hbm = pl.BlockSpec(memory_space=pl.ANY)
    pairs = tok_rows * (width // 128) * 2560
    return pl.pallas_call(
        functools.partial(attend_kernel, tok_rows),
        out_shape=(
            jax.ShapeDtypeStruct((tok_rows, width), jnp.bfloat16),
            jax.ShapeDtypeStruct((tiles, groups, 8, rows), jnp.float32),
            jax.ShapeDtypeStruct((4,) + grads.shape, jnp.bfloat16),
        ),
        grid=(tiles, groups),
        in_specs=[
            tile_spec,
            pl.BlockSpec(kv.shape, lambda i, g: (0, 0)),
            pl.BlockSpec((TILE, 128), lambda i, g: (i, 0)),
            hbm,
        ],
        out_specs=[
            tile_spec,
            pl.BlockSpec((1, 1, 8, rows), lambda i, g: (i, g, 0, 0)),
            hbm,
        ],
        scratch_shapes=[
            pltpu.VMEM(kv.shape, jnp.bfloat16),
            pltpu.VMEM((rows, 128), jnp.float32),
            pltpu.VMEM((rows, 256), jnp.float32),
            pltpu.VMEM(grads.shape, jnp.bfloat16),
            pltpu.SemaphoreType.DMA((2, 4)),
            pltpu.SemaphoreType.DMA,
        ],
        compiler_params=pltpu.CompilerParams(
            collective_id=4, has_side_effects=True, vmem_limit_bytes=40 << 20
        ),
        cost_estimate=pl.CostEstimate(
            flops=pairs * 3000, transcendentals=pairs, bytes_accessed=16 << 20
        ),
        name="attend",
    )(queries, kv, low, grads)


def attend_back_kernel(
    fsdp_size,
    tok_rows,
    q_ref,
    kv_ref,
    cos_ref,
    sin_ref,
    low_ref,
    mixed_ref,
    d_mixed_ref,
    log_ref,
    rows_ref,
    branch_ref,
    d_q_ref,
    d_kv_ref,
    output_ref,
    sums,
    d_q,
    *refs,
):
    scale = 128**-0.5
    factor = scale * LOG2E
    at_end = (pl.program_id(0) == pl.num_programs(0) - 1) & (
        pl.program_id(1) == pl.num_programs(1) - 1
    )

    place = position(fsdp_size)
    grad = make_collect(place, refs)
    count = place[4]

    def begin():
        sums[...] = jnp.zeros_like(sums)
        greet(*place[:3], count)
        outer(grad, rows_ref, branch_ref, False)
        outer(grad, rows_ref, branch_ref, True)

    def cores():
        for shard in range(count):
            grad.core_add(shard)
            grad.diag_start(shard)

    def sum_quarters():
        each(count, grad.quarter_add)
        grad.line_hop(count - 1)

    def hops():
        for hop in range(count - 2, 0, -1):
            grad.line_hop(hop)

    def gather():
        grad.line_end()
        grad.gather_start()

    stages = {
        0: begin,
        1: cores,
        5: lambda: each(count, grad.quarter_start),
        10: sum_quarters,
        11: hops,
        12: gather,
        14: grad.gather_relay,
    }
    now = pl.program_id(0) * pl.num_programs(1) + pl.program_id(1)
    for step_at, stage in stages.items():
        pl.when(now == step_at)(stage)

    first, full, last = chunk_plan(tok_rows)
    queries = stack_heads(q_ref[...])
    d_rows = stack_heads(d_mixed_ref[...])
    mixed = stack_heads(mixed_ref[...])
    rows = queries.shape[0]
    products = d_rows.astype(jnp.float32) * mixed.astype(jnp.float32)
    delta = jnp.sum(products.T, axis=0, keepdims=True)
    log_total = log_ref[0, 0, :1]
    d_q[...] = jnp.zeros_like(d_q)

    def step(start, masked):
        keys = kv_ref[pl.ds(start, CHUNK), :128]
        values = kv_ref[pl.ds(start, CHUNK), 128:]
        scores = contract(keys, queries, 1, 1) * factor
        probs = jnp.exp2(scores - log_total)
        if masked:
            key_at = start + lax.broadcasted_iota(jnp.int32, (CHUNK, rows), 0)
            row_at = lax.broadcasted_iota(jnp.int32, (1, rows), 1) % TILE + first
            low = jnp.concatenate([low_ref[:1]] * HEAD_GROUP, axis=1)
            probs = jnp.where((key_at <= row_at) & (key_at >= low), probs, 0.0)
        d_probs = contract(values, d_rows, 1, 1)
        d_scores = (probs * (d_probs - delta)).astype(jnp.bfloat16)
        sums[pl.ds(start, CHUNK), 128:] += matmul(probs.astype(jnp.bfloat16), d_rows)
        sums[pl.ds(start, CHUNK), :128] += matmul(d_scores, queries)
        d_q[...] += contract(d_scores, keys, 0, 0)

    @pl.loop(0, full)
    def _(at):
        step(pl.multiple_of(at * CHUNK, CHUNK), False)

    step(last, True)
    cos_table, sin_table = cos_ref[...] * scale, sin_ref[...] * scale
    for h in range(HEAD_GROUP):
        turned = d_q[h * TILE : (h + 1) * TILE]
        raw = turned * cos_table - pltpu.roll(turned, 64, 1) * sin_table
        d_q_ref[:, h * 128 : (h + 1) * 128] = raw.astype(jnp.bfloat16)

    @pl.when(at_end)
    def _():
        d_kv_ref[:, :128] = (sums[:, :128] * scale).astype(jnp.bfloat16)
        d_kv_ref[:, 128:] = sums[:, 128:].astype(jnp.bfloat16)
        grad.gather_end()
        output_ref[...] = grad.full[...].astype(jnp.float32)
        grad.drain()


def attend_back(queries, kv, cos_table, sin_table, low, mixed, d_mixed, logs, d_branch):
    tok_rows, width = queries.shape
    fsdp_size = lax.axis_size("fsdp")
    shard = width // fsdp_size
    tiles, groups = tok_rows // TILE, width // (128 * HEAD_GROUP)
    lanes, rows = 128 * HEAD_GROUP, TILE * HEAD_GROUP
    tile_spec = pl.BlockSpec((TILE, lanes), lambda i, g: (i, g))
    row_spec = pl.BlockSpec((TILE, 128), lambda i, g: (i, 0))
    whole = pl.BlockSpec(kv.shape, lambda i, g: (0, 0))
    pairs = tok_rows * (width // 128) * 2560
    return pl.pallas_call(
        functools.partial(attend_back_kernel, fsdp_size, tok_rows),
        out_shape=(
            jax.ShapeDtypeStruct((tok_rows, width), jnp.bfloat16),
            jax.ShapeDtypeStruct(kv.shape, jnp.bfloat16),
            jax.ShapeDtypeStruct((shard, width), jnp.float32),
        ),
        grid=(tiles, groups),
        in_specs=[
            tile_spec,
            whole,
            row_spec,
            row_spec,
            pl.BlockSpec((8, TILE), lambda i, g: (0, i)),
            tile_spec,
            tile_spec,
            pl.BlockSpec((1, 1, 8, rows), lambda i, g: (i, g, 0, 0)),
            pl.BlockSpec(mixed.shape, lambda i, g: (0, 0)),
            pl.BlockSpec(mixed.shape, lambda i, g: (0, 0)),
        ],
        out_specs=[tile_spec, whole, pl.BlockSpec((shard, width), lambda i, g: (0, 0))],
        scratch_shapes=[
            pltpu.VMEM(kv.shape, jnp.float32),
            pltpu.VMEM((rows, 128), jnp.float32),
        ]
        + collect_scratch(fsdp_size, shard, width),
        compiler_params=pltpu.CompilerParams(
            collective_id=1, has_side_effects=True, vmem_limit_bytes=50 << 20
        ),
        cost_estimate=pl.CostEstimate(
            flops=pairs * 3000, transcendentals=pairs, bytes_accessed=16 << 20
        ),
        name="attend_back",
    )(queries, kv, cos_table, sin_table, low, mixed, d_mixed, logs, mixed, d_branch)


class Chain:
    def __init__(self, place, count, at, replica, fsdp, sends, recvs):
        self.place, self.count, self.at = place, count, at
        self.replica, self.fsdp, self.sends, self.recvs = replica, fsdp, sends, recvs

    def copy(self, shard, way):
        target = self.fsdp + (2 if way == 0 else -2)
        return pltpu.make_async_remote_copy(
            src_ref=self.place(shard),
            dst_ref=self.place(shard),
            send_sem=self.sends.at[way, shard],
            recv_sem=self.recvs.at[way, shard],
            device_id=(self.replica, target),
            device_id_type=MESH,
        )

    def begin(self):
        @pl.when(self.at < self.count - 1)
        def _():
            self.copy(self.at, 0).start()

        @pl.when(self.at > 0)
        def _():
            self.copy(self.at, 1).start()

    def step(self, hop, arrived=None):
        left, right = self.at - hop, self.at + hop

        @pl.when(left >= 0)
        def _():
            self.copy(left, 0).wait_recv()

        @pl.when((left >= 0) & (self.at < self.count - 1))
        def _():
            self.copy(left, 0).start()

        if arrived is not None:

            @pl.when(left >= 0)
            def _():
                arrived(left)

        @pl.when(right < self.count)
        def _():
            self.copy(right, 1).wait_recv()

        @pl.when((right < self.count) & (self.at > 0))
        def _():
            self.copy(right, 1).start()

        if arrived is not None:

            @pl.when(right < self.count)
            def _():
                arrived(right)

    def finish(self):
        for hop in range(self.count):

            @pl.when((self.at - hop >= 0) & (self.at < self.count - 1))
            def _(hop=hop):
                self.copy(self.at - hop, 0).wait_send()

            @pl.when((self.at + hop < self.count) & (self.at > 0))
            def _(hop=hop):
                self.copy(self.at + hop, 1).wait_send()


class Spread:
    def __init__(self, buffer, count, at, core, replica, fsdp, sems):
        self.buffer, self.count, self.at, self.core = buffer, count, at, core
        self.replica, self.fsdp, self.sems = replica, fsdp, sems
        self.rows = buffer.shape[1] // 4

    def rows_of(self, shard, copy, half=None):
        start, size = copy * self.rows, self.rows
        if half is not None:
            size = size // 2
            start = start + half * size
        return self.buffer.at[2 * shard + self.core, pl.ds(start, size)]

    def copy(self, kind, shard):
        beside, across = flip(self.replica, 1), flip(self.replica, 2)
        if kind == 0:
            ref, target = self.rows_of(shard, self.replica), (beside, self.fsdp)
        elif kind == 1:
            ref, target = self.rows_of(shard, self.replica), (across, self.fsdp)
        elif kind == 2:
            ref, target = self.rows_of(shard, beside, 0), (across, self.fsdp)
        elif kind == 3:
            ref, target = self.rows_of(shard, across, 1), (beside, self.fsdp)
        else:
            ref, target = self.buffer.at[2 * shard + self.core], (self.replica, flip(self.fsdp, 1))
        return pltpu.make_async_remote_copy(
            src_ref=ref,
            dst_ref=ref,
            send_sem=self.sems.at[0, kind, shard],
            recv_sem=self.sems.at[1, kind, shard],
            device_id=target,
            device_id_type=MESH,
        )

    def recv(self, kind, shard):
        beside, across = flip(self.replica, 1), flip(self.replica, 2)
        if kind == 0:
            ref = self.rows_of(shard, beside)
        elif kind == 1:
            ref = self.rows_of(shard, across)
        elif kind < 4:
            ref = self.rows_of(shard, flip(beside, 2), kind - 2)
        else:
            ref = self.buffer.at[2 * shard + 1 - self.core]
        return pltpu.make_async_remote_copy(
            src_ref=ref,
            dst_ref=ref,
            send_sem=self.sems.at[0, kind, shard],
            recv_sem=self.sems.at[1, kind, shard],
            device_id=(self.replica, flip(self.fsdp, 1)),
            device_id_type=MESH,
        )

    def arrived(self, shard):
        self.copy(0, shard).start()
        self.copy(1, shard).start()

    def others(self):
        return [(self.at + hop) % self.count for hop in range(1, self.count)]

    def relay(self):
        for shard in self.others():
            self.recv(0, shard).wait_recv()
            self.copy(2, shard).start()
            self.recv(1, shard).wait_recv()
            self.copy(3, shard).start()

    def cores(self):
        self.copy(4, self.at).start()
        for shard in self.others():
            self.recv(2, shard).wait_recv()
            self.recv(3, shard).wait_recv()
            self.copy(4, shard).start()

    def finish(self):
        for shard in self.others() + [self.at]:
            self.recv(4, shard).wait_recv()
        for shard in self.others():
            for kind in range(5):
                self.copy(kind, shard).wait_send()
        self.copy(4, self.at).wait_send()


def project_kernel(
    fsdp_size,
    tokens_ref,
    wq_ref,
    wo_ref,
    kvg_ref,
    cos_ref,
    sin_ref,
    q_ref,
    normed_ref,
    gain_ref,
    wq_all,
    wo_all,
    kvg_all,
    kv_all,
    wq_vmem,
    kvg_vmem,
    kv_vmem,
    local_sems,
    kvg_sems,
    kvg_core,
    wq_line,
    wq_sems,
    wo_line,
    wo_sems,
    kv_sems,
    kv_core,
):
    replica, fsdp = lax.axis_index("replica"), lax.axis_index("fsdp")
    count, at, core = fsdp_size // 2, fsdp // 2, fsdp % 2
    width = tokens_ref.shape[1]
    partner = (replica, flip(fsdp, 1))

    spare = flip(fsdp, 1)
    load_own = [
        pltpu.make_async_copy(kvg_ref, kvg_vmem.at[fsdp], local_sems.at[0]),
        pltpu.make_async_copy(wq_ref, wq_vmem.at[fsdp], local_sems.at[1]),
        pltpu.make_async_copy(wo_ref, wq_vmem.at[spare], local_sems.at[2]),
    ]
    own = [
        pltpu.make_async_copy(kvg_vmem.at[fsdp], kvg_all.at[fsdp], local_sems.at[0]),
        pltpu.make_async_copy(wq_vmem.at[fsdp], wq_all.at[fsdp], local_sems.at[1]),
        pltpu.make_async_copy(wq_vmem.at[spare], wo_all.at[fsdp], local_sems.at[2]),
    ]
    for copy in load_own:
        copy.start()
    for load, copy in zip(load_own, own):
        load.wait()
        copy.start()
    greet(replica, fsdp, at, count)

    def core_copy(buffer, sems, shard, lands=False):
        ref = buffer.at[2 * shard + (1 - core if lands else core)]
        return pltpu.make_async_remote_copy(
            src_ref=ref,
            dst_ref=ref,
            send_sem=sems.at[0, shard],
            recv_sem=sems.at[1, shard],
            device_id=partner,
            device_id_type=MESH,
        )

    def line(place, sems):
        return Chain(place, count, at, replica, fsdp, sems.at[0], sems.at[1])

    kvg = line(lambda shard: kvg_all.at[2 * shard + core], kvg_sems)
    kv = line(lambda shard: kv_all.at[2 * shard + core], kv_sems)
    wq = Spread(wq_all, count, at, core, replica, fsdp, wq_sems)
    wo = Spread(wo_all, count, at, core, replica, fsdp, wo_sems)
    wq_chain = line(lambda shard: wq.rows_of(shard, replica), wq_line)
    wo_chain = line(lambda shard: wo.rows_of(shard, replica), wo_line)
    own[0].wait()
    kvg.begin()
    core_copy(kvg_all, kvg_core, at).start()
    own[1].wait()
    wq_chain.begin()
    own[2].wait()
    wo_chain.begin()

    inputs = tokens_ref[...].astype(jnp.float32)
    inverse = lax.rsqrt(jnp.mean(inputs * inputs, axis=1, keepdims=True) + EPSILON)

    for hop in range(1, count):
        kvg.step(hop, lambda shard: core_copy(kvg_all, kvg_core, shard).start())
        wq_chain.step(hop, wq.arrived)
        wo_chain.step(hop, wo.arrived)
    for shard in range(count):
        core_copy(kvg_all, kvg_core, shard, True).wait_recv()
    load = pltpu.make_async_copy(kvg_all, kvg_vmem, local_sems.at[0])
    load.start()
    load.wait()
    table = kvg_vmem[...].reshape(width, kvg_vmem.shape[2])
    gains = table[:, 256:].astype(jnp.float32).T[:8]
    gain_ref[...] = gains
    normed_ref[...] = (inputs * inverse * gains[:1]).astype(jnp.bfloat16)
    kv_raw = matmul(normed_ref[...], table[:, :256])
    cos_table, sin_table = cos_ref[...], sin_ref[...]
    key_raw = kv_raw[:, :128]
    key_rot = key_raw * cos_table + pltpu.roll(key_raw, 64, 1) * sin_table
    kv_vmem[:, :128] = key_rot.astype(jnp.bfloat16)
    kv_vmem[:, 128:] = kv_raw[:, 128:].astype(jnp.bfloat16)
    store = pltpu.make_async_copy(kv_vmem, kv_all.at[fsdp], local_sems.at[0])
    store.start()
    store.wait()
    kv.begin()
    core_copy(kv_all, kv_core, at).start()
    wq.relay()
    kv.step(1, lambda shard: core_copy(kv_all, kv_core, shard).start())
    wq.cores()
    wo.relay()
    for shard in wq.others() + [at]:
        wq.recv(4, shard).wait_recv()
    load = pltpu.make_async_copy(wq_all, wq_vmem, local_sems.at[1])
    load.start()
    for hop in range(2, count):
        kv.step(hop, lambda shard: core_copy(kv_all, kv_core, shard).start())
    load.wait()
    weight = wq_vmem.reshape(width, width)

    def columns(block):
        start = pl.multiple_of(block * 512, 512)
        raw = matmul(normed_ref[...], weight[:, pl.ds(start, 512)])
        for h in range(4):
            head = raw[:, h * 128 : (h + 1) * 128]
            turned = head * cos_table + pltpu.roll(head, 64, 1) * sin_table
            q_ref[:, pl.ds(start + h * 128, 128)] = turned.astype(jnp.bfloat16)

    pl.loop(0, width // 512)(columns)
    wo.cores()
    for shard in range(count):
        core_copy(kv_all, kv_core, shard, True).wait_recv()
    wo.finish()
    for shard in wq.others():
        for kind in range(5):
            wq.copy(kind, shard).wait_send()
    wq.copy(4, at).wait_send()
    for shard in range(count):
        core_copy(kvg_all, kvg_core, shard).wait_send()
        core_copy(kv_all, kv_core, shard).wait_send()
    for chain in (kvg, kv, wq_chain, wo_chain):
        chain.finish()


def project(tokens, wq, wo, kvg, cos_table, sin_table):
    rows, width = tokens.shape
    shard = wq.shape[0]
    fsdp_size = lax.axis_size("fsdp")
    count = fsdp_size // 2
    low = jnp.bfloat16
    vmem, hbm = pl.BlockSpec(memory_space=pltpu.VMEM), pl.BlockSpec(memory_space=pl.ANY)
    dma = pltpu.SemaphoreType.DMA
    return pl.pallas_call(
        functools.partial(project_kernel, fsdp_size),
        out_shape=(
            jax.ShapeDtypeStruct((rows, width), low),
            jax.ShapeDtypeStruct((rows, width), low),
            jax.ShapeDtypeStruct((8, width), jnp.float32),
            jax.ShapeDtypeStruct((fsdp_size, shard, width), low),
            jax.ShapeDtypeStruct((fsdp_size, shard, width), low),
            jax.ShapeDtypeStruct((fsdp_size, shard, kvg.shape[1]), low),
            jax.ShapeDtypeStruct((fsdp_size, rows, 256), low),
        ),
        in_specs=[vmem, hbm, hbm, hbm, vmem, vmem],
        out_specs=(vmem, vmem, vmem, hbm, hbm, hbm, hbm),
        scratch_shapes=[
            pltpu.VMEM((fsdp_size, shard, width), low),
            pltpu.VMEM((fsdp_size, shard, kvg.shape[1]), low),
            pltpu.VMEM((rows, 256), low),
            dma((3,)),
            dma((2, 2, count)),
            dma((2, count)),
            dma((2, 2, count)),
            dma((2, 5, count)),
            dma((2, 2, count)),
            dma((2, 5, count)),
            dma((2, 2, count)),
            dma((2, count)),
        ],
        compiler_params=pltpu.CompilerParams(
            collective_id=0, has_side_effects=True, vmem_limit_bytes=48 << 20
        ),
        cost_estimate=pl.CostEstimate(
            flops=2 * rows * width * (width + 256), transcendentals=0, bytes_accessed=40 << 20
        ),
        name="project",
    )(tokens, wq, wo, kvg, cos_table, sin_table)


def greet(replica, fsdp, at, count):
    barrier = pltpu.get_barrier_semaphore()
    for target in (
        (replica, flip(fsdp, 1)),
        (flip(replica, 1), fsdp),
        (flip(replica, 2), fsdp),
    ):
        pl.semaphore_signal(barrier, inc=1, device_id=target, device_id_type=MESH)

    @pl.when(at > 0)
    def _():
        pl.semaphore_signal(barrier, inc=1, device_id=(replica, fsdp - 2), device_id_type=MESH)

    @pl.when(at < count - 1)
    def _():
        pl.semaphore_signal(barrier, inc=1, device_id=(replica, fsdp + 2), device_id_type=MESH)

    inside = (at > 0) & (at < count - 1)

    @pl.when(inside)
    def _():
        pl.semaphore_wait(barrier, 5)

    @pl.when(jnp.logical_not(inside))
    def _():
        pl.semaphore_wait(barrier, 4)


def add_into(ref, index, *others):
    total = ref[index].astype(jnp.float32)
    for other in others:
        total = total + other.astype(jnp.float32)
    ref[index] = total.astype(ref.dtype)


class Collect:
    def __init__(self, place, grad, core_in, line_in, core_sems, line_sems, copies=None):
        self.replica, self.fsdp, self.at, self.core, self.count = place
        self.grad, self.core_in, self.line_in = grad, core_in, line_in
        self.core_sems, self.line_sems = core_sems, line_sems
        self.beside, self.across = flip(self.replica, 1), flip(self.replica, 2)
        self.opposite = flip(self.beside, 2)
        if copies is None:
            self.rows = pl.ds(0, grad.shape[1])
        else:
            self.diag_in, self.quarter_in, self.full = copies[:3]
            self.diag_sems, self.quarter_sems, self.full_sems = copies[3:]
            self.size = grad.shape[1] // 4
            self.rows = self.quarter(self.replica)

    def quarter(self, copy, half=None):
        size = self.size if half is None else self.size // 2
        start = copy * self.size + (0 if half is None else half * size)
        return pl.ds(pl.multiple_of(start, size), size)

    def remote(self, src, dst, sems, index, target):
        return pltpu.make_async_remote_copy(
            src_ref=src,
            dst_ref=dst,
            send_sem=sems.at[(0,) + index],
            recv_sem=sems.at[(1,) + index],
            device_id=target,
            device_id_type=MESH,
        )

    def core_copy(self, shard):
        return self.remote(
            self.grad.at[2 * shard + 1 - self.core],
            self.core_in.at[shard],
            self.core_sems,
            (shard,),
            (self.replica, flip(self.fsdp, 1)),
        )

    def core_add(self, shard):
        self.core_copy(shard).wait_recv()
        add_into(self.grad, 2 * shard + self.core, self.core_in[shard])

    def diag_copy(self, shard, half):
        return self.remote(
            self.grad.at[2 * shard + self.core, self.quarter(self.opposite, half)],
            self.diag_in.at[half, shard],
            self.diag_sems,
            (half, shard),
            (self.beside if half == 0 else self.across, self.fsdp),
        )

    def diag_start(self, shard):
        self.diag_copy(shard, 0).start()
        self.diag_copy(shard, 1).start()

    def quarter_copy(self, shard, way):
        return self.remote(
            self.grad.at[2 * shard + self.core, self.quarter(self.across if way else self.beside)],
            self.quarter_in.at[way, shard],
            self.quarter_sems,
            (way, shard),
            (self.across if way else self.beside, self.fsdp),
        )

    def quarter_start(self, shard):
        at = 2 * shard + self.core
        for half, copy in ((0, self.across), (1, self.beside)):
            self.diag_copy(shard, half).wait_recv()
            add_into(self.grad, (at, self.quarter(copy, half)), self.diag_in[half, shard])
            self.quarter_copy(shard, 1 - half).start()

    def quarter_add(self, shard):
        self.quarter_copy(shard, 0).wait_recv()
        self.quarter_copy(shard, 1).wait_recv()
        add_into(
            self.grad,
            (2 * shard + self.core, self.rows),
            self.quarter_in[0, shard],
            self.quarter_in[1, shard],
        )

    def line_copy(self, shard, way):
        return self.remote(
            self.grad.at[2 * shard + self.core, self.rows],
            self.line_in.at[way, shard],
            self.line_sems,
            (way, shard),
            (self.replica, self.fsdp + (2 if way == 0 else -2)),
        )

    def line_receive(self, shard, way):
        self.line_copy(shard, way).wait_recv()
        add_into(self.grad, (2 * shard + self.core, self.rows), self.line_in[way, shard])

    def line_hop(self, hop):
        for way, shard, there, fed in (
            (0, self.at + hop, self.at + hop < self.count, self.at > 0),
            (1, self.at - hop, self.at - hop >= 0, self.at < self.count - 1),
        ):

            @pl.when(there & fed)
            def _(shard=shard, way=way):
                self.line_receive(shard, way)

            @pl.when(there)
            def _(shard=shard, way=way):
                self.line_copy(shard, way).start()

    def line_end(self):
        @pl.when(self.at > 0)
        def _():
            self.line_receive(self.at, 0)

        @pl.when(self.at < self.count - 1)
        def _():
            self.line_receive(self.at, 1)

    def full_copy(self, kind):
        own = self.replica
        rows, target = (
            (self.quarter(own), self.beside),
            (self.quarter(own), self.across),
            (self.quarter(self.beside, 0), self.across),
            (self.quarter(self.across, 1), self.beside),
        )[kind]
        return self.remote(
            self.full.at[rows],
            self.full.at[rows],
            self.full_sems,
            (kind,),
            (target, self.fsdp),
        )

    def full_recv(self, kind):
        rows = (
            self.quarter(self.beside),
            self.quarter(self.across),
            self.quarter(self.opposite, 0),
            self.quarter(self.opposite, 1),
        )[kind]
        ref = self.full.at[rows]
        self.remote(ref, ref, self.full_sems, (kind,), (self.beside, self.fsdp)).wait_recv()

    def gather_start(self):
        self.full[self.rows] = self.grad[2 * self.at + self.core, self.rows]
        self.full_copy(0).start()
        self.full_copy(1).start()

    def gather_relay(self):
        self.full_recv(0)
        self.full_copy(2).start()
        self.full_recv(1)
        self.full_copy(3).start()

    def gather_end(self):
        self.full_recv(2)
        self.full_recv(3)

    def drain(self):
        for shard in range(self.count):
            self.core_copy(shard).wait_send()
            if hasattr(self, "size"):
                for way in (0, 1):
                    self.diag_copy(shard, way).wait_send()
                    self.quarter_copy(shard, way).wait_send()
        for hop in range(1, self.count):

            @pl.when(self.at + hop < self.count)
            def _(hop=hop):
                self.line_copy(self.at + hop, 0).wait_send()

            @pl.when(self.at - hop >= 0)
            def _(hop=hop):
                self.line_copy(self.at - hop, 1).wait_send()

        if hasattr(self, "size"):
            for kind in range(4):
                self.full_copy(kind).wait_send()


def collect_scratch(fsdp_size, rows, width, copies=True):
    count = fsdp_size // 2
    low, dma = jnp.bfloat16, pltpu.SemaphoreType.DMA
    size = rows // 4 if copies else rows
    shapes = [
        pltpu.VMEM((fsdp_size, rows, width), low),
        pltpu.VMEM((count, rows, width), low),
        pltpu.VMEM((2, count, size, width), low),
        dma((2, count)),
        dma((2, 2, count)),
    ]
    if copies:
        shapes += [
            pltpu.VMEM((2, count, size // 2, width), low),
            pltpu.VMEM((2, count, size, width), low),
            pltpu.VMEM((rows, width), low),
            dma((2, 2, count)),
            dma((2, 2, count)),
            dma((2, 4)),
        ]
    return shapes


def make_collect(place, refs, copies=True):
    return Collect(place, *refs[:5], copies=refs[5:11] if copies else None)


def position(fsdp_size):
    replica, fsdp = lax.axis_index("replica"), lax.axis_index("fsdp")
    return replica, fsdp, fsdp // 2, fsdp % 2, fsdp_size // 2


def outer(collect, left_ref, right_ref, own_core):
    rows = collect.grad.shape[1]
    core = collect.core if own_core else 1 - collect.core

    @pl.loop(0, collect.count)
    def _(shard):
        start = pl.multiple_of((2 * shard + core) * rows, rows)
        part = contract(left_ref[:, pl.ds(start, rows)], right_ref[...], 0, 0)
        collect.grad[2 * shard + core] = part.astype(jnp.bfloat16)
        if not own_core:
            collect.core_copy(shard).start()


def each(count, step):
    for shard in range(count):
        step(shard)


def finish_kernel(
    fsdp_size,
    normed_ref,
    d_q_ref,
    tokens_ref,
    d_hidden_ref,
    gain_ref,
    term_ref,
    cos_ref,
    sin_ref,
    d_kv_ref,
    wq_ref,
    kvg_ref,
    ffn_ref,
    input_grad_ref,
    q_grad_ref,
    kv_grad_ref,
    ffn_all,
    wq_buf,
    kvg_vmem,
    d_kv_raw,
    term_sum,
    hidden_buf,
    local_sems,
    ffn_sems,
    *refs,
):
    place = position(fsdp_size)
    replica, fsdp, at, core, count = place
    greet(replica, fsdp, at, count)
    q_sums = make_collect(place, refs[:11])
    kv_sums = make_collect(place, refs[11:22])
    d_kv = make_collect(place, refs[22:27], False)
    beside, across = flip(replica, 1), flip(replica, 2)
    width = tokens_ref.shape[1]
    half = width // 2

    def ffn_copy(kind, lands=False):
        piece = (replica, replica, beside, across)[kind]
        if lands:
            piece = (beside, across, flip(beside, 2), flip(beside, 2))[kind]
        columns = (slice(None), slice(None), pl.ds(0, half), pl.ds(half, half))[kind]
        dst = ffn_all.at[piece, :, :, columns]
        return pltpu.make_async_remote_copy(
            src_ref=ffn_ref if kind < 2 and not lands else dst,
            dst_ref=dst,
            send_sem=ffn_sems.at[0, kind],
            recv_sem=ffn_sems.at[1, kind],
            device_id=((beside, across, across, beside)[kind], fsdp),
            device_id_type=MESH,
        )

    ffn_copy(0).start()
    ffn_copy(1).start()
    ffn_rows = ffn_ref.shape[1]

    def keep_ffn(part, slot, out):
        held = wq_buf.at[slot, pl.ds(0, ffn_rows)]
        place_at = ffn_all.at[replica, part]
        return pltpu.make_async_copy(
            held if out else ffn_ref.at[part], place_at if out else held, local_sems.at[0]
        )

    load = pltpu.make_async_copy(d_kv_ref, d_kv.grad, local_sems.at[1])
    load.start()
    load_kvg = pltpu.make_async_copy(kvg_ref, kvg_vmem, local_sems.at[2])
    load_kvg.start()
    load.wait()
    each(count, lambda shard: d_kv.core_copy(shard).start())
    outer(q_sums, normed_ref, d_q_ref, False)
    for part in range(3):
        for out in (False, True):
            keep_ffn(part, 0, out).start()
            keep_ffn(part, 0, out).wait()
    each(count, d_kv.core_add)
    d_kv.line_hop(count - 1)
    outer(q_sums, normed_ref, d_q_ref, True)
    for hop in range(count - 2, 0, -1):
        d_kv.line_hop(hop)
    for shard in range(count):
        q_sums.core_add(shard)
        q_sums.diag_start(shard)
    d_kv.line_end()
    each(count, q_sums.quarter_start)

    summed = d_kv.grad[fsdp].astype(jnp.float32)
    d_key = summed[:, :128]
    d_key = d_key * cos_ref[...] - pltpu.roll(d_key, 64, 1) * sin_ref[...]
    d_kv_raw[:, :128] = d_key.astype(jnp.bfloat16)
    d_kv_raw[:, 128:] = summed[:, 128:].astype(jnp.bfloat16)
    load_kvg.wait()
    rows = kvg_vmem.shape[1]

    def fetch(shard):
        return pltpu.make_async_copy(wq_ref.at[shard], wq_buf.at[shard % 2], local_sems.at[shard % 2])

    fetch(0).start()
    for shard in range(fsdp_size):
        fetch(shard).wait()
        if shard + 1 < fsdp_size:
            fetch(shard + 1).start()
        input_grad_ref[:, shard * rows : (shard + 1) * rows] = contract(
            d_q_ref[...], wq_buf[shard % 2], 1, 1
        ) + contract(d_kv_raw[...], kvg_vmem[shard, :, :256], 1, 1)
    for kind in (0, 1):
        ffn_copy(kind, True).wait_recv()
        ffn_copy(2 + kind).start()
    each(count, q_sums.quarter_add)
    for hop in range(count - 1, 0, -1):
        q_sums.line_hop(hop)

    term_sum[...] = jnp.zeros_like(term_sum)

    @pl.loop(0, tokens_ref.shape[0] // 128)
    def _(block):
        part = pl.ds(pl.multiple_of(block * 128, 128), 128)
        fetch_hidden = pltpu.make_async_copy(d_hidden_ref.at[part], hidden_buf, local_sems.at[0])
        fetch_hidden.start()
        d_normed = input_grad_ref[part]
        inputs = tokens_ref[part].astype(jnp.float32)
        inverse = lax.rsqrt(jnp.mean(inputs * inputs, axis=1, keepdims=True) + EPSILON)
        scaled = d_normed * gain_ref[:1]
        inner = jnp.mean(scaled * inputs, axis=1, keepdims=True)
        term_sum[:1] += jnp.sum(d_normed * inputs * inverse, axis=0, keepdims=True)
        step = inverse * scaled - inputs * (inverse**3 * inner)
        fetch_hidden.wait()
        input_grad_ref[part] = hidden_buf[...] + step

    term = term_sum[:1]
    line = lax.broadcasted_iota(jnp.int32, (128, width), 0)
    terms = jnp.where(line == 0, term, jnp.where(line == 1, term_ref[:1], 0.0)).T
    terms = terms.astype(jnp.bfloat16)
    for shard in range(fsdp_size):
        left = normed_ref[:, shard * rows : (shard + 1) * rows]
        kv_sums.grad[shard, :, :256] = contract(left, d_kv_raw[...], 0, 0).astype(jnp.bfloat16)
        kv_sums.grad[shard, :, 256:] = terms[shard * rows : (shard + 1) * rows]
    each(count, lambda shard: kv_sums.core_copy(shard).start())
    q_sums.line_end()
    q_sums.gather_start()
    for shard in range(count):
        kv_sums.core_add(shard)
        kv_sums.diag_start(shard)
    each(count, kv_sums.quarter_start)
    q_sums.gather_relay()
    each(count, kv_sums.quarter_add)
    for hop in range(count - 1, 0, -1):
        kv_sums.line_hop(hop)
    kv_sums.line_end()
    kv_sums.gather_start()
    q_sums.gather_end()
    q_grad_ref[...] = q_sums.full[...].astype(jnp.float32)
    kv_sums.gather_relay()
    kv_sums.gather_end()
    kv_grad_ref[...] = kv_sums.full[...].astype(jnp.float32)
    for kind in (2, 3):
        ffn_copy(kind, True).wait_recv()
    for kind in range(4):
        ffn_copy(kind).wait_send()
    for sums in (q_sums, kv_sums, d_kv):
        sums.drain()


def finish(
    normed, d_q, tokens, d_hidden, gains, term, cos_table, sin_table, d_kv, wq_all, kvg_all, ffn
):
    fsdp_size, rows, width = wq_all.shape
    tok_rows = tokens.shape[0]
    low, dma = jnp.bfloat16, pltpu.SemaphoreType.DMA
    vmem, hbm = pl.BlockSpec(memory_space=pltpu.VMEM), pl.BlockSpec(memory_space=pl.ANY)
    return pl.pallas_call(
        functools.partial(finish_kernel, fsdp_size),
        out_shape=(
            jax.ShapeDtypeStruct((tok_rows, width), jnp.float32),
            jax.ShapeDtypeStruct((rows, width), jnp.float32),
            jax.ShapeDtypeStruct((rows, 384), jnp.float32),
            jax.ShapeDtypeStruct((4,) + ffn.shape, low),
        ),
        in_specs=[vmem] * 3 + [hbm] + [vmem] * 4 + [hbm] * 4,
        out_specs=(vmem, vmem, vmem, hbm),
        scratch_shapes=[
            pltpu.VMEM((2, rows, width), low),
            pltpu.VMEM((fsdp_size, rows, 384), low),
            pltpu.VMEM((tok_rows, 256), low),
            pltpu.VMEM((8, width), jnp.float32),
            pltpu.VMEM((128, width), jnp.float32),
            dma((3,)),
            dma((2, 4)),
        ]
        + collect_scratch(fsdp_size, rows, width)
        + collect_scratch(fsdp_size, rows, 384)
        + collect_scratch(fsdp_size, tok_rows, 256, False),
        compiler_params=pltpu.CompilerParams(
            collective_id=2, has_side_effects=True, vmem_limit_bytes=54 << 20
        ),
        cost_estimate=pl.CostEstimate(
            flops=100 * tok_rows * width * width, transcendentals=0, bytes_accessed=40 << 20
        ),
        name="finish",
    )(normed, d_q, tokens, d_hidden, gains, term, cos_table, sin_table, d_kv, wq_all, kvg_all, ffn)


def swap(value, step):
    copies = lax.axis_size("replica")
    return lax.ppermute(value, "replica", [(r, r ^ step) for r in range(copies)])


def pass_on(beside, across, got):
    half = got.shape[1]
    low, wide = jnp.bfloat16, jnp.float32
    got = got.astype(wide)
    across = jnp.concatenate([across[:half].astype(wide) + got[0], across[half:].astype(wide)])
    beside = jnp.concatenate([beside[:half].astype(wide), beside[half:].astype(wide) + got[1]])
    return beside.astype(low), across.astype(low)


def gather_shards(value):
    return lax.all_gather(value, "fsdp", axis=0, tiled=True)


def scatter_shards(value):
    return lax.psum_scatter(value, "fsdp", scatter_dimension=0, tiled=True)


def after(value, *others):
    return lax.optimization_barrier((value, others))[0]


def quarter(shard, copy_index):
    rows = shard.shape[0] // lax.axis_size("replica")
    return lax.dynamic_slice_in_dim(shard, copy_index * rows, rows, 0)


def shards(
    tokens,
    segments,
    positions,
    query_weight,
    key_weight,
    value_weight,
    output_weight,
    attn_gain,
    gate_weight,
    up_weight,
    down_weight,
    ffn_gain,
    grad_out,
):
    tok_rows, model_width = tokens.shape
    head_dim = key_weight.shape[1]
    fsdp_size = lax.axis_size("fsdp")
    fsdp_index = lax.axis_index("fsdp")
    copy_index = lax.axis_index("replica")
    copies = lax.axis_size("replica")
    low = jnp.bfloat16

    w_down = gather_shards(quarter(down_weight, copy_index))
    cos_table, sin_table = rope_tables(positions, head_dim)
    gain_columns = jnp.stack([attn_gain, ffn_gain], axis=1)
    queries, normed, gains, wq_all, w_out, kvg_all, kv_all = project(
        tokens,
        query_weight,
        output_weight,
        jnp.concatenate(
            [key_weight, value_weight, jnp.pad(gain_columns, ((0, 0), (0, 126)))], axis=1
        ),
        cos_table,
        sin_table,
    )
    w_out = w_out.reshape(model_width, model_width)
    kv_all = kv_all.reshape(fsdp_size * tok_rows, 2 * head_dim)
    gain_ffn = gains[1]
    inputs = tokens.astype(jnp.float32)
    key_width = max(GROUP_TOK, tok_rows)
    window_start = fsdp_index * tok_rows // key_width * key_width
    one_group = fsdp_size * tok_rows == key_width
    kv = kv_all if one_group else lax.dynamic_slice_in_dim(kv_all, window_start, key_width, 0)

    row_at = fsdp_index * tok_rows - window_start + jnp.arange(tok_rows, dtype=jnp.int32)
    lowest = jnp.where(positions < PROMPT, 0, row_at - (positions - PROMPT))
    w_gate = gather_shards(after(quarter(gate_weight.T, copy_index), normed))
    w_up = gather_shards(after(quarter(up_weight.T, copy_index), normed))
    mixed_rows, logs, grads = attend(
        queries, kv, jnp.broadcast_to(lowest[:, None], (tok_rows, 128)), after(grad_out, w_down)
    )

    hidden = inputs + matmul(mixed_rows, w_out)
    normed_ffn_full, inverse_ffn = norm_forward(hidden, gain_ffn)
    normed_ffn = normed_ffn_full.astype(low)

    x_all, activation, d_gate, d_up, *parts = feed_forward(
        normed_ffn, grads, w_gate, w_up, w_down
    )
    own_part, own_out = parts[0], parts[4]
    beside, across = pass_on(*parts[1:4])
    all_rows = copies * tok_rows
    x_all, grads = x_all.reshape(all_rows, -1), grads.reshape(all_rows, -1)
    activation = activation.reshape(all_rows, -1)
    d_gate = after(d_gate, beside, across)
    gate_part = contract(d_gate.reshape(all_rows, -1), x_all, 0, 0).astype(low)
    d_up, activation = after((d_up, activation), gate_part)
    d_normed_ffn = (
        own_part.astype(jnp.float32)
        + swap(beside, 1).astype(jnp.float32)
        + swap(across, 2).astype(jnp.float32)
    )
    up_part = contract(d_up.reshape(all_rows, -1), x_all, 0, 0).astype(low)
    down_part = contract(activation, grads, 0, 0).astype(low)

    cotangent = grad_out.astype(jnp.float32)
    resid_ffn, ffn_gain_term = norm_backward(hidden, inverse_ffn, gain_ffn, d_normed_ffn)
    d_hidden = cotangent + resid_ffn
    d_branch = d_hidden.astype(low)
    d_mixed = contract(d_branch, w_out, 1, 1).astype(low)
    d_mixed = after(d_mixed, gate_part, up_part, down_part)
    gate_sum = scatter_shards(gate_part)
    up_sum = scatter_shards(up_part)
    down_sum = scatter_shards(down_part)
    out_beside, out_across = pass_on(*after(parts[5:8], down_part))
    out_beside, out_across = after((out_beside, out_across), d_mixed)
    other_outs = [swap(out_beside, 1), swap(out_across, 2)]
    d_query_raw, d_kv, output_grad = attend_back(
        queries,
        kv,
        cos_table,
        sin_table,
        jnp.broadcast_to(lowest[None, :], (8, tok_rows)),
        mixed_rows,
        d_mixed,
        logs,
        d_branch,
    )
    layer_out = hidden + own_out.astype(jnp.float32)
    for part in after(other_outs, d_kv):
        layer_out = layer_out + part.astype(jnp.float32)
    layer_out = layer_out.astype(low)
    if not one_group:
        d_kv = lax.dynamic_update_slice_in_dim(
            jnp.zeros((fsdp_size * tok_rows, 2 * head_dim), low), d_kv, window_start, 0
        )
    input_grad, query_grad, kv_grad, ffn_all = finish(
        normed,
        d_query_raw,
        tokens,
        d_hidden,
        gains,
        jnp.broadcast_to(ffn_gain_term[None], (8, model_width)),
        cos_table,
        sin_table,
        d_kv.reshape(fsdp_size, tok_rows, 2 * head_dim),
        wq_all,
        kvg_all,
        jnp.stack([gate_sum, up_sum, down_sum]),
    )
    gate_grad, up_grad, down_grad = (
        ffn_all[:, i].reshape(-1, model_width).astype(jnp.float32) for i in range(3)
    )
    return (
        layer_out,
        input_grad,
        query_grad,
        kv_grad[:, :head_dim],
        kv_grad[:, head_dim : 2 * head_dim],
        output_grad,
        kv_grad[:, 2 * head_dim],
        gate_grad.T,
        up_grad.T,
        down_grad,
        kv_grad[:, 2 * head_dim + 1],
    )


def half_tables(pos_ids, head_dim):
    half_width = head_dim // 2
    frequency = ROPE_BASE ** (-jnp.arange(half_width, dtype=jnp.float32) * 2.0 / head_dim)
    angles = pos_ids.astype(jnp.float32)[:, None] * frequency[None, :]
    return (jnp.cos(angles), jnp.sin(angles))


def rotate(values, cos_table, sin_table):
    half_width = values.shape[-1] // 2
    front_half = values[..., :half_width]
    back_half = values[..., half_width:]
    return jnp.concatenate(
        [
            front_half * cos_table - back_half * sin_table,
            back_half * cos_table + front_half * sin_table,
        ],
        axis=-1,
    )


def any_shards(
    tokens,
    segments,
    positions,
    query_weight,
    key_weight,
    value_weight,
    output_weight,
    attn_gain,
    gate_weight,
    up_weight,
    down_weight,
    ffn_gain,
    grad_out,
):
    tok_rows, model_width = tokens.shape
    head_dim = key_weight.shape[1]
    head_count = model_width // head_dim
    block_count = head_count // HEAD_BLOCK
    block_width = HEAD_BLOCK * head_dim
    score_scale = head_dim ** (-0.5)
    fsdp_size = lax.axis_size("fsdp")
    fsdp_index = lax.axis_index("fsdp")
    gathered = (
        lax.all_gather(query_weight, "fsdp", axis=0, tiled=True),
        lax.all_gather(key_weight, "fsdp", axis=0, tiled=True),
        lax.all_gather(value_weight, "fsdp", axis=0, tiled=True),
        lax.all_gather(output_weight, "fsdp", axis=0, tiled=True),
        lax.all_gather(attn_gain, "fsdp", axis=0, tiled=True),
        lax.all_gather(ffn_gain, "fsdp", axis=0, tiled=True),
    )
    w_query, w_key, w_value, w_out, gain_attn, gain_ffn = gathered
    gain_attn = gain_attn.astype(jnp.float32)
    gain_ffn = gain_ffn.astype(jnp.float32)
    inputs = tokens.astype(jnp.float32)
    normed_full, inverse_attn = norm_forward(inputs, gain_attn)
    normed = normed_full.astype(jnp.bfloat16)
    query_raw = matmul(normed, w_query)
    key_raw = matmul(normed, w_key)
    value_rows = matmul(normed, w_value).astype(jnp.bfloat16)
    cos_table, sin_table = half_tables(positions, head_dim)
    queries = rotate(
        query_raw.reshape(tok_rows, head_count, head_dim), cos_table[:, None], sin_table[:, None]
    ).astype(jnp.bfloat16)
    key_rot = rotate(key_raw, cos_table, sin_table).astype(jnp.bfloat16)
    key_rows, value_all = (
        lax.all_gather(key_rot, "fsdp", axis=0, tiled=True),
        lax.all_gather(value_rows, "fsdp", axis=0, tiled=True),
    )
    seg_all, pos_all = (
        lax.all_gather(segments, "fsdp", axis=0, tiled=True),
        lax.all_gather(positions, "fsdp", axis=0, tiled=True),
    )
    key_width = max(GROUP_TOK, tok_rows)
    window_start = fsdp_index * tok_rows // GROUP_TOK * GROUP_TOK
    key_window = lax.dynamic_slice_in_dim(key_rows, window_start, key_width, 0)
    value_window = lax.dynamic_slice_in_dim(value_all, window_start, key_width, 0)
    seg_window = lax.dynamic_slice_in_dim(seg_all, window_start, key_width, 0)
    pos_window = lax.dynamic_slice_in_dim(pos_all, window_start, key_width, 0)
    key_index = window_start + jnp.arange(key_width, dtype=jnp.int32)
    query_index = fsdp_index * tok_rows + jnp.arange(tok_rows, dtype=jnp.int32)
    visible = (
        (key_index[None, :] // GROUP_TOK == query_index[:, None] // GROUP_TOK)
        & (pos_window[None, :] <= positions[:, None])
        & ((seg_window[None, :] == 0) | (seg_window[None, :] == segments[:, None]))
    )
    query_blocks = queries.reshape(tok_rows, block_count, block_width).transpose(1, 0, 2)

    def block_scores(query_block):
        flat_queries = query_block.reshape(tok_rows * HEAD_BLOCK, head_dim)
        scores = (
            contract(flat_queries, key_window, 1, 1).reshape(tok_rows, HEAD_BLOCK, key_width)
            * score_scale
        )
        return (flat_queries, scores)

    def attend_block(query_block):
        flat_queries, scores = block_scores(query_block)
        scores = jnp.where(visible[:, None, :], scores, MASKED)
        row_max = jnp.max(scores, axis=-1, keepdims=True)
        exp_scores = jnp.exp(scores - row_max)
        totals = jnp.sum(exp_scores, axis=-1, keepdims=True)
        weights = (
            (exp_scores / totals).astype(jnp.bfloat16).reshape(tok_rows * HEAD_BLOCK, key_width)
        )
        mixed_block = matmul(weights, value_window).reshape(tok_rows, block_width)
        return (mixed_block, (row_max + jnp.log(totals))[..., 0])

    mixed_blocks, log_totals = lax.map(attend_block, query_blocks)
    mixed_rows = mixed_blocks.transpose(1, 0, 2).reshape(tok_rows, model_width).astype(jnp.bfloat16)
    hidden = inputs + matmul(mixed_rows, w_out)
    normed_ffn_full, inverse_ffn = norm_forward(hidden, gain_ffn)
    normed_ffn = normed_ffn_full.astype(jnp.bfloat16)
    cotangent = grad_out.astype(jnp.float32)
    w_gate, w_up, w_down = (
        lax.all_gather(gate_weight, "fsdp", axis=1, tiled=True),
        lax.all_gather(up_weight, "fsdp", axis=1, tiled=True),
        lax.all_gather(down_weight, "fsdp", axis=0, tiled=True),
    )
    gate_proj = matmul(normed_ffn, w_gate)
    up_proj = matmul(normed_ffn, w_up)
    activation = (jax.nn.silu(gate_proj) * up_proj).astype(jnp.bfloat16)
    layer_out = (hidden + matmul(activation, w_down)).astype(jnp.bfloat16)
    d_activation = contract(grad_out, w_down, 1, 1)
    d_gate, d_up = swiglu_back(d_activation, gate_proj, up_proj)
    d_normed_ffn = contract(d_gate, w_gate, 1, 1) + contract(d_up, w_up, 1, 1)
    gate_up_part = lax.psum_scatter(
        jnp.concatenate(
            [contract(d_gate, normed_ffn, 0, 0), contract(d_up, normed_ffn, 0, 0)], axis=1
        ).astype(jnp.bfloat16),
        "fsdp",
        scatter_dimension=0,
        tiled=True,
    ).astype(jnp.float32)
    gate_part = gate_up_part[:, :model_width].T
    up_part = gate_up_part[:, model_width:].T
    down_part = lax.psum_scatter(
        contract(activation, grad_out, 0, 0).astype(jnp.bfloat16),
        "fsdp",
        scatter_dimension=0,
        tiled=True,
    )
    resid_ffn, ffn_gain_term = norm_backward(hidden, inverse_ffn, gain_ffn, d_normed_ffn)
    d_hidden = cotangent + resid_ffn
    d_branch = d_hidden.astype(jnp.bfloat16)
    d_mixed = contract(d_branch, w_out, 1, 1).astype(jnp.bfloat16)
    d_mixed_blocks = d_mixed.reshape(tok_rows, block_count, block_width).transpose(1, 0, 2)

    def back_block(totals, block_items):
        query_block, d_block, log_block = block_items
        flat_queries, scores = block_scores(query_block)
        probs = jnp.where(visible[:, None, :], jnp.exp(scores - log_block[..., None]), 0.0)
        d_flat = d_block.reshape(tok_rows * HEAD_BLOCK, head_dim)
        d_probs = contract(d_flat, value_window, 1, 1).reshape(tok_rows, HEAD_BLOCK, key_width)
        row_delta = jnp.sum(probs * d_probs, axis=-1, keepdims=True)
        d_scores = (
            (probs * (d_probs - row_delta))
            .astype(jnp.bfloat16)
            .reshape(tok_rows * HEAD_BLOCK, key_width)
        )
        weights = probs.astype(jnp.bfloat16).reshape(tok_rows * HEAD_BLOCK, key_width)
        d_query_block = matmul(d_scores, key_window) * score_scale
        key_total = totals[0] + contract(d_scores, flat_queries, 0, 0) * score_scale
        value_total = totals[1] + contract(weights, d_flat, 0, 0)
        return ((key_total, value_total), d_query_block.reshape(tok_rows, block_width))

    zero_window = jnp.zeros((key_width, head_dim), jnp.float32)
    window_grads, d_query_blocks = lax.scan(
        back_block, (zero_window, zero_window), (query_blocks, d_mixed_blocks, log_totals)
    )
    d_queries = d_query_blocks.transpose(1, 0, 2).reshape(tok_rows, head_count, head_dim)
    d_query_raw = (
        rotate(d_queries, cos_table[:, None], -sin_table[:, None])
        .astype(jnp.bfloat16)
        .reshape(tok_rows, model_width)
    )
    row_zeros = jnp.zeros((fsdp_size * tok_rows, head_dim), jnp.float32)
    key_term = lax.dynamic_update_slice_in_dim(row_zeros, window_grads[0], window_start, 0)
    value_term = lax.dynamic_update_slice_in_dim(row_zeros, window_grads[1], window_start, 0)
    key_sum, value_sum = (
        lax.psum_scatter(
            key_term.astype(jnp.bfloat16), "fsdp", scatter_dimension=0, tiled=True
        ).astype(jnp.float32),
        lax.psum_scatter(
            value_term.astype(jnp.bfloat16), "fsdp", scatter_dimension=0, tiled=True
        ).astype(jnp.float32),
    )
    d_key_raw = rotate(key_sum, cos_table, -sin_table).astype(jnp.bfloat16)
    d_value = value_sum.astype(jnp.bfloat16)
    d_normed = (
        contract(d_query_raw, w_query, 1, 1)
        + contract(d_key_raw, w_key, 1, 1)
        + contract(d_value, w_value, 1, 1)
    )
    resid_attn, attn_gain_term = norm_backward(inputs, inverse_attn, gain_attn, d_normed)
    input_grad = d_hidden + resid_attn
    attn_part = lax.psum_scatter(
        jnp.concatenate(
            [
                contract(normed, d_query_raw, 0, 0),
                contract(normed, d_key_raw, 0, 0),
                contract(normed, d_value, 0, 0),
                contract(mixed_rows, d_branch, 0, 0),
            ],
            axis=1,
        ).astype(jnp.bfloat16),
        "fsdp",
        scatter_dimension=0,
        tiled=True,
    )
    attn_gain_part, ffn_gain_part = (
        lax.psum_scatter(attn_gain_term, "fsdp", scatter_dimension=0, tiled=True),
        lax.psum_scatter(ffn_gain_term, "fsdp", scatter_dimension=0, tiled=True),
    )
    summed = (
        lax.psum(attn_part, "replica").astype(jnp.float32),
        lax.psum(attn_gain_part.astype(jnp.bfloat16), "replica").astype(jnp.float32),
        lax.psum(ffn_gain_part.astype(jnp.bfloat16), "replica").astype(jnp.float32),
        lax.psum(gate_part.astype(jnp.bfloat16), "replica").astype(jnp.float32),
        lax.psum(up_part.astype(jnp.bfloat16), "replica").astype(jnp.float32),
        lax.psum(down_part, "replica").astype(jnp.float32),
    )
    attn_total, attn_gain_grad, ffn_gain_grad, gate_grad, up_grad, down_grad = summed
    query_grad = attn_total[:, :model_width]
    key_grad = attn_total[:, model_width : model_width + head_dim]
    value_grad = attn_total[:, model_width + head_dim : model_width + 2 * head_dim]
    output_grad = attn_total[:, model_width + 2 * head_dim :]
    return (
        layer_out,
        input_grad,
        query_grad,
        key_grad,
        value_grad,
        output_grad,
        attn_gain_grad,
        gate_grad,
        up_grad,
        down_grad,
        ffn_gain_grad,
    )


def suits(mesh):
    fsdp_size = mesh.shape["fsdp"]
    return mesh.shape["replica"] == 4 and fsdp_size % 2 == 0 and 2048 % (128 * fsdp_size) == 0


def solution(mesh):
    return jax.shard_map(
        shards if suits(mesh) else any_shards,
        mesh=mesh,
        in_specs=(
            P(("replica", "fsdp"), None),
            P(("replica", "fsdp")),
            P(("replica", "fsdp")),
            P("fsdp", None),
            P("fsdp", None),
            P("fsdp", None),
            P("fsdp", None),
            P("fsdp"),
            P(None, "fsdp"),
            P(None, "fsdp"),
            P("fsdp", None),
            P("fsdp"),
            P(("replica", "fsdp"), None),
        ),
        out_specs=(
            P(("replica", "fsdp"), None),
            P(("replica", "fsdp"), None),
            P("fsdp", None),
            P("fsdp", None),
            P("fsdp", None),
            P("fsdp", None),
            P("fsdp"),
            P(None, "fsdp"),
            P(None, "fsdp"),
            P("fsdp", None),
            P("fsdp"),
        ),
        check_vma=False,
    )
```

```python
import functools

import jax
import jax.numpy as jnp
from jax import lax
from jax.experimental import pallas as pl
from jax.experimental.pallas import tpu as pltpu
from jax.sharding import PartitionSpec as P

GROUP_TOK = 4096
PROMPT = 2048
MAX_CONT = 384
EPSILON = 1e-05
ROPE_BASE = 10000.0
MASKED = -1e30
LOG2E = 1.4426950408889634

TILE = 128
CHUNK = 512
HEAD_GROUP = 4
FFN_ROWS = 256
HEAD_BLOCK = 4


def matmul(left, right):
    return jnp.dot(left, right, preferred_element_type=jnp.float32)


def contract(left, right, left_dim, right_dim):
    return lax.dot_general(
        left, right, (((left_dim,), (right_dim,)), ((), ())), preferred_element_type=jnp.float32
    )


def rope_tables(pos_ids, head_dim):
    half_width = head_dim // 2
    frequency = ROPE_BASE ** (-jnp.arange(half_width, dtype=jnp.float32) * 2.0 / head_dim)
    angles = pos_ids.astype(jnp.float32)[:, None] * frequency[None, :]
    cos_half, sin_half = jnp.cos(angles), jnp.sin(angles)
    return (
        jnp.concatenate([cos_half, cos_half], axis=1),
        jnp.concatenate([-sin_half, sin_half], axis=1),
    )


def swap_halves(values):
    half_width = values.shape[-1] // 2
    return jnp.concatenate([values[..., half_width:], values[..., :half_width]], axis=-1)


def norm_forward(values, gain):
    inverse = lax.rsqrt(jnp.mean(values * values, axis=-1, keepdims=True) + EPSILON)
    return (values * inverse * gain, inverse)


def norm_backward(values, inverse, gain, grad):
    scaled = grad * gain
    inner_mean = jnp.mean(scaled * values, axis=-1, keepdims=True)
    return (
        inverse * scaled - values * inverse**3 * inner_mean,
        jnp.sum(grad * values * inverse, axis=0),
    )


def swiglu_back(d_activation, gate_proj, up_proj):
    sigmoid_gate = jax.nn.sigmoid(gate_proj)
    d_gate = (
        d_activation * up_proj * sigmoid_gate * (1.0 + gate_proj * (1.0 - sigmoid_gate))
    ).astype(jnp.bfloat16)
    d_up = (d_activation * gate_proj * sigmoid_gate).astype(jnp.bfloat16)
    return (d_gate, d_up)


MESH = pl.DeviceIdType.MESH


def flip(index, bit):
    return index + bit - 2 * bit * (index // bit % 2)


class Exchange:
    def __init__(self, source, buffer, sems):
        self.replica, self.fsdp = lax.axis_index("replica"), lax.axis_index("fsdp")
        self.source, self.buffer, self.sems = source, buffer, sems
        self.beside, self.across = flip(self.replica, 1), flip(self.replica, 2)
        self.half = buffer.shape[1] // 2

    def greet(self):
        barrier = pltpu.get_barrier_semaphore()
        for target in (self.beside, self.across):
            pl.semaphore_signal(
                barrier, inc=1, device_id=(target, self.fsdp), device_id_type=MESH
            )
        pl.semaphore_wait(barrier, 2)

    def copy(self, kind):
        first, second = pl.ds(0, self.half), pl.ds(self.half, self.half)
        source, dest, target = (
            (self.source, self.buffer.at[1], self.beside),
            (self.source, self.buffer.at[2], self.across),
            (self.buffer.at[1, first], self.buffer.at[3, first], self.across),
            (self.buffer.at[2, second], self.buffer.at[3, second], self.beside),
        )[kind]
        return pltpu.make_async_remote_copy(
            src_ref=source,
            dst_ref=dest,
            send_sem=self.sems.at[0, kind],
            recv_sem=self.sems.at[1, kind],
            device_id=(target, self.fsdp),
            device_id_type=MESH,
        )

    def begin(self):
        self.copy(0).start()
        self.copy(1).start()

    def relay(self):
        self.copy(0).wait_recv()
        self.copy(2).start()
        self.copy(1).wait_recv()
        self.copy(3).start()

    def end(self):
        self.copy(2).wait_recv()
        self.copy(3).wait_recv()

    def drain(self):
        for kind in range(4):
            self.copy(kind).wait_send()


def ffn_kernel(
    x_ref,
    grads_ref,
    gate_ref,
    up_ref,
    down_ref,
    x_all,
    act_all,
    d_gate_all,
    d_up_all,
    d_x_own,
    d_x_beside,
    d_x_across,
    d_x_got,
    out_own,
    out_beside,
    out_across,
    out_got,
    gate_w,
    up_w,
    down_w,
    block,
    d_act,
    act,
    d_gate,
    d_up,
    d_x,
    out,
    out_far,
    load_sems,
    store_sems,
    x_sems,
    far_sems,
):
    exchange = Exchange(x_ref, x_all, x_sems)
    exchange.greet()
    exchange.begin()
    loads = [
        pltpu.make_async_copy(src, dst, load_sems.at[1 + i])
        for i, (src, dst) in enumerate(
            ((down_ref, down_w), (gate_ref, gate_w), (up_ref, up_w))
        )
    ]
    for load in loads:
        load.start()

    def fetch(source, at, slot):
        return pltpu.make_async_copy(source.at[at], block.at[slot], load_sems.at[4 + slot])

    fetch(grads_ref, 0, 0).start()
    loads[0].wait()
    rows = d_act.shape[1]
    parts = rows // FFN_ROWS
    for at in range(4):
        fetch(grads_ref, at, at % 2).wait()
        if at < 3:
            fetch(grads_ref, at + 1, (at + 1) % 2).start()

        @pl.loop(0, parts)
        def _(part, at=at):
            some = pl.ds(pl.multiple_of(part * FFN_ROWS, FFN_ROWS), FFN_ROWS)
            d_act[at, some] = contract(block[at % 2, some], down_w[...], 1, 1).astype(jnp.bfloat16)

    loads[1].wait()
    loads[2].wait()

    def stores(at):
        pairs = [(act, act_all.at[at]), (d_gate, d_gate_all.at[at]), (d_up, d_up_all.at[at])]
        if at < 3:
            pairs.append((d_x, (d_x_own, d_x_beside, d_x_across)[at]))
            pairs.append((out, (out_own, out_beside, out_across)[at]))
        return [
            pltpu.make_async_copy(src, dst, store_sems.at[i])
            for i, (src, dst) in enumerate(pairs)
        ]

    def far(kind):
        size, half = rows // 2, kind % 2
        source = block.at[1] if kind < 2 else out_far
        return pltpu.make_async_remote_copy(
            src_ref=source.at[pl.ds(half * size, size)],
            dst_ref=(d_x_got if kind < 2 else out_got).at[half],
            send_sem=far_sems.at[0, kind],
            recv_sem=far_sems.at[1, kind],
            device_id=((exchange.beside, exchange.across)[half], exchange.fsdp),
            device_id_type=MESH,
        )

    order = (0, 1, 3, 2)
    for turn, at in enumerate(order):
        if at == 1:
            exchange.relay()
        if at == 3:
            exchange.end()
        load = (
            fetch(x_all, at, 0)
            if at
            else pltpu.make_async_copy(x_ref, block.at[0], load_sems.at[0])
        )
        load.start()
        load.wait()
        if at == 0:
            keep = pltpu.make_async_copy(block.at[0], x_all.at[0], load_sems.at[0])
            keep.start()
        if turn > 0:
            for store in stores(order[turn - 1]):
                store.wait()

        @pl.loop(0, parts)
        def _(part, at=at):
            some = pl.ds(pl.multiple_of(part * FFN_ROWS, FFN_ROWS), FFN_ROWS)
            x = block[0, some]
            gate = contract(x, gate_w[...], 1, 1)
            up = contract(x, up_w[...], 1, 1)
            slope = jax.nn.sigmoid(gate)
            d = d_act[at, some].astype(jnp.float32)
            swish = gate * slope
            act[some] = (swish * up).astype(jnp.bfloat16)
            by_gate = (d * up * (slope + swish * (1.0 - slope))).astype(jnp.bfloat16)
            by_up = (d * swish).astype(jnp.bfloat16)
            d_gate[some] = by_gate
            d_up[some] = by_up
            (out_far if at == 3 else out)[some] = matmul(act[some], down_w[...]).astype(
                jnp.bfloat16
            )
            (block.at[1] if at == 3 else d_x)[some] = (
                matmul(by_gate, gate_w[...]) + matmul(by_up, up_w[...])
            ).astype(jnp.bfloat16)

        for store in stores(at):
            store.start()
        if at == 0:
            keep.wait()
        if at == 3:
            for kind in range(4):
                far(kind).start()
    for store in stores(order[3]):
        store.wait()
    for kind in range(4):
        far(kind).wait()
    exchange.drain()


def feed_forward(x, grads, w_gate, w_up, w_down):
    rows, width = x.shape
    hidden = w_gate.shape[0]
    low, dma = jnp.bfloat16, pltpu.SemaphoreType.DMA
    hbm = pl.BlockSpec(memory_space=pl.ANY)
    block = jax.ShapeDtypeStruct((rows, width), low)
    halves = jax.ShapeDtypeStruct((2, rows // 2, width), low)
    wide = jax.ShapeDtypeStruct((4, rows, width), low)
    thin = jax.ShapeDtypeStruct((4, rows, hidden), low)
    return pl.pallas_call(
        ffn_kernel,
        out_shape=(wide, thin, thin, thin, block, block, block, halves, block, block, block, halves),
        in_specs=[hbm] * 5,
        out_specs=(hbm,) * 12,
        scratch_shapes=[pltpu.VMEM((hidden, width), low)] * 3
        + [
            pltpu.VMEM((2, rows, width), low),
            pltpu.VMEM((4, rows, hidden), low),
            pltpu.VMEM((rows, hidden), low),
            pltpu.VMEM((rows, hidden), low),
            pltpu.VMEM((rows, hidden), low),
            pltpu.VMEM((rows, width), low),
            pltpu.VMEM((rows, width), low),
            pltpu.VMEM((rows, width), low),
            dma((6,)),
            dma((5,)),
            dma((2, 4)),
            dma((2, 4)),
        ],
        compiler_params=pltpu.CompilerParams(
            collective_id=3, has_side_effects=True, vmem_limit_bytes=50 << 20
        ),
        cost_estimate=pl.CostEstimate(
            flops=40 * rows * width * hidden, transcendentals=0, bytes_accessed=40 << 20
        ),
        name="feed_forward",
    )(x, grads, w_gate, w_up, w_down)


def stack_heads(block):
    heads = block.shape[1] // 128
    return jnp.concatenate([block[:, h * 128 : (h + 1) * 128] for h in range(heads)], axis=0)


def chunk_plan(tok_rows):
    first = lax.axis_index("fsdp") * tok_rows % GROUP_TOK + pl.program_id(0) * TILE
    in_prompt = first < PROMPT
    full = jnp.where(in_prompt, first // CHUNK, PROMPT // CHUNK)
    last = jnp.where(
        in_prompt, first // CHUNK * CHUNK, jnp.maximum(PROMPT, first + TILE - CHUNK)
    )
    return first, full, pl.multiple_of(last, TILE)


def attend_kernel(
    tok_rows,
    q_ref,
    kv_ref,
    low_ref,
    grads_ref,
    mixed_ref,
    log_ref,
    grads_all,
    values,
    top,
    acc,
    own_rows,
    sems,
    own_sem,
):
    factor = 128**-0.5 * LOG2E

    exchange = Exchange(grads_ref, grads_all, sems)
    load_own = pltpu.make_async_copy(grads_ref, own_rows, own_sem)
    keep_own = pltpu.make_async_copy(own_rows, grads_all.at[0], own_sem)

    @pl.when((pl.program_id(0) == 0) & (pl.program_id(1) == 0))
    def _():
        load_own.start()
        exchange.greet()
        exchange.begin()
        load_own.wait()
        keep_own.start()
        values[:, :128] = kv_ref[:, 128:]
        values[:, 128:] = jnp.ones_like(values[:, 128:])

    @pl.when((pl.program_id(0) == pl.num_programs(0) // 2) & (pl.program_id(1) == 0))
    def _():
        exchange.relay()

    first, full, last = chunk_plan(tok_rows)
    queries = stack_heads(q_ref[...])
    rows = queries.shape[0]
    top[...] = jnp.full_like(top, MASKED)
    acc[...] = jnp.zeros_like(acc)

    def step(start, masked):
        scores = contract(queries, kv_ref[pl.ds(start, CHUNK), :128], 1, 1) * factor
        if masked:
            key_at = start + lax.broadcasted_iota(jnp.int32, (rows, CHUNK), 1)
            row_at = lax.broadcasted_iota(jnp.int32, (rows, 1), 0) % TILE + first
            low = jnp.concatenate([low_ref[:, :1]] * HEAD_GROUP, axis=0)
            scores = jnp.where((key_at <= row_at) & (key_at >= low), scores, MASKED)
        before = top[:, :1]
        after = jnp.maximum(before, jnp.max(scores, axis=1, keepdims=True))
        weights = jnp.exp2(scores - after).astype(jnp.bfloat16)
        acc[...] = acc[...] * jnp.exp2(before - after) + matmul(
            weights, values[pl.ds(start, CHUNK), :]
        )
        top[...] = jnp.broadcast_to(after, top.shape)

    @pl.loop(0, full)
    def _(at):
        step(pl.multiple_of(at * CHUNK, CHUNK), False)

    step(last, True)
    total = acc[:, 128:]
    mixed = acc[:, :128] / total
    for h in range(HEAD_GROUP):
        mixed_ref[:, h * 128 : (h + 1) * 128] = mixed[h * TILE : (h + 1) * TILE].astype(jnp.bfloat16)
    log_ref[0, 0] = (top[...] + jnp.log2(total)).T[:8]

    @pl.when(
        (pl.program_id(0) == pl.num_programs(0) - 1) & (pl.program_id(1) == pl.num_programs(1) - 1)
    )
    def _():
        keep_own.wait()
        exchange.end()
        exchange.drain()


def attend(queries, kv, low, grads):
    tok_rows, width = queries.shape
    tiles, groups = tok_rows // TILE, width // (128 * HEAD_GROUP)
    lanes, rows = 128 * HEAD_GROUP, TILE * HEAD_GROUP
    tile_spec = pl.BlockSpec((TILE, lanes), lambda i, g: (i, g))
    hbm = pl.BlockSpec(memory_space=pl.ANY)
    pairs = tok_rows * (width // 128) * 2560
    return pl.pallas_call(
        functools.partial(attend_kernel, tok_rows),
        out_shape=(
            jax.ShapeDtypeStruct((tok_rows, width), jnp.bfloat16),
            jax.ShapeDtypeStruct((tiles, groups, 8, rows), jnp.float32),
            jax.ShapeDtypeStruct((4,) + grads.shape, jnp.bfloat16),
        ),
        grid=(tiles, groups),
        in_specs=[
            tile_spec,
            pl.BlockSpec(kv.shape, lambda i, g: (0, 0)),
            pl.BlockSpec((TILE, 128), lambda i, g: (i, 0)),
            hbm,
        ],
        out_specs=[
            tile_spec,
            pl.BlockSpec((1, 1, 8, rows), lambda i, g: (i, g, 0, 0)),
            hbm,
        ],
        scratch_shapes=[
            pltpu.VMEM(kv.shape, jnp.bfloat16),
            pltpu.VMEM((rows, 128), jnp.float32),
            pltpu.VMEM((rows, 256), jnp.float32),
            pltpu.VMEM(grads.shape, jnp.bfloat16),
            pltpu.SemaphoreType.DMA((2, 4)),
            pltpu.SemaphoreType.DMA,
        ],
        compiler_params=pltpu.CompilerParams(
            collective_id=4, has_side_effects=True, vmem_limit_bytes=40 << 20
        ),
        cost_estimate=pl.CostEstimate(
            flops=pairs * 3000, transcendentals=pairs, bytes_accessed=16 << 20
        ),
        name="attend",
    )(queries, kv, low, grads)


def attend_back_kernel(
    fsdp_size,
    tok_rows,
    q_ref,
    kv_ref,
    cos_ref,
    sin_ref,
    low_ref,
    mixed_ref,
    d_mixed_ref,
    log_ref,
    rows_ref,
    branch_ref,
    d_q_ref,
    d_kv_ref,
    output_ref,
    sums,
    d_q,
    *refs,
):
    scale = 128**-0.5
    factor = scale * LOG2E
    at_end = (pl.program_id(0) == pl.num_programs(0) - 1) & (
        pl.program_id(1) == pl.num_programs(1) - 1
    )

    place = position(fsdp_size)
    grad = make_collect(place, refs)
    count = place[4]

    def begin():
        sums[...] = jnp.zeros_like(sums)
        greet(*place[:3], count)
        outer(grad, rows_ref, branch_ref, False)
        outer(grad, rows_ref, branch_ref, True)

    def cores():
        for shard in range(count):
            grad.core_add(shard)
            grad.diag_start(shard)

    def sum_quarters():
        each(count, grad.quarter_add)
        grad.line_hop(count - 1)

    def hops():
        for hop in range(count - 2, 0, -1):
            grad.line_hop(hop)

    def gather():
        grad.line_end()
        grad.gather_start()

    stages = {
        0: begin,
        1: cores,
        5: lambda: each(count, grad.quarter_start),
        10: sum_quarters,
        11: hops,
        12: gather,
        14: grad.gather_relay,
    }
    now = pl.program_id(0) * pl.num_programs(1) + pl.program_id(1)
    for step_at, stage in stages.items():
        pl.when(now == step_at)(stage)

    first, full, last = chunk_plan(tok_rows)
    queries = stack_heads(q_ref[...])
    d_rows = stack_heads(d_mixed_ref[...])
    mixed = stack_heads(mixed_ref[...])
    rows = queries.shape[0]
    products = d_rows.astype(jnp.float32) * mixed.astype(jnp.float32)
    delta = jnp.sum(products.T, axis=0, keepdims=True)
    log_total = log_ref[0, 0, :1]
    d_q[...] = jnp.zeros_like(d_q)

    def step(start, masked):
        keys = kv_ref[pl.ds(start, CHUNK), :128]
        values = kv_ref[pl.ds(start, CHUNK), 128:]
        scores = contract(keys, queries, 1, 1) * factor
        probs = jnp.exp2(scores - log_total)
        if masked:
            key_at = start + lax.broadcasted_iota(jnp.int32, (CHUNK, rows), 0)
            row_at = lax.broadcasted_iota(jnp.int32, (1, rows), 1) % TILE + first
            low = jnp.concatenate([low_ref[:1]] * HEAD_GROUP, axis=1)
            probs = jnp.where((key_at <= row_at) & (key_at >= low), probs, 0.0)
        d_probs = contract(values, d_rows, 1, 1)
        d_scores = (probs * (d_probs - delta)).astype(jnp.bfloat16)
        sums[pl.ds(start, CHUNK), 128:] += matmul(probs.astype(jnp.bfloat16), d_rows)
        sums[pl.ds(start, CHUNK), :128] += matmul(d_scores, queries)
        d_q[...] += contract(d_scores, keys, 0, 0)

    @pl.loop(0, full)
    def _(at):
        step(pl.multiple_of(at * CHUNK, CHUNK), False)

    step(last, True)
    cos_table, sin_table = cos_ref[...] * scale, sin_ref[...] * scale
    for h in range(HEAD_GROUP):
        turned = d_q[h * TILE : (h + 1) * TILE]
        raw = turned * cos_table - pltpu.roll(turned, 64, 1) * sin_table
        d_q_ref[:, h * 128 : (h + 1) * 128] = raw.astype(jnp.bfloat16)

    @pl.when(at_end)
    def _():
        d_kv_ref[:, :128] = (sums[:, :128] * scale).astype(jnp.bfloat16)
        d_kv_ref[:, 128:] = sums[:, 128:].astype(jnp.bfloat16)
        grad.gather_end()
        output_ref[...] = grad.full[...].astype(jnp.float32)
        grad.drain()


def attend_back(queries, kv, cos_table, sin_table, low, mixed, d_mixed, logs, d_branch):
    tok_rows, width = queries.shape
    fsdp_size = lax.axis_size("fsdp")
    shard = width // fsdp_size
    tiles, groups = tok_rows // TILE, width // (128 * HEAD_GROUP)
    lanes, rows = 128 * HEAD_GROUP, TILE * HEAD_GROUP
    tile_spec = pl.BlockSpec((TILE, lanes), lambda i, g: (i, g))
    row_spec = pl.BlockSpec((TILE, 128), lambda i, g: (i, 0))
    whole = pl.BlockSpec(kv.shape, lambda i, g: (0, 0))
    pairs = tok_rows * (width // 128) * 2560
    return pl.pallas_call(
        functools.partial(attend_back_kernel, fsdp_size, tok_rows),
        out_shape=(
            jax.ShapeDtypeStruct((tok_rows, width), jnp.bfloat16),
            jax.ShapeDtypeStruct(kv.shape, jnp.bfloat16),
            jax.ShapeDtypeStruct((shard, width), jnp.float32),
        ),
        grid=(tiles, groups),
        in_specs=[
            tile_spec,
            whole,
            row_spec,
            row_spec,
            pl.BlockSpec((8, TILE), lambda i, g: (0, i)),
            tile_spec,
            tile_spec,
            pl.BlockSpec((1, 1, 8, rows), lambda i, g: (i, g, 0, 0)),
            pl.BlockSpec(mixed.shape, lambda i, g: (0, 0)),
            pl.BlockSpec(mixed.shape, lambda i, g: (0, 0)),
        ],
        out_specs=[tile_spec, whole, pl.BlockSpec((shard, width), lambda i, g: (0, 0))],
        scratch_shapes=[
            pltpu.VMEM(kv.shape, jnp.float32),
            pltpu.VMEM((rows, 128), jnp.float32),
        ]
        + collect_scratch(fsdp_size, shard, width),
        compiler_params=pltpu.CompilerParams(
            collective_id=1, has_side_effects=True, vmem_limit_bytes=50 << 20
        ),
        cost_estimate=pl.CostEstimate(
            flops=pairs * 3000, transcendentals=pairs, bytes_accessed=16 << 20
        ),
        name="attend_back",
    )(queries, kv, cos_table, sin_table, low, mixed, d_mixed, logs, mixed, d_branch)


class Chain:
    def __init__(self, place, count, at, replica, fsdp, sends, recvs):
        self.place, self.count, self.at = place, count, at
        self.replica, self.fsdp, self.sends, self.recvs = replica, fsdp, sends, recvs

    def copy(self, shard, way):
        target = self.fsdp + (2 if way == 0 else -2)
        return pltpu.make_async_remote_copy(
            src_ref=self.place(shard),
            dst_ref=self.place(shard),
            send_sem=self.sends.at[way, shard],
            recv_sem=self.recvs.at[way, shard],
            device_id=(self.replica, target),
            device_id_type=MESH,
        )

    def begin(self):
        @pl.when(self.at < self.count - 1)
        def _():
            self.copy(self.at, 0).start()

        @pl.when(self.at > 0)
        def _():
            self.copy(self.at, 1).start()

    def step(self, hop, arrived=None):
        left, right = self.at - hop, self.at + hop

        @pl.when(left >= 0)
        def _():
            self.copy(left, 0).wait_recv()

        @pl.when((left >= 0) & (self.at < self.count - 1))
        def _():
            self.copy(left, 0).start()

        if arrived is not None:

            @pl.when(left >= 0)
            def _():
                arrived(left)

        @pl.when(right < self.count)
        def _():
            self.copy(right, 1).wait_recv()

        @pl.when((right < self.count) & (self.at > 0))
        def _():
            self.copy(right, 1).start()

        if arrived is not None:

            @pl.when(right < self.count)
            def _():
                arrived(right)

    def finish(self):
        for hop in range(self.count):

            @pl.when((self.at - hop >= 0) & (self.at < self.count - 1))
            def _(hop=hop):
                self.copy(self.at - hop, 0).wait_send()

            @pl.when((self.at + hop < self.count) & (self.at > 0))
            def _(hop=hop):
                self.copy(self.at + hop, 1).wait_send()


class Spread:
    def __init__(self, buffer, count, at, core, replica, fsdp, sems):
        self.buffer, self.count, self.at, self.core = buffer, count, at, core
        self.replica, self.fsdp, self.sems = replica, fsdp, sems
        self.rows = buffer.shape[1] // 4

    def rows_of(self, shard, copy, half=None):
        start, size = copy * self.rows, self.rows
        if half is not None:
            size = size // 2
            start = start + half * size
        return self.buffer.at[2 * shard + self.core, pl.ds(start, size)]

    def copy(self, kind, shard):
        beside, across = flip(self.replica, 1), flip(self.replica, 2)
        if kind == 0:
            ref, target = self.rows_of(shard, self.replica), (beside, self.fsdp)
        elif kind == 1:
            ref, target = self.rows_of(shard, self.replica), (across, self.fsdp)
        elif kind == 2:
            ref, target = self.rows_of(shard, beside, 0), (across, self.fsdp)
        elif kind == 3:
            ref, target = self.rows_of(shard, across, 1), (beside, self.fsdp)
        else:
            ref, target = self.buffer.at[2 * shard + self.core], (self.replica, flip(self.fsdp, 1))
        return pltpu.make_async_remote_copy(
            src_ref=ref,
            dst_ref=ref,
            send_sem=self.sems.at[0, kind, shard],
            recv_sem=self.sems.at[1, kind, shard],
            device_id=target,
            device_id_type=MESH,
        )

    def recv(self, kind, shard):
        beside, across = flip(self.replica, 1), flip(self.replica, 2)
        if kind == 0:
            ref = self.rows_of(shard, beside)
        elif kind == 1:
            ref = self.rows_of(shard, across)
        elif kind < 4:
            ref = self.rows_of(shard, flip(beside, 2), kind - 2)
        else:
            ref = self.buffer.at[2 * shard + 1 - self.core]
        return pltpu.make_async_remote_copy(
            src_ref=ref,
            dst_ref=ref,
            send_sem=self.sems.at[0, kind, shard],
            recv_sem=self.sems.at[1, kind, shard],
            device_id=(self.replica, flip(self.fsdp, 1)),
            device_id_type=MESH,
        )

    def arrived(self, shard):
        self.copy(0, shard).start()
        self.copy(1, shard).start()

    def others(self):
        return [(self.at + hop) % self.count for hop in range(1, self.count)]

    def relay(self):
        for shard in self.others():
            self.recv(0, shard).wait_recv()
            self.copy(2, shard).start()
            self.recv(1, shard).wait_recv()
            self.copy(3, shard).start()

    def cores(self):
        self.copy(4, self.at).start()
        for shard in self.others():
            self.recv(2, shard).wait_recv()
            self.recv(3, shard).wait_recv()
            self.copy(4, shard).start()

    def finish(self):
        for shard in self.others() + [self.at]:
            self.recv(4, shard).wait_recv()
        for shard in self.others():
            for kind in range(5):
                self.copy(kind, shard).wait_send()
        self.copy(4, self.at).wait_send()


def project_kernel(
    fsdp_size,
    tokens_ref,
    wq_ref,
    wo_ref,
    kvg_ref,
    cos_ref,
    sin_ref,
    q_ref,
    normed_ref,
    gain_ref,
    wq_all,
    wo_all,
    kvg_all,
    kv_all,
    wq_vmem,
    kvg_vmem,
    kv_vmem,
    local_sems,
    kvg_sems,
    kvg_core,
    wq_line,
    wq_sems,
    wo_line,
    wo_sems,
    kv_sems,
    kv_core,
):
    replica, fsdp = lax.axis_index("replica"), lax.axis_index("fsdp")
    count, at, core = fsdp_size // 2, fsdp // 2, fsdp % 2
    width = tokens_ref.shape[1]
    partner = (replica, flip(fsdp, 1))

    spare = flip(fsdp, 1)
    load_own = [
        pltpu.make_async_copy(kvg_ref, kvg_vmem.at[fsdp], local_sems.at[0]),
        pltpu.make_async_copy(wq_ref, wq_vmem.at[fsdp], local_sems.at[1]),
        pltpu.make_async_copy(wo_ref, wq_vmem.at[spare], local_sems.at[2]),
    ]
    own = [
        pltpu.make_async_copy(kvg_vmem.at[fsdp], kvg_all.at[fsdp], local_sems.at[0]),
        pltpu.make_async_copy(wq_vmem.at[fsdp], wq_all.at[fsdp], local_sems.at[1]),
        pltpu.make_async_copy(wq_vmem.at[spare], wo_all.at[fsdp], local_sems.at[2]),
    ]
    for copy in load_own:
        copy.start()
    for load, copy in zip(load_own, own):
        load.wait()
        copy.start()
    greet(replica, fsdp, at, count)

    def core_copy(buffer, sems, shard, lands=False):
        ref = buffer.at[2 * shard + (1 - core if lands else core)]
        return pltpu.make_async_remote_copy(
            src_ref=ref,
            dst_ref=ref,
            send_sem=sems.at[0, shard],
            recv_sem=sems.at[1, shard],
            device_id=partner,
            device_id_type=MESH,
        )

    def line(place, sems):
        return Chain(place, count, at, replica, fsdp, sems.at[0], sems.at[1])

    kvg = line(lambda shard: kvg_all.at[2 * shard + core], kvg_sems)
    kv = line(lambda shard: kv_all.at[2 * shard + core], kv_sems)
    wq = Spread(wq_all, count, at, core, replica, fsdp, wq_sems)
    wo = Spread(wo_all, count, at, core, replica, fsdp, wo_sems)
    wq_chain = line(lambda shard: wq.rows_of(shard, replica), wq_line)
    wo_chain = line(lambda shard: wo.rows_of(shard, replica), wo_line)
    own[0].wait()
    kvg.begin()
    core_copy(kvg_all, kvg_core, at).start()
    own[1].wait()
    wq_chain.begin()
    own[2].wait()
    wo_chain.begin()

    inputs = tokens_ref[...].astype(jnp.float32)
    inverse = lax.rsqrt(jnp.mean(inputs * inputs, axis=1, keepdims=True) + EPSILON)

    for hop in range(1, count):
        kvg.step(hop, lambda shard: core_copy(kvg_all, kvg_core, shard).start())
        wq_chain.step(hop, wq.arrived)
        wo_chain.step(hop, wo.arrived)
    for shard in range(count):
        core_copy(kvg_all, kvg_core, shard, True).wait_recv()
    load = pltpu.make_async_copy(kvg_all, kvg_vmem, local_sems.at[0])
    load.start()
    load.wait()
    table = kvg_vmem[...].reshape(width, kvg_vmem.shape[2])
    gains = table[:, 256:].astype(jnp.float32).T[:8]
    gain_ref[...] = gains
    normed_ref[...] = (inputs * inverse * gains[:1]).astype(jnp.bfloat16)
    kv_raw = matmul(normed_ref[...], table[:, :256])
    cos_table, sin_table = cos_ref[...], sin_ref[...]
    key_raw = kv_raw[:, :128]
    key_rot = key_raw * cos_table + pltpu.roll(key_raw, 64, 1) * sin_table
    kv_vmem[:, :128] = key_rot.astype(jnp.bfloat16)
    kv_vmem[:, 128:] = kv_raw[:, 128:].astype(jnp.bfloat16)
    store = pltpu.make_async_copy(kv_vmem, kv_all.at[fsdp], local_sems.at[0])
    store.start()
    store.wait()
    kv.begin()
    core_copy(kv_all, kv_core, at).start()
    wq.relay()
    kv.step(1, lambda shard: core_copy(kv_all, kv_core, shard).start())
    wq.cores()
    wo.relay()
    for shard in wq.others() + [at]:
        wq.recv(4, shard).wait_recv()
    load = pltpu.make_async_copy(wq_all, wq_vmem, local_sems.at[1])
    load.start()
    for hop in range(2, count):
        kv.step(hop, lambda shard: core_copy(kv_all, kv_core, shard).start())
    load.wait()
    weight = wq_vmem.reshape(width, width)

    def columns(block):
        start = pl.multiple_of(block * 512, 512)
        raw = matmul(normed_ref[...], weight[:, pl.ds(start, 512)])
        for h in range(4):
            head = raw[:, h * 128 : (h + 1) * 128]
            turned = head * cos_table + pltpu.roll(head, 64, 1) * sin_table
            q_ref[:, pl.ds(start + h * 128, 128)] = turned.astype(jnp.bfloat16)

    pl.loop(0, width // 512)(columns)
    wo.cores()
    for shard in range(count):
        core_copy(kv_all, kv_core, shard, True).wait_recv()
    wo.finish()
    for shard in wq.others():
        for kind in range(5):
            wq.copy(kind, shard).wait_send()
    wq.copy(4, at).wait_send()
    for shard in range(count):
        core_copy(kvg_all, kvg_core, shard).wait_send()
        core_copy(kv_all, kv_core, shard).wait_send()
    for chain in (kvg, kv, wq_chain, wo_chain):
        chain.finish()


def project(tokens, wq, wo, kvg, cos_table, sin_table):
    rows, width = tokens.shape
    shard = wq.shape[0]
    fsdp_size = lax.axis_size("fsdp")
    count = fsdp_size // 2
    low = jnp.bfloat16
    vmem, hbm = pl.BlockSpec(memory_space=pltpu.VMEM), pl.BlockSpec(memory_space=pl.ANY)
    dma = pltpu.SemaphoreType.DMA
    return pl.pallas_call(
        functools.partial(project_kernel, fsdp_size),
        out_shape=(
            jax.ShapeDtypeStruct((rows, width), low),
            jax.ShapeDtypeStruct((rows, width), low),
            jax.ShapeDtypeStruct((8, width), jnp.float32),
            jax.ShapeDtypeStruct((fsdp_size, shard, width), low),
            jax.ShapeDtypeStruct((fsdp_size, shard, width), low),
            jax.ShapeDtypeStruct((fsdp_size, shard, kvg.shape[1]), low),
            jax.ShapeDtypeStruct((fsdp_size, rows, 256), low),
        ),
        in_specs=[vmem, hbm, hbm, hbm, vmem, vmem],
        out_specs=(vmem, vmem, vmem, hbm, hbm, hbm, hbm),
        scratch_shapes=[
            pltpu.VMEM((fsdp_size, shard, width), low),
            pltpu.VMEM((fsdp_size, shard, kvg.shape[1]), low),
            pltpu.VMEM((rows, 256), low),
            dma((3,)),
            dma((2, 2, count)),
            dma((2, count)),
            dma((2, 2, count)),
            dma((2, 5, count)),
            dma((2, 2, count)),
            dma((2, 5, count)),
            dma((2, 2, count)),
            dma((2, count)),
        ],
        compiler_params=pltpu.CompilerParams(
            collective_id=0, has_side_effects=True, vmem_limit_bytes=48 << 20
        ),
        cost_estimate=pl.CostEstimate(
            flops=2 * rows * width * (width + 256), transcendentals=0, bytes_accessed=40 << 20
        ),
        name="project",
    )(tokens, wq, wo, kvg, cos_table, sin_table)


def greet(replica, fsdp, at, count):
    barrier = pltpu.get_barrier_semaphore()
    for target in (
        (replica, flip(fsdp, 1)),
        (flip(replica, 1), fsdp),
        (flip(replica, 2), fsdp),
    ):
        pl.semaphore_signal(barrier, inc=1, device_id=target, device_id_type=MESH)

    @pl.when(at > 0)
    def _():
        pl.semaphore_signal(barrier, inc=1, device_id=(replica, fsdp - 2), device_id_type=MESH)

    @pl.when(at < count - 1)
    def _():
        pl.semaphore_signal(barrier, inc=1, device_id=(replica, fsdp + 2), device_id_type=MESH)

    inside = (at > 0) & (at < count - 1)

    @pl.when(inside)
    def _():
        pl.semaphore_wait(barrier, 5)

    @pl.when(jnp.logical_not(inside))
    def _():
        pl.semaphore_wait(barrier, 4)


def add_into(ref, index, *others):
    total = ref[index].astype(jnp.float32)
    for other in others:
        total = total + other.astype(jnp.float32)
    ref[index] = total.astype(ref.dtype)


class Collect:
    def __init__(self, place, grad, core_in, line_in, core_sems, line_sems, copies=None):
        self.replica, self.fsdp, self.at, self.core, self.count = place
        self.grad, self.core_in, self.line_in = grad, core_in, line_in
        self.core_sems, self.line_sems = core_sems, line_sems
        self.beside, self.across = flip(self.replica, 1), flip(self.replica, 2)
        self.opposite = flip(self.beside, 2)
        if copies is None:
            self.rows = pl.ds(0, grad.shape[1])
        else:
            self.diag_in, self.quarter_in, self.full = copies[:3]
            self.diag_sems, self.quarter_sems, self.full_sems = copies[3:]
            self.size = grad.shape[1] // 4
            self.rows = self.quarter(self.replica)

    def quarter(self, copy, half=None):
        size = self.size if half is None else self.size // 2
        start = copy * self.size + (0 if half is None else half * size)
        return pl.ds(pl.multiple_of(start, size), size)

    def remote(self, src, dst, sems, index, target):
        return pltpu.make_async_remote_copy(
            src_ref=src,
            dst_ref=dst,
            send_sem=sems.at[(0,) + index],
            recv_sem=sems.at[(1,) + index],
            device_id=target,
            device_id_type=MESH,
        )

    def core_copy(self, shard):
        return self.remote(
            self.grad.at[2 * shard + 1 - self.core],
            self.core_in.at[shard],
            self.core_sems,
            (shard,),
            (self.replica, flip(self.fsdp, 1)),
        )

    def core_add(self, shard):
        self.core_copy(shard).wait_recv()
        add_into(self.grad, 2 * shard + self.core, self.core_in[shard])

    def diag_copy(self, shard, half):
        return self.remote(
            self.grad.at[2 * shard + self.core, self.quarter(self.opposite, half)],
            self.diag_in.at[half, shard],
            self.diag_sems,
            (half, shard),
            (self.beside if half == 0 else self.across, self.fsdp),
        )

    def diag_start(self, shard):
        self.diag_copy(shard, 0).start()
        self.diag_copy(shard, 1).start()

    def quarter_copy(self, shard, way):
        return self.remote(
            self.grad.at[2 * shard + self.core, self.quarter(self.across if way else self.beside)],
            self.quarter_in.at[way, shard],
            self.quarter_sems,
            (way, shard),
            (self.across if way else self.beside, self.fsdp),
        )

    def quarter_start(self, shard):
        at = 2 * shard + self.core
        for half, copy in ((0, self.across), (1, self.beside)):
            self.diag_copy(shard, half).wait_recv()
            add_into(self.grad, (at, self.quarter(copy, half)), self.diag_in[half, shard])
            self.quarter_copy(shard, 1 - half).start()

    def quarter_add(self, shard):
        self.quarter_copy(shard, 0).wait_recv()
        self.quarter_copy(shard, 1).wait_recv()
        add_into(
            self.grad,
            (2 * shard + self.core, self.rows),
            self.quarter_in[0, shard],
            self.quarter_in[1, shard],
        )

    def line_copy(self, shard, way):
        return self.remote(
            self.grad.at[2 * shard + self.core, self.rows],
            self.line_in.at[way, shard],
            self.line_sems,
            (way, shard),
            (self.replica, self.fsdp + (2 if way == 0 else -2)),
        )

    def line_receive(self, shard, way):
        self.line_copy(shard, way).wait_recv()
        add_into(self.grad, (2 * shard + self.core, self.rows), self.line_in[way, shard])

    def line_hop(self, hop):
        for way, shard, there, fed in (
            (0, self.at + hop, self.at + hop < self.count, self.at > 0),
            (1, self.at - hop, self.at - hop >= 0, self.at < self.count - 1),
        ):

            @pl.when(there & fed)
            def _(shard=shard, way=way):
                self.line_receive(shard, way)

            @pl.when(there)
            def _(shard=shard, way=way):
                self.line_copy(shard, way).start()

    def line_end(self):
        @pl.when(self.at > 0)
        def _():
            self.line_receive(self.at, 0)

        @pl.when(self.at < self.count - 1)
        def _():
            self.line_receive(self.at, 1)

    def full_copy(self, kind):
        own = self.replica
        rows, target = (
            (self.quarter(own), self.beside),
            (self.quarter(own), self.across),
            (self.quarter(self.beside, 0), self.across),
            (self.quarter(self.across, 1), self.beside),
        )[kind]
        return self.remote(
            self.full.at[rows],
            self.full.at[rows],
            self.full_sems,
            (kind,),
            (target, self.fsdp),
        )

    def full_recv(self, kind):
        rows = (
            self.quarter(self.beside),
            self.quarter(self.across),
            self.quarter(self.opposite, 0),
            self.quarter(self.opposite, 1),
        )[kind]
        ref = self.full.at[rows]
        self.remote(ref, ref, self.full_sems, (kind,), (self.beside, self.fsdp)).wait_recv()

    def gather_start(self):
        self.full[self.rows] = self.grad[2 * self.at + self.core, self.rows]
        self.full_copy(0).start()
        self.full_copy(1).start()

    def gather_relay(self):
        self.full_recv(0)
        self.full_copy(2).start()
        self.full_recv(1)
        self.full_copy(3).start()

    def gather_end(self):
        self.full_recv(2)
        self.full_recv(3)

    def drain(self):
        for shard in range(self.count):
            self.core_copy(shard).wait_send()
            if hasattr(self, "size"):
                for way in (0, 1):
                    self.diag_copy(shard, way).wait_send()
                    self.quarter_copy(shard, way).wait_send()
        for hop in range(1, self.count):

            @pl.when(self.at + hop < self.count)
            def _(hop=hop):
                self.line_copy(self.at + hop, 0).wait_send()

            @pl.when(self.at - hop >= 0)
            def _(hop=hop):
                self.line_copy(self.at - hop, 1).wait_send()

        if hasattr(self, "size"):
            for kind in range(4):
                self.full_copy(kind).wait_send()


def collect_scratch(fsdp_size, rows, width, copies=True):
    count = fsdp_size // 2
    low, dma = jnp.bfloat16, pltpu.SemaphoreType.DMA
    size = rows // 4 if copies else rows
    shapes = [
        pltpu.VMEM((fsdp_size, rows, width), low),
        pltpu.VMEM((count, rows, width), low),
        pltpu.VMEM((2, count, size, width), low),
        dma((2, count)),
        dma((2, 2, count)),
    ]
    if copies:
        shapes += [
            pltpu.VMEM((2, count, size // 2, width), low),
            pltpu.VMEM((2, count, size, width), low),
            pltpu.VMEM((rows, width), low),
            dma((2, 2, count)),
            dma((2, 2, count)),
            dma((2, 4)),
        ]
    return shapes


def make_collect(place, refs, copies=True):
    return Collect(place, *refs[:5], copies=refs[5:11] if copies else None)


def position(fsdp_size):
    replica, fsdp = lax.axis_index("replica"), lax.axis_index("fsdp")
    return replica, fsdp, fsdp // 2, fsdp % 2, fsdp_size // 2


def outer(collect, left_ref, right_ref, own_core):
    rows = collect.grad.shape[1]
    core = collect.core if own_core else 1 - collect.core

    @pl.loop(0, collect.count)
    def _(shard):
        start = pl.multiple_of((2 * shard + core) * rows, rows)
        part = contract(left_ref[:, pl.ds(start, rows)], right_ref[...], 0, 0)
        collect.grad[2 * shard + core] = part.astype(jnp.bfloat16)
        if not own_core:
            collect.core_copy(shard).start()


def each(count, step):
    for shard in range(count):
        step(shard)


def finish_kernel(
    fsdp_size,
    normed_ref,
    d_q_ref,
    tokens_ref,
    d_hidden_ref,
    gain_ref,
    term_ref,
    cos_ref,
    sin_ref,
    d_kv_ref,
    wq_ref,
    kvg_ref,
    ffn_ref,
    input_grad_ref,
    q_grad_ref,
    kv_grad_ref,
    ffn_all,
    wq_buf,
    kvg_vmem,
    d_kv_raw,
    term_sum,
    hidden_buf,
    local_sems,
    ffn_sems,
    *refs,
):
    place = position(fsdp_size)
    replica, fsdp, at, core, count = place
    greet(replica, fsdp, at, count)
    q_sums = make_collect(place, refs[:11])
    kv_sums = make_collect(place, refs[11:22])
    d_kv = make_collect(place, refs[22:27], False)
    beside, across = flip(replica, 1), flip(replica, 2)
    width = tokens_ref.shape[1]
    half = width // 2

    def ffn_copy(kind, lands=False):
        piece = (replica, replica, beside, across)[kind]
        if lands:
            piece = (beside, across, flip(beside, 2), flip(beside, 2))[kind]
        columns = (slice(None), slice(None), pl.ds(0, half), pl.ds(half, half))[kind]
        dst = ffn_all.at[piece, :, :, columns]
        return pltpu.make_async_remote_copy(
            src_ref=ffn_ref if kind < 2 and not lands else dst,
            dst_ref=dst,
            send_sem=ffn_sems.at[0, kind],
            recv_sem=ffn_sems.at[1, kind],
            device_id=((beside, across, across, beside)[kind], fsdp),
            device_id_type=MESH,
        )

    ffn_copy(0).start()
    ffn_copy(1).start()
    ffn_rows = ffn_ref.shape[1]

    def keep_ffn(part, slot, out):
        held = wq_buf.at[slot, pl.ds(0, ffn_rows)]
        place_at = ffn_all.at[replica, part]
        return pltpu.make_async_copy(
            held if out else ffn_ref.at[part], place_at if out else held, local_sems.at[0]
        )

    load = pltpu.make_async_copy(d_kv_ref, d_kv.grad, local_sems.at[1])
    load.start()
    load_kvg = pltpu.make_async_copy(kvg_ref, kvg_vmem, local_sems.at[2])
    load_kvg.start()
    load.wait()
    each(count, lambda shard: d_kv.core_copy(shard).start())
    outer(q_sums, normed_ref, d_q_ref, False)
    for part in range(3):
        for out in (False, True):
            keep_ffn(part, 0, out).start()
            keep_ffn(part, 0, out).wait()
    each(count, d_kv.core_add)
    d_kv.line_hop(count - 1)
    outer(q_sums, normed_ref, d_q_ref, True)
    for hop in range(count - 2, 0, -1):
        d_kv.line_hop(hop)
    for shard in range(count):
        q_sums.core_add(shard)
        q_sums.diag_start(shard)
    d_kv.line_end()
    each(count, q_sums.quarter_start)

    summed = d_kv.grad[fsdp].astype(jnp.float32)
    d_key = summed[:, :128]
    d_key = d_key * cos_ref[...] - pltpu.roll(d_key, 64, 1) * sin_ref[...]
    d_kv_raw[:, :128] = d_key.astype(jnp.bfloat16)
    d_kv_raw[:, 128:] = summed[:, 128:].astype(jnp.bfloat16)
    load_kvg.wait()
    rows = kvg_vmem.shape[1]

    def fetch(shard):
        return pltpu.make_async_copy(wq_ref.at[shard], wq_buf.at[shard % 2], local_sems.at[shard % 2])

    fetch(0).start()
    for shard in range(fsdp_size):
        fetch(shard).wait()
        if shard + 1 < fsdp_size:
            fetch(shard + 1).start()
        input_grad_ref[:, shard * rows : (shard + 1) * rows] = contract(
            d_q_ref[...], wq_buf[shard % 2], 1, 1
        ) + contract(d_kv_raw[...], kvg_vmem[shard, :, :256], 1, 1)
    for kind in (0, 1):
        ffn_copy(kind, True).wait_recv()
        ffn_copy(2 + kind).start()
    each(count, q_sums.quarter_add)
    for hop in range(count - 1, 0, -1):
        q_sums.line_hop(hop)

    term_sum[...] = jnp.zeros_like(term_sum)

    @pl.loop(0, tokens_ref.shape[0] // 128)
    def _(block):
        part = pl.ds(pl.multiple_of(block * 128, 128), 128)
        fetch_hidden = pltpu.make_async_copy(d_hidden_ref.at[part], hidden_buf, local_sems.at[0])
        fetch_hidden.start()
        d_normed = input_grad_ref[part]
        inputs = tokens_ref[part].astype(jnp.float32)
        inverse = lax.rsqrt(jnp.mean(inputs * inputs, axis=1, keepdims=True) + EPSILON)
        scaled = d_normed * gain_ref[:1]
        inner = jnp.mean(scaled * inputs, axis=1, keepdims=True)
        term_sum[:1] += jnp.sum(d_normed * inputs * inverse, axis=0, keepdims=True)
        step = inverse * scaled - inputs * (inverse**3 * inner)
        fetch_hidden.wait()
        input_grad_ref[part] = hidden_buf[...] + step

    term = term_sum[:1]
    line = lax.broadcasted_iota(jnp.int32, (128, width), 0)
    terms = jnp.where(line == 0, term, jnp.where(line == 1, term_ref[:1], 0.0)).T
    terms = terms.astype(jnp.bfloat16)
    for shard in range(fsdp_size):
        left = normed_ref[:, shard * rows : (shard + 1) * rows]
        kv_sums.grad[shard, :, :256] = contract(left, d_kv_raw[...], 0, 0).astype(jnp.bfloat16)
        kv_sums.grad[shard, :, 256:] = terms[shard * rows : (shard + 1) * rows]
    each(count, lambda shard: kv_sums.core_copy(shard).start())
    q_sums.line_end()
    q_sums.gather_start()
    for shard in range(count):
        kv_sums.core_add(shard)
        kv_sums.diag_start(shard)
    each(count, kv_sums.quarter_start)
    q_sums.gather_relay()
    each(count, kv_sums.quarter_add)
    for hop in range(count - 1, 0, -1):
        kv_sums.line_hop(hop)
    kv_sums.line_end()
    kv_sums.gather_start()
    q_sums.gather_end()
    q_grad_ref[...] = q_sums.full[...].astype(jnp.float32)
    kv_sums.gather_relay()
    kv_sums.gather_end()
    kv_grad_ref[...] = kv_sums.full[...].astype(jnp.float32)
    for kind in (2, 3):
        ffn_copy(kind, True).wait_recv()
    for kind in range(4):
        ffn_copy(kind).wait_send()
    for sums in (q_sums, kv_sums, d_kv):
        sums.drain()


def finish(
    normed, d_q, tokens, d_hidden, gains, term, cos_table, sin_table, d_kv, wq_all, kvg_all, ffn
):
    fsdp_size, rows, width = wq_all.shape
    tok_rows = tokens.shape[0]
    low, dma = jnp.bfloat16, pltpu.SemaphoreType.DMA
    vmem, hbm = pl.BlockSpec(memory_space=pltpu.VMEM), pl.BlockSpec(memory_space=pl.ANY)
    return pl.pallas_call(
        functools.partial(finish_kernel, fsdp_size),
        out_shape=(
            jax.ShapeDtypeStruct((tok_rows, width), jnp.float32),
            jax.ShapeDtypeStruct((rows, width), jnp.float32),
            jax.ShapeDtypeStruct((rows, 384), jnp.float32),
            jax.ShapeDtypeStruct((4,) + ffn.shape, low),
        ),
        in_specs=[vmem] * 3 + [hbm] + [vmem] * 4 + [hbm] * 4,
        out_specs=(vmem, vmem, vmem, hbm),
        scratch_shapes=[
            pltpu.VMEM((2, rows, width), low),
            pltpu.VMEM((fsdp_size, rows, 384), low),
            pltpu.VMEM((tok_rows, 256), low),
            pltpu.VMEM((8, width), jnp.float32),
            pltpu.VMEM((128, width), jnp.float32),
            dma((3,)),
            dma((2, 4)),
        ]
        + collect_scratch(fsdp_size, rows, width)
        + collect_scratch(fsdp_size, rows, 384)
        + collect_scratch(fsdp_size, tok_rows, 256, False),
        compiler_params=pltpu.CompilerParams(
            collective_id=2, has_side_effects=True, vmem_limit_bytes=54 << 20
        ),
        cost_estimate=pl.CostEstimate(
            flops=100 * tok_rows * width * width, transcendentals=0, bytes_accessed=40 << 20
        ),
        name="finish",
    )(normed, d_q, tokens, d_hidden, gains, term, cos_table, sin_table, d_kv, wq_all, kvg_all, ffn)


def swap(value, step):
    copies = lax.axis_size("replica")
    return lax.ppermute(value, "replica", [(r, r ^ step) for r in range(copies)])


def pass_on(beside, across, got):
    half = got.shape[1]
    low, wide = jnp.bfloat16, jnp.float32
    got = got.astype(wide)
    across = jnp.concatenate([across[:half].astype(wide) + got[0], across[half:].astype(wide)])
    beside = jnp.concatenate([beside[:half].astype(wide), beside[half:].astype(wide) + got[1]])
    return beside.astype(low), across.astype(low)


def gather_shards(value):
    return lax.all_gather(value, "fsdp", axis=0, tiled=True)


def scatter_shards(value):
    return lax.psum_scatter(value, "fsdp", scatter_dimension=0, tiled=True)


def after(value, *others):
    return lax.optimization_barrier((value, others))[0]


def quarter(shard, copy_index):
    rows = shard.shape[0] // lax.axis_size("replica")
    return lax.dynamic_slice_in_dim(shard, copy_index * rows, rows, 0)


def shards(
    tokens,
    segments,
    positions,
    query_weight,
    key_weight,
    value_weight,
    output_weight,
    attn_gain,
    gate_weight,
    up_weight,
    down_weight,
    ffn_gain,
    grad_out,
):
    tok_rows, model_width = tokens.shape
    head_dim = key_weight.shape[1]
    fsdp_size = lax.axis_size("fsdp")
    fsdp_index = lax.axis_index("fsdp")
    copy_index = lax.axis_index("replica")
    copies = lax.axis_size("replica")
    low = jnp.bfloat16

    w_down = gather_shards(quarter(down_weight, copy_index))
    cos_table, sin_table = rope_tables(positions, head_dim)
    gain_columns = jnp.stack([attn_gain, ffn_gain], axis=1)
    queries, normed, gains, wq_all, w_out, kvg_all, kv_all = project(
        tokens,
        query_weight,
        output_weight,
        jnp.concatenate(
            [key_weight, value_weight, jnp.pad(gain_columns, ((0, 0), (0, 126)))], axis=1
        ),
        cos_table,
        sin_table,
    )
    w_out = w_out.reshape(model_width, model_width)
    kv_all = kv_all.reshape(fsdp_size * tok_rows, 2 * head_dim)
    gain_ffn = gains[1]
    inputs = tokens.astype(jnp.float32)
    key_width = max(GROUP_TOK, tok_rows)
    window_start = fsdp_index * tok_rows // key_width * key_width
    one_group = fsdp_size * tok_rows == key_width
    kv = kv_all if one_group else lax.dynamic_slice_in_dim(kv_all, window_start, key_width, 0)

    row_at = fsdp_index * tok_rows - window_start + jnp.arange(tok_rows, dtype=jnp.int32)
    lowest = jnp.where(positions < PROMPT, 0, row_at - (positions - PROMPT))
    w_gate = gather_shards(after(quarter(gate_weight.T, copy_index), normed))
    w_up = gather_shards(after(quarter(up_weight.T, copy_index), normed))
    mixed_rows, logs, grads = attend(
        queries, kv, jnp.broadcast_to(lowest[:, None], (tok_rows, 128)), after(grad_out, w_down)
    )

    hidden = inputs + matmul(mixed_rows, w_out)
    normed_ffn_full, inverse_ffn = norm_forward(hidden, gain_ffn)
    normed_ffn = normed_ffn_full.astype(low)

    x_all, activation, d_gate, d_up, *parts = feed_forward(
        normed_ffn, grads, w_gate, w_up, w_down
    )
    own_part, own_out = parts[0], parts[4]
    beside, across = pass_on(*parts[1:4])
    all_rows = copies * tok_rows
    x_all, grads = x_all.reshape(all_rows, -1), grads.reshape(all_rows, -1)
    activation = activation.reshape(all_rows, -1)
    d_gate = after(d_gate, beside, across)
    gate_part = contract(d_gate.reshape(all_rows, -1), x_all, 0, 0).astype(low)
    beside, across = swap(beside, 1), swap(across, 2)
    d_up, activation = after((d_up, activation), gate_part, beside, across)
    d_normed_ffn = (
        own_part.astype(jnp.float32) + beside.astype(jnp.float32) + across.astype(jnp.float32)
    )
    up_part = contract(d_up.reshape(all_rows, -1), x_all, 0, 0).astype(low)
    down_part = contract(activation, grads, 0, 0).astype(low)

    cotangent = grad_out.astype(jnp.float32)
    resid_ffn, ffn_gain_term = norm_backward(hidden, inverse_ffn, gain_ffn, d_normed_ffn)
    d_hidden = cotangent + resid_ffn
    d_branch = d_hidden.astype(low)
    d_mixed = contract(d_branch, w_out, 1, 1).astype(low)
    d_mixed = after(d_mixed, gate_part, up_part, down_part)
    gate_sum = scatter_shards(gate_part)
    up_sum = scatter_shards(up_part)
    down_sum = scatter_shards(down_part)
    out_beside, out_across = pass_on(*after(parts[5:8], down_part))
    out_beside, out_across = after((out_beside, out_across), d_mixed)
    other_outs = [swap(out_beside, 1), swap(out_across, 2)]
    d_query_raw, d_kv, output_grad = attend_back(
        queries,
        kv,
        cos_table,
        sin_table,
        jnp.broadcast_to(lowest[None, :], (8, tok_rows)),
        mixed_rows,
        d_mixed,
        logs,
        d_branch,
    )
    layer_out = hidden + own_out.astype(jnp.float32)
    for part in after(other_outs, d_kv):
        layer_out = layer_out + part.astype(jnp.float32)
    layer_out = layer_out.astype(low)
    if not one_group:
        d_kv = lax.dynamic_update_slice_in_dim(
            jnp.zeros((fsdp_size * tok_rows, 2 * head_dim), low), d_kv, window_start, 0
        )
    input_grad, query_grad, kv_grad, ffn_all = finish(
        normed,
        d_query_raw,
        tokens,
        d_hidden,
        gains,
        jnp.broadcast_to(ffn_gain_term[None], (8, model_width)),
        cos_table,
        sin_table,
        d_kv.reshape(fsdp_size, tok_rows, 2 * head_dim),
        wq_all,
        kvg_all,
        jnp.stack([gate_sum, up_sum, down_sum]),
    )
    gate_grad, up_grad, down_grad = (
        ffn_all[:, i].reshape(-1, model_width).astype(jnp.float32) for i in range(3)
    )
    return (
        layer_out,
        input_grad,
        query_grad,
        kv_grad[:, :head_dim],
        kv_grad[:, head_dim : 2 * head_dim],
        output_grad,
        kv_grad[:, 2 * head_dim],
        gate_grad.T,
        up_grad.T,
        down_grad,
        kv_grad[:, 2 * head_dim + 1],
    )


def half_tables(pos_ids, head_dim):
    half_width = head_dim // 2
    frequency = ROPE_BASE ** (-jnp.arange(half_width, dtype=jnp.float32) * 2.0 / head_dim)
    angles = pos_ids.astype(jnp.float32)[:, None] * frequency[None, :]
    return (jnp.cos(angles), jnp.sin(angles))


def rotate(values, cos_table, sin_table):
    half_width = values.shape[-1] // 2
    front_half = values[..., :half_width]
    back_half = values[..., half_width:]
    return jnp.concatenate(
        [
            front_half * cos_table - back_half * sin_table,
            back_half * cos_table + front_half * sin_table,
        ],
        axis=-1,
    )


def any_shards(
    tokens,
    segments,
    positions,
    query_weight,
    key_weight,
    value_weight,
    output_weight,
    attn_gain,
    gate_weight,
    up_weight,
    down_weight,
    ffn_gain,
    grad_out,
):
    tok_rows, model_width = tokens.shape
    head_dim = key_weight.shape[1]
    head_count = model_width // head_dim
    block_count = head_count // HEAD_BLOCK
    block_width = HEAD_BLOCK * head_dim
    score_scale = head_dim ** (-0.5)
    fsdp_size = lax.axis_size("fsdp")
    fsdp_index = lax.axis_index("fsdp")
    gathered = (
        lax.all_gather(query_weight, "fsdp", axis=0, tiled=True),
        lax.all_gather(key_weight, "fsdp", axis=0, tiled=True),
        lax.all_gather(value_weight, "fsdp", axis=0, tiled=True),
        lax.all_gather(output_weight, "fsdp", axis=0, tiled=True),
        lax.all_gather(attn_gain, "fsdp", axis=0, tiled=True),
        lax.all_gather(ffn_gain, "fsdp", axis=0, tiled=True),
    )
    w_query, w_key, w_value, w_out, gain_attn, gain_ffn = gathered
    gain_attn = gain_attn.astype(jnp.float32)
    gain_ffn = gain_ffn.astype(jnp.float32)
    inputs = tokens.astype(jnp.float32)
    normed_full, inverse_attn = norm_forward(inputs, gain_attn)
    normed = normed_full.astype(jnp.bfloat16)
    query_raw = matmul(normed, w_query)
    key_raw = matmul(normed, w_key)
    value_rows = matmul(normed, w_value).astype(jnp.bfloat16)
    cos_table, sin_table = half_tables(positions, head_dim)
    queries = rotate(
        query_raw.reshape(tok_rows, head_count, head_dim), cos_table[:, None], sin_table[:, None]
    ).astype(jnp.bfloat16)
    key_rot = rotate(key_raw, cos_table, sin_table).astype(jnp.bfloat16)
    key_rows, value_all = (
        lax.all_gather(key_rot, "fsdp", axis=0, tiled=True),
        lax.all_gather(value_rows, "fsdp", axis=0, tiled=True),
    )
    seg_all, pos_all = (
        lax.all_gather(segments, "fsdp", axis=0, tiled=True),
        lax.all_gather(positions, "fsdp", axis=0, tiled=True),
    )
    key_width = max(GROUP_TOK, tok_rows)
    window_start = fsdp_index * tok_rows // GROUP_TOK * GROUP_TOK
    key_window = lax.dynamic_slice_in_dim(key_rows, window_start, key_width, 0)
    value_window = lax.dynamic_slice_in_dim(value_all, window_start, key_width, 0)
    seg_window = lax.dynamic_slice_in_dim(seg_all, window_start, key_width, 0)
    pos_window = lax.dynamic_slice_in_dim(pos_all, window_start, key_width, 0)
    key_index = window_start + jnp.arange(key_width, dtype=jnp.int32)
    query_index = fsdp_index * tok_rows + jnp.arange(tok_rows, dtype=jnp.int32)
    visible = (
        (key_index[None, :] // GROUP_TOK == query_index[:, None] // GROUP_TOK)
        & (pos_window[None, :] <= positions[:, None])
        & ((seg_window[None, :] == 0) | (seg_window[None, :] == segments[:, None]))
    )
    query_blocks = queries.reshape(tok_rows, block_count, block_width).transpose(1, 0, 2)

    def block_scores(query_block):
        flat_queries = query_block.reshape(tok_rows * HEAD_BLOCK, head_dim)
        scores = (
            contract(flat_queries, key_window, 1, 1).reshape(tok_rows, HEAD_BLOCK, key_width)
            * score_scale
        )
        return (flat_queries, scores)

    def attend_block(query_block):
        flat_queries, scores = block_scores(query_block)
        scores = jnp.where(visible[:, None, :], scores, MASKED)
        row_max = jnp.max(scores, axis=-1, keepdims=True)
        exp_scores = jnp.exp(scores - row_max)
        totals = jnp.sum(exp_scores, axis=-1, keepdims=True)
        weights = (
            (exp_scores / totals).astype(jnp.bfloat16).reshape(tok_rows * HEAD_BLOCK, key_width)
        )
        mixed_block = matmul(weights, value_window).reshape(tok_rows, block_width)
        return (mixed_block, (row_max + jnp.log(totals))[..., 0])

    mixed_blocks, log_totals = lax.map(attend_block, query_blocks)
    mixed_rows = mixed_blocks.transpose(1, 0, 2).reshape(tok_rows, model_width).astype(jnp.bfloat16)
    hidden = inputs + matmul(mixed_rows, w_out)
    normed_ffn_full, inverse_ffn = norm_forward(hidden, gain_ffn)
    normed_ffn = normed_ffn_full.astype(jnp.bfloat16)
    cotangent = grad_out.astype(jnp.float32)
    w_gate, w_up, w_down = (
        lax.all_gather(gate_weight, "fsdp", axis=1, tiled=True),
        lax.all_gather(up_weight, "fsdp", axis=1, tiled=True),
        lax.all_gather(down_weight, "fsdp", axis=0, tiled=True),
    )
    gate_proj = matmul(normed_ffn, w_gate)
    up_proj = matmul(normed_ffn, w_up)
    activation = (jax.nn.silu(gate_proj) * up_proj).astype(jnp.bfloat16)
    layer_out = (hidden + matmul(activation, w_down)).astype(jnp.bfloat16)
    d_activation = contract(grad_out, w_down, 1, 1)
    d_gate, d_up = swiglu_back(d_activation, gate_proj, up_proj)
    d_normed_ffn = contract(d_gate, w_gate, 1, 1) + contract(d_up, w_up, 1, 1)
    gate_up_part = lax.psum_scatter(
        jnp.concatenate(
            [contract(d_gate, normed_ffn, 0, 0), contract(d_up, normed_ffn, 0, 0)], axis=1
        ).astype(jnp.bfloat16),
        "fsdp",
        scatter_dimension=0,
        tiled=True,
    ).astype(jnp.float32)
    gate_part = gate_up_part[:, :model_width].T
    up_part = gate_up_part[:, model_width:].T
    down_part = lax.psum_scatter(
        contract(activation, grad_out, 0, 0).astype(jnp.bfloat16),
        "fsdp",
        scatter_dimension=0,
        tiled=True,
    )
    resid_ffn, ffn_gain_term = norm_backward(hidden, inverse_ffn, gain_ffn, d_normed_ffn)
    d_hidden = cotangent + resid_ffn
    d_branch = d_hidden.astype(jnp.bfloat16)
    d_mixed = contract(d_branch, w_out, 1, 1).astype(jnp.bfloat16)
    d_mixed_blocks = d_mixed.reshape(tok_rows, block_count, block_width).transpose(1, 0, 2)

    def back_block(totals, block_items):
        query_block, d_block, log_block = block_items
        flat_queries, scores = block_scores(query_block)
        probs = jnp.where(visible[:, None, :], jnp.exp(scores - log_block[..., None]), 0.0)
        d_flat = d_block.reshape(tok_rows * HEAD_BLOCK, head_dim)
        d_probs = contract(d_flat, value_window, 1, 1).reshape(tok_rows, HEAD_BLOCK, key_width)
        row_delta = jnp.sum(probs * d_probs, axis=-1, keepdims=True)
        d_scores = (
            (probs * (d_probs - row_delta))
            .astype(jnp.bfloat16)
            .reshape(tok_rows * HEAD_BLOCK, key_width)
        )
        weights = probs.astype(jnp.bfloat16).reshape(tok_rows * HEAD_BLOCK, key_width)
        d_query_block = matmul(d_scores, key_window) * score_scale
        key_total = totals[0] + contract(d_scores, flat_queries, 0, 0) * score_scale
        value_total = totals[1] + contract(weights, d_flat, 0, 0)
        return ((key_total, value_total), d_query_block.reshape(tok_rows, block_width))

    zero_window = jnp.zeros((key_width, head_dim), jnp.float32)
    window_grads, d_query_blocks = lax.scan(
        back_block, (zero_window, zero_window), (query_blocks, d_mixed_blocks, log_totals)
    )
    d_queries = d_query_blocks.transpose(1, 0, 2).reshape(tok_rows, head_count, head_dim)
    d_query_raw = (
        rotate(d_queries, cos_table[:, None], -sin_table[:, None])
        .astype(jnp.bfloat16)
        .reshape(tok_rows, model_width)
    )
    row_zeros = jnp.zeros((fsdp_size * tok_rows, head_dim), jnp.float32)
    key_term = lax.dynamic_update_slice_in_dim(row_zeros, window_grads[0], window_start, 0)
    value_term = lax.dynamic_update_slice_in_dim(row_zeros, window_grads[1], window_start, 0)
    key_sum, value_sum = (
        lax.psum_scatter(
            key_term.astype(jnp.bfloat16), "fsdp", scatter_dimension=0, tiled=True
        ).astype(jnp.float32),
        lax.psum_scatter(
            value_term.astype(jnp.bfloat16), "fsdp", scatter_dimension=0, tiled=True
        ).astype(jnp.float32),
    )
    d_key_raw = rotate(key_sum, cos_table, -sin_table).astype(jnp.bfloat16)
    d_value = value_sum.astype(jnp.bfloat16)
    d_normed = (
        contract(d_query_raw, w_query, 1, 1)
        + contract(d_key_raw, w_key, 1, 1)
        + contract(d_value, w_value, 1, 1)
    )
    resid_attn, attn_gain_term = norm_backward(inputs, inverse_attn, gain_attn, d_normed)
    input_grad = d_hidden + resid_attn
    attn_part = lax.psum_scatter(
        jnp.concatenate(
            [
                contract(normed, d_query_raw, 0, 0),
                contract(normed, d_key_raw, 0, 0),
                contract(normed, d_value, 0, 0),
                contract(mixed_rows, d_branch, 0, 0),
            ],
            axis=1,
        ).astype(jnp.bfloat16),
        "fsdp",
        scatter_dimension=0,
        tiled=True,
    )
    attn_gain_part, ffn_gain_part = (
        lax.psum_scatter(attn_gain_term, "fsdp", scatter_dimension=0, tiled=True),
        lax.psum_scatter(ffn_gain_term, "fsdp", scatter_dimension=0, tiled=True),
    )
    summed = (
        lax.psum(attn_part, "replica").astype(jnp.float32),
        lax.psum(attn_gain_part.astype(jnp.bfloat16), "replica").astype(jnp.float32),
        lax.psum(ffn_gain_part.astype(jnp.bfloat16), "replica").astype(jnp.float32),
        lax.psum(gate_part.astype(jnp.bfloat16), "replica").astype(jnp.float32),
        lax.psum(up_part.astype(jnp.bfloat16), "replica").astype(jnp.float32),
        lax.psum(down_part, "replica").astype(jnp.float32),
    )
    attn_total, attn_gain_grad, ffn_gain_grad, gate_grad, up_grad, down_grad = summed
    query_grad = attn_total[:, :model_width]
    key_grad = attn_total[:, model_width : model_width + head_dim]
    value_grad = attn_total[:, model_width + head_dim : model_width + 2 * head_dim]
    output_grad = attn_total[:, model_width + 2 * head_dim :]
    return (
        layer_out,
        input_grad,
        query_grad,
        key_grad,
        value_grad,
        output_grad,
        attn_gain_grad,
        gate_grad,
        up_grad,
        down_grad,
        ffn_gain_grad,
    )


def suits(mesh):
    fsdp_size = mesh.shape["fsdp"]
    return mesh.shape["replica"] == 4 and fsdp_size % 2 == 0 and 2048 % (128 * fsdp_size) == 0


def solution(mesh):
    return jax.shard_map(
        shards if suits(mesh) else any_shards,
        mesh=mesh,
        in_specs=(
            P(("replica", "fsdp"), None),
            P(("replica", "fsdp")),
            P(("replica", "fsdp")),
            P("fsdp", None),
            P("fsdp", None),
            P("fsdp", None),
            P("fsdp", None),
            P("fsdp"),
            P(None, "fsdp"),
            P(None, "fsdp"),
            P("fsdp", None),
            P("fsdp"),
            P(("replica", "fsdp"), None),
        ),
        out_specs=(
            P(("replica", "fsdp"), None),
            P(("replica", "fsdp"), None),
            P("fsdp", None),
            P("fsdp", None),
            P("fsdp", None),
            P("fsdp", None),
            P("fsdp"),
            P(None, "fsdp"),
            P(None, "fsdp"),
            P("fsdp", None),
            P("fsdp"),
        ),
        check_vma=False,
    )
```
